32 devices in a mesh: ctx: 8 (over y, x, core), wt: 4 (over z).
Axes of the slice: x: 2, y: 2, z: 4, core: 2. Of those that a mesh axis runs over, the one named last changes fastest.
Arguments:
- tokens: bfloat16 [2, 4, 1024, 768], P(None, 'wt', 'ctx'), may hold values from -6 to 6
- doc_lengths: int32 [2, 4, 16], P(None, 'wt'), may hold values from 1 to 512, 1024 in all within a row
- query_weight: bfloat16 [768, 768], P('wt'), may hold values from -0.3125 to 0.3125
- query_bias: bfloat16 [768], P('wt'), may hold values from -1.5 to 1.5
- key_weight: bfloat16 [768, 768], P('wt'), may hold values from -0.3125 to 0.3125
- value_weight: bfloat16 [768, 768], P('wt'), may hold values from -0.21875 to 0.21875
- value_bias: bfloat16 [768], P('wt'), may hold values from -1.5 to 1.5
- out_weight: bfloat16 [768, 768], P('wt'), may hold values from -1.25 to 1.25
- out_bias: bfloat16 [768], P('wt'), may hold values from -1.5 to 1.5
- first_gain: bfloat16 [768], P('wt'), may hold values from 0.5 to 1.5
- first_shift: bfloat16 [768], P('wt'), may hold values from -1.5 to 1.5
- inner_weight: bfloat16 [768, 3072], P('wt'), may hold values from -0.21875 to 0.21875
- inner_bias: bfloat16 [3072], P('wt'), may hold values from -1.5 to 1.5
- outer_weight: bfloat16 [3072, 768], P('wt'), may hold values from -0.109375 to 0.109375
- outer_bias: bfloat16 [768], P('wt'), may hold values from -1.5 to 1.5
- second_gain: bfloat16 [768], P('wt'), may hold values from 0.5 to 1.5
- second_shift: bfloat16 [768], P('wt'), may hold values from -1.5 to 1.5
- cotangent: bfloat16 [2, 4, 1024, 768], P(None, 'wt', 'ctx'), may hold values from -6 to 6
Outputs:
- block_output: bfloat16 [2, 4, 1024, 768], P(None, 'wt', 'ctx')
- tokens_gradient: float32 [2, 4, 1024, 768], P(None, 'wt', 'ctx')
- query_weight_gradient: float32 [768, 768], P('wt')
- query_bias_gradient: float32 [768], P('wt')
- key_weight_gradient: float32 [768, 768], P('wt')
- value_weight_gradient: float32 [768, 768], P('wt')
- value_bias_gradient: float32 [768], P('wt')
- out_weight_gradient: float32 [768, 768], P('wt')
- out_bias_gradient: float32 [768], P('wt')
- first_gain_gradient: float32 [768], P('wt')
- first_shift_gradient: float32 [768], P('wt')
- inner_weight_gradient: float32 [768, 3072], P('wt')
- inner_bias_gradient: float32 [3072], P('wt')
- outer_weight_gradient: float32 [3072, 768], P('wt')
- outer_bias_gradient: float32 [768], P('wt')
- second_gain_gradient: float32 [768], P('wt')
- second_shift_gradient: float32 [768], P('wt')
The draws below stay inside these ranges and needn't reach their ends.
Inputs may be any that keep to these rules, and one draw needn't show every extreme that they name: `doc_lengths`: each row holds the lengths of the 16 documents of one packed sequence in order; a row sums to 1024 and its longest document has exactly 512 tokens.
All inputs are finite; a program needn't handle non-finite values.
Results may differ from the reference program's by a relative error of at most 0.02.
Values may be sent and summed in bfloat16 or wider, within the bound.
No kernel may reach another device: no remote copies, remote signals or barrier semaphores. Data moves between devices by JAX's collectives and lax.ppermute only.
A program may use at most 256 MiB of HBM per device.

```python
import math
import jax
import jax.numpy as jnp
import numpy as np
from jax import lax

DIM = 768
HEADS = 12
HEAD_DIM = 64
FFN = 3072
MICRO = 2
DOCS = 16
SEQ = 1024
MAXDOC = 512
PACKS = 4


def level_of(stream_key, dims, split, least, high):
    factor_of, own = 1.0, jax.random.fold_in(stream_key, 6)
    for dim, blocks in split:
        draws = jnp.exp(jax.random.uniform(jax.random.fold_in(own, dim), (blocks,), jnp.float32, least / len(split), high / len(split)))
        factor_of = factor_of * jnp.repeat(draws, dims[dim] // blocks).reshape([-1 if axis == dim else 1 for axis in range(len(dims))])
    return factor_of


def length_profile(count, total, limit, lean):
    weights = [(1 << 20) // math.isqrt(grade ** lean) + 1 for grade in range(2, count + 1)]
    rest, holding = total - limit - (count - 1), [1] * (count - 1)
    while rest > 0:
        free = [i for i in range(count - 1) if holding[i] < limit]
        whole, budget = sum([weights[i] for i in free]), rest
        for i in free:
            more = min(limit - holding[i], max(1, budget * weights[i] // whole), rest)
            holding[i] = holding[i] + more
            rest = rest - more
    return np.array([limit] + holding)


def uneven_parts(stream_key, amount, total, most, lean):
    if amount == 2:
        one = jax.random.randint(stream_key, (), max(1, total - most), min(most, total - 1) + 1)
        return jnp.stack([one, total - one])
    sizes = jnp.asarray(length_profile(amount, total, most, lean), jnp.int32)
    twos = (amount - 1) // 2
    giver, sink = sizes[1:1 + 2 * twos:2], sizes[2:2 + 2 * twos:2]
    room = jnp.minimum(giver - 1, most - sink)
    moved = jax.random.randint(jax.random.fold_in(stream_key, 1), (twos,), 0, 1 << 20) % (room + 1)
    sizes = sizes.at[1:1 + 2 * twos:2].set(giver - moved).at[2:2 + 2 * twos:2].set(sink + moved)
    return sizes[jax.random.permutation(jax.random.fold_in(stream_key, 2), amount)]


def centred(rng, shape, deviation, most, split=(), held_as=jnp.bfloat16):
    entries = jax.random.normal(rng, shape, jnp.float32) * deviation
    if len(split) > 0:
        entries = level_of(rng, shape, split, -0.22, 0.18) * entries
    return jnp.clip(entries, min=-most, max=most).astype(held_as)


def setup_inputs(seed: int = 0) -> dict:
    seeds = jax.random.split(jax.random.key(seed), 19)
    return {
        "tokens": centred(seeds[0], (MICRO, PACKS, SEQ, DIM), 1.0, 6.0, ((1, 4), (2, 8))),
        "doc_lengths": jax.vmap(lambda own: uneven_parts(own, DOCS, SEQ, MAXDOC, 2))(jax.random.split(seeds[1], MICRO * PACKS)).reshape((MICRO, PACKS, DOCS)).astype(jnp.int32),
        "query_weight": centred(seeds[2], (DIM, DIM), (DIM // 2) ** -0.5, 0.3125, ((0, 4),)),
        "query_bias": centred(seeds[3], (DIM,), 0.3, 1.5, ((0, 4),)),
        "key_weight": centred(seeds[4], (DIM, DIM), (DIM // 2) ** -0.5, 0.3125, ((0, 4),)),
        "value_weight": centred(seeds[5], (DIM, DIM), DIM ** -0.5, 0.21875, ((0, 4),)),
        "value_bias": centred(seeds[6], (DIM,), 0.3, 1.5, ((0, 4),)),
        "out_weight": centred(seeds[7], (DIM, DIM), (DIM // 32) ** -0.5, 1.25, ((0, 4),)),
        "out_bias": centred(seeds[8], (DIM,), 0.3, 1.5, ((0, 4),)),
        "first_gain": jnp.clip(1.0 + 0.1 * jax.random.normal(seeds[9], (DIM,), jnp.float32), 0.5, 1.5).astype(jnp.bfloat16),
        "first_shift": centred(seeds[10], (DIM,), 0.3, 1.5, ((0, 4),)),
        "inner_weight": centred(seeds[11], (DIM, FFN), DIM ** -0.5, 0.21875, ((0, 4),)),
        "inner_bias": centred(seeds[12], (FFN,), 0.3, 1.5, ((0, 4),)),
        "outer_weight": centred(seeds[13], (FFN, DIM), FFN ** -0.5, 0.109375, ((0, 4),)),
        "outer_bias": centred(seeds[14], (DIM,), 0.3, 1.5, ((0, 4),)),
        "second_gain": jnp.clip(1.0 + 0.1 * jax.random.normal(seeds[15], (DIM,), jnp.float32), 0.5, 1.5).astype(jnp.bfloat16),
        "second_shift": centred(seeds[16], (DIM,), 0.3, 1.5, ((0, 4),)),
        "cotangent": centred(seeds[17], (MICRO, PACKS, SEQ, DIM), 1.0, 6.0, ((1, 4), (2, 8))),
    }


@jax.custom_vjp
def low(v):
    return lax.optimization_barrier(v.astype(jnp.bfloat16)).astype(jnp.float32)

@jax.custom_vjp
def low_back(v):
    return v

def low_keep(v):
    return (low(v), None)

def low_pass(kept, grad):
    return (grad,)

def back_keep(v):
    return (v, None)

def back_low(kept, grad):
    return (low(grad),)
low.defvjp(low_keep, low_pass)
low_back.defvjp(back_keep, back_low)
EPS = 1e-12
NEG = -1e+30
ROOT_HALF = 0.7071067811865476
HIGH = lax.Precision.HIGHEST

def normalize(rows, gain, shift):
    mean = lax.optimization_barrier(jnp.mean(rows, axis=-1, keepdims=True))
    centered = rows - mean
    spread = lax.optimization_barrier(jnp.mean(centered * centered, axis=-1, keepdims=True))
    return centered * lax.rsqrt(spread + EPS) * gain + shift

def gelu(inner):
    return 0.5 * inner * (1.0 + lax.erf(inner * ROOT_HALF))

def dense(left, right):
    return jnp.dot(left, right, precision=HIGH, preferred_element_type=jnp.float32)

def segments_of(lengths):
    lengths = lengths.astype(jnp.int32)
    starts = (jnp.cumsum(lengths, axis=-1) - lengths).astype(jnp.int32)
    positions = jnp.arange(SEQ, dtype=jnp.int32)
    found = (starts[:, None, :] <= positions[None, :, None]).astype(jnp.int32)
    return (lax.optimization_barrier(jnp.sum(found, axis=-1)) - 1).astype(jnp.int32)

def attend_pack(queries, keys, values, segment):
    block = math.gcd(SEQ, 512)
    scale = HEAD_DIM ** (-0.5)
    query_blocks = queries.reshape(SEQ // block, block, HEADS, HEAD_DIM)
    seg_blocks = segment.reshape(SEQ // block, block)

    def one_block(pair):
        query_part, seg_part = pair
        scores = low_back(jnp.einsum('qhd,khd->hqk', query_part, keys, precision=HIGH) * scale)
        mask = (seg_part[:, None] == segment[None, :])[None]
        scores = jnp.where(mask, scores, NEG)
        expd = jnp.exp(scores - lax.optimization_barrier(jnp.max(scores, axis=-1, keepdims=True)))
        probs = low(expd / lax.optimization_barrier(jnp.sum(expd, axis=-1, keepdims=True)))
        return jnp.einsum('hqk,khd->qhd', probs, values, precision=HIGH)
    mixed = lax.map(jax.checkpoint(one_block), (query_blocks, seg_blocks))
    return mixed.reshape(SEQ, HEADS, HEAD_DIM)

def layer(params, pack_tokens, segment):
    query_weight, query_bias, key_weight, value_weight, value_bias, out_weight, out_bias, first_gain, first_shift, inner_weight, inner_bias, outer_weight, outer_bias, second_gain, second_shift = params
    flat = pack_tokens.reshape(-1, DIM)
    queries = low(low_back(dense(flat, query_weight) + query_bias))
    keys = low(low_back(dense(flat, key_weight)))
    values = low(low_back(dense(flat, value_weight) + value_bias))
    shape = (pack_tokens.shape[0], SEQ, HEADS, HEAD_DIM)
    mixed = jax.vmap(attend_pack)(queries.reshape(shape), keys.reshape(shape), values.reshape(shape), segment)
    mixed = low(low_back(mixed.reshape(-1, DIM)))
    first = normalize(flat + low_back(dense(mixed, out_weight) + out_bias), first_gain, first_shift)
    inner = low_back(dense(low(first), inner_weight) + inner_bias)
    active = low(gelu(inner))
    second = normalize(first + low_back(dense(active, outer_weight) + outer_bias), second_gain, second_shift)
    return second.reshape(pack_tokens.shape)

def reference(tokens, doc_lengths, query_weight, query_bias, key_weight, value_weight, value_bias, out_weight, out_bias, first_gain, first_shift, inner_weight, inner_bias, outer_weight, outer_bias, second_gain, second_shift, cotangent):
    params = tuple((item.astype(jnp.float32) for item in (query_weight, query_bias, key_weight, value_weight, value_bias, out_weight, out_bias, first_gain, first_shift, inner_weight, inner_bias, outer_weight, outer_bias, second_gain, second_shift)))
    pack_tokens = tokens.astype(jnp.float32).reshape(-1, SEQ, DIM)
    segment = segments_of(doc_lengths.reshape(-1, DOCS))

    def apply(params_in, tokens_in):
        return layer(params_in, tokens_in, segment)
    result, pullback = jax.vjp(apply, params, pack_tokens)
    grads, token_grads = pullback(cotangent.astype(jnp.float32).reshape(-1, SEQ, DIM))
    output = result.astype(jnp.bfloat16).reshape(tokens.shape)
    return (output, token_grads.reshape(tokens.shape), grads[0], grads[1], grads[2], grads[3], grads[4], grads[5], grads[6], grads[7], grads[8], grads[9], grads[10], grads[11], grads[12], grads[13], grads[14])
```

```python
import math

import jax
import jax.numpy as jnp
from jax import lax
from jax.experimental import pallas as pl
from jax.experimental.pallas import tpu as pltpu
from jax.sharding import PartitionSpec as P

HEADS = 12
HEAD_DIM = 64


EPS = 1e-12
NEG = -1e30
ROOT_HALF = 0.7071067811865476


def for_sending(shard):

    def short(part):
        return part.astype(jnp.bfloat16) if part.dtype == jnp.float32 else part

    return jax.tree.map(short, shard)


def normalize(rows, gain, shift):
    mean = jnp.mean(rows, axis=-1, keepdims=True)
    centered = rows - mean
    spread = jnp.mean(centered * centered, axis=-1, keepdims=True)
    return centered * lax.rsqrt(spread + EPS) * gain + shift


def gelu(inner):
    return 0.5 * inner * (1.0 + lax.erf(inner * ROOT_HALF))


def segment_of(starts, positions):
    found = (starts[:, None, :] <= positions[:, :, None]).astype(jnp.int32)
    return jnp.sum(found, axis=-1) - 1


def project(inputs, weight):
    return jnp.einsum("btd,de->bte", inputs, weight, preferred_element_type=jnp.float32)


def project_back(grads, weight):
    return jnp.einsum("bte,de->btd", grads, weight, preferred_element_type=jnp.float32)


def outer_sum(inputs, grads):
    return jnp.einsum("btd,bte->de", inputs, grads, preferred_element_type=jnp.float32)


def row_sum(grads):
    return jnp.sum(grads.astype(jnp.float32), axis=(0, 1))


def heads_of(array):
    return array.reshape(array.shape[0], array.shape[1], HEADS, HEAD_DIM)


def block_loop(width, carry, visit):
    block = math.gcd(width, 512)

    def step(state, index):
        return (visit(state, index * block, block), None)

    carry, unused = lax.scan(step, carry, jnp.arange(width // block, dtype=jnp.int32))
    return carry


def reaches(starts, own_seg, first, count):
    positions = first + jnp.arange(count, dtype=jnp.int32)
    other = segment_of(starts, jnp.broadcast_to(positions, (starts.shape[0], count)))
    touch = jnp.any((other[:, 0] <= own_seg[:, -1]) & (other[:, -1] >= own_seg[:, 0]))
    return (other, touch)


def keep_state(state):
    return state


def forward_attention(queries, query_seg, starts, keys, values):
    scale = HEAD_DIM ** (-0.5)
    batch, rows = (queries.shape[0], queries.shape[1])
    query_heads = heads_of(queries)

    def forward_fold(carry, piece, start):
        key_piece, value_piece = piece

        def visit(state, offset, count):
            other, touch = reaches(starts, query_seg, offset, count)

            def compute(state):
                top, total, accum = state
                key_block = heads_of(lax.dynamic_slice_in_dim(key_piece, offset, count, 1))
                value_block = heads_of(lax.dynamic_slice_in_dim(value_piece, offset, count, 1))
                scores = (
                    jnp.einsum(
                        "bqhd,bkhd->bhqk",
                        query_heads,
                        key_block,
                        preferred_element_type=jnp.float32,
                    )
                    * scale
                )
                mask = (query_seg[:, :, None] == other[:, None, :])[:, None]
                scores = jnp.where(mask, scores, NEG)
                new_top = jnp.maximum(top, jnp.max(scores, axis=-1))
                expd = jnp.where(mask, jnp.exp(scores - new_top[..., None]), 0.0)
                factor = jnp.exp(top - new_top)
                total = total * factor + jnp.sum(expd, axis=-1)
                added = jnp.einsum(
                    "bhqk,bkhd->bqhd",
                    expd.astype(jnp.bfloat16),
                    value_block,
                    preferred_element_type=jnp.float32,
                )
                accum = accum * jnp.transpose(factor, (0, 2, 1))[..., None] + added
                return (new_top, total, accum)

            return lax.cond(touch, compute, keep_state, state)

        return block_loop(key_piece.shape[1], carry, visit)

    init = (
        jnp.full((batch, HEADS, rows), NEG, jnp.float32),
        jnp.zeros((batch, HEADS, rows), jnp.float32),
        jnp.zeros((batch, rows, HEADS, HEAD_DIM), jnp.float32),
    )
    whole = (keys, values)
    top, total, accum = forward_fold(
        init,
        (
            lax.all_gather(keys, "ctx", axis=1, tiled=True),
            lax.all_gather(values, "ctx", axis=1, tiled=True),
        ),
        jnp.int32(0),
    )
    mixed = accum / jnp.transpose(total, (0, 2, 1))[..., None]
    return (mixed, top + jnp.log(total), whole)


def query_gradient(queries, query_seg, starts, keys, values, dmixed, logsum, delta):
    scale = HEAD_DIM ** (-0.5)
    query_heads = heads_of(queries)
    grad_heads = heads_of(dmixed)

    def query_fold(carry, piece, start):
        key_piece, value_piece = piece

        def visit(state, offset, count):
            other, touch = reaches(starts, query_seg, offset, count)

            def compute(state):
                key_block = heads_of(lax.dynamic_slice_in_dim(key_piece, offset, count, 1))
                value_block = heads_of(lax.dynamic_slice_in_dim(value_piece, offset, count, 1))
                scores = (
                    jnp.einsum(
                        "bqhd,bkhd->bhqk",
                        query_heads,
                        key_block,
                        preferred_element_type=jnp.float32,
                    )
                    * scale
                )
                mask = (query_seg[:, :, None] == other[:, None, :])[:, None]
                probs = jnp.where(
                    mask, jnp.exp(jnp.where(mask, scores, NEG) - logsum[..., None]), 0.0
                )
                dprobs = jnp.einsum(
                    "bqhd,bkhd->bhqk", grad_heads, value_block, preferred_element_type=jnp.float32
                )
                dscores = (probs * (dprobs - delta[..., None])).astype(jnp.bfloat16)
                return (
                    state
                    + jnp.einsum(
                        "bhqk,bkhd->bqhd", dscores, key_block, preferred_element_type=jnp.float32
                    )
                    * scale
                )

            return lax.cond(touch, compute, keep_state, state)

        return block_loop(key_piece.shape[1], carry, visit)

    init = jnp.zeros(query_heads.shape, jnp.float32)
    return query_fold(
        init,
        (
            lax.all_gather(keys, "ctx", axis=1, tiled=True),
            lax.all_gather(values, "ctx", axis=1, tiled=True),
        ),
        jnp.int32(0),
    )


def key_gradient(keys, values, key_seg, starts, queries, dmixed, logsum, delta):
    scale = HEAD_DIM ** (-0.5)
    key_heads = heads_of(keys)
    value_heads = heads_of(values)
    every_top, every_delta = (
        lax.all_gather(logsum, "ctx", axis=2, tiled=True),
        lax.all_gather(delta, "ctx", axis=2, tiled=True),
    )

    def key_fold(carry, piece, start):
        query_piece, grad_piece = piece

        def visit(state, offset, count):
            other, touch = reaches(starts, key_seg, offset, count)

            def compute(state):
                dkeys, dvalues = state
                query_block = heads_of(lax.dynamic_slice_in_dim(query_piece, offset, count, 1))
                grad_block = heads_of(lax.dynamic_slice_in_dim(grad_piece, offset, count, 1))
                top_block = lax.dynamic_slice_in_dim(every_top, offset, count, 2)
                delta_block = lax.dynamic_slice_in_dim(every_delta, offset, count, 2)
                scores = (
                    jnp.einsum(
                        "bqhd,bkhd->bhqk",
                        query_block,
                        key_heads,
                        preferred_element_type=jnp.float32,
                    )
                    * scale
                )
                mask = (other[:, :, None] == key_seg[:, None, :])[:, None]
                probs = jnp.where(
                    mask, jnp.exp(jnp.where(mask, scores, NEG) - top_block[..., None]), 0.0
                )
                dvalues = dvalues + jnp.einsum(
                    "bhqk,bqhd->bkhd",
                    probs.astype(jnp.bfloat16),
                    grad_block,
                    preferred_element_type=jnp.float32,
                )
                dprobs = jnp.einsum(
                    "bqhd,bkhd->bhqk", grad_block, value_heads, preferred_element_type=jnp.float32
                )
                dscores = (probs * (dprobs - delta_block[..., None])).astype(jnp.bfloat16)
                dkeys = (
                    dkeys
                    + jnp.einsum(
                        "bhqk,bqhd->bkhd", dscores, query_block, preferred_element_type=jnp.float32
                    )
                    * scale
                )
                return (dkeys, dvalues)

            return lax.cond(touch, compute, keep_state, state)

        return block_loop(query_piece.shape[1], carry, visit)

    empty = jnp.zeros(key_heads.shape, jnp.float32)
    return key_fold(
        (empty, empty),
        (
            lax.all_gather(queries, "ctx", axis=1, tiled=True),
            lax.all_gather(dmixed, "ctx", axis=1, tiled=True),
        ),
        jnp.int32(0),
    )


def forward_pass(tokens, starts, weights, base):
    (
        query_weight,
        query_bias,
        key_weight,
        value_weight,
        value_bias,
        out_weight,
        out_bias,
        first_gain,
        first_shift,
        inner_weight,
        inner_bias,
        outer_weight,
        outer_bias,
        second_gain,
        second_shift,
    ) = weights
    rows = tokens.shape[1]
    positions = base + jnp.arange(rows, dtype=jnp.int32)
    query_seg = segment_of(starts, jnp.broadcast_to(positions, (tokens.shape[0], rows)))
    queries = (project(tokens, query_weight) + query_bias.astype(jnp.float32)).astype(jnp.bfloat16)
    keys = project(tokens, key_weight).astype(jnp.bfloat16)
    values = (project(tokens, value_weight) + value_bias.astype(jnp.float32)).astype(jnp.bfloat16)
    mixed, logsum, whole = forward_attention(queries, query_seg, starts, keys, values)
    mixed_low = mixed.reshape(tokens.shape).astype(jnp.bfloat16)
    first_sum = (
        tokens.astype(jnp.float32) + project(mixed_low, out_weight) + out_bias.astype(jnp.float32)
    )
    first = normalize(first_sum, first_gain.astype(jnp.float32), first_shift.astype(jnp.float32))
    first_low = first.astype(jnp.bfloat16)
    inner = project(first_low, inner_weight) + inner_bias.astype(jnp.float32)
    active = gelu(inner).astype(jnp.bfloat16)
    second_sum = first + project(active, outer_weight) + outer_bias.astype(jnp.float32)
    output = normalize(
        second_sum, second_gain.astype(jnp.float32), second_shift.astype(jnp.float32)
    ).astype(jnp.bfloat16)
    saved = (
        tokens,
        query_seg,
        queries,
        keys,
        values,
        mixed,
        logsum,
        mixed_low,
        first_sum,
        first_low,
        inner,
        active,
        second_sum,
        whole,
    )
    return (output, saved)


def backward_pass(saved, starts, weights, cotangent):
    (
        query_weight,
        query_bias,
        key_weight,
        value_weight,
        value_bias,
        out_weight,
        out_bias,
        first_gain,
        first_shift,
        inner_weight,
        inner_bias,
        outer_weight,
        outer_bias,
        second_gain,
        second_shift,
    ) = weights
    (
        tokens,
        query_seg,
        queries,
        keys,
        values,
        mixed,
        logsum,
        mixed_low,
        first_sum,
        first_low,
        inner,
        active,
        second_sum,
        whole,
    ) = saved
    unused, second_back = jax.vjp(
        normalize, second_sum, second_gain.astype(jnp.float32), second_shift.astype(jnp.float32)
    )
    dsecond, dgain_second, dshift_second = second_back(cotangent.astype(jnp.float32))
    douter = dsecond.astype(jnp.bfloat16)
    dactive = project_back(douter, outer_weight)
    unused, gelu_back = jax.vjp(gelu, inner)
    dinner = gelu_back(dactive)[0].astype(jnp.bfloat16)
    dfirst = dsecond + project_back(dinner, inner_weight)
    unused, first_back = jax.vjp(
        normalize, first_sum, first_gain.astype(jnp.float32), first_shift.astype(jnp.float32)
    )
    dfirst_sum, dgain_first, dshift_first = first_back(dfirst)
    dbranch = dfirst_sum.astype(jnp.bfloat16)
    dmixed = project_back(dbranch, out_weight).astype(jnp.bfloat16)
    delta = jnp.einsum("bqhd,bqhd->bhq", heads_of(dmixed).astype(jnp.float32), mixed)
    dqueries = query_gradient(queries, query_seg, starts, keys, values, dmixed, logsum, delta)
    dkeys, dvalues = key_gradient(keys, values, query_seg, starts, queries, dmixed, logsum, delta)
    dqueries = dqueries.reshape(tokens.shape).astype(jnp.bfloat16)
    dkeys = dkeys.reshape(tokens.shape).astype(jnp.bfloat16)
    dvalues = dvalues.reshape(tokens.shape).astype(jnp.bfloat16)
    tokens_grad = (
        dfirst_sum
        + project_back(dqueries, query_weight)
        + project_back(dkeys, key_weight)
        + project_back(dvalues, value_weight)
    )
    sums = (
        outer_sum(tokens, dqueries),
        row_sum(dqueries),
        outer_sum(tokens, dkeys),
        outer_sum(tokens, dvalues),
        row_sum(dvalues),
        outer_sum(mixed_low, dbranch),
        row_sum(dbranch),
        dgain_first,
        dshift_first,
        outer_sum(first_low, dinner),
        row_sum(dinner),
        outer_sum(active, douter),
        row_sum(douter),
        dgain_second,
        dshift_second,
    )
    return (tokens_grad, sums)


def general_device(
    tokens,
    doc_lengths,
    query_weight,
    query_bias,
    key_weight,
    value_weight,
    value_bias,
    out_weight,
    out_bias,
    first_gain,
    first_shift,
    inner_weight,
    inner_bias,
    outer_weight,
    outer_bias,
    second_gain,
    second_shift,
    cotangent,
):
    params = (
        query_weight,
        query_bias,
        key_weight,
        value_weight,
        value_bias,
        out_weight,
        out_bias,
        first_gain,
        first_shift,
        inner_weight,
        inner_bias,
        outer_weight,
        outer_bias,
        second_gain,
        second_shift,
    )
    rows = tokens.shape[2]
    base = lax.axis_index("ctx") * rows
    lengths = doc_lengths[:, 0]
    starts = jnp.cumsum(lengths, axis=-1) - lengths
    outputs = []
    token_parts = []
    sums = None
    for index in range(tokens.shape[0]):
        weights = (
            lax.all_gather(params[0], "wt", axis=0, tiled=True),
            lax.all_gather(params[1], "wt", axis=0, tiled=True),
            lax.all_gather(params[2], "wt", axis=0, tiled=True),
            lax.all_gather(params[3], "wt", axis=0, tiled=True),
            lax.all_gather(params[4], "wt", axis=0, tiled=True),
            lax.all_gather(params[5], "wt", axis=0, tiled=True),
            lax.all_gather(params[6], "wt", axis=0, tiled=True),
            lax.all_gather(params[7], "wt", axis=0, tiled=True),
            lax.all_gather(params[8], "wt", axis=0, tiled=True),
            lax.all_gather(params[9], "wt", axis=0, tiled=True),
            lax.all_gather(params[10], "wt", axis=0, tiled=True),
            lax.all_gather(params[11], "wt", axis=0, tiled=True),
            lax.all_gather(params[12], "wt", axis=0, tiled=True),
            lax.all_gather(params[13], "wt", axis=0, tiled=True),
            lax.all_gather(params[14], "wt", axis=0, tiled=True),
        )
        part_out, saved = forward_pass(
            tokens[index : index + 1, 0], starts[index : index + 1], weights, base
        )
        again = (
            lax.all_gather(params[0], "wt", axis=0, tiled=True),
            lax.all_gather(params[1], "wt", axis=0, tiled=True),
            lax.all_gather(params[2], "wt", axis=0, tiled=True),
            lax.all_gather(params[3], "wt", axis=0, tiled=True),
            lax.all_gather(params[4], "wt", axis=0, tiled=True),
            lax.all_gather(params[5], "wt", axis=0, tiled=True),
            lax.all_gather(params[6], "wt", axis=0, tiled=True),
            lax.all_gather(params[7], "wt", axis=0, tiled=True),
            lax.all_gather(params[8], "wt", axis=0, tiled=True),
            lax.all_gather(params[9], "wt", axis=0, tiled=True),
            lax.all_gather(params[10], "wt", axis=0, tiled=True),
            lax.all_gather(params[11], "wt", axis=0, tiled=True),
            lax.all_gather(params[12], "wt", axis=0, tiled=True),
            lax.all_gather(params[13], "wt", axis=0, tiled=True),
            lax.all_gather(params[14], "wt", axis=0, tiled=True),
        )
        part_grad, part_sums = backward_pass(
            saved, starts[index : index + 1], again, cotangent[index : index + 1, 0]
        )
        outputs.append(part_out)
        token_parts.append(part_grad)
        sums = part_sums if sums is None else jax.tree.map(jnp.add, sums, part_sums)
    output = jnp.concatenate(outputs, axis=0)
    tokens_grad = jnp.concatenate(token_parts, axis=0)
    shards = jax.tree.map(
        lambda part: part.astype(jnp.float32),
        lax.psum_scatter(for_sending(sums), "wt", scatter_dimension=0, tiled=True),
    )
    totals = lax.psum(shards, "ctx")
    return (output[:, None], tokens_grad[:, None]) + tuple(totals)


def flip(value, bits):
    return lax.ppermute(value, "ctx", [(i, i ^ bits) for i in range(8)])


def turn(value, step):
    return lax.ppermute(value, "wt", [(i, (i - step) % 4) for i in range(4)])


def pick(value, index, axis=0):
    return lax.dynamic_index_in_dim(value, index, axis, keepdims=False)


def pair(own, other, bit, axis=0):
    return jnp.where(bit == 0, jnp.stack([own, other], axis), jnp.stack([other, own], axis))


def place(shape, parts):
    count = len(parts)

    def kernel(*refs):
        inputs, out, sems = refs[:count], refs[count], refs[count + 1]
        ctx, own = lax.axis_index("ctx"), lax.axis_index("wt")
        copies = []
        for index, (unused, first, rows, start) in enumerate(parts):
            at = pl.multiple_of(start(ctx, own), 16)
            copies.append(
                pltpu.make_async_copy(
                    inputs[index].at[pl.ds(first, rows), :],
                    out.at[pl.ds(at, rows), :],
                    sems.at[index],
                )
            )
        for copy in copies:
            copy.start()
        for copy in copies:
            copy.wait()

    return pl.pallas_call(
        kernel,
        out_shape=jax.ShapeDtypeStruct(shape, jnp.bfloat16),
        in_specs=[pl.BlockSpec(memory_space=pl.ANY)] * count,
        out_specs=pl.BlockSpec(memory_space=pl.ANY),
        scratch_shapes=[pltpu.SemaphoreType.DMA((count,))],
    )(*[part[0] for part in parts])


def attend_kernel(near, far, weight, bias, seg_col, seg_row, qkv, mixed, logsum):
    scale = HEAD_DIM ** (-0.5)
    group = weight.shape[1] // (3 * HEAD_DIM)
    half = near.shape[0]
    block = 256
    for index, source in enumerate((near, far)):

        def project_rows(step, carry, index=index, source=source):
            at = pl.multiple_of(step * block, block)
            rows = source[pl.ds(at, block), :]
            full = jnp.dot(rows, weight[...], preferred_element_type=jnp.float32) + bias[...]
            low = full.astype(jnp.bfloat16)
            for slot in range(3 * group):
                qkv[slot, pl.ds(at + index * half, block), :] = low[
                    :, slot * HEAD_DIM : (slot + 1) * HEAD_DIM
                ]
            return carry

        lax.fori_loop(0, half // block, project_rows, 0)

    def attend_rows(step, carry):
        at = pl.multiple_of(step * block, block)
        mask = seg_col[pl.ds(at, block), :] == seg_row[...]
        sums = []
        outs = []
        for head in range(group):
            query = qkv[head, pl.ds(at, block), :]
            scores = lax.dot_general(
                query,
                qkv[group + head],
                (((1,), (1,)), ((), ())),
                preferred_element_type=jnp.float32,
            )
            scores = jnp.where(mask, scores * scale, NEG)
            top = jnp.max(scores, axis=-1, keepdims=True)
            expd = jnp.exp(scores - top)
            total = jnp.sum(expd, axis=-1, keepdims=True)
            probs = (expd * (1.0 / total)).astype(jnp.bfloat16)
            out = jnp.dot(probs, qkv[2 * group + head], preferred_element_type=jnp.float32)
            outs.append(out.astype(jnp.bfloat16))
            sums.append(top + jnp.log(total))
        mixed[pl.ds(at, block), :] = jnp.concatenate(outs, axis=1)
        logsum[pl.ds(at, block), :] = jnp.concatenate(
            sums + [jnp.zeros_like(sums[0])] * (128 - group), axis=1
        )
        return carry

    lax.fori_loop(0, mixed.shape[0] // block, attend_rows, 0)


def attend(near, far, weight, bias, seg):
    rows = 2 * near.shape[0]
    width = weight.shape[1] // 3
    return pl.pallas_call(
        attend_kernel,
        out_shape=(
            jax.ShapeDtypeStruct((3 * width // HEAD_DIM, rows, HEAD_DIM), jnp.bfloat16),
            jax.ShapeDtypeStruct((rows, width), jnp.bfloat16),
            jax.ShapeDtypeStruct((rows, 128), jnp.float32),
        ),
        compiler_params=pltpu.CompilerParams(vmem_limit_bytes=48 * 1024 * 1024),
    )(near, far, weight, bias, seg[:, None], seg[None, :])


def attend_back_kernel(
    qkv, logsum, seg_col, seg_row, part0, part1, part2, part3, grads, dkeys, dvalues
):
    scale = HEAD_DIM ** (-0.5)
    group = qkv.shape[0] // 3
    width = group * HEAD_DIM
    block = part0.shape[0]
    dkeys[...] = jnp.zeros_like(dkeys)
    dvalues[...] = jnp.zeros_like(dvalues)
    for index, part in enumerate((part0, part1, part2, part3)):
        at = index * block
        mask = seg_col[at : at + block, :] == seg_row[...]
        for head in range(group):
            query = qkv[head, at : at + block, :]
            grad = part[:, head * HEAD_DIM : (head + 1) * HEAD_DIM]
            keys = qkv[group + head]
            scores = lax.dot_general(
                query, keys, (((1,), (1,)), ((), ())), preferred_element_type=jnp.float32
            )
            scores = jnp.where(mask, scores * scale, NEG)
            probs = jnp.exp(scores - logsum[at : at + block, head : head + 1])
            dprobs = lax.dot_general(
                grad,
                qkv[2 * group + head],
                (((1,), (1,)), ((), ())),
                preferred_element_type=jnp.float32,
            )
            delta = jnp.sum(probs * dprobs, axis=-1, keepdims=True)
            dscores = (probs * (dprobs - delta)).astype(jnp.bfloat16)
            dquery = jnp.dot(dscores, keys, preferred_element_type=jnp.float32) * scale
            grads[at : at + block, head * HEAD_DIM : (head + 1) * HEAD_DIM] = dquery.astype(
                jnp.bfloat16
            )
            dkeys[head] += lax.dot_general(
                dscores, query, (((0,), (0,)), ((), ())), preferred_element_type=jnp.float32
            )
            dvalues[head] += lax.dot_general(
                probs.astype(jnp.bfloat16),
                grad,
                (((0,), (0,)), ((), ())),
                preferred_element_type=jnp.float32,
            )
    for head in range(group):
        lanes = slice(width + head * HEAD_DIM, width + (head + 1) * HEAD_DIM)
        grads[:, lanes] = (dkeys[head] * scale).astype(jnp.bfloat16)
        lanes = slice(2 * width + head * HEAD_DIM, 2 * width + (head + 1) * HEAD_DIM)
        grads[:, lanes] = dvalues[head].astype(jnp.bfloat16)


def attend_back(qkv, logsum, seg, parts):
    slots, rows, unused = qkv.shape
    return pl.pallas_call(
        attend_back_kernel,
        out_shape=jax.ShapeDtypeStruct((rows, slots * HEAD_DIM), jnp.bfloat16),
        scratch_shapes=[
            pltpu.VMEM((slots // 3, rows, HEAD_DIM), jnp.float32),
            pltpu.VMEM((slots // 3, rows, HEAD_DIM), jnp.float32),
        ],
        compiler_params=pltpu.CompilerParams(vmem_limit_bytes=48 * 1024 * 1024),
    )(qkv, logsum, seg[:, None], seg[None, :], *parts)


def dot(left, right):
    return jnp.dot(left, right, preferred_element_type=jnp.float32)


def dot_back(left, right):
    return lax.dot_general(
        left, right, (((1,), (1,)), ((), ())), preferred_element_type=jnp.float32
    )


def dot_sum(left, right):
    return lax.dot_general(
        left, right, (((0,), (0,)), ((), ())), preferred_element_type=jnp.float32
    )


def norm_parts(rows):
    mean = jnp.mean(rows, axis=-1, keepdims=True)
    centered = rows - mean
    spread = jnp.mean(centered * centered, axis=-1, keepdims=True)
    root = lax.rsqrt(spread + EPS)
    return centered * root, root


def norm_back(upstream, normed, root, gain):
    grad = upstream * gain
    mean = jnp.mean(grad, axis=-1, keepdims=True)
    along = jnp.mean(grad * normed, axis=-1, keepdims=True)
    return root * (grad - mean - normed * along)


def short(value):
    return value.astype(jnp.bfloat16)


def wide(value):
    return value.astype(jnp.float32)


def add_sent(kept, received):
    return short(wide(kept) + wide(received))


def sum_owned(pieces, own):
    total = wide(pick(pieces, own))
    for step in (1, 2, 3):
        total = total + wide(turn(pick(pieces, (own - step) % 4), step))
    return short(total)


def plane_device(
    tokens,
    doc_lengths,
    query_weight,
    query_bias,
    key_weight,
    value_weight,
    value_bias,
    out_weight,
    out_bias,
    first_gain,
    first_shift,
    inner_weight,
    inner_bias,
    outer_weight,
    outer_bias,
    second_gain,
    second_shift,
    cotangent,
):
    ctx, own = lax.axis_index("ctx"), lax.axis_index("wt")
    core, x, y, group = ctx & 1, (ctx >> 1) & 1, ctx >> 2, ctx & 3
    quarter = 2 * y + x
    rows, dim = tokens.shape[2], tokens.shape[3]
    shard = query_weight.shape[0]
    hidden = outer_weight.shape[0]
    half = hidden // 2
    width = dim // 4

    mine = jnp.concatenate([pick(tokens[:, 0], y), flip(pick(tokens[:, 0], 1 - y), 4)])
    near = jnp.concatenate([mine, flip(mine, 2)])
    far = flip(near, 1)

    slices = [
        lax.dynamic_slice_in_dim(w, group * width, width, 1)
        for w in (query_weight, key_weight, value_weight)
    ]
    heads_own = jnp.concatenate(slices, axis=1)
    heads_half = pick(heads_own.reshape(2, shard // 2, 3 * width), y)
    parts = [(heads_own, 0, shard, lambda c, z: shard * z)]
    for step in (1, 2, 3):
        got = turn(heads_half, step)
        parts.append(
            (
                got,
                0,
                shard // 2,
                lambda c, z, s=step: shard * ((z + s) % 4) + (shard // 2) * (c >> 2),
            )
        )
        parts.append(
            (
                flip(got, 4),
                0,
                shard // 2,
                lambda c, z, s=step: shard * ((z + s) % 4) + (shard // 2) * (1 - (c >> 2)),
            )
        )
    heads_weight = place((dim, 3 * width), parts)

    packed = jnp.concatenate(
        [
            v.reshape(-1, shard)
            for v in (
                query_bias,
                value_bias,
                out_bias,
                first_gain,
                first_shift,
                outer_bias,
                second_gain,
                second_shift,
                inner_bias,
            )
        ]
    )
    rel = jnp.stack([packed] + [turn(packed, step) for step in (1, 2, 3)])
    vectors = wide(lax.dynamic_slice_in_dim(jnp.concatenate([rel, rel]), (4 - own) % 4, 4))
    rest = [vectors[:, i].reshape(dim) for i in range(2, 8)]
    out_b, gain1, shift1, outer_b, gain2, shift2 = rest
    mine_b = pick(vectors, group)
    heads_bias = jnp.concatenate([mine_b[0], jnp.zeros_like(mine_b[0]), mine_b[1]])[None]
    inner_b = pick(vectors[:, 8:].reshape(4, 2, half), core, 1).reshape(4 * half)

    inner_half = pick(inner_weight.reshape(shard, 4, 2, half), core, 2).reshape(shard, 4 * half)
    outer_half = lax.dynamic_slice_in_dim(outer_weight, core * half, half, 0)
    out_send = pick(out_weight.reshape(4, shard // 4, dim), quarter)
    inner_send = pick(inner_half.reshape(4, shard // 4, 4 * half), quarter)
    outer_send = pick(outer_half.reshape(4, half // 4, dim), quarter)

    def quarters(piece, size, at, first, second):
        one = flip(piece, 2 * first)
        two = flip(piece, 2 * second)
        both = flip(one, 2 * second)
        found = []
        for value, bits in ((piece, 0), (one, first), (two, second), (both, first | second)):
            found.append(
                (value, 0, size, lambda c, z, b=bits: at(c, z) + size * (((c >> 1) & 3) ^ b))
            )
        return found

    def spread(piece, whole, size, at, first, second):
        found = [(whole, 0, 4 * size, lambda c, z: at(c, z))]
        for step in (1, 2, 3):
            found += quarters(
                turn(piece, step), size, lambda c, z, s=step: at(c, (z + s) % 4), first, second
            )
        return found

    out_parts = spread(
        out_send, out_weight, shard // 4, lambda c, z: shard * (z ^ (c & 3)), 1, 2
    )
    inner_parts = spread(inner_send, inner_half, shard // 4, lambda c, z: shard * z, 2, 1)
    outer_parts = spread(outer_send, outer_half, half // 4, lambda c, z: half * z, 1, 2)
    out_full = place((dim, dim), out_parts)
    inner_full = place((dim, 4 * half), inner_parts)
    outer_full = place((4 * half, dim), outer_parts)

    lengths = pick(doc_lengths[:, 0], y)
    starts = jnp.cumsum(lengths) - lengths
    index = jnp.arange(8 * rows, dtype=jnp.int32)
    code = index // rows
    code = (code >> 2) | (code & 2) | ((code & 1) << 2)
    positions = (ctx ^ code) * rows + index % rows
    seg = jnp.sum((starts[None, :] <= positions[:, None]).astype(jnp.int32), axis=-1) - 1

    qkv, mixed, logsum = attend(near, far, heads_weight, heads_bias, seg)

    def to_owner(value):
        blocks = value.reshape(4, 2 * rows, width)
        return [blocks[0]] + [flip(blocks[2 * (b & 1) + (b >> 1)], b) for b in (1, 2, 3)]

    mixed_own = jnp.concatenate(to_owner(mixed), axis=1)
    first_sum = wide(mine) + dot(mixed_own, out_full) + out_b
    normed1, root1 = norm_parts(first_sum)
    first = normed1 * gain1 + shift1
    first_low = short(first)
    first_both = jnp.concatenate([first_low, flip(first_low, 1)])
    inner = dot(first_both, inner_full) + inner_b
    active = short(gelu(inner))
    second_part = dot(active, outer_full)
    second_sum = (
        first + outer_b + second_part[: 2 * rows] + flip(second_part[2 * rows :], 1)
    )
    normed2, root2 = norm_parts(second_sum)
    output_own = short(normed2 * gain2 + shift2)
    output = pair(output_own[:rows], flip(output_own[rows:], 4), y)

    upstream = wide(
        jnp.concatenate([pick(cotangent[:, 0], y), flip(pick(cotangent[:, 0], 1 - y), 4)])
    )
    dsecond = norm_back(upstream, normed2, root2, gain2)
    douter = short(dsecond)
    dgain2, dshift2 = jnp.sum(upstream * normed2, axis=0), jnp.sum(upstream, axis=0)
    douter_b = jnp.sum(wide(douter), axis=0)
    douter_both = jnp.concatenate([douter, flip(douter, 1)])
    dactive = dot_back(douter_both, outer_full)
    unused, gelu_back = jax.vjp(gelu, inner)
    dinner = short(gelu_back(dactive)[0])
    dfirst_part = dot_back(dinner, inner_full)
    dfirst = dsecond + dfirst_part[: 2 * rows] + flip(dfirst_part[2 * rows :], 1)
    dinner_w = short(dot_sum(first_both, dinner))
    douter_w = short(dot_sum(active, douter_both))
    dinner_b = jnp.sum(wide(dinner), axis=0)

    dfirst_sum = norm_back(dfirst, normed1, root1, gain1)
    dbranch = short(dfirst_sum)
    dgain1, dshift1 = jnp.sum(dfirst * normed1, axis=0), jnp.sum(dfirst, axis=0)
    dout_b = jnp.sum(wide(dbranch), axis=0)
    dmixed_own = short(dot_back(dbranch, out_full))
    dparts = [dmixed_own[:, b * width : (b + 1) * width] for b in range(4)]
    dparts = [dparts[0]] + [flip(dparts[b], b) for b in (1, 2, 3)]
    dqkv = attend_back(qkv, logsum, seg, [dparts[0], dparts[2], dparts[1], dparts[3]])

    dout_w = short(dot_sum(mixed_own, dbranch)).reshape(4, shard, dim)
    dout_w = jnp.where(
        (group & 1) == 0, dout_w, dout_w.reshape(2, 2, shard, dim)[:, ::-1].reshape(dout_w.shape)
    )
    dout_w = jnp.where(
        (group & 2) == 0, dout_w, dout_w.reshape(2, 2, shard, dim)[::-1].reshape(dout_w.shape)
    )

    dtokens = dot_back(dqkv, heads_weight)
    dtokens = dtokens[: 4 * rows] + wide(flip(short(dtokens[4 * rows :]), 1))
    dtokens = dtokens[: 2 * rows] + wide(flip(short(dtokens[2 * rows :]), 2)) + dfirst_sum
    tokens_grad = pair(dtokens[:rows], wide(flip(short(dtokens[rows:]), 4)), y)

    both = jnp.concatenate([near, far])
    dheads = short(dot_sum(both, dqkv)).reshape(4, shard, 3 * width)
    dheads = sum_owned(dheads, own)
    dheads = add_sent(dheads, flip(dheads, 4))
    dheads = pair(dheads, flip(dheads, 2), x)
    dheads = pair(dheads, flip(dheads, 1), core)
    dheads = wide(jnp.transpose(dheads.reshape(2, 2, shard, 3, width), (3, 2, 1, 0, 4)))
    dheads = dheads.reshape(3, shard, dim)
    dheads_b = jnp.sum(wide(dqkv), axis=0).reshape(3, width)
    dheads_b = dheads_b + turn(dheads_b, 1) + turn(dheads_b, 2) + turn(dheads_b, 3)
    dheads_b = dheads_b + flip(dheads_b, 4)
    dheads_b = pair(dheads_b, flip(dheads_b, 2), x)
    dheads_b = pair(dheads_b, flip(dheads_b, 1), core)
    dheads_b = pick(jnp.transpose(dheads_b, (1, 0, 2, 3)).reshape(4, 3, width), own)

    def shares(value, first, second):
        part = value.reshape(4, 2, 2, -1, value.shape[-1])
        bits = {1: x, 2: y}
        axes = {1: 2, 2: 1}
        at = axes[first]
        part = add_sent(
            pick(part, bits[first], at), flip(pick(part, 1 - bits[first], at), 2 * first)
        )
        part = add_sent(
            pick(part, bits[second], 1), flip(pick(part, 1 - bits[second], 1), 2 * second)
        )
        return sum_owned(part, own)

    def joined(piece, first, second):
        bits = {1: x, 2: y}
        piece = pair(piece, flip(piece, 2 * first), bits[first])
        piece = pair(piece, flip(piece, 2 * second), bits[second])
        if first == 2:
            piece = jnp.swapaxes(piece, 0, 1)
        return piece.reshape(-1, piece.shape[-1])

    dinner_w = joined(shares(dinner_w, 1, 2), 1, 2)
    dinner_w = pair(
        dinner_w.reshape(shard, 4, half), flip(dinner_w, 1).reshape(shard, 4, half), core, 2
    )
    dinner_w = wide(dinner_w.reshape(shard, 8 * half))
    douter_w = joined(shares(douter_w, 2, 1), 2, 1)
    douter_w = wide(pair(douter_w, flip(douter_w, 1), core).reshape(hidden, dim))
    dout_w = dout_w.reshape(dim, dim)
    dout_w = add_sent(dout_w, flip(dout_w, 1))
    dout_w = wide(joined(shares(dout_w, 1, 2), 1, 2))

    sums = jnp.stack([dout_b, dgain1, dshift1, douter_b, dgain2, dshift2])
    sums = sums + flip(sums, 1)
    inner_sums = pair(dinner_b.reshape(4, half), flip(dinner_b.reshape(4, half), 1), core, 1)
    sums = jnp.concatenate([sums, inner_sums.reshape(-1, dim)])
    sums = sums + flip(sums, 2)
    sums = sums + flip(sums, 4)
    sums = sums + turn(sums, 1) + turn(sums, 2) + turn(sums, 3)
    small = lax.dynamic_slice_in_dim(sums[:6], own * shard, shard, 1)
    dinner_b = pick(sums[6:].reshape(4, hidden), own)

    return (
        output[:, None],
        tokens_grad[:, None],
        dheads[0],
        dheads_b[0],
        dheads[1],
        dheads[2],
        dheads_b[2],
        dout_w,
        small[0],
        small[1],
        small[2],
        dinner_w,
        dinner_b,
        douter_w,
        small[3],
        small[4],
        small[5],
    )


def solution(mesh):
    placed = (
        P(None, "wt", "ctx", None),
        P(None, "wt", None),
        P("wt", None),
        P("wt"),
        P("wt", None),
        P("wt", None),
        P("wt"),
        P("wt", None),
        P("wt"),
        P("wt"),
        P("wt"),
        P("wt", None),
        P("wt"),
        P("wt", None),
        P("wt"),
        P("wt"),
        P("wt"),
        P(None, "wt", "ctx", None),
    )
    fits = mesh.shape["ctx"] == 8 and mesh.shape["wt"] == 4
    return jax.shard_map(
        plane_device if fits else general_device,
        mesh=mesh,
        in_specs=placed,
        out_specs=(
            P(None, "wt", "ctx", None),
            P(None, "wt", "ctx", None),
            P("wt", None),
            P("wt"),
            P("wt", None),
            P("wt", None),
            P("wt"),
            P("wt", None),
            P("wt"),
            P("wt"),
            P("wt"),
            P("wt", None),
            P("wt"),
            P("wt", None),
            P("wt"),
            P("wt"),
            P("wt"),
        ),
        check_vma=False,
    )
```

```python
import math

import jax
import jax.numpy as jnp
from jax import lax
from jax.experimental import pallas as pl
from jax.experimental.pallas import tpu as pltpu
from jax.sharding import PartitionSpec as P

HEADS = 12
HEAD_DIM = 64


EPS = 1e-12
NEG = -1e30
ROOT_HALF = 0.7071067811865476


def for_sending(shard):

    def short(part):
        return part.astype(jnp.bfloat16) if part.dtype == jnp.float32 else part

    return jax.tree.map(short, shard)


def normalize(rows, gain, shift):
    mean = jnp.mean(rows, axis=-1, keepdims=True)
    centered = rows - mean
    spread = jnp.mean(centered * centered, axis=-1, keepdims=True)
    return centered * lax.rsqrt(spread + EPS) * gain + shift


def gelu(inner):
    return 0.5 * inner * (1.0 + lax.erf(inner * ROOT_HALF))


def segment_of(starts, positions):
    found = (starts[:, None, :] <= positions[:, :, None]).astype(jnp.int32)
    return jnp.sum(found, axis=-1) - 1


def project(inputs, weight):
    return jnp.einsum("btd,de->bte", inputs, weight, preferred_element_type=jnp.float32)


def project_back(grads, weight):
    return jnp.einsum("bte,de->btd", grads, weight, preferred_element_type=jnp.float32)


def outer_sum(inputs, grads):
    return jnp.einsum("btd,bte->de", inputs, grads, preferred_element_type=jnp.float32)


def row_sum(grads):
    return jnp.sum(grads.astype(jnp.float32), axis=(0, 1))


def heads_of(array):
    return array.reshape(array.shape[0], array.shape[1], HEADS, HEAD_DIM)


def block_loop(width, carry, visit):
    block = math.gcd(width, 512)

    def step(state, index):
        return (visit(state, index * block, block), None)

    carry, unused = lax.scan(step, carry, jnp.arange(width // block, dtype=jnp.int32))
    return carry


def reaches(starts, own_seg, first, count):
    positions = first + jnp.arange(count, dtype=jnp.int32)
    other = segment_of(starts, jnp.broadcast_to(positions, (starts.shape[0], count)))
    touch = jnp.any((other[:, 0] <= own_seg[:, -1]) & (other[:, -1] >= own_seg[:, 0]))
    return (other, touch)


def keep_state(state):
    return state


def forward_attention(queries, query_seg, starts, keys, values):
    scale = HEAD_DIM ** (-0.5)
    batch, rows = (queries.shape[0], queries.shape[1])
    query_heads = heads_of(queries)

    def forward_fold(carry, piece, start):
        key_piece, value_piece = piece

        def visit(state, offset, count):
            other, touch = reaches(starts, query_seg, offset, count)

            def compute(state):
                top, total, accum = state
                key_block = heads_of(lax.dynamic_slice_in_dim(key_piece, offset, count, 1))
                value_block = heads_of(lax.dynamic_slice_in_dim(value_piece, offset, count, 1))
                scores = (
                    jnp.einsum(
                        "bqhd,bkhd->bhqk",
                        query_heads,
                        key_block,
                        preferred_element_type=jnp.float32,
                    )
                    * scale
                )
                mask = (query_seg[:, :, None] == other[:, None, :])[:, None]
                scores = jnp.where(mask, scores, NEG)
                new_top = jnp.maximum(top, jnp.max(scores, axis=-1))
                expd = jnp.where(mask, jnp.exp(scores - new_top[..., None]), 0.0)
                factor = jnp.exp(top - new_top)
                total = total * factor + jnp.sum(expd, axis=-1)
                added = jnp.einsum(
                    "bhqk,bkhd->bqhd",
                    expd.astype(jnp.bfloat16),
                    value_block,
                    preferred_element_type=jnp.float32,
                )
                accum = accum * jnp.transpose(factor, (0, 2, 1))[..., None] + added
                return (new_top, total, accum)

            return lax.cond(touch, compute, keep_state, state)

        return block_loop(key_piece.shape[1], carry, visit)

    init = (
        jnp.full((batch, HEADS, rows), NEG, jnp.float32),
        jnp.zeros((batch, HEADS, rows), jnp.float32),
        jnp.zeros((batch, rows, HEADS, HEAD_DIM), jnp.float32),
    )
    whole = (keys, values)
    top, total, accum = forward_fold(
        init,
        (
            lax.all_gather(keys, "ctx", axis=1, tiled=True),
            lax.all_gather(values, "ctx", axis=1, tiled=True),
        ),
        jnp.int32(0),
    )
    mixed = accum / jnp.transpose(total, (0, 2, 1))[..., None]
    return (mixed, top + jnp.log(total), whole)


def query_gradient(queries, query_seg, starts, keys, values, dmixed, logsum, delta):
    scale = HEAD_DIM ** (-0.5)
    query_heads = heads_of(queries)
    grad_heads = heads_of(dmixed)

    def query_fold(carry, piece, start):
        key_piece, value_piece = piece

        def visit(state, offset, count):
            other, touch = reaches(starts, query_seg, offset, count)

            def compute(state):
                key_block = heads_of(lax.dynamic_slice_in_dim(key_piece, offset, count, 1))
                value_block = heads_of(lax.dynamic_slice_in_dim(value_piece, offset, count, 1))
                scores = (
                    jnp.einsum(
                        "bqhd,bkhd->bhqk",
                        query_heads,
                        key_block,
                        preferred_element_type=jnp.float32,
                    )
                    * scale
                )
                mask = (query_seg[:, :, None] == other[:, None, :])[:, None]
                probs = jnp.where(
                    mask, jnp.exp(jnp.where(mask, scores, NEG) - logsum[..., None]), 0.0
                )
                dprobs = jnp.einsum(
                    "bqhd,bkhd->bhqk", grad_heads, value_block, preferred_element_type=jnp.float32
                )
                dscores = (probs * (dprobs - delta[..., None])).astype(jnp.bfloat16)
                return (
                    state
                    + jnp.einsum(
                        "bhqk,bkhd->bqhd", dscores, key_block, preferred_element_type=jnp.float32
                    )
                    * scale
                )

            return lax.cond(touch, compute, keep_state, state)

        return block_loop(key_piece.shape[1], carry, visit)

    init = jnp.zeros(query_heads.shape, jnp.float32)
    return query_fold(
        init,
        (
            lax.all_gather(keys, "ctx", axis=1, tiled=True),
            lax.all_gather(values, "ctx", axis=1, tiled=True),
        ),
        jnp.int32(0),
    )


def key_gradient(keys, values, key_seg, starts, queries, dmixed, logsum, delta):
    scale = HEAD_DIM ** (-0.5)
    key_heads = heads_of(keys)
    value_heads = heads_of(values)
    every_top, every_delta = (
        lax.all_gather(logsum, "ctx", axis=2, tiled=True),
        lax.all_gather(delta, "ctx", axis=2, tiled=True),
    )

    def key_fold(carry, piece, start):
        query_piece, grad_piece = piece

        def visit(state, offset, count):
            other, touch = reaches(starts, key_seg, offset, count)

            def compute(state):
                dkeys, dvalues = state
                query_block = heads_of(lax.dynamic_slice_in_dim(query_piece, offset, count, 1))
                grad_block = heads_of(lax.dynamic_slice_in_dim(grad_piece, offset, count, 1))
                top_block = lax.dynamic_slice_in_dim(every_top, offset, count, 2)
                delta_block = lax.dynamic_slice_in_dim(every_delta, offset, count, 2)
                scores = (
                    jnp.einsum(
                        "bqhd,bkhd->bhqk",
                        query_block,
                        key_heads,
                        preferred_element_type=jnp.float32,
                    )
                    * scale
                )
                mask = (other[:, :, None] == key_seg[:, None, :])[:, None]
                probs = jnp.where(
                    mask, jnp.exp(jnp.where(mask, scores, NEG) - top_block[..., None]), 0.0
                )
                dvalues = dvalues + jnp.einsum(
                    "bhqk,bqhd->bkhd",
                    probs.astype(jnp.bfloat16),
                    grad_block,
                    preferred_element_type=jnp.float32,
                )
                dprobs = jnp.einsum(
                    "bqhd,bkhd->bhqk", grad_block, value_heads, preferred_element_type=jnp.float32
                )
                dscores = (probs * (dprobs - delta_block[..., None])).astype(jnp.bfloat16)
                dkeys = (
                    dkeys
                    + jnp.einsum(
                        "bhqk,bqhd->bkhd", dscores, query_block, preferred_element_type=jnp.float32
                    )
                    * scale
                )
                return (dkeys, dvalues)

            return lax.cond(touch, compute, keep_state, state)

        return block_loop(query_piece.shape[1], carry, visit)

    empty = jnp.zeros(key_heads.shape, jnp.float32)
    return key_fold(
        (empty, empty),
        (
            lax.all_gather(queries, "ctx", axis=1, tiled=True),
            lax.all_gather(dmixed, "ctx", axis=1, tiled=True),
        ),
        jnp.int32(0),
    )


def forward_pass(tokens, starts, weights, base):
    (
        query_weight,
        query_bias,
        key_weight,
        value_weight,
        value_bias,
        out_weight,
        out_bias,
        first_gain,
        first_shift,
        inner_weight,
        inner_bias,
        outer_weight,
        outer_bias,
        second_gain,
        second_shift,
    ) = weights
    rows = tokens.shape[1]
    positions = base + jnp.arange(rows, dtype=jnp.int32)
    query_seg = segment_of(starts, jnp.broadcast_to(positions, (tokens.shape[0], rows)))
    queries = (project(tokens, query_weight) + query_bias.astype(jnp.float32)).astype(jnp.bfloat16)
    keys = project(tokens, key_weight).astype(jnp.bfloat16)
    values = (project(tokens, value_weight) + value_bias.astype(jnp.float32)).astype(jnp.bfloat16)
    mixed, logsum, whole = forward_attention(queries, query_seg, starts, keys, values)
    mixed_low = mixed.reshape(tokens.shape).astype(jnp.bfloat16)
    first_sum = (
        tokens.astype(jnp.float32) + project(mixed_low, out_weight) + out_bias.astype(jnp.float32)
    )
    first = normalize(first_sum, first_gain.astype(jnp.float32), first_shift.astype(jnp.float32))
    first_low = first.astype(jnp.bfloat16)
    inner = project(first_low, inner_weight) + inner_bias.astype(jnp.float32)
    active = gelu(inner).astype(jnp.bfloat16)
    second_sum = first + project(active, outer_weight) + outer_bias.astype(jnp.float32)
    output = normalize(
        second_sum, second_gain.astype(jnp.float32), second_shift.astype(jnp.float32)
    ).astype(jnp.bfloat16)
    saved = (
        tokens,
        query_seg,
        queries,
        keys,
        values,
        mixed,
        logsum,
        mixed_low,
        first_sum,
        first_low,
        inner,
        active,
        second_sum,
        whole,
    )
    return (output, saved)


def backward_pass(saved, starts, weights, cotangent):
    (
        query_weight,
        query_bias,
        key_weight,
        value_weight,
        value_bias,
        out_weight,
        out_bias,
        first_gain,
        first_shift,
        inner_weight,
        inner_bias,
        outer_weight,
        outer_bias,
        second_gain,
        second_shift,
    ) = weights
    (
        tokens,
        query_seg,
        queries,
        keys,
        values,
        mixed,
        logsum,
        mixed_low,
        first_sum,
        first_low,
        inner,
        active,
        second_sum,
        whole,
    ) = saved
    unused, second_back = jax.vjp(
        normalize, second_sum, second_gain.astype(jnp.float32), second_shift.astype(jnp.float32)
    )
    dsecond, dgain_second, dshift_second = second_back(cotangent.astype(jnp.float32))
    douter = dsecond.astype(jnp.bfloat16)
    dactive = project_back(douter, outer_weight)
    unused, gelu_back = jax.vjp(gelu, inner)
    dinner = gelu_back(dactive)[0].astype(jnp.bfloat16)
    dfirst = dsecond + project_back(dinner, inner_weight)
    unused, first_back = jax.vjp(
        normalize, first_sum, first_gain.astype(jnp.float32), first_shift.astype(jnp.float32)
    )
    dfirst_sum, dgain_first, dshift_first = first_back(dfirst)
    dbranch = dfirst_sum.astype(jnp.bfloat16)
    dmixed = project_back(dbranch, out_weight).astype(jnp.bfloat16)
    delta = jnp.einsum("bqhd,bqhd->bhq", heads_of(dmixed).astype(jnp.float32), mixed)
    dqueries = query_gradient(queries, query_seg, starts, keys, values, dmixed, logsum, delta)
    dkeys, dvalues = key_gradient(keys, values, query_seg, starts, queries, dmixed, logsum, delta)
    dqueries = dqueries.reshape(tokens.shape).astype(jnp.bfloat16)
    dkeys = dkeys.reshape(tokens.shape).astype(jnp.bfloat16)
    dvalues = dvalues.reshape(tokens.shape).astype(jnp.bfloat16)
    tokens_grad = (
        dfirst_sum
        + project_back(dqueries, query_weight)
        + project_back(dkeys, key_weight)
        + project_back(dvalues, value_weight)
    )
    sums = (
        outer_sum(tokens, dqueries),
        row_sum(dqueries),
        outer_sum(tokens, dkeys),
        outer_sum(tokens, dvalues),
        row_sum(dvalues),
        outer_sum(mixed_low, dbranch),
        row_sum(dbranch),
        dgain_first,
        dshift_first,
        outer_sum(first_low, dinner),
        row_sum(dinner),
        outer_sum(active, douter),
        row_sum(douter),
        dgain_second,
        dshift_second,
    )
    return (tokens_grad, sums)


def general_device(
    tokens,
    doc_lengths,
    query_weight,
    query_bias,
    key_weight,
    value_weight,
    value_bias,
    out_weight,
    out_bias,
    first_gain,
    first_shift,
    inner_weight,
    inner_bias,
    outer_weight,
    outer_bias,
    second_gain,
    second_shift,
    cotangent,
):
    params = (
        query_weight,
        query_bias,
        key_weight,
        value_weight,
        value_bias,
        out_weight,
        out_bias,
        first_gain,
        first_shift,
        inner_weight,
        inner_bias,
        outer_weight,
        outer_bias,
        second_gain,
        second_shift,
    )
    rows = tokens.shape[2]
    base = lax.axis_index("ctx") * rows
    lengths = doc_lengths[:, 0]
    starts = jnp.cumsum(lengths, axis=-1) - lengths
    outputs = []
    token_parts = []
    sums = None
    for index in range(tokens.shape[0]):
        weights = (
            lax.all_gather(params[0], "wt", axis=0, tiled=True),
            lax.all_gather(params[1], "wt", axis=0, tiled=True),
            lax.all_gather(params[2], "wt", axis=0, tiled=True),
            lax.all_gather(params[3], "wt", axis=0, tiled=True),
            lax.all_gather(params[4], "wt", axis=0, tiled=True),
            lax.all_gather(params[5], "wt", axis=0, tiled=True),
            lax.all_gather(params[6], "wt", axis=0, tiled=True),
            lax.all_gather(params[7], "wt", axis=0, tiled=True),
            lax.all_gather(params[8], "wt", axis=0, tiled=True),
            lax.all_gather(params[9], "wt", axis=0, tiled=True),
            lax.all_gather(params[10], "wt", axis=0, tiled=True),
            lax.all_gather(params[11], "wt", axis=0, tiled=True),
            lax.all_gather(params[12], "wt", axis=0, tiled=True),
            lax.all_gather(params[13], "wt", axis=0, tiled=True),
            lax.all_gather(params[14], "wt", axis=0, tiled=True),
        )
        part_out, saved = forward_pass(
            tokens[index : index + 1, 0], starts[index : index + 1], weights, base
        )
        again = (
            lax.all_gather(params[0], "wt", axis=0, tiled=True),
            lax.all_gather(params[1], "wt", axis=0, tiled=True),
            lax.all_gather(params[2], "wt", axis=0, tiled=True),
            lax.all_gather(params[3], "wt", axis=0, tiled=True),
            lax.all_gather(params[4], "wt", axis=0, tiled=True),
            lax.all_gather(params[5], "wt", axis=0, tiled=True),
            lax.all_gather(params[6], "wt", axis=0, tiled=True),
            lax.all_gather(params[7], "wt", axis=0, tiled=True),
            lax.all_gather(params[8], "wt", axis=0, tiled=True),
            lax.all_gather(params[9], "wt", axis=0, tiled=True),
            lax.all_gather(params[10], "wt", axis=0, tiled=True),
            lax.all_gather(params[11], "wt", axis=0, tiled=True),
            lax.all_gather(params[12], "wt", axis=0, tiled=True),
            lax.all_gather(params[13], "wt", axis=0, tiled=True),
            lax.all_gather(params[14], "wt", axis=0, tiled=True),
        )
        part_grad, part_sums = backward_pass(
            saved, starts[index : index + 1], again, cotangent[index : index + 1, 0]
        )
        outputs.append(part_out)
        token_parts.append(part_grad)
        sums = part_sums if sums is None else jax.tree.map(jnp.add, sums, part_sums)
    output = jnp.concatenate(outputs, axis=0)
    tokens_grad = jnp.concatenate(token_parts, axis=0)
    shards = jax.tree.map(
        lambda part: part.astype(jnp.float32),
        lax.psum_scatter(for_sending(sums), "wt", scatter_dimension=0, tiled=True),
    )
    totals = lax.psum(shards, "ctx")
    return (output[:, None], tokens_grad[:, None]) + tuple(totals)


def flip(value, bits):
    return lax.ppermute(value, "ctx", [(i, i ^ bits) for i in range(8)])


def turn(value, step):
    return lax.ppermute(value, "wt", [(i, (i - step) % 4) for i in range(4)])


def pick(value, index, axis=0):
    return lax.dynamic_index_in_dim(value, index, axis, keepdims=False)


def pair(own, other, bit, axis=0):
    return jnp.where(bit == 0, jnp.stack([own, other], axis), jnp.stack([other, own], axis))


def place(shape, parts):
    count = len(parts)

    def kernel(*refs):
        inputs, out = refs[:count], refs[count]
        ctx, own = lax.axis_index("ctx"), lax.axis_index("wt")
        for source, (unused, first, rows, start) in zip(inputs, parts):
            at = pl.multiple_of(start(ctx, own), 16)
            out[pl.ds(at, rows), :] = source[first : first + rows, :]

    return pl.pallas_call(
        kernel,
        out_shape=jax.ShapeDtypeStruct(shape, jnp.bfloat16),
        compiler_params=pltpu.CompilerParams(vmem_limit_bytes=32 * 1024 * 1024),
    )(*[part[0] for part in parts])


def attend_kernel(near, far, weight, bias, seg_col, seg_row, qkv, mixed, logsum):
    scale = HEAD_DIM ** (-0.5)
    group = weight.shape[1] // (3 * HEAD_DIM)
    half = near.shape[0]
    block = 256
    for index, source in enumerate((near, far)):

        def project_rows(step, carry, index=index, source=source):
            at = pl.multiple_of(step * block, block)
            rows = source[pl.ds(at, block), :]
            full = jnp.dot(rows, weight[...], preferred_element_type=jnp.float32) + bias[...]
            low = full.astype(jnp.bfloat16)
            for slot in range(3 * group):
                qkv[slot, pl.ds(at + index * half, block), :] = low[
                    :, slot * HEAD_DIM : (slot + 1) * HEAD_DIM
                ]
            return carry

        lax.fori_loop(0, half // block, project_rows, 0)

    def attend_rows(step, carry):
        at = pl.multiple_of(step * block, block)
        mask = seg_col[pl.ds(at, block), :] == seg_row[...]
        sums = []
        outs = []
        for head in range(group):
            query = qkv[head, pl.ds(at, block), :]
            scores = lax.dot_general(
                query,
                qkv[group + head],
                (((1,), (1,)), ((), ())),
                preferred_element_type=jnp.float32,
            )
            scores = jnp.where(mask, scores * scale, NEG)
            top = jnp.max(scores, axis=-1, keepdims=True)
            expd = jnp.exp(scores - top)
            total = jnp.sum(expd, axis=-1, keepdims=True)
            probs = (expd * (1.0 / total)).astype(jnp.bfloat16)
            out = jnp.dot(probs, qkv[2 * group + head], preferred_element_type=jnp.float32)
            outs.append(out.astype(jnp.bfloat16))
            sums.append(top + jnp.log(total))
        mixed[pl.ds(at, block), :] = jnp.concatenate(outs, axis=1)
        logsum[pl.ds(at, block), :] = jnp.concatenate(
            sums + [jnp.zeros_like(sums[0])] * (128 - group), axis=1
        )
        return carry

    lax.fori_loop(0, mixed.shape[0] // block, attend_rows, 0)


def attend(near, far, weight, bias, seg):
    rows = 2 * near.shape[0]
    width = weight.shape[1] // 3
    return pl.pallas_call(
        attend_kernel,
        out_shape=(
            jax.ShapeDtypeStruct((3 * width // HEAD_DIM, rows, HEAD_DIM), jnp.bfloat16),
            jax.ShapeDtypeStruct((rows, width), jnp.bfloat16),
            jax.ShapeDtypeStruct((rows, 128), jnp.float32),
        ),
        compiler_params=pltpu.CompilerParams(vmem_limit_bytes=48 * 1024 * 1024),
    )(near, far, weight, bias, seg[:, None], seg[None, :])


def attend_back_kernel(
    qkv, logsum, seg_col, seg_row, part0, part1, part2, part3, grads, dkeys, dvalues
):
    scale = HEAD_DIM ** (-0.5)
    group = qkv.shape[0] // 3
    width = group * HEAD_DIM
    block = part0.shape[0]
    dkeys[...] = jnp.zeros_like(dkeys)
    dvalues[...] = jnp.zeros_like(dvalues)
    for index, part in enumerate((part0, part1, part2, part3)):
        at = index * block
        mask = seg_col[at : at + block, :] == seg_row[...]
        for head in range(group):
            query = qkv[head, at : at + block, :]
            grad = part[:, head * HEAD_DIM : (head + 1) * HEAD_DIM]
            keys = qkv[group + head]
            scores = lax.dot_general(
                query, keys, (((1,), (1,)), ((), ())), preferred_element_type=jnp.float32
            )
            scores = jnp.where(mask, scores * scale, NEG)
            probs = jnp.exp(scores - logsum[at : at + block, head : head + 1])
            dprobs = lax.dot_general(
                grad,
                qkv[2 * group + head],
                (((1,), (1,)), ((), ())),
                preferred_element_type=jnp.float32,
            )
            delta = jnp.sum(probs * dprobs, axis=-1, keepdims=True)
            dscores = (probs * (dprobs - delta)).astype(jnp.bfloat16)
            dquery = jnp.dot(dscores, keys, preferred_element_type=jnp.float32) * scale
            grads[at : at + block, head * HEAD_DIM : (head + 1) * HEAD_DIM] = dquery.astype(
                jnp.bfloat16
            )
            dkeys[head] += lax.dot_general(
                dscores, query, (((0,), (0,)), ((), ())), preferred_element_type=jnp.float32
            )
            dvalues[head] += lax.dot_general(
                probs.astype(jnp.bfloat16),
                grad,
                (((0,), (0,)), ((), ())),
                preferred_element_type=jnp.float32,
            )
    for head in range(group):
        lanes = slice(width + head * HEAD_DIM, width + (head + 1) * HEAD_DIM)
        grads[:, lanes] = (dkeys[head] * scale).astype(jnp.bfloat16)
        lanes = slice(2 * width + head * HEAD_DIM, 2 * width + (head + 1) * HEAD_DIM)
        grads[:, lanes] = dvalues[head].astype(jnp.bfloat16)


def attend_back(qkv, logsum, seg, parts):
    slots, rows, unused = qkv.shape
    return pl.pallas_call(
        attend_back_kernel,
        out_shape=jax.ShapeDtypeStruct((rows, slots * HEAD_DIM), jnp.bfloat16),
        scratch_shapes=[
            pltpu.VMEM((slots // 3, rows, HEAD_DIM), jnp.float32),
            pltpu.VMEM((slots // 3, rows, HEAD_DIM), jnp.float32),
        ],
        compiler_params=pltpu.CompilerParams(vmem_limit_bytes=48 * 1024 * 1024),
    )(qkv, logsum, seg[:, None], seg[None, :], *parts)


def dot(left, right):
    return jnp.dot(left, right, preferred_element_type=jnp.float32)


def dot_back(left, right):
    return lax.dot_general(
        left, right, (((1,), (1,)), ((), ())), preferred_element_type=jnp.float32
    )


def dot_sum(left, right):
    return lax.dot_general(
        left, right, (((0,), (0,)), ((), ())), preferred_element_type=jnp.float32
    )


def norm_parts(rows):
    mean = jnp.mean(rows, axis=-1, keepdims=True)
    centered = rows - mean
    spread = jnp.mean(centered * centered, axis=-1, keepdims=True)
    root = lax.rsqrt(spread + EPS)
    return centered * root, root


def norm_back(upstream, normed, root, gain):
    grad = upstream * gain
    mean = jnp.mean(grad, axis=-1, keepdims=True)
    along = jnp.mean(grad * normed, axis=-1, keepdims=True)
    return root * (grad - mean - normed * along)


def short(value):
    return value.astype(jnp.bfloat16)


def wide(value):
    return value.astype(jnp.float32)


def add_sent(kept, received):
    return short(wide(kept) + wide(received))


def sum_owned(pieces, own):
    total = wide(pick(pieces, own))
    for step in (1, 2, 3):
        total = total + wide(turn(pick(pieces, (own - step) % 4), step))
    return short(total)


def plane_device(
    tokens,
    doc_lengths,
    query_weight,
    query_bias,
    key_weight,
    value_weight,
    value_bias,
    out_weight,
    out_bias,
    first_gain,
    first_shift,
    inner_weight,
    inner_bias,
    outer_weight,
    outer_bias,
    second_gain,
    second_shift,
    cotangent,
):
    ctx, own = lax.axis_index("ctx"), lax.axis_index("wt")
    core, x, y, group = ctx & 1, (ctx >> 1) & 1, ctx >> 2, ctx & 3
    quarter = 2 * y + x
    rows, dim = tokens.shape[2], tokens.shape[3]
    shard = query_weight.shape[0]
    hidden = outer_weight.shape[0]
    half = hidden // 2
    width = dim // 4

    mine = jnp.concatenate([pick(tokens[:, 0], y), flip(pick(tokens[:, 0], 1 - y), 4)])
    near = jnp.concatenate([mine, flip(mine, 2)])
    far = flip(near, 1)

    slices = [
        lax.dynamic_slice_in_dim(w, group * width, width, 1)
        for w in (query_weight, key_weight, value_weight)
    ]
    heads_own = jnp.concatenate(slices, axis=1)
    heads_half = pick(heads_own.reshape(2, shard // 2, 3 * width), y)
    parts = [(heads_own, 0, shard, lambda c, z: shard * z)]
    for step in (1, 2, 3):
        got = turn(heads_half, step)
        parts.append(
            (
                got,
                0,
                shard // 2,
                lambda c, z, s=step: shard * ((z + s) % 4) + (shard // 2) * (c >> 2),
            )
        )
        parts.append(
            (
                flip(got, 4),
                0,
                shard // 2,
                lambda c, z, s=step: shard * ((z + s) % 4) + (shard // 2) * (1 - (c >> 2)),
            )
        )
    heads_weight = place((dim, 3 * width), parts)

    packed = jnp.concatenate(
        [
            v.reshape(-1, shard)
            for v in (
                query_bias,
                value_bias,
                out_bias,
                first_gain,
                first_shift,
                outer_bias,
                second_gain,
                second_shift,
                inner_bias,
            )
        ]
    )
    rel = jnp.stack([packed] + [turn(packed, step) for step in (1, 2, 3)])
    vectors = wide(lax.dynamic_slice_in_dim(jnp.concatenate([rel, rel]), (4 - own) % 4, 4))
    rest = [vectors[:, i].reshape(dim) for i in range(2, 8)]
    out_b, gain1, shift1, outer_b, gain2, shift2 = rest
    mine_b = pick(vectors, group)
    heads_bias = jnp.concatenate([mine_b[0], jnp.zeros_like(mine_b[0]), mine_b[1]])[None]
    inner_b = pick(vectors[:, 8:].reshape(4, 2, half), core, 1).reshape(4 * half)

    inner_half = pick(inner_weight.reshape(shard, 4, 2, half), core, 2).reshape(shard, 4 * half)
    outer_half = lax.dynamic_slice_in_dim(outer_weight, core * half, half, 0)
    out_send = pick(out_weight.reshape(4, shard // 4, dim), quarter)
    inner_send = pick(inner_half.reshape(4, shard // 4, 4 * half), quarter)
    outer_send = pick(outer_half.reshape(4, half // 4, dim), quarter)

    def quarters(piece, size, at, first, second):
        one = flip(piece, 2 * first)
        two = flip(piece, 2 * second)
        both = flip(one, 2 * second)
        found = []
        for value, bits in ((piece, 0), (one, first), (two, second), (both, first | second)):
            found.append(
                (value, 0, size, lambda c, z, b=bits: at(c, z) + size * (((c >> 1) & 3) ^ b))
            )
        return found

    def spread(piece, whole, size, at, first, second):
        found = [(whole, 0, 4 * size, lambda c, z: at(c, z))]
        for step in (1, 2, 3):
            found += quarters(
                turn(piece, step), size, lambda c, z, s=step: at(c, (z + s) % 4), first, second
            )
        return found

    out_parts = spread(
        out_send, out_weight, shard // 4, lambda c, z: shard * (z ^ (c & 3)), 1, 2
    )
    inner_parts = spread(inner_send, inner_half, shard // 4, lambda c, z: shard * z, 2, 1)
    outer_parts = spread(outer_send, outer_half, half // 4, lambda c, z: half * z, 1, 2)
    out_full = place((dim, dim), out_parts)
    inner_full = place((dim, 4 * half), inner_parts)
    outer_full = place((4 * half, dim), outer_parts)

    lengths = pick(doc_lengths[:, 0], y)
    starts = jnp.cumsum(lengths) - lengths
    index = jnp.arange(8 * rows, dtype=jnp.int32)
    code = index // rows
    code = (code >> 2) | (code & 2) | ((code & 1) << 2)
    positions = (ctx ^ code) * rows + index % rows
    seg = jnp.sum((starts[None, :] <= positions[:, None]).astype(jnp.int32), axis=-1) - 1

    qkv, mixed, logsum = attend(near, far, heads_weight, heads_bias, seg)

    def to_owner(value):
        blocks = value.reshape(4, 2 * rows, width)
        return [blocks[0]] + [flip(blocks[2 * (b & 1) + (b >> 1)], b) for b in (1, 2, 3)]

    mixed_own = jnp.concatenate(to_owner(mixed), axis=1)
    first_sum = wide(mine) + dot(mixed_own, out_full) + out_b
    normed1, root1 = norm_parts(first_sum)
    first = normed1 * gain1 + shift1
    first_low = short(first)
    first_both = jnp.concatenate([first_low, flip(first_low, 1)])
    inner = dot(first_both, inner_full) + inner_b
    active = short(gelu(inner))
    second_part = dot(active, outer_full)
    second_sum = (
        first + outer_b + second_part[: 2 * rows] + flip(second_part[2 * rows :], 1)
    )
    normed2, root2 = norm_parts(second_sum)
    output_own = short(normed2 * gain2 + shift2)
    output = pair(output_own[:rows], flip(output_own[rows:], 4), y)

    upstream = wide(
        jnp.concatenate([pick(cotangent[:, 0], y), flip(pick(cotangent[:, 0], 1 - y), 4)])
    )
    dsecond = norm_back(upstream, normed2, root2, gain2)
    douter = short(dsecond)
    dgain2, dshift2 = jnp.sum(upstream * normed2, axis=0), jnp.sum(upstream, axis=0)
    douter_b = jnp.sum(wide(douter), axis=0)
    douter_both = jnp.concatenate([douter, flip(douter, 1)])
    dactive = dot_back(douter_both, outer_full)
    unused, gelu_back = jax.vjp(gelu, inner)
    dinner = short(gelu_back(dactive)[0])
    dfirst_part = dot_back(dinner, inner_full)
    dfirst = dsecond + dfirst_part[: 2 * rows] + flip(dfirst_part[2 * rows :], 1)
    dinner_w = short(dot_sum(first_both, dinner))
    douter_w = short(dot_sum(active, douter_both))
    dinner_b = jnp.sum(wide(dinner), axis=0)

    dfirst_sum = norm_back(dfirst, normed1, root1, gain1)
    dbranch = short(dfirst_sum)
    dgain1, dshift1 = jnp.sum(dfirst * normed1, axis=0), jnp.sum(dfirst, axis=0)
    dout_b = jnp.sum(wide(dbranch), axis=0)
    dmixed_own = short(dot_back(dbranch, out_full))
    dparts = [dmixed_own[:, b * width : (b + 1) * width] for b in range(4)]
    dparts = [dparts[0]] + [flip(dparts[b], b) for b in (1, 2, 3)]
    dqkv = attend_back(qkv, logsum, seg, [dparts[0], dparts[2], dparts[1], dparts[3]])

    dout_w = short(dot_sum(mixed_own, dbranch)).reshape(4, shard, dim)
    dout_w = jnp.where(
        (group & 1) == 0, dout_w, dout_w.reshape(2, 2, shard, dim)[:, ::-1].reshape(dout_w.shape)
    )
    dout_w = jnp.where(
        (group & 2) == 0, dout_w, dout_w.reshape(2, 2, shard, dim)[::-1].reshape(dout_w.shape)
    )

    dtokens = dot_back(dqkv, heads_weight)
    dtokens = dtokens[: 4 * rows] + wide(flip(short(dtokens[4 * rows :]), 1))
    dtokens = dtokens[: 2 * rows] + wide(flip(short(dtokens[2 * rows :]), 2)) + dfirst_sum
    tokens_grad = pair(dtokens[:rows], wide(flip(short(dtokens[rows:]), 4)), y)

    both = jnp.concatenate([near, far])
    dheads = short(dot_sum(both, dqkv)).reshape(4, shard, 3 * width)
    dheads = sum_owned(dheads, own)
    dheads = add_sent(dheads, flip(dheads, 4))
    dheads = pair(dheads, flip(dheads, 2), x)
    dheads = pair(dheads, flip(dheads, 1), core)
    dheads = wide(jnp.transpose(dheads.reshape(2, 2, shard, 3, width), (3, 2, 1, 0, 4)))
    dheads = dheads.reshape(3, shard, dim)
    dheads_b = jnp.sum(wide(dqkv), axis=0).reshape(3, width)
    dheads_b = dheads_b + turn(dheads_b, 1) + turn(dheads_b, 2) + turn(dheads_b, 3)
    dheads_b = dheads_b + flip(dheads_b, 4)
    dheads_b = pair(dheads_b, flip(dheads_b, 2), x)
    dheads_b = pair(dheads_b, flip(dheads_b, 1), core)
    dheads_b = pick(jnp.transpose(dheads_b, (1, 0, 2, 3)).reshape(4, 3, width), own)

    def shares(value, first, second):
        part = value.reshape(4, 2, 2, -1, value.shape[-1])
        bits = {1: x, 2: y}
        axes = {1: 2, 2: 1}
        at = axes[first]
        part = add_sent(
            pick(part, bits[first], at), flip(pick(part, 1 - bits[first], at), 2 * first)
        )
        part = add_sent(
            pick(part, bits[second], 1), flip(pick(part, 1 - bits[second], 1), 2 * second)
        )
        return sum_owned(part, own)

    def joined(piece, first, second):
        bits = {1: x, 2: y}
        piece = pair(piece, flip(piece, 2 * first), bits[first])
        piece = pair(piece, flip(piece, 2 * second), bits[second])
        if first == 2:
            piece = jnp.swapaxes(piece, 0, 1)
        return piece.reshape(-1, piece.shape[-1])

    dinner_w = joined(shares(dinner_w, 1, 2), 1, 2)
    dinner_w = pair(
        dinner_w.reshape(shard, 4, half), flip(dinner_w, 1).reshape(shard, 4, half), core, 2
    )
    dinner_w = wide(dinner_w.reshape(shard, 8 * half))
    douter_w = joined(shares(douter_w, 2, 1), 2, 1)
    douter_w = wide(pair(douter_w, flip(douter_w, 1), core).reshape(hidden, dim))
    dout_w = dout_w.reshape(dim, dim)
    dout_w = add_sent(dout_w, flip(dout_w, 1))
    dout_w = wide(joined(shares(dout_w, 1, 2), 1, 2))

    sums = jnp.stack([dout_b, dgain1, dshift1, douter_b, dgain2, dshift2])
    sums = sums + flip(sums, 1)
    inner_sums = pair(dinner_b.reshape(4, half), flip(dinner_b.reshape(4, half), 1), core, 1)
    sums = jnp.concatenate([sums, inner_sums.reshape(-1, dim)])
    sums = sums + flip(sums, 2)
    sums = sums + flip(sums, 4)
    sums = sums + turn(sums, 1) + turn(sums, 2) + turn(sums, 3)
    small = lax.dynamic_slice_in_dim(sums[:6], own * shard, shard, 1)
    dinner_b = pick(sums[6:].reshape(4, hidden), own)

    return (
        output[:, None],
        tokens_grad[:, None],
        dheads[0],
        dheads_b[0],
        dheads[1],
        dheads[2],
        dheads_b[2],
        dout_w,
        small[0],
        small[1],
        small[2],
        dinner_w,
        dinner_b,
        douter_w,
        small[3],
        small[4],
        small[5],
    )


def solution(mesh):
    placed = (
        P(None, "wt", "ctx", None),
        P(None, "wt", None),
        P("wt", None),
        P("wt"),
        P("wt", None),
        P("wt", None),
        P("wt"),
        P("wt", None),
        P("wt"),
        P("wt"),
        P("wt"),
        P("wt", None),
        P("wt"),
        P("wt", None),
        P("wt"),
        P("wt"),
        P("wt"),
        P(None, "wt", "ctx", None),
    )
    fits = mesh.shape["ctx"] == 8 and mesh.shape["wt"] == 4
    return jax.shard_map(
        plane_device if fits else general_device,
        mesh=mesh,
        in_specs=placed,
        out_specs=(
            P(None, "wt", "ctx", None),
            P(None, "wt", "ctx", None),
            P("wt", None),
            P("wt"),
            P("wt", None),
            P("wt", None),
            P("wt"),
            P("wt", None),
            P("wt"),
            P("wt"),
            P("wt"),
            P("wt", None),
            P("wt"),
            P("wt", None),
            P("wt"),
            P("wt"),
            P("wt"),
        ),
        check_vma=False,
    )
```

```python
import math

import jax
import jax.numpy as jnp
from jax import lax
from jax.experimental import pallas as pl
from jax.experimental.pallas import tpu as pltpu
from jax.sharding import PartitionSpec as P

HEADS = 12
HEAD_DIM = 64


EPS = 1e-12
NEG = -1e30
ROOT_HALF = 0.7071067811865476


def for_sending(shard):

    def short(part):
        return part.astype(jnp.bfloat16) if part.dtype == jnp.float32 else part

    return jax.tree.map(short, shard)


def normalize(rows, gain, shift):
    mean = jnp.mean(rows, axis=-1, keepdims=True)
    centered = rows - mean
    spread = jnp.mean(centered * centered, axis=-1, keepdims=True)
    return centered * lax.rsqrt(spread + EPS) * gain + shift


def gelu(inner):
    return 0.5 * inner * (1.0 + lax.erf(inner * ROOT_HALF))


def segment_of(starts, positions):
    found = (starts[:, None, :] <= positions[:, :, None]).astype(jnp.int32)
    return jnp.sum(found, axis=-1) - 1


def project(inputs, weight):
    return jnp.einsum("btd,de->bte", inputs, weight, preferred_element_type=jnp.float32)


def project_back(grads, weight):
    return jnp.einsum("bte,de->btd", grads, weight, preferred_element_type=jnp.float32)


def outer_sum(inputs, grads):
    return jnp.einsum("btd,bte->de", inputs, grads, preferred_element_type=jnp.float32)


def row_sum(grads):
    return jnp.sum(grads.astype(jnp.float32), axis=(0, 1))


def heads_of(array):
    return array.reshape(array.shape[0], array.shape[1], HEADS, HEAD_DIM)


def block_loop(width, carry, visit):
    block = math.gcd(width, 512)

    def step(state, index):
        return (visit(state, index * block, block), None)

    carry, unused = lax.scan(step, carry, jnp.arange(width // block, dtype=jnp.int32))
    return carry


def reaches(starts, own_seg, first, count):
    positions = first + jnp.arange(count, dtype=jnp.int32)
    other = segment_of(starts, jnp.broadcast_to(positions, (starts.shape[0], count)))
    touch = jnp.any((other[:, 0] <= own_seg[:, -1]) & (other[:, -1] >= own_seg[:, 0]))
    return (other, touch)


def keep_state(state):
    return state


def forward_attention(queries, query_seg, starts, keys, values):
    scale = HEAD_DIM ** (-0.5)
    batch, rows = (queries.shape[0], queries.shape[1])
    query_heads = heads_of(queries)

    def forward_fold(carry, piece, start):
        key_piece, value_piece = piece

        def visit(state, offset, count):
            other, touch = reaches(starts, query_seg, offset, count)

            def compute(state):
                top, total, accum = state
                key_block = heads_of(lax.dynamic_slice_in_dim(key_piece, offset, count, 1))
                value_block = heads_of(lax.dynamic_slice_in_dim(value_piece, offset, count, 1))
                scores = (
                    jnp.einsum(
                        "bqhd,bkhd->bhqk",
                        query_heads,
                        key_block,
                        preferred_element_type=jnp.float32,
                    )
                    * scale
                )
                mask = (query_seg[:, :, None] == other[:, None, :])[:, None]
                scores = jnp.where(mask, scores, NEG)
                new_top = jnp.maximum(top, jnp.max(scores, axis=-1))
                expd = jnp.where(mask, jnp.exp(scores - new_top[..., None]), 0.0)
                factor = jnp.exp(top - new_top)
                total = total * factor + jnp.sum(expd, axis=-1)
                added = jnp.einsum(
                    "bhqk,bkhd->bqhd",
                    expd.astype(jnp.bfloat16),
                    value_block,
                    preferred_element_type=jnp.float32,
                )
                accum = accum * jnp.transpose(factor, (0, 2, 1))[..., None] + added
                return (new_top, total, accum)

            return lax.cond(touch, compute, keep_state, state)

        return block_loop(key_piece.shape[1], carry, visit)

    init = (
        jnp.full((batch, HEADS, rows), NEG, jnp.float32),
        jnp.zeros((batch, HEADS, rows), jnp.float32),
        jnp.zeros((batch, rows, HEADS, HEAD_DIM), jnp.float32),
    )
    whole = (keys, values)
    top, total, accum = forward_fold(
        init,
        (
            lax.all_gather(keys, "ctx", axis=1, tiled=True),
            lax.all_gather(values, "ctx", axis=1, tiled=True),
        ),
        jnp.int32(0),
    )
    mixed = accum / jnp.transpose(total, (0, 2, 1))[..., None]
    return (mixed, top + jnp.log(total), whole)


def query_gradient(queries, query_seg, starts, keys, values, dmixed, logsum, delta):
    scale = HEAD_DIM ** (-0.5)
    query_heads = heads_of(queries)
    grad_heads = heads_of(dmixed)

    def query_fold(carry, piece, start):
        key_piece, value_piece = piece

        def visit(state, offset, count):
            other, touch = reaches(starts, query_seg, offset, count)

            def compute(state):
                key_block = heads_of(lax.dynamic_slice_in_dim(key_piece, offset, count, 1))
                value_block = heads_of(lax.dynamic_slice_in_dim(value_piece, offset, count, 1))
                scores = (
                    jnp.einsum(
                        "bqhd,bkhd->bhqk",
                        query_heads,
                        key_block,
                        preferred_element_type=jnp.float32,
                    )
                    * scale
                )
                mask = (query_seg[:, :, None] == other[:, None, :])[:, None]
                probs = jnp.where(
                    mask, jnp.exp(jnp.where(mask, scores, NEG) - logsum[..., None]), 0.0
                )
                dprobs = jnp.einsum(
                    "bqhd,bkhd->bhqk", grad_heads, value_block, preferred_element_type=jnp.float32
                )
                dscores = (probs * (dprobs - delta[..., None])).astype(jnp.bfloat16)
                return (
                    state
                    + jnp.einsum(
                        "bhqk,bkhd->bqhd", dscores, key_block, preferred_element_type=jnp.float32
                    )
                    * scale
                )

            return lax.cond(touch, compute, keep_state, state)

        return block_loop(key_piece.shape[1], carry, visit)

    init = jnp.zeros(query_heads.shape, jnp.float32)
    return query_fold(
        init,
        (
            lax.all_gather(keys, "ctx", axis=1, tiled=True),
            lax.all_gather(values, "ctx", axis=1, tiled=True),
        ),
        jnp.int32(0),
    )


def key_gradient(keys, values, key_seg, starts, queries, dmixed, logsum, delta):
    scale = HEAD_DIM ** (-0.5)
    key_heads = heads_of(keys)
    value_heads = heads_of(values)
    every_top, every_delta = (
        lax.all_gather(logsum, "ctx", axis=2, tiled=True),
        lax.all_gather(delta, "ctx", axis=2, tiled=True),
    )

    def key_fold(carry, piece, start):
        query_piece, grad_piece = piece

        def visit(state, offset, count):
            other, touch = reaches(starts, key_seg, offset, count)

            def compute(state):
                dkeys, dvalues = state
                query_block = heads_of(lax.dynamic_slice_in_dim(query_piece, offset, count, 1))
                grad_block = heads_of(lax.dynamic_slice_in_dim(grad_piece, offset, count, 1))
                top_block = lax.dynamic_slice_in_dim(every_top, offset, count, 2)
                delta_block = lax.dynamic_slice_in_dim(every_delta, offset, count, 2)
                scores = (
                    jnp.einsum(
                        "bqhd,bkhd->bhqk",
                        query_block,
                        key_heads,
                        preferred_element_type=jnp.float32,
                    )
                    * scale
                )
                mask = (other[:, :, None] == key_seg[:, None, :])[:, None]
                probs = jnp.where(
                    mask, jnp.exp(jnp.where(mask, scores, NEG) - top_block[..., None]), 0.0
                )
                dvalues = dvalues + jnp.einsum(
                    "bhqk,bqhd->bkhd",
                    probs.astype(jnp.bfloat16),
                    grad_block,
                    preferred_element_type=jnp.float32,
                )
                dprobs = jnp.einsum(
                    "bqhd,bkhd->bhqk", grad_block, value_heads, preferred_element_type=jnp.float32
                )
                dscores = (probs * (dprobs - delta_block[..., None])).astype(jnp.bfloat16)
                dkeys = (
                    dkeys
                    + jnp.einsum(
                        "bhqk,bqhd->bkhd", dscores, query_block, preferred_element_type=jnp.float32
                    )
                    * scale
                )
                return (dkeys, dvalues)

            return lax.cond(touch, compute, keep_state, state)

        return block_loop(query_piece.shape[1], carry, visit)

    empty = jnp.zeros(key_heads.shape, jnp.float32)
    return key_fold(
        (empty, empty),
        (
            lax.all_gather(queries, "ctx", axis=1, tiled=True),
            lax.all_gather(dmixed, "ctx", axis=1, tiled=True),
        ),
        jnp.int32(0),
    )


def forward_pass(tokens, starts, weights, base):
    (
        query_weight,
        query_bias,
        key_weight,
        value_weight,
        value_bias,
        out_weight,
        out_bias,
        first_gain,
        first_shift,
        inner_weight,
        inner_bias,
        outer_weight,
        outer_bias,
        second_gain,
        second_shift,
    ) = weights
    rows = tokens.shape[1]
    positions = base + jnp.arange(rows, dtype=jnp.int32)
    query_seg = segment_of(starts, jnp.broadcast_to(positions, (tokens.shape[0], rows)))
    queries = (project(tokens, query_weight) + query_bias.astype(jnp.float32)).astype(jnp.bfloat16)
    keys = project(tokens, key_weight).astype(jnp.bfloat16)
    values = (project(tokens, value_weight) + value_bias.astype(jnp.float32)).astype(jnp.bfloat16)
    mixed, logsum, whole = forward_attention(queries, query_seg, starts, keys, values)
    mixed_low = mixed.reshape(tokens.shape).astype(jnp.bfloat16)
    first_sum = (
        tokens.astype(jnp.float32) + project(mixed_low, out_weight) + out_bias.astype(jnp.float32)
    )
    first = normalize(first_sum, first_gain.astype(jnp.float32), first_shift.astype(jnp.float32))
    first_low = first.astype(jnp.bfloat16)
    inner = project(first_low, inner_weight) + inner_bias.astype(jnp.float32)
    active = gelu(inner).astype(jnp.bfloat16)
    second_sum = first + project(active, outer_weight) + outer_bias.astype(jnp.float32)
    output = normalize(
        second_sum, second_gain.astype(jnp.float32), second_shift.astype(jnp.float32)
    ).astype(jnp.bfloat16)
    saved = (
        tokens,
        query_seg,
        queries,
        keys,
        values,
        mixed,
        logsum,
        mixed_low,
        first_sum,
        first_low,
        inner,
        active,
        second_sum,
        whole,
    )
    return (output, saved)


def backward_pass(saved, starts, weights, cotangent):
    (
        query_weight,
        query_bias,
        key_weight,
        value_weight,
        value_bias,
        out_weight,
        out_bias,
        first_gain,
        first_shift,
        inner_weight,
        inner_bias,
        outer_weight,
        outer_bias,
        second_gain,
        second_shift,
    ) = weights
    (
        tokens,
        query_seg,
        queries,
        keys,
        values,
        mixed,
        logsum,
        mixed_low,
        first_sum,
        first_low,
        inner,
        active,
        second_sum,
        whole,
    ) = saved
    unused, second_back = jax.vjp(
        normalize, second_sum, second_gain.astype(jnp.float32), second_shift.astype(jnp.float32)
    )
    dsecond, dgain_second, dshift_second = second_back(cotangent.astype(jnp.float32))
    douter = dsecond.astype(jnp.bfloat16)
    dactive = project_back(douter, outer_weight)
    unused, gelu_back = jax.vjp(gelu, inner)
    dinner = gelu_back(dactive)[0].astype(jnp.bfloat16)
    dfirst = dsecond + project_back(dinner, inner_weight)
    unused, first_back = jax.vjp(
        normalize, first_sum, first_gain.astype(jnp.float32), first_shift.astype(jnp.float32)
    )
    dfirst_sum, dgain_first, dshift_first = first_back(dfirst)
    dbranch = dfirst_sum.astype(jnp.bfloat16)
    dmixed = project_back(dbranch, out_weight).astype(jnp.bfloat16)
    delta = jnp.einsum("bqhd,bqhd->bhq", heads_of(dmixed).astype(jnp.float32), mixed)
    dqueries = query_gradient(queries, query_seg, starts, keys, values, dmixed, logsum, delta)
    dkeys, dvalues = key_gradient(keys, values, query_seg, starts, queries, dmixed, logsum, delta)
    dqueries = dqueries.reshape(tokens.shape).astype(jnp.bfloat16)
    dkeys = dkeys.reshape(tokens.shape).astype(jnp.bfloat16)
    dvalues = dvalues.reshape(tokens.shape).astype(jnp.bfloat16)
    tokens_grad = (
        dfirst_sum
        + project_back(dqueries, query_weight)
        + project_back(dkeys, key_weight)
        + project_back(dvalues, value_weight)
    )
    sums = (
        outer_sum(tokens, dqueries),
        row_sum(dqueries),
        outer_sum(tokens, dkeys),
        outer_sum(tokens, dvalues),
        row_sum(dvalues),
        outer_sum(mixed_low, dbranch),
        row_sum(dbranch),
        dgain_first,
        dshift_first,
        outer_sum(first_low, dinner),
        row_sum(dinner),
        outer_sum(active, douter),
        row_sum(douter),
        dgain_second,
        dshift_second,
    )
    return (tokens_grad, sums)


def general_device(
    tokens,
    doc_lengths,
    query_weight,
    query_bias,
    key_weight,
    value_weight,
    value_bias,
    out_weight,
    out_bias,
    first_gain,
    first_shift,
    inner_weight,
    inner_bias,
    outer_weight,
    outer_bias,
    second_gain,
    second_shift,
    cotangent,
):
    params = (
        query_weight,
        query_bias,
        key_weight,
        value_weight,
        value_bias,
        out_weight,
        out_bias,
        first_gain,
        first_shift,
        inner_weight,
        inner_bias,
        outer_weight,
        outer_bias,
        second_gain,
        second_shift,
    )
    rows = tokens.shape[2]
    base = lax.axis_index("ctx") * rows
    lengths = doc_lengths[:, 0]
    starts = jnp.cumsum(lengths, axis=-1) - lengths
    outputs = []
    token_parts = []
    sums = None
    for index in range(tokens.shape[0]):
        weights = (
            lax.all_gather(params[0], "wt", axis=0, tiled=True),
            lax.all_gather(params[1], "wt", axis=0, tiled=True),
            lax.all_gather(params[2], "wt", axis=0, tiled=True),
            lax.all_gather(params[3], "wt", axis=0, tiled=True),
            lax.all_gather(params[4], "wt", axis=0, tiled=True),
            lax.all_gather(params[5], "wt", axis=0, tiled=True),
            lax.all_gather(params[6], "wt", axis=0, tiled=True),
            lax.all_gather(params[7], "wt", axis=0, tiled=True),
            lax.all_gather(params[8], "wt", axis=0, tiled=True),
            lax.all_gather(params[9], "wt", axis=0, tiled=True),
            lax.all_gather(params[10], "wt", axis=0, tiled=True),
            lax.all_gather(params[11], "wt", axis=0, tiled=True),
            lax.all_gather(params[12], "wt", axis=0, tiled=True),
            lax.all_gather(params[13], "wt", axis=0, tiled=True),
            lax.all_gather(params[14], "wt", axis=0, tiled=True),
        )
        part_out, saved = forward_pass(
            tokens[index : index + 1, 0], starts[index : index + 1], weights, base
        )
        again = (
            lax.all_gather(params[0], "wt", axis=0, tiled=True),
            lax.all_gather(params[1], "wt", axis=0, tiled=True),
            lax.all_gather(params[2], "wt", axis=0, tiled=True),
            lax.all_gather(params[3], "wt", axis=0, tiled=True),
            lax.all_gather(params[4], "wt", axis=0, tiled=True),
            lax.all_gather(params[5], "wt", axis=0, tiled=True),
            lax.all_gather(params[6], "wt", axis=0, tiled=True),
            lax.all_gather(params[7], "wt", axis=0, tiled=True),
            lax.all_gather(params[8], "wt", axis=0, tiled=True),
            lax.all_gather(params[9], "wt", axis=0, tiled=True),
            lax.all_gather(params[10], "wt", axis=0, tiled=True),
            lax.all_gather(params[11], "wt", axis=0, tiled=True),
            lax.all_gather(params[12], "wt", axis=0, tiled=True),
            lax.all_gather(params[13], "wt", axis=0, tiled=True),
            lax.all_gather(params[14], "wt", axis=0, tiled=True),
        )
        part_grad, part_sums = backward_pass(
            saved, starts[index : index + 1], again, cotangent[index : index + 1, 0]
        )
        outputs.append(part_out)
        token_parts.append(part_grad)
        sums = part_sums if sums is None else jax.tree.map(jnp.add, sums, part_sums)
    output = jnp.concatenate(outputs, axis=0)
    tokens_grad = jnp.concatenate(token_parts, axis=0)
    shards = jax.tree.map(
        lambda part: part.astype(jnp.float32),
        lax.psum_scatter(for_sending(sums), "wt", scatter_dimension=0, tiled=True),
    )
    totals = lax.psum(shards, "ctx")
    return (output[:, None], tokens_grad[:, None]) + tuple(totals)


def flip(value, bits):
    return lax.ppermute(value, "ctx", [(i, i ^ bits) for i in range(8)])


def turn(value, step):
    return lax.ppermute(value, "wt", [(i, (i - step) % 4) for i in range(4)])


def pick(value, index, axis=0):
    return lax.dynamic_index_in_dim(value, index, axis, keepdims=False)


def pair(own, other, bit, axis=0):
    return jnp.where(bit == 0, jnp.stack([own, other], axis), jnp.stack([other, own], axis))


def short(value):
    return value.astype(jnp.bfloat16)


def wide(value):
    return value.astype(jnp.float32)


def dot(left, right):
    return jnp.dot(left, right, preferred_element_type=jnp.float32)


def dot_back(left, right):
    return lax.dot_general(
        left, right, (((1,), (1,)), ((), ())), preferred_element_type=jnp.float32
    )


def dot_sum(left, right):
    return lax.dot_general(
        left, right, (((0,), (0,)), ((), ())), preferred_element_type=jnp.float32
    )


def norm_parts(rows):
    mean = jnp.mean(rows, axis=-1, keepdims=True)
    centered = rows - mean
    spread = jnp.mean(centered * centered, axis=-1, keepdims=True)
    root = lax.rsqrt(spread + EPS)
    return centered * root, root


def norm_back(upstream, normed, root, gain):
    grad = upstream * gain
    mean = jnp.mean(grad, axis=-1, keepdims=True)
    along = jnp.mean(grad * normed, axis=-1, keepdims=True)
    return root * (grad - mean - normed * along)


def gelu_slope(inner):
    bell = jnp.exp(-0.5 * inner * inner) * (1.0 / math.sqrt(2.0 * math.pi))
    return 0.5 * (1.0 + lax.erf(inner * ROOT_HALF)) + inner * bell


def run(kernel, outs, args, scratch=()):
    shapes = tuple(jax.ShapeDtypeStruct(shape, dtype) for shape, dtype in outs)
    return pl.pallas_call(kernel, out_shape=shapes, scratch_shapes=list(scratch))(*args)


BF = jnp.bfloat16
F32 = jnp.float32


def where_am_i():
    ctx, own = lax.axis_index("ctx"), lax.axis_index("wt")
    return ctx & 1, (ctx >> 1) & 3, ctx & 3, own


def some_rows(start, count):
    return pl.ds(pl.multiple_of(start, 16), count)


def prepare_kernel(wq, wk, wv, wo, wi, wo2, vec, heads_own, heads_send, w2_send, inner_half, outer_half):
    core, quarter, group, own = where_am_i()
    shard, dim = wq.shape
    width, half = dim // 4, wo2.shape[0] // 2
    for index in range(4):

        @pl.when(group == index)
        def _():
            for slot, ref in enumerate((wq, wk, wv)):
                heads_own[:, slot * width : (slot + 1) * width] = ref[
                    :, index * width : (index + 1) * width
                ]

    for index in range(2):

        @pl.when(core == index)
        def _():
            for block in range(4):
                at = block * 2 * half + index * half
                inner_half[:, block * half : (block + 1) * half] = wi[:, at : at + half]
            outer_half[...] = wo2[index * half : (index + 1) * half, :]

    part = shard // 2
    heads_send[0:part, :] = heads_own[some_rows((quarter >> 1) * part, part), :]
    heads_send[part:, :] = vec[...]
    part = shard // 4
    rows = some_rows(quarter * part, part)
    w2_send[0:part, :] = inner_half[rows, 0:dim]
    w2_send[part : 2 * part, :] = inner_half[rows, dim:]
    step = half // 4
    w2_send[2 * part : 2 * part + step, :] = outer_half[some_rows(quarter * step, step), :]
    w2_send[2 * part + step :, :] = wo[rows, :]


def attend_kernel(
    mine, other, far, heads_own, g1, g2, g3, h1, h2, h3, bias, seg_col, seg_row,
    qkv, m0, m1, m2, m3, logsum, weight,
):
    core, quarter, place, own = where_am_i()
    scale = HEAD_DIM ** (-0.5)
    shard = heads_own.shape[0]
    part = shard // 2
    y = quarter >> 1
    weight[some_rows(own * shard, shard), :] = heads_own[...]
    for step, near_half, far_half in ((1, g1, h1), (2, g2, h2), (3, g3, h3)):
        at = ((own + step) & 3) * shard
        weight[some_rows(at + part * y, part), :] = near_half[0:part, :]
        weight[some_rows(at + part * (1 - y), part), :] = far_half[0:part, :]
    group = weight.shape[1] // (3 * HEAD_DIM)
    block = mine.shape[0]
    at = 0
    for source in (mine, other, far):
        for first in range(0, source.shape[0], block):
            rows = source[first : first + block, :]
            low = short(dot(rows, weight[...]) + bias[...])
            for slot in range(3 * group):
                qkv[slot, at : at + block, :] = low[:, slot * HEAD_DIM : (slot + 1) * HEAD_DIM]
            at += block

    for index, out_ref in enumerate((m0, m2, m1, m3)):
        at = index * block
        mask = seg_col[at : at + block, :] == seg_row[...]
        sums = []
        for head in range(group):
            scores = dot_back(qkv[head, at : at + block, :], qkv[group + head])
            scores = jnp.where(mask, scores * scale, NEG)
            top = jnp.max(scores, axis=-1, keepdims=True)
            expd = jnp.exp(scores - top)
            total = jnp.sum(expd, axis=-1, keepdims=True)
            probs = short(expd * (1.0 / total))
            out_ref[:, head * HEAD_DIM : (head + 1) * HEAD_DIM] = short(
                dot(probs, qkv[2 * group + head])
            )
            sums.append(top + jnp.log(total))
        logsum[at : at + block, :] = jnp.concatenate(
            sums + [jnp.zeros_like(sums[0])] * (128 - group), axis=1
        )


def project_kernel(m0, m1, m2, m3, mine, wo, vec, *refs):
    pieces, (first_sum, first_low, out_full) = refs[:12], refs[12:]
    core, quarter, group, own = where_am_i()
    shard = wo.shape[0]
    part = shard // 4
    out_full[some_rows(own * shard, shard), :] = wo[...]
    for index, piece in enumerate(pieces):
        at = ((own + 1 + index // 4) & 3) * shard + part * (quarter ^ (index % 4))
        out_full[some_rows(at, part), :] = piece[piece.shape[0] - part :, :]
    total = wide(mine[...]) + vec[2:3, :]
    for code, ref in enumerate((m0, m1, m2, m3)):
        total += dot(ref[...], out_full[some_rows((group ^ code) * shard, shard), :])
    first_sum[...] = total
    first_low[...] = short(norm_parts(total)[0] * vec[3:4, :] + vec[4:5, :])


def forward_kernel(near, far, inner_half, outer_half, bias, *refs):
    pieces, (keep, send, inner, active, wi_full, wo2_full) = refs[:12], refs[12:]
    core, quarter, group, own = where_am_i()
    shard, half = inner_half.shape[0], outer_half.shape[0]
    dim = keep.shape[1]
    part, step = shard // 4, half // 4
    wi_full[some_rows(own * shard, shard), :] = inner_half[...]
    wo2_full[some_rows(own * half, half), :] = outer_half[...]
    for index, piece in enumerate(pieces):
        row, spot = (own + 1 + index // 4) & 3, quarter ^ (index % 4)
        rows = some_rows(row * shard + part * spot, part)
        wi_full[rows, 0:dim] = piece[0:part, :]
        wi_full[rows, dim:] = piece[part : 2 * part, :]
        wo2_full[some_rows(row * half + step * spot, step), :] = piece[
            2 * part : 2 * part + step, :
        ]
    count = near.shape[0]
    chunk = 512
    for index, (source, out) in enumerate(((far, send), (near, keep))):
        at = (1 - index) * count
        total = None
        for lane in range(0, inner.shape[1], chunk):
            lanes = slice(lane, lane + chunk)
            value = dot(source[...], wi_full[:, lanes]) + bias[:, lanes]
            inner[at : at + count, lanes] = value
            low = short(gelu(value))
            active[at : at + count, lanes] = low
            added = dot(low, wo2_full[lanes, :])
            total = added if total is None else total + added
        out[...] = total


def turnaround_kernel(first_sum, keep, got, vec, cot0, cot1, out0, out1, dsecond, douter, sums):
    rows = cot0.shape[0]
    first = norm_parts(first_sum[...])[0] * vec[3:4, :] + vec[4:5, :]
    normed, root = norm_parts(first + vec[5:6, :] + keep[...] + got[...])
    output = short(normed * vec[6:7, :] + vec[7:8, :])
    out0[...] = output[:rows]
    out1[...] = output[rows:]
    upstream = jnp.concatenate([wide(cot0[...]), wide(cot1[...])])
    back = norm_back(upstream, normed, root, vec[6:7, :])
    low = short(back)
    dsecond[...] = back
    douter[...] = low
    sums[0:1, :] = jnp.sum(wide(low), axis=0, keepdims=True)
    sums[1:2, :] = jnp.sum(upstream * normed, axis=0, keepdims=True)
    sums[2:3, :] = jnp.sum(upstream, axis=0, keepdims=True)
    sums[3:, :] = jnp.zeros_like(sums[3:, :])


def backward_kernel(near, far, inner, wi_full, wo2_full, keep, send, dinner, sums):
    count, dim = near.shape
    chunk = 512
    for index, (source, out) in enumerate(((far, send), (near, keep))):
        at = (1 - index) * count
        total = None
        for lane in range(0, inner.shape[1], chunk):
            lanes = slice(lane, lane + chunk)
            slope = gelu_slope(inner[at : at + count, lanes])
            low = short(dot_back(source[...], wo2_full[lanes, :]) * slope)
            dinner[at : at + count, lanes] = low
            added = dot_back(low, wi_full[:, lanes])
            total = added if total is None else total + added
        out[...] = total
    total = jnp.sum(wide(dinner[...]), axis=0, keepdims=True)
    sums[0:1, :] = total[:, :dim]
    sums[1:2, :] = total[:, dim:]
    sums[2:, :] = jnp.zeros_like(sums[2:, :])


def weights_kernel(first0, first1, douter0, douter1, dinner, active, ak, az, bk, bz, left, right):
    core, quarter, group, own = where_am_i()
    x, y = quarter & 1, quarter >> 1
    count = first0.shape[0]
    part, step = first0.shape[1] // 16, active.shape[1] // 16
    left[...] = short(dot_sum(first0[...], dinner[:count]) + dot_sum(first1[...], dinner[count:]))
    for block in range(8):
        rows = slice(block * part, (block + 1) * part)
        ak[rows, :] = left[some_rows((2 * block + x) * part, part), :]
        az[rows, :] = left[some_rows((2 * block + 1 - x) * part, part), :]
    right[...] = short(
        dot_sum(active[:count], douter0[...]) + dot_sum(active[count:], douter1[...])
    )
    for block in range(8):
        row, side = block // 2, block % 2
        rows = slice(block * step, (block + 1) * step)
        bk[rows, :] = right[some_rows((4 * row + 2 * y + side) * step, step), :]
        bz[rows, :] = right[some_rows((4 * row + 2 * (1 - y) + side) * step, step), :]


def branch_kernel(first_sum, dsecond, keep, got, vec, out_full, dfirst_sum, dbranch, d0, d1, d2, d3, sums):
    core, quarter, group, own = where_am_i()
    shard = d0.shape[1]
    normed, root = norm_parts(first_sum[...])
    dfirst = dsecond[...] + keep[...] + got[...]
    back = norm_back(dfirst, normed, root, vec[3:4, :])
    low = short(back)
    dfirst_sum[...] = back
    dbranch[...] = low
    for code, ref in enumerate((d0, d1, d2, d3)):
        ref[...] = short(dot_back(low, out_full[some_rows((group ^ code) * shard, shard), :]))
    sums[0:1, :] = jnp.sum(wide(low), axis=0, keepdims=True)
    sums[1:2, :] = jnp.sum(dfirst * normed, axis=0, keepdims=True)
    sums[2:3, :] = jnp.sum(dfirst, axis=0, keepdims=True)
    sums[3:, :] = jnp.zeros_like(sums[3:, :])


def out_weight_kernel(m0, m1, m2, m3, dbranch, sums1, sums2, sums3, packed):
    core, quarter, group, own = where_am_i()
    shard, dim = m0.shape[1], dbranch.shape[1]
    for code, ref in enumerate((m0, m1, m2, m3)):
        packed[some_rows((group ^ code) * shard, shard), :] = short(
            dot_sum(ref[...], dbranch[...])
        )
    rows = jnp.concatenate(
        [sums1[0:3, :], sums2[0:3, :], sums3[0:2, :], jnp.zeros_like(sums1[...])]
    )
    packed[dim:, :] = short(rows)


def out_split_kernel(packed, got, ck, cz):
    core, quarter, group, own = where_am_i()
    x = quarter & 1
    dim = packed.shape[1]
    part = dim // 16
    for block in range(8):
        rows = slice(block * part, (block + 1) * part)
        for ref, side in ((ck, x), (cz, 1 - x)):
            take = some_rows((2 * block + side) * part, part)
            ref[rows, :] = short(wide(packed[take, :]) + wide(got[take, :]))
    mine, other = wide(packed[dim:, :]), wide(got[dim:, :])
    low = jnp.where(core == 0, mine, other)[6:8]
    high = jnp.where(core == 0, other, mine)[6:8]
    rows = jnp.concatenate([(mine + other)[0:6], low, high, jnp.zeros((6, dim), F32)])
    for ref in (ck, cz):
        ref[8 * part :, :] = short(rows)


def reduce_kernel(ak, ar, bk, br, ck, cr, a2k, a2z, b2k, b2z, c2k, c2z):
    core, quarter, group, own = where_am_i()
    x, y = quarter & 1, quarter >> 1
    for keep, got, outs, bit in (
        (ak, ar, (a2k, a2z), y),
        (bk, br, (b2k, b2z), x),
        (ck, cr, (c2k, c2z), y),
    ):
        size = keep.shape[0] // 8
        size -= size % 16
        for block in range(4):
            for out, side in zip(outs, (bit, 1 - bit)):
                take = some_rows((2 * block + side) * size, size)
                out[block * size : (block + 1) * size, :] = short(
                    wide(keep[take, :]) + wide(got[take, :])
                )
        if keep.shape[0] > 8 * size:
            for out in outs:
                out[4 * size :, :] = short(wide(keep[8 * size :, :]) + wide(got[8 * size :, :]))


def owners_kernel(ak, ar, bk, br, ck, cr, p0, p1, p2, p3):
    core, quarter, group, own = where_am_i()
    dim = bk.shape[1]
    part, step = ak.shape[0] // 4, bk.shape[0] // 4
    size = (ck.shape[0] - 16) // 4
    for index, out in enumerate((p0, p1, p2, p3)):
        row = (own - index) & 3
        rows = some_rows(row * part, part)
        total = wide(ak[rows, :]) + wide(ar[rows, :])
        out[0:part, :] = total[:, :dim].astype(out.dtype)
        out[part : 2 * part, :] = total[:, dim:].astype(out.dtype)
        at = 2 * part
        rows = some_rows(row * step, step)
        out[at : at + step, :] = (wide(bk[rows, :]) + wide(br[rows, :])).astype(out.dtype)
        at += step
        rows = some_rows(row * size, size)
        out[at : at + size, :] = (wide(ck[rows, :]) + wide(cr[rows, :])).astype(out.dtype)
        at += size
        out[at:, :] = (wide(ck[4 * size :, :]) + wide(cr[4 * size :, :])).astype(out.dtype)


def total_kernel(mine, *refs):
    total = wide(mine[...])
    for ref in refs[:-1]:
        total += wide(ref[...])
    refs[-1][...] = short(total)


def finish_kernel(*refs):
    pieces, (dwi, dwo2, dwo, small) = refs[:8], refs[8:]
    core, quarter, group, own = where_am_i()
    part, half, dim = dwi.shape[0] // 4, dwi.shape[1] // 8, dwo.shape[1]
    step = half // 4
    for index, piece in enumerate(pieces[:4]):
        at = 2 * part + step
        dwo[some_rows((quarter ^ index) * part, part), :] = wide(piece[at : at + part, :])
    for side in range(2):

        @pl.when(core == side)
        def _():
            for index, piece in enumerate(pieces):
                spot = quarter ^ (index % 4)
                which = side if index < 4 else 1 - side
                rows = some_rows(spot * part, part)
                for block in range(4):
                    at = block * 2 * half + which * half
                    up, lane = part * (block // 2), half * (block % 2)
                    dwi[rows, at : at + half] = wide(piece[up : up + part, lane : lane + half])
                dwo2[some_rows(which * half + spot * step, step), :] = wide(
                    piece[2 * part : 2 * part + step, :]
                )

    small[...] = wide(pieces[0][3 * part + step :, :])


def attend_back_kernel(
    qkv, logsum, seg_col, seg_row, p0, p1, p2, p3, mine, other, far, weight,
    h0, h1, h2, h3, keep, send, grads, dkeys, dvalues, dweight,
):
    core, quarter, spot, own = where_am_i()
    scale = HEAD_DIM ** (-0.5)
    group = qkv.shape[0] // 3
    width = group * HEAD_DIM
    block = p0.shape[0]
    dkeys[...] = jnp.zeros_like(dkeys)
    dvalues[...] = jnp.zeros_like(dvalues)
    for index, part in enumerate((p0, p2, p1, p3)):
        at = index * block
        mask = seg_col[at : at + block, :] == seg_row[...]
        for head in range(group):
            query = qkv[head, at : at + block, :]
            grad = part[:, head * HEAD_DIM : (head + 1) * HEAD_DIM]
            keys = qkv[group + head]
            scores = jnp.where(mask, dot_back(query, keys) * scale, NEG)
            probs = jnp.exp(scores - logsum[at : at + block, head : head + 1])
            dprobs = dot_back(grad, qkv[2 * group + head])
            delta = jnp.sum(probs * dprobs, axis=-1, keepdims=True)
            dscores = short(probs * (dprobs - delta))
            grads[at : at + block, head * HEAD_DIM : (head + 1) * HEAD_DIM] = short(
                dot(dscores, keys) * scale
            )
            dkeys[head] += dot_sum(dscores, query)
            dvalues[head] += dot_sum(short(probs), grad)
    for head in range(group):
        lanes = slice(width + head * HEAD_DIM, width + (head + 1) * HEAD_DIM)
        grads[:, lanes] = short(dkeys[head] * scale)
        lanes = slice(2 * width + head * HEAD_DIM, 2 * width + (head + 1) * HEAD_DIM)
        grads[:, lanes] = short(dvalues[head])
    rows = 2 * block
    dweight[...] = (
        dot_sum(mine[...], grads[:block])
        + dot_sum(other[...], grads[block:rows])
        + dot_sum(far[...], grads[rows:])
    )
    sums = jnp.sum(wide(grads[...]), axis=0, keepdims=True)
    tail = jnp.concatenate([sums, jnp.zeros((15, sums.shape[1]), F32)])
    for index, out in enumerate((h0, h1, h2, h3)):
        take = pl.ds(pl.multiple_of(((own - index) & 3) * width, 16), width)
        out[0:width, :] = dweight[take, :].astype(out.dtype)
        out[width:, :] = tail.astype(out.dtype)
    keep[...] = dot_back(grads[:rows], weight[...])
    send[...] = short(dot_back(grads[rows:], weight[...]))


def heads_kernel(s0, s1, s2, s3, dq, dk, dv, bias):
    core, quarter, group, own = where_am_i()
    shard = dq.shape[0]
    for index in range(4):

        @pl.when(group == index)
        def _():
            for code, ref in enumerate((s0, s1, s2, s3)):
                at = (index ^ code) * shard
                for slot, out in enumerate((dq, dk, dv)):
                    out[:, at : at + shard] = wide(
                        ref[0:shard, slot * shard : (slot + 1) * shard]
                    )

                @pl.when(own == index ^ code)
                def _():
                    bias[...] = wide(ref[shard:, :])


def plane_device(
    tokens,
    doc_lengths,
    query_weight,
    query_bias,
    key_weight,
    value_weight,
    value_bias,
    out_weight,
    out_bias,
    first_gain,
    first_shift,
    inner_weight,
    inner_bias,
    outer_weight,
    outer_bias,
    second_gain,
    second_shift,
    cotangent,
):
    ctx, own = lax.axis_index("ctx"), lax.axis_index("wt")
    core, x, y, group = ctx & 1, (ctx >> 1) & 1, ctx >> 2, ctx & 3
    rows, dim = tokens.shape[2], tokens.shape[3]
    shard = query_weight.shape[0]
    hidden = outer_weight.shape[0]
    half = hidden // 2
    count = 2 * rows

    mine = jnp.concatenate([pick(tokens[:, 0], y), flip(pick(tokens[:, 0], 1 - y), 4)])
    other = flip(mine, 2)
    far = flip(jnp.concatenate([mine, other]), 1)

    vector_list = (
        query_bias,
        value_bias,
        out_bias,
        first_gain,
        first_shift,
        outer_bias,
        second_gain,
        second_shift,
        inner_bias,
    )
    vec = jnp.concatenate(vector_list).reshape(4, 3 * shard)
    vec = jnp.concatenate([vec, jnp.zeros((12, 3 * shard), BF)])
    heads_own, heads_send, w2_send, inner_half, outer_half = run(
        prepare_kernel,
        [
            ((shard, 3 * shard), BF),
            ((shard // 2 + 16, 3 * shard), BF),
            ((shard // 4 * 3 + half // 4, dim), BF),
            ((shard, 4 * half), BF),
            ((half, dim), BF),
        ],
        (query_weight, key_weight, value_weight, out_weight, inner_weight, outer_weight, vec),
    )
    got = [turn(heads_send, step) for step in (1, 2, 3)]
    gone = [flip(value, 4) for value in got]
    pieces = []
    for step in (1, 2, 3):
        piece = turn(w2_send, step)
        pieces += [piece, flip(piece, 2), flip(piece, 4), flip(piece, 6)]

    at = shard // 2
    rel = jnp.stack([vec[:4]] + [value[at : at + 4] for value in got]).reshape(4, 12, shard)
    vectors = wide(lax.dynamic_slice_in_dim(jnp.concatenate([rel, rel]), (4 - own) % 4, 4))
    mine_b = pick(vectors, group)
    heads_bias = jnp.concatenate([mine_b[0], jnp.zeros_like(mine_b[0]), mine_b[1]])[None]
    inner_b = pick(vectors[:, 8:].reshape(4, 2, half), core, 1).reshape(1, 4 * half)
    vectors = jnp.swapaxes(vectors[:, :8], 0, 1).reshape(8, dim)

    lengths = pick(doc_lengths[:, 0], y)
    starts = jnp.cumsum(lengths) - lengths
    index = jnp.arange(8 * rows, dtype=jnp.int32)
    code = index // rows
    code = (code >> 2) | (code & 2) | ((code & 1) << 2)
    positions = (ctx ^ code) * rows + index % rows
    seg = jnp.sum((starts[None, :] <= positions[:, None]).astype(jnp.int32), axis=-1) - 1
    segs = (seg[:, None], seg[None, :])

    qkv, m0, m1, m2, m3, logsum, heads_weight = run(
        attend_kernel,
        [((9, 8 * rows, HEAD_DIM), BF)]
        + [((count, shard), BF)] * 4
        + [((8 * rows, 128), F32), ((dim, 3 * shard), BF)],
        (mine, other, far, heads_own, *got, *gone, heads_bias, *segs),
    )
    mixed = [m0, flip(m1, 1), flip(m2, 2), flip(m3, 3)]

    first_sum, first_low, out_full = run(
        project_kernel,
        [((count, dim), F32), ((count, dim), BF), ((dim, dim), BF)],
        (*mixed, mine, out_weight, vectors, *pieces),
    )
    first_far = flip(first_low, 1)
    keep, send, inner, active, wi_full, wo2_full = run(
        forward_kernel,
        [
            ((count, dim), F32),
            ((count, dim), F32),
            ((2 * count, 4 * half), F32),
            ((2 * count, 4 * half), BF),
            ((dim, 4 * half), BF),
            ((4 * half, dim), BF),
        ],
        (first_low, first_far, inner_half, outer_half, inner_b, *pieces),
    )
    cot = pick(cotangent[:, 0], y), flip(pick(cotangent[:, 0], 1 - y), 4)
    out0, out1, dsecond, douter, sums2 = run(
        turnaround_kernel,
        [
            ((rows, dim), BF),
            ((rows, dim), BF),
            ((count, dim), F32),
            ((count, dim), BF),
            ((8, dim), F32),
        ],
        (first_sum, keep, flip(send, 1), vectors, *cot),
    )
    output = pair(out0, flip(out1, 4), y)

    douter_far = flip(douter, 1)
    keep, send, dinner, sums3 = run(
        backward_kernel,
        [
            ((count, dim), F32),
            ((count, dim), F32),
            ((2 * count, 4 * half), BF),
            ((8, dim), F32),
        ],
        (douter, douter_far, inner, wi_full, wo2_full),
    )
    dfirst_sum, dbranch, d0, d1, d2, d3, sums1 = run(
        branch_kernel,
        [((count, dim), F32), ((count, dim), BF)] + [((count, shard), BF)] * 4 + [((8, dim), F32)],
        (first_sum, dsecond, keep, flip(send, 1), vectors, out_full),
    )
    dmixed = [d0, flip(d1, 1), flip(d2, 2), flip(d3, 3)]

    ak, az, bk, bz = run(
        weights_kernel,
        [((dim // 2, 4 * half), BF)] * 2 + [((2 * half, dim), BF)] * 2,
        (first_low, first_far, douter, douter_far, dinner, active),
        [pltpu.VMEM((dim, 4 * half), BF), pltpu.VMEM((4 * half, dim), BF)],
    )
    ar, br = flip(az, 2), flip(bz, 4)
    (packed,) = run(
        out_weight_kernel, [((dim + 16, dim), BF)], (*mixed, dbranch, sums1, sums2, sums3)
    )
    ck, cz = run(out_split_kernel, [((dim // 2 + 16, dim), BF)] * 2, (packed, flip(packed, 1)))
    cr = flip(cz, 2)

    h0, h1, h2, h3, keep, send = run(
        attend_back_kernel,
        [((shard + 16, 3 * shard), F32)]
        + [((shard + 16, 3 * shard), BF)] * 3
        + [((2 * count, dim), F32), ((2 * count, dim), BF)],
        (qkv, logsum, *segs, *dmixed, mine, other, far, heads_weight),
        [
            pltpu.VMEM((4 * count, 3 * shard), BF),
            pltpu.VMEM((3, 4 * count, HEAD_DIM), F32),
            pltpu.VMEM((3, 4 * count, HEAD_DIM), F32),
            pltpu.VMEM((dim, 3 * shard), F32),
        ],
    )

    a2k, a2z, b2k, b2z, c2k, c2z = run(
        reduce_kernel,
        [((dim // 4, 4 * half), BF)] * 2
        + [((half, dim), BF)] * 2
        + [((dim // 4 + 16, dim), BF)] * 2,
        (ak, ar, bk, br, ck, cr),
    )
    size = shard // 4 * 3 + half // 4 + 16
    p0, p1, p2, p3 = run(
        owners_kernel,
        [((size, dim), F32)] + [((size, dim), BF)] * 3,
        (a2k, flip(a2z, 4), b2k, flip(b2z, 2), c2k, flip(c2z, 4)),
    )
    (mine_p,) = run(
        total_kernel, [((size, dim), BF)], (p0, turn(p1, 1), turn(p2, 2), turn(p3, 3))
    )
    plane = [mine_p, flip(mine_p, 2), flip(mine_p, 4), flip(mine_p, 6)]
    plane += [flip(piece, 1) for piece in plane]
    dinner_w, douter_w, dout_w, small = run(
        finish_kernel,
        [((shard, 8 * half), F32), ((hidden, dim), F32), ((shard, dim), F32), ((16, dim), F32)],
        plane,
    )
    dinner_b = pick(small[6:10].reshape(2, 4, half), own, 1).reshape(hidden)
    small = lax.dynamic_slice_in_dim(small[:6], own * shard, shard, 1)

    (heads,) = run(
        total_kernel,
        [((shard + 16, 3 * shard), BF)],
        (h0, turn(h1, 1), turn(h2, 2), turn(h3, 3)),
    )
    (heads,) = run(total_kernel, [((shard + 16, 3 * shard), BF)], (heads, flip(heads, 4)))
    dquery_w, dkey_w, dvalue_w, heads_b = run(
        heads_kernel,
        [((shard, dim), F32)] * 3 + [((16, 3 * shard), F32)],
        (heads, flip(heads, 1), flip(heads, 2), flip(heads, 3)),
    )

    dtokens = keep + wide(flip(send, 1))
    dtokens = dtokens[:count] + wide(flip(short(dtokens[count:]), 2)) + dfirst_sum
    tokens_grad = pair(dtokens[:rows], wide(flip(short(dtokens[rows:]), 4)), y)

    return (
        output[:, None],
        tokens_grad[:, None],
        dquery_w,
        heads_b[0, :shard],
        dkey_w,
        dvalue_w,
        heads_b[0, 2 * shard :],
        dout_w,
        small[0],
        small[1],
        small[2],
        dinner_w,
        dinner_b,
        douter_w,
        small[3],
        small[4],
        small[5],
    )


def solution(mesh):
    placed = (
        P(None, "wt", "ctx", None),
        P(None, "wt", None),
        P("wt", None),
        P("wt"),
        P("wt", None),
        P("wt", None),
        P("wt"),
        P("wt", None),
        P("wt"),
        P("wt"),
        P("wt"),
        P("wt", None),
        P("wt"),
        P("wt", None),
        P("wt"),
        P("wt"),
        P("wt"),
        P(None, "wt", "ctx", None),
    )
    fits = mesh.shape["ctx"] == 8 and mesh.shape["wt"] == 4
    return jax.shard_map(
        plane_device if fits else general_device,
        mesh=mesh,
        in_specs=placed,
        out_specs=(
            P(None, "wt", "ctx", None),
            P(None, "wt", "ctx", None),
            P("wt", None),
            P("wt"),
            P("wt", None),
            P("wt", None),
            P("wt"),
            P("wt", None),
            P("wt"),
            P("wt"),
            P("wt"),
            P("wt", None),
            P("wt"),
            P("wt", None),
            P("wt"),
            P("wt"),
            P("wt"),
        ),
        check_vma=False,
    )
```

```python
import math

import jax
import jax.numpy as jnp
from jax import lax
from jax.experimental import pallas as pl
from jax.experimental.pallas import tpu as pltpu
from jax.sharding import PartitionSpec as P


HEADS = 12
HEAD_DIM = 64


EPS = 1e-12
NEG = -1e30
ROOT_HALF = 0.7071067811865476


def for_sending(shard):

    def short(part):
        return part.astype(jnp.bfloat16) if part.dtype == jnp.float32 else part

    return jax.tree.map(short, shard)


def normalize(rows, gain, shift):
    mean = jnp.mean(rows, axis=-1, keepdims=True)
    centered = rows - mean
    spread = jnp.mean(centered * centered, axis=-1, keepdims=True)
    return centered * lax.rsqrt(spread + EPS) * gain + shift


def gelu(inner):
    return 0.5 * inner * (1.0 + lax.erf(inner * ROOT_HALF))


def segment_of(starts, positions):
    found = (starts[:, None, :] <= positions[:, :, None]).astype(jnp.int32)
    return jnp.sum(found, axis=-1) - 1


def project(inputs, weight):
    return jnp.einsum("btd,de->bte", inputs, weight, preferred_element_type=jnp.float32)


def project_back(grads, weight):
    return jnp.einsum("bte,de->btd", grads, weight, preferred_element_type=jnp.float32)


def outer_sum(inputs, grads):
    return jnp.einsum("btd,bte->de", inputs, grads, preferred_element_type=jnp.float32)


def row_sum(grads):
    return jnp.sum(grads.astype(jnp.float32), axis=(0, 1))


def heads_of(array):
    return array.reshape(array.shape[0], array.shape[1], HEADS, HEAD_DIM)


def block_loop(width, carry, visit):
    block = math.gcd(width, 512)

    def step(state, index):
        return (visit(state, index * block, block), None)

    carry, _ = lax.scan(step, carry, jnp.arange(width // block, dtype=jnp.int32))
    return carry


def reaches(starts, own_seg, first, count):
    positions = first + jnp.arange(count, dtype=jnp.int32)
    other = segment_of(starts, jnp.broadcast_to(positions, (starts.shape[0], count)))
    touch = jnp.any((other[:, 0] <= own_seg[:, -1]) & (other[:, -1] >= own_seg[:, 0]))
    return (other, touch)


def keep_state(state):
    return state


def forward_attention(queries, query_seg, starts, keys, values):
    scale = HEAD_DIM ** (-0.5)
    batch, rows = (queries.shape[0], queries.shape[1])
    query_heads = heads_of(queries)

    def forward_fold(carry, piece, start):
        key_piece, value_piece = piece

        def visit(state, offset, count):
            other, touch = reaches(starts, query_seg, offset, count)

            def compute(state):
                top, total, accum = state
                key_block = heads_of(lax.dynamic_slice_in_dim(key_piece, offset, count, 1))
                value_block = heads_of(lax.dynamic_slice_in_dim(value_piece, offset, count, 1))
                scores = (
                    jnp.einsum(
                        "bqhd,bkhd->bhqk",
                        query_heads,
                        key_block,
                        preferred_element_type=jnp.float32,
                    )
                    * scale
                )
                mask = (query_seg[:, :, None] == other[:, None, :])[:, None]
                scores = jnp.where(mask, scores, NEG)
                new_top = jnp.maximum(top, jnp.max(scores, axis=-1))
                expd = jnp.where(mask, jnp.exp(scores - new_top[..., None]), 0.0)
                factor = jnp.exp(top - new_top)
                total = total * factor + jnp.sum(expd, axis=-1)
                added = jnp.einsum(
                    "bhqk,bkhd->bqhd",
                    expd.astype(jnp.bfloat16),
                    value_block,
                    preferred_element_type=jnp.float32,
                )
                accum = accum * jnp.transpose(factor, (0, 2, 1))[..., None] + added
                return (new_top, total, accum)

            return lax.cond(touch, compute, keep_state, state)

        return block_loop(key_piece.shape[1], carry, visit)

    init = (
        jnp.full((batch, HEADS, rows), NEG, jnp.float32),
        jnp.zeros((batch, HEADS, rows), jnp.float32),
        jnp.zeros((batch, rows, HEADS, HEAD_DIM), jnp.float32),
    )
    whole = (keys, values)
    top, total, accum = forward_fold(
        init,
        (
            lax.all_gather(keys, "ctx", axis=1, tiled=True),
            lax.all_gather(values, "ctx", axis=1, tiled=True),
        ),
        jnp.int32(0),
    )
    mixed = accum / jnp.transpose(total, (0, 2, 1))[..., None]
    return (mixed, top + jnp.log(total), whole)


def query_gradient(queries, query_seg, starts, keys, values, dmixed, logsum, delta):
    scale = HEAD_DIM ** (-0.5)
    query_heads = heads_of(queries)
    grad_heads = heads_of(dmixed)

    def query_fold(carry, piece, start):
        key_piece, value_piece = piece

        def visit(state, offset, count):
            other, touch = reaches(starts, query_seg, offset, count)

            def compute(state):
                key_block = heads_of(lax.dynamic_slice_in_dim(key_piece, offset, count, 1))
                value_block = heads_of(lax.dynamic_slice_in_dim(value_piece, offset, count, 1))
                scores = (
                    jnp.einsum(
                        "bqhd,bkhd->bhqk",
                        query_heads,
                        key_block,
                        preferred_element_type=jnp.float32,
                    )
                    * scale
                )
                mask = (query_seg[:, :, None] == other[:, None, :])[:, None]
                probs = jnp.where(
                    mask, jnp.exp(jnp.where(mask, scores, NEG) - logsum[..., None]), 0.0
                )
                dprobs = jnp.einsum(
                    "bqhd,bkhd->bhqk", grad_heads, value_block, preferred_element_type=jnp.float32
                )
                dscores = (probs * (dprobs - delta[..., None])).astype(jnp.bfloat16)
                return (
                    state
                    + jnp.einsum(
                        "bhqk,bkhd->bqhd", dscores, key_block, preferred_element_type=jnp.float32
                    )
                    * scale
                )

            return lax.cond(touch, compute, keep_state, state)

        return block_loop(key_piece.shape[1], carry, visit)

    init = jnp.zeros(query_heads.shape, jnp.float32)
    return query_fold(
        init,
        (
            lax.all_gather(keys, "ctx", axis=1, tiled=True),
            lax.all_gather(values, "ctx", axis=1, tiled=True),
        ),
        jnp.int32(0),
    )


def key_gradient(keys, values, key_seg, starts, queries, dmixed, logsum, delta):
    scale = HEAD_DIM ** (-0.5)
    key_heads = heads_of(keys)
    value_heads = heads_of(values)
    every_top, every_delta = (
        lax.all_gather(logsum, "ctx", axis=2, tiled=True),
        lax.all_gather(delta, "ctx", axis=2, tiled=True),
    )

    def key_fold(carry, piece, start):
        query_piece, grad_piece = piece

        def visit(state, offset, count):
            other, touch = reaches(starts, key_seg, offset, count)

            def compute(state):
                dkeys, dvalues = state
                query_block = heads_of(lax.dynamic_slice_in_dim(query_piece, offset, count, 1))
                grad_block = heads_of(lax.dynamic_slice_in_dim(grad_piece, offset, count, 1))
                top_block = lax.dynamic_slice_in_dim(every_top, offset, count, 2)
                delta_block = lax.dynamic_slice_in_dim(every_delta, offset, count, 2)
                scores = (
                    jnp.einsum(
                        "bqhd,bkhd->bhqk",
                        query_block,
                        key_heads,
                        preferred_element_type=jnp.float32,
                    )
                    * scale
                )
                mask = (other[:, :, None] == key_seg[:, None, :])[:, None]
                probs = jnp.where(
                    mask, jnp.exp(jnp.where(mask, scores, NEG) - top_block[..., None]), 0.0
                )
                dvalues = dvalues + jnp.einsum(
                    "bhqk,bqhd->bkhd",
                    probs.astype(jnp.bfloat16),
                    grad_block,
                    preferred_element_type=jnp.float32,
                )
                dprobs = jnp.einsum(
                    "bqhd,bkhd->bhqk", grad_block, value_heads, preferred_element_type=jnp.float32
                )
                dscores = (probs * (dprobs - delta_block[..., None])).astype(jnp.bfloat16)
                dkeys = (
                    dkeys
                    + jnp.einsum(
                        "bhqk,bqhd->bkhd", dscores, query_block, preferred_element_type=jnp.float32
                    )
                    * scale
                )
                return (dkeys, dvalues)

            return lax.cond(touch, compute, keep_state, state)

        return block_loop(query_piece.shape[1], carry, visit)

    empty = jnp.zeros(key_heads.shape, jnp.float32)
    return key_fold(
        (empty, empty),
        (
            lax.all_gather(queries, "ctx", axis=1, tiled=True),
            lax.all_gather(dmixed, "ctx", axis=1, tiled=True),
        ),
        jnp.int32(0),
    )


def forward_pass(tokens, starts, weights, base):
    (
        query_weight,
        query_bias,
        key_weight,
        value_weight,
        value_bias,
        out_weight,
        out_bias,
        first_gain,
        first_shift,
        inner_weight,
        inner_bias,
        outer_weight,
        outer_bias,
        second_gain,
        second_shift,
    ) = weights
    rows = tokens.shape[1]
    positions = base + jnp.arange(rows, dtype=jnp.int32)
    query_seg = segment_of(starts, jnp.broadcast_to(positions, (tokens.shape[0], rows)))
    queries = (project(tokens, query_weight) + query_bias.astype(jnp.float32)).astype(jnp.bfloat16)
    keys = project(tokens, key_weight).astype(jnp.bfloat16)
    values = (project(tokens, value_weight) + value_bias.astype(jnp.float32)).astype(jnp.bfloat16)
    mixed, logsum, whole = forward_attention(queries, query_seg, starts, keys, values)
    mixed_low = mixed.reshape(tokens.shape).astype(jnp.bfloat16)
    first_sum = (
        tokens.astype(jnp.float32) + project(mixed_low, out_weight) + out_bias.astype(jnp.float32)
    )
    first = normalize(first_sum, first_gain.astype(jnp.float32), first_shift.astype(jnp.float32))
    first_low = first.astype(jnp.bfloat16)
    inner = project(first_low, inner_weight) + inner_bias.astype(jnp.float32)
    active = gelu(inner).astype(jnp.bfloat16)
    second_sum = first + project(active, outer_weight) + outer_bias.astype(jnp.float32)
    output = normalize(
        second_sum, second_gain.astype(jnp.float32), second_shift.astype(jnp.float32)
    ).astype(jnp.bfloat16)
    saved = (
        tokens,
        query_seg,
        queries,
        keys,
        values,
        mixed,
        logsum,
        mixed_low,
        first_sum,
        first_low,
        inner,
        active,
        second_sum,
        whole,
    )
    return (output, saved)


def backward_pass(saved, starts, weights, cotangent):
    (
        query_weight,
        _,
        key_weight,
        value_weight,
        _,
        out_weight,
        _,
        first_gain,
        first_shift,
        inner_weight,
        _,
        outer_weight,
        _,
        second_gain,
        second_shift,
    ) = weights
    (
        tokens,
        query_seg,
        queries,
        keys,
        values,
        mixed,
        logsum,
        mixed_low,
        first_sum,
        first_low,
        inner,
        active,
        second_sum,
        _,
    ) = saved
    unused, second_back = jax.vjp(
        normalize, second_sum, second_gain.astype(jnp.float32), second_shift.astype(jnp.float32)
    )
    dsecond, dgain_second, dshift_second = second_back(cotangent.astype(jnp.float32))
    douter = dsecond.astype(jnp.bfloat16)
    dactive = project_back(douter, outer_weight)
    unused, gelu_back = jax.vjp(gelu, inner)
    dinner = gelu_back(dactive)[0].astype(jnp.bfloat16)
    dfirst = dsecond + project_back(dinner, inner_weight)
    unused, first_back = jax.vjp(
        normalize, first_sum, first_gain.astype(jnp.float32), first_shift.astype(jnp.float32)
    )
    dfirst_sum, dgain_first, dshift_first = first_back(dfirst)
    dbranch = dfirst_sum.astype(jnp.bfloat16)
    dmixed = project_back(dbranch, out_weight).astype(jnp.bfloat16)
    delta = jnp.einsum("bqhd,bqhd->bhq", heads_of(dmixed).astype(jnp.float32), mixed)
    dqueries = query_gradient(queries, query_seg, starts, keys, values, dmixed, logsum, delta)
    dkeys, dvalues = key_gradient(keys, values, query_seg, starts, queries, dmixed, logsum, delta)
    dqueries = dqueries.reshape(tokens.shape).astype(jnp.bfloat16)
    dkeys = dkeys.reshape(tokens.shape).astype(jnp.bfloat16)
    dvalues = dvalues.reshape(tokens.shape).astype(jnp.bfloat16)
    tokens_grad = (
        dfirst_sum
        + project_back(dqueries, query_weight)
        + project_back(dkeys, key_weight)
        + project_back(dvalues, value_weight)
    )
    sums = (
        outer_sum(tokens, dqueries),
        row_sum(dqueries),
        outer_sum(tokens, dkeys),
        outer_sum(tokens, dvalues),
        row_sum(dvalues),
        outer_sum(mixed_low, dbranch),
        row_sum(dbranch),
        dgain_first,
        dshift_first,
        outer_sum(first_low, dinner),
        row_sum(dinner),
        outer_sum(active, douter),
        row_sum(douter),
        dgain_second,
        dshift_second,
    )
    return (tokens_grad, sums)


def general_device(
    tokens,
    doc_lengths,
    query_weight,
    query_bias,
    key_weight,
    value_weight,
    value_bias,
    out_weight,
    out_bias,
    first_gain,
    first_shift,
    inner_weight,
    inner_bias,
    outer_weight,
    outer_bias,
    second_gain,
    second_shift,
    cotangent,
):
    params = (
        query_weight,
        query_bias,
        key_weight,
        value_weight,
        value_bias,
        out_weight,
        out_bias,
        first_gain,
        first_shift,
        inner_weight,
        inner_bias,
        outer_weight,
        outer_bias,
        second_gain,
        second_shift,
    )
    rows = tokens.shape[2]
    base = lax.axis_index("ctx") * rows
    lengths = doc_lengths[:, 0]
    starts = jnp.cumsum(lengths, axis=-1) - lengths
    outputs = []
    token_parts = []
    sums = None
    for index in range(tokens.shape[0]):
        weights = (
            lax.all_gather(params[0], "wt", axis=0, tiled=True),
            lax.all_gather(params[1], "wt", axis=0, tiled=True),
            lax.all_gather(params[2], "wt", axis=0, tiled=True),
            lax.all_gather(params[3], "wt", axis=0, tiled=True),
            lax.all_gather(params[4], "wt", axis=0, tiled=True),
            lax.all_gather(params[5], "wt", axis=0, tiled=True),
            lax.all_gather(params[6], "wt", axis=0, tiled=True),
            lax.all_gather(params[7], "wt", axis=0, tiled=True),
            lax.all_gather(params[8], "wt", axis=0, tiled=True),
            lax.all_gather(params[9], "wt", axis=0, tiled=True),
            lax.all_gather(params[10], "wt", axis=0, tiled=True),
            lax.all_gather(params[11], "wt", axis=0, tiled=True),
            lax.all_gather(params[12], "wt", axis=0, tiled=True),
            lax.all_gather(params[13], "wt", axis=0, tiled=True),
            lax.all_gather(params[14], "wt", axis=0, tiled=True),
        )
        part_out, saved = forward_pass(
            tokens[index : index + 1, 0], starts[index : index + 1], weights, base
        )
        again = (
            lax.all_gather(params[0], "wt", axis=0, tiled=True),
            lax.all_gather(params[1], "wt", axis=0, tiled=True),
            lax.all_gather(params[2], "wt", axis=0, tiled=True),
            lax.all_gather(params[3], "wt", axis=0, tiled=True),
            lax.all_gather(params[4], "wt", axis=0, tiled=True),
            lax.all_gather(params[5], "wt", axis=0, tiled=True),
            lax.all_gather(params[6], "wt", axis=0, tiled=True),
            lax.all_gather(params[7], "wt", axis=0, tiled=True),
            lax.all_gather(params[8], "wt", axis=0, tiled=True),
            lax.all_gather(params[9], "wt", axis=0, tiled=True),
            lax.all_gather(params[10], "wt", axis=0, tiled=True),
            lax.all_gather(params[11], "wt", axis=0, tiled=True),
            lax.all_gather(params[12], "wt", axis=0, tiled=True),
            lax.all_gather(params[13], "wt", axis=0, tiled=True),
            lax.all_gather(params[14], "wt", axis=0, tiled=True),
        )
        part_grad, part_sums = backward_pass(
            saved, starts[index : index + 1], again, cotangent[index : index + 1, 0]
        )
        outputs.append(part_out)
        token_parts.append(part_grad)
        sums = part_sums if sums is None else jax.tree.map(jnp.add, sums, part_sums)
    output = jnp.concatenate(outputs, axis=0)
    tokens_grad = jnp.concatenate(token_parts, axis=0)
    shards = jax.tree.map(
        lambda part: part.astype(jnp.float32),
        lax.psum_scatter(for_sending(sums), "wt", scatter_dimension=0, tiled=True),
    )
    totals = lax.psum(shards, "ctx")
    return (output[:, None], tokens_grad[:, None]) + tuple(totals)


def flip(value, bits):
    return lax.ppermute(value, "ctx", [(i, i ^ bits) for i in range(8)])


def turn(value, step):
    return lax.ppermute(value, "wt", [(i, (i - step) % 4) for i in range(4)])


def pick(value, index, axis=0):
    return lax.dynamic_index_in_dim(value, index, axis, keepdims=False)


def pair(own, other, bit, axis=0):
    return jnp.where(bit == 0, jnp.stack([own, other], axis), jnp.stack([other, own], axis))


def short(value):
    return value.astype(jnp.bfloat16)


def wide(value):
    return value.astype(jnp.float32)


def dot(left, right):
    return jnp.dot(left, right, preferred_element_type=jnp.float32)


def dot_back(left, right):
    return lax.dot_general(
        left, right, (((1,), (1,)), ((), ())), preferred_element_type=jnp.float32
    )


def dot_sum(left, right):
    return lax.dot_general(
        left, right, (((0,), (0,)), ((), ())), preferred_element_type=jnp.float32
    )


def norm_parts(rows):
    mean = jnp.mean(rows, axis=-1, keepdims=True)
    centered = rows - mean
    spread = jnp.mean(centered * centered, axis=-1, keepdims=True)
    root = lax.rsqrt(spread + EPS)
    return centered * root, root


def norm_back(upstream, normed, root, gain):
    grad = upstream * gain
    mean = jnp.mean(grad, axis=-1, keepdims=True)
    along = jnp.mean(grad * normed, axis=-1, keepdims=True)
    return root * (grad - mean - normed * along)


def gelu_slope(inner):
    bell = jnp.exp(-0.5 * inner * inner) * (1.0 / math.sqrt(2.0 * math.pi))
    return 0.5 * (1.0 + lax.erf(inner * ROOT_HALF)) + inner * bell


def run(kernel, outs, args, scratch=()):
    shapes = tuple(jax.ShapeDtypeStruct(shape, dtype) for shape, dtype in outs)
    return pl.pallas_call(kernel, out_shape=shapes, scratch_shapes=list(scratch))(*args)


BF = jnp.bfloat16
F32 = jnp.float32


def where_am_i():
    ctx, own = lax.axis_index("ctx"), lax.axis_index("wt")
    return ctx & 1, (ctx >> 1) & 3, ctx & 3, own


def some_rows(start, count):
    return pl.ds(pl.multiple_of(start, 16), count)


def prepare_kernel(wq, wk, wv, wo, wi, wo2, vec, heads_own, heads_send, w2_send, inner_half, outer_half):
    core, quarter, group, _ = where_am_i()
    shard, dim = wq.shape
    width, half = dim // 4, wo2.shape[0] // 2
    for index in range(4):

        @pl.when(group == index)
        def _():
            for slot, ref in enumerate((wq, wk, wv)):
                heads_own[:, slot * width : (slot + 1) * width] = ref[
                    :, index * width : (index + 1) * width
                ]

    for index in range(2):

        @pl.when(core == index)
        def _():
            for block in range(4):
                at = block * 2 * half + index * half
                inner_half[:, block * half : (block + 1) * half] = wi[:, at : at + half]
            outer_half[...] = wo2[index * half : (index + 1) * half, :]

    part = shard // 2
    heads_send[0:part, :] = heads_own[some_rows((quarter >> 1) * part, part), :]
    heads_send[part:, 0:width] = vec[...]
    heads_send[part:, width:] = jnp.zeros((16, 2 * width), BF)
    part = shard // 4
    rows = some_rows(quarter * part, part)
    w2_send[0:part, :] = inner_half[rows, 0:dim]
    w2_send[part : 2 * part, :] = inner_half[rows, dim:]
    step = half // 4
    w2_send[2 * part : 2 * part + step, :] = outer_half[some_rows(quarter * step, step), :]
    w2_send[2 * part + step :, :] = wo[rows, :]


def attend_kernel(
    mine, other, far, heads_own, g1, g2, g3, h1, h2, h3, bias, seg_col, seg_row,
    qkv, m0, m1, m2, m3, logsum, weight,
):
    _, quarter, _, own = where_am_i()
    scale = HEAD_DIM ** (-0.5)
    shard = heads_own.shape[0]
    part = shard // 2
    y = quarter >> 1
    weight[some_rows(own * shard, shard), :] = heads_own[...]
    for step, near_half, far_half in ((1, g1, h1), (2, g2, h2), (3, g3, h3)):
        at = ((own + step) & 3) * shard
        weight[some_rows(at + part * y, part), :] = near_half[0:part, :]
        weight[some_rows(at + part * (1 - y), part), :] = far_half[0:part, :]
    group = weight.shape[1] // (3 * HEAD_DIM)
    block = mine.shape[0]
    at = 0
    for source in (mine, other, far):
        for first in range(0, source.shape[0], block):
            rows = source[first : first + block, :]
            low = short(dot(rows, weight[...]) + bias[...])
            for slot in range(3 * group):
                qkv[slot, at : at + block, :] = low[:, slot * HEAD_DIM : (slot + 1) * HEAD_DIM]
            at += block

    for index, out_ref in enumerate((m0, m2, m1, m3)):
        at = index * block
        mask = seg_col[at : at + block, :] == seg_row[...]
        sums = []
        for head in range(group):
            scores = dot_back(qkv[head, at : at + block, :], qkv[group + head])
            scores = jnp.where(mask, scores * scale, NEG)
            top = jnp.max(scores, axis=-1, keepdims=True)
            expd = jnp.exp(scores - top)
            total = jnp.sum(expd, axis=-1, keepdims=True)
            probs = short(expd * (1.0 / total))
            out_ref[:, head * HEAD_DIM : (head + 1) * HEAD_DIM] = short(
                dot(probs, qkv[2 * group + head])
            )
            sums.append(top + jnp.log(total))
        logsum[at : at + block, :] = jnp.concatenate(
            sums + [jnp.zeros_like(sums[0])] * (128 - group), axis=1
        )


def project_kernel(m0, m1, m2, m3, mine, wo, vec, *refs):
    pieces, (first_sum, first_low, out_full) = refs[:12], refs[12:]
    _, quarter, group, own = where_am_i()
    shard = wo.shape[0]
    part = shard // 4
    out_full[some_rows(own * shard, shard), :] = wo[...]
    for index, piece in enumerate(pieces):
        at = ((own + 1 + index // 4) & 3) * shard + part * (quarter ^ (index % 4))
        out_full[some_rows(at, part), :] = piece[piece.shape[0] - part :, :]
    total = wide(mine[...]) + vec[2:3, :]
    for code, ref in enumerate((m0, m1, m2, m3)):
        total += dot(ref[...], out_full[some_rows((group ^ code) * shard, shard), :])
    first_sum[...] = total
    first_low[...] = short(norm_parts(total)[0] * vec[3:4, :] + vec[4:5, :])


def forward_kernel(near, far, inner_half, outer_half, bias, *refs):
    pieces, (keep, send, inner, active, wi_full, wo2_full) = refs[:12], refs[12:]
    _, quarter, _, own = where_am_i()
    shard, half = inner_half.shape[0], outer_half.shape[0]
    dim = keep.shape[1]
    part, step = shard // 4, half // 4
    wi_full[some_rows(own * shard, shard), :] = inner_half[...]
    wo2_full[some_rows(own * half, half), :] = outer_half[...]
    for index, piece in enumerate(pieces):
        row, spot = (own + 1 + index // 4) & 3, quarter ^ (index % 4)
        rows = some_rows(row * shard + part * spot, part)
        wi_full[rows, 0:dim] = piece[0:part, :]
        wi_full[rows, dim:] = piece[part : 2 * part, :]
        wo2_full[some_rows(row * half + step * spot, step), :] = piece[
            2 * part : 2 * part + step, :
        ]
    count = near.shape[0]
    chunk = 512
    for index, (source, out) in enumerate(((far, send), (near, keep))):
        at = (1 - index) * count
        total = None
        for lane in range(0, inner.shape[1], chunk):
            lanes = slice(lane, lane + chunk)
            value = dot(source[...], wi_full[:, lanes]) + bias[:, lanes]
            inner[at : at + count, lanes] = value
            low = short(gelu(value))
            active[at : at + count, lanes] = low
            added = dot(low, wo2_full[lanes, :])
            total = added if total is None else total + added
        out[...] = total


def turnaround_kernel(first_sum, keep, got, vec, cot0, cot1, out0, out1, dsecond, douter, sums):
    rows = cot0.shape[0]
    first = norm_parts(first_sum[...])[0] * vec[3:4, :] + vec[4:5, :]
    normed, root = norm_parts(first + vec[5:6, :] + keep[...] + got[...])
    output = short(normed * vec[6:7, :] + vec[7:8, :])
    out0[...] = output[:rows]
    out1[...] = output[rows:]
    upstream = jnp.concatenate([wide(cot0[...]), wide(cot1[...])])
    back = norm_back(upstream, normed, root, vec[6:7, :])
    low = short(back)
    dsecond[...] = back
    douter[...] = low
    sums[0:1, :] = jnp.sum(wide(low), axis=0, keepdims=True)
    sums[1:2, :] = jnp.sum(upstream * normed, axis=0, keepdims=True)
    sums[2:3, :] = jnp.sum(upstream, axis=0, keepdims=True)
    sums[3:, :] = jnp.zeros_like(sums[3:, :])


def backward_kernel(near, far, inner, wi_full, wo2_full, keep, send, dinner, sums):
    count, dim = near.shape
    chunk = 512
    for index, (source, out) in enumerate(((far, send), (near, keep))):
        at = (1 - index) * count
        total = None
        for lane in range(0, inner.shape[1], chunk):
            lanes = slice(lane, lane + chunk)
            slope = gelu_slope(inner[at : at + count, lanes])
            low = short(dot_back(source[...], wo2_full[lanes, :]) * slope)
            dinner[at : at + count, lanes] = low
            added = dot_back(low, wi_full[:, lanes])
            total = added if total is None else total + added
        out[...] = total
    total = jnp.sum(wide(dinner[...]), axis=0, keepdims=True)
    sums[0:1, :] = total[:, :dim]
    sums[1:2, :] = total[:, dim:]
    sums[2:, :] = jnp.zeros_like(sums[2:, :])


def weights_kernel(first0, first1, douter0, douter1, dinner, active, ak, az, bk, bz, left, right):
    _, quarter, _, _ = where_am_i()
    x, y = quarter & 1, quarter >> 1
    count = first0.shape[0]
    part, step = first0.shape[1] // 16, active.shape[1] // 16
    left[...] = short(dot_sum(first0[...], dinner[:count]) + dot_sum(first1[...], dinner[count:]))
    for block in range(8):
        rows = slice(block * part, (block + 1) * part)
        ak[rows, :] = left[some_rows((2 * block + x) * part, part), :]
        az[rows, :] = left[some_rows((2 * block + 1 - x) * part, part), :]
    right[...] = short(
        dot_sum(active[:count], douter0[...]) + dot_sum(active[count:], douter1[...])
    )
    for block in range(8):
        row, side = block // 2, block % 2
        rows = slice(block * step, (block + 1) * step)
        bk[rows, :] = right[some_rows((4 * row + 2 * y + side) * step, step), :]
        bz[rows, :] = right[some_rows((4 * row + 2 * (1 - y) + side) * step, step), :]


def branch_kernel(first_sum, dsecond, keep, got, vec, out_full, dfirst_sum, dbranch, d0, d1, d2, d3, sums):
    _, _, group, _ = where_am_i()
    shard = d0.shape[1]
    normed, root = norm_parts(first_sum[...])
    dfirst = dsecond[...] + keep[...] + got[...]
    back = norm_back(dfirst, normed, root, vec[3:4, :])
    low = short(back)
    dfirst_sum[...] = back
    dbranch[...] = low
    for code, ref in enumerate((d0, d1, d2, d3)):
        ref[...] = short(dot_back(low, out_full[some_rows((group ^ code) * shard, shard), :]))
    sums[0:1, :] = jnp.sum(wide(low), axis=0, keepdims=True)
    sums[1:2, :] = jnp.sum(dfirst * normed, axis=0, keepdims=True)
    sums[2:3, :] = jnp.sum(dfirst, axis=0, keepdims=True)
    sums[3:, :] = jnp.zeros_like(sums[3:, :])


def out_weight_kernel(m0, m1, m2, m3, dbranch, sums1, sums2, sums3, packed):
    _, _, group, _ = where_am_i()
    shard, dim = m0.shape[1], dbranch.shape[1]
    for code, ref in enumerate((m0, m1, m2, m3)):
        packed[some_rows((group ^ code) * shard, shard), :] = short(
            dot_sum(ref[...], dbranch[...])
        )
    rows = jnp.concatenate(
        [sums1[0:3, :], sums2[0:3, :], sums3[0:2, :], jnp.zeros_like(sums1[...])]
    )
    packed[dim:, :] = short(rows)


def out_split_kernel(packed, got, ck, cz):
    core, quarter, _, _ = where_am_i()
    x = quarter & 1
    dim = packed.shape[1]
    part = dim // 16
    for block in range(8):
        rows = slice(block * part, (block + 1) * part)
        for ref, side in ((ck, x), (cz, 1 - x)):
            take = some_rows((2 * block + side) * part, part)
            ref[rows, :] = short(wide(packed[take, :]) + wide(got[take, :]))
    mine, other = wide(packed[dim:, :]), wide(got[dim:, :])
    low = jnp.where(core == 0, mine, other)[6:8]
    high = jnp.where(core == 0, other, mine)[6:8]
    rows = jnp.concatenate([(mine + other)[0:6], low, high, jnp.zeros((6, dim), F32)])
    for ref in (ck, cz):
        ref[8 * part :, :] = short(rows)


def reduce_kernel(ak, ar, bk, br, ck, cr, a2k, a2z, b2k, b2z, c2k, c2z):
    _, quarter, _, _ = where_am_i()
    x, y = quarter & 1, quarter >> 1
    for keep, got, outs, bit in (
        (ak, ar, (a2k, a2z), y),
        (bk, br, (b2k, b2z), x),
        (ck, cr, (c2k, c2z), y),
    ):
        size = keep.shape[0] // 8
        size -= size % 16
        for block in range(4):
            for out, side in zip(outs, (bit, 1 - bit)):
                take = some_rows((2 * block + side) * size, size)
                out[block * size : (block + 1) * size, :] = short(
                    wide(keep[take, :]) + wide(got[take, :])
                )
        if keep.shape[0] > 8 * size:
            for out in outs:
                out[4 * size :, :] = short(wide(keep[8 * size :, :]) + wide(got[8 * size :, :]))


def owners_kernel(ak, ar, bk, br, ck, cr, p0, p1, p2, p3):
    _, _, _, own = where_am_i()
    dim = bk.shape[1]
    part, step = ak.shape[0] // 4, bk.shape[0] // 4
    size = (ck.shape[0] - 16) // 4
    for index, out in enumerate((p0, p1, p2, p3)):
        row = (own - index) & 3
        rows = some_rows(row * part, part)
        total = wide(ak[rows, :]) + wide(ar[rows, :])
        out[0:part, :] = total[:, :dim].astype(out.dtype)
        out[part : 2 * part, :] = total[:, dim:].astype(out.dtype)
        at = 2 * part
        rows = some_rows(row * step, step)
        out[at : at + step, :] = (wide(bk[rows, :]) + wide(br[rows, :])).astype(out.dtype)
        at += step
        rows = some_rows(row * size, size)
        out[at : at + size, :] = (wide(ck[rows, :]) + wide(cr[rows, :])).astype(out.dtype)
        at += size
        out[at:, :] = (wide(ck[4 * size :, :]) + wide(cr[4 * size :, :])).astype(out.dtype)


def total_kernel(mine, *refs):
    total = wide(mine[...])
    for ref in refs[:-1]:
        total += wide(ref[...])
    refs[-1][...] = short(total)


def finish_kernel(*refs):
    pieces, (dwi, dwo2, dwo, small) = refs[:8], refs[8:]
    core, quarter, _, _ = where_am_i()
    part, half = dwi.shape[0] // 4, dwi.shape[1] // 8
    step = half // 4
    for index, piece in enumerate(pieces[:4]):
        at = 2 * part + step
        dwo[some_rows((quarter ^ index) * part, part), :] = wide(piece[at : at + part, :])
    for side in range(2):

        @pl.when(core == side)
        def _():
            for index, piece in enumerate(pieces):
                spot = quarter ^ (index % 4)
                which = side if index < 4 else 1 - side
                rows = some_rows(spot * part, part)
                for block in range(4):
                    at = block * 2 * half + which * half
                    up, lane = part * (block // 2), half * (block % 2)
                    dwi[rows, at : at + half] = wide(piece[up : up + part, lane : lane + half])
                dwo2[some_rows(which * half + spot * step, step), :] = wide(
                    piece[2 * part : 2 * part + step, :]
                )

    small[...] = wide(pieces[0][3 * part + step :, :])


def attend_back_kernel(
    qkv, logsum, seg_col, seg_row, p0, p1, p2, p3, mine, other, far, weight,
    h0, h1, h2, h3, keep, send, grads, dkeys, dvalues, dweight,
):
    _, _, _, own = where_am_i()
    scale = HEAD_DIM ** (-0.5)
    group = qkv.shape[0] // 3
    width = group * HEAD_DIM
    block = p0.shape[0]
    dkeys[...] = jnp.zeros_like(dkeys)
    dvalues[...] = jnp.zeros_like(dvalues)
    for index, part in enumerate((p0, p2, p1, p3)):
        at = index * block
        mask = seg_col[at : at + block, :] == seg_row[...]
        for head in range(group):
            query = qkv[head, at : at + block, :]
            grad = part[:, head * HEAD_DIM : (head + 1) * HEAD_DIM]
            keys = qkv[group + head]
            scores = jnp.where(mask, dot_back(query, keys) * scale, NEG)
            probs = jnp.exp(scores - logsum[at : at + block, head : head + 1])
            dprobs = dot_back(grad, qkv[2 * group + head])
            delta = jnp.sum(probs * dprobs, axis=-1, keepdims=True)
            dscores = short(probs * (dprobs - delta))
            grads[at : at + block, head * HEAD_DIM : (head + 1) * HEAD_DIM] = short(
                dot(dscores, keys) * scale
            )
            dkeys[head] += dot_sum(dscores, query)
            dvalues[head] += dot_sum(short(probs), grad)
    for head in range(group):
        lanes = slice(width + head * HEAD_DIM, width + (head + 1) * HEAD_DIM)
        grads[:, lanes] = short(dkeys[head] * scale)
        lanes = slice(2 * width + head * HEAD_DIM, 2 * width + (head + 1) * HEAD_DIM)
        grads[:, lanes] = short(dvalues[head])
    rows = 2 * block
    dweight[...] = (
        dot_sum(mine[...], grads[:block])
        + dot_sum(other[...], grads[block:rows])
        + dot_sum(far[...], grads[rows:])
    )
    sums = jnp.sum(wide(grads[...]), axis=0, keepdims=True)
    tail = jnp.concatenate([sums, jnp.zeros((15, sums.shape[1]), F32)])
    for index, out in enumerate((h0, h1, h2, h3)):
        take = pl.ds(pl.multiple_of(((own - index) & 3) * width, 16), width)
        out[0:width, :] = dweight[take, :].astype(out.dtype)
        out[width:, :] = tail.astype(out.dtype)
    keep[...] = dot_back(grads[:rows], weight[...])
    send[...] = short(dot_back(grads[rows:], weight[...]))


def heads_kernel(s0, s1, s2, s3, dq, dk, dv, bias):
    _, _, group, own = where_am_i()
    shard = dq.shape[0]
    for index in range(4):

        @pl.when(group == index)
        def _():
            for code, ref in enumerate((s0, s1, s2, s3)):
                at = (index ^ code) * shard
                for slot, out in enumerate((dq, dk, dv)):
                    out[:, at : at + shard] = wide(
                        ref[0:shard, slot * shard : (slot + 1) * shard]
                    )

                @pl.when(own == index ^ code)
                def _():
                    bias[...] = wide(ref[shard:, :])


def plane_steps(
    tokens,
    doc_lengths,
    query_weight,
    query_bias,
    key_weight,
    value_weight,
    value_bias,
    out_weight,
    out_bias,
    first_gain,
    first_shift,
    inner_weight,
    inner_bias,
    outer_weight,
    outer_bias,
    second_gain,
    second_shift,
    cotangent,
):
    ctx, own = lax.axis_index("ctx"), lax.axis_index("wt")
    core, y, group = ctx & 1, ctx >> 2, ctx & 3
    rows, dim = tokens.shape[2], tokens.shape[3]
    shard = query_weight.shape[0]
    hidden = outer_weight.shape[0]
    half = hidden // 2
    count = 2 * rows

    mine = jnp.concatenate([pick(tokens[:, 0], y), flip(pick(tokens[:, 0], 1 - y), 4)])
    other = flip(mine, 2)
    far = flip(jnp.concatenate([mine, other]), 1)

    vector_list = (
        query_bias,
        value_bias,
        out_bias,
        first_gain,
        first_shift,
        outer_bias,
        second_gain,
        second_shift,
        *[inner_bias[at : at + shard] for at in range(0, 4 * shard, shard)],
    )
    line = lax.broadcasted_iota(jnp.int32, (16, shard), 0)
    vec = jnp.zeros((16, shard), BF)
    for index, value in enumerate(vector_list):
        vec = jnp.where(line == index, value[None, :], vec)
    heads_own, heads_send, w2_send, inner_half, outer_half = run(
        prepare_kernel,
        [
            ((shard, 3 * shard), BF),
            ((shard // 2 + 16, 3 * shard), BF),
            ((shard // 4 * 3 + half // 4, dim), BF),
            ((shard, 4 * half), BF),
            ((half, dim), BF),
        ],
        (query_weight, key_weight, value_weight, out_weight, inner_weight, outer_weight, vec),
    )
    got = [turn(heads_send, step) for step in (1, 2, 3)]
    gone = [flip(value, 4) for value in got]
    pieces = []
    for step in (1, 2, 3):
        piece = turn(w2_send, step)
        pieces += [piece] + [flip(piece, bits) for bits in (2, 4, 6)]

    at = shard // 2
    rel = jnp.stack([vec] + [value[at:, :shard] for value in got])
    vectors = wide(lax.dynamic_slice_in_dim(jnp.concatenate([rel, rel]), (4 - own) % 4, 4))
    mine_b = pick(vectors, group)
    heads_bias = jnp.concatenate([mine_b[0], jnp.zeros_like(mine_b[0]), mine_b[1]])[None]
    inner_b = pick(vectors[:, 8:12].reshape(4, 2, half), core, 1).reshape(1, 4 * half)
    vectors = jnp.swapaxes(vectors[:, :8], 0, 1).reshape(8, dim)

    lengths = pick(doc_lengths[:, 0], y)
    starts = jnp.cumsum(lengths) - lengths
    index = jnp.arange(8 * rows, dtype=jnp.int32)
    code = index // rows
    code = (code >> 2) | (code & 2) | ((code & 1) << 2)
    positions = (ctx ^ code) * rows + index % rows
    seg = jnp.sum((starts[None, :] <= positions[:, None]).astype(jnp.int32), axis=-1) - 1
    segs = (seg[:, None], seg[None, :])

    qkv, m0, m1, m2, m3, logsum, heads_weight = run(
        attend_kernel,
        [((9, 8 * rows, HEAD_DIM), BF)]
        + [((count, shard), BF)] * 4
        + [((8 * rows, 128), F32), ((dim, 3 * shard), BF)],
        (mine, other, far, heads_own, *got, *gone, heads_bias, *segs),
    )
    mixed = [m0, flip(m1, 1), flip(m2, 2), flip(m3, 3)]

    first_sum, first_low, out_full = run(
        project_kernel,
        [((count, dim), F32), ((count, dim), BF), ((dim, dim), BF)],
        (*mixed, mine, out_weight, vectors, *pieces),
    )
    first_far = flip(first_low, 1)
    keep, send, inner, active, wi_full, wo2_full = run(
        forward_kernel,
        [
            ((count, dim), F32),
            ((count, dim), F32),
            ((2 * count, 4 * half), F32),
            ((2 * count, 4 * half), BF),
            ((dim, 4 * half), BF),
            ((4 * half, dim), BF),
        ],
        (first_low, first_far, inner_half, outer_half, inner_b, *pieces),
    )
    cot = pick(cotangent[:, 0], y), flip(pick(cotangent[:, 0], 1 - y), 4)
    out0, out1, dsecond, douter, sums2 = run(
        turnaround_kernel,
        [
            ((rows, dim), BF),
            ((rows, dim), BF),
            ((count, dim), F32),
            ((count, dim), BF),
            ((8, dim), F32),
        ],
        (first_sum, keep, flip(send, 1), vectors, *cot),
    )
    output = pair(out0, flip(out1, 4), y)

    douter_far = flip(douter, 1)
    keep, send, dinner, sums3 = run(
        backward_kernel,
        [
            ((count, dim), F32),
            ((count, dim), F32),
            ((2 * count, 4 * half), BF),
            ((8, dim), F32),
        ],
        (douter, douter_far, inner, wi_full, wo2_full),
    )
    dfirst_sum, dbranch, d0, d1, d2, d3, sums1 = run(
        branch_kernel,
        [((count, dim), F32), ((count, dim), BF)] + [((count, shard), BF)] * 4 + [((8, dim), F32)],
        (first_sum, dsecond, keep, flip(send, 1), vectors, out_full),
    )
    dmixed = [d0, flip(d1, 1), flip(d2, 2), flip(d3, 3)]

    ak, az, bk, bz = run(
        weights_kernel,
        [((dim // 2, 4 * half), BF)] * 2 + [((2 * half, dim), BF)] * 2,
        (first_low, first_far, douter, douter_far, dinner, active),
        [pltpu.VMEM((dim, 4 * half), BF), pltpu.VMEM((4 * half, dim), BF)],
    )
    ar, br = flip(az, 2), flip(bz, 4)
    (packed,) = run(
        out_weight_kernel, [((dim + 16, dim), BF)], (*mixed, dbranch, sums1, sums2, sums3)
    )
    ck, cz = run(
        out_split_kernel, [((dim // 2 + 16, dim), BF)] * 2, (packed, flip(packed, 1)))
    cr = flip(cz, 2)

    h0, h1, h2, h3, keep, send = run(
        attend_back_kernel,
        [((shard + 16, 3 * shard), F32)]
        + [((shard + 16, 3 * shard), BF)] * 3
        + [((2 * count, dim), F32), ((2 * count, dim), BF)],
        (qkv, logsum, *segs, *dmixed, mine, other, far, heads_weight),
        [
            pltpu.VMEM((4 * count, 3 * shard), BF),
            pltpu.VMEM((3, 4 * count, HEAD_DIM), F32),
            pltpu.VMEM((3, 4 * count, HEAD_DIM), F32),
            pltpu.VMEM((dim, 3 * shard), F32),
        ],
    )

    a2k, a2z, b2k, b2z, c2k, c2z = run(
        reduce_kernel,
        [((dim // 4, 4 * half), BF)] * 2
        + [((half, dim), BF)] * 2
        + [((dim // 4 + 16, dim), BF)] * 2,
        (ak, ar, bk, br, ck, cr),
    )
    size = shard // 4 * 3 + half // 4 + 16
    p0, p1, p2, p3 = run(
        owners_kernel,
        [((size, dim), F32)] + [((size, dim), BF)] * 3,
        (a2k, flip(a2z, 4), b2k, flip(b2z, 2), c2k, flip(c2z, 4)),
    )
    (mine_p,) = run(total_kernel, [((size, dim), BF)], (p0, turn(p1, 1), turn(p2, 2), turn(p3, 3)))
    plane = [mine_p] + [flip(mine_p, bits) for bits in (2, 4, 6)]
    plane += [flip(piece, 1) for piece in plane]
    dinner_w, douter_w, dout_w, small = run(
        finish_kernel,
        [((shard, 8 * half), F32), ((hidden, dim), F32), ((shard, dim), F32), ((16, dim), F32)],
        plane,
    )
    dinner_b = pick(small[6:10].reshape(2, 4, half), own, 1).reshape(hidden)
    small = lax.dynamic_slice_in_dim(small[:6], own * shard, shard, 1)

    (heads,) = run(
        total_kernel, [((shard + 16, 3 * shard), BF)], (h0, turn(h1, 1), turn(h2, 2), turn(h3, 3))
    )
    (heads,) = run(total_kernel, [((shard + 16, 3 * shard), BF)], (heads, flip(heads, 4)))
    dquery_w, dkey_w, dvalue_w, heads_b = run(
        heads_kernel,
        [((shard, dim), F32)] * 3 + [((16, 3 * shard), F32)],
        (heads, flip(heads, 1), flip(heads, 2), flip(heads, 3)),
    )

    dtokens = keep + wide(flip(send, 1))
    dtokens = dtokens[:count] + wide(flip(short(dtokens[count:]), 2)) + dfirst_sum
    tokens_grad = pair(dtokens[:rows], wide(flip(short(dtokens[rows:]), 4)), y)

    return (
        output[:, None],
        tokens_grad[:, None],
        dquery_w,
        heads_b[0, :shard],
        dkey_w,
        dvalue_w,
        heads_b[0, 2 * shard :],
        dout_w,
        small[0],
        small[1],
        small[2],
        dinner_w,
        dinner_b,
        douter_w,
        small[3],
        small[4],
        small[5],
    )


def plane_device(*args):
    return plane_steps(*args)


def solution(mesh):
    placed = (
        P(None, "wt", "ctx", None),
        P(None, "wt", None),
        P("wt", None),
        P("wt"),
        P("wt", None),
        P("wt", None),
        P("wt"),
        P("wt", None),
        P("wt"),
        P("wt"),
        P("wt"),
        P("wt", None),
        P("wt"),
        P("wt", None),
        P("wt"),
        P("wt"),
        P("wt"),
        P(None, "wt", "ctx", None),
    )
    fits = mesh.shape["ctx"] == 8 and mesh.shape["wt"] == 4
    return jax.shard_map(
        plane_device if fits else general_device,
        mesh=mesh,
        in_specs=placed,
        out_specs=(
            P(None, "wt", "ctx", None),
            P(None, "wt", "ctx", None),
            P("wt", None),
            P("wt"),
            P("wt", None),
            P("wt", None),
            P("wt"),
            P("wt", None),
            P("wt"),
            P("wt"),
            P("wt"),
            P("wt", None),
            P("wt"),
            P("wt", None),
            P("wt"),
            P("wt"),
            P("wt"),
        ),
        check_vma=False,
    )
```

```python
import math

import jax
import jax.numpy as jnp
from jax import lax
from jax.experimental import pallas as pl
from jax.experimental.pallas import tpu as pltpu
from jax.sharding import PartitionSpec as P


HEADS = 12
HEAD_DIM = 64


EPS = 1e-12
NEG = -1e30
ROOT_HALF = 0.7071067811865476


def for_sending(shard):

    def short(part):
        return part.astype(jnp.bfloat16) if part.dtype == jnp.float32 else part

    return jax.tree.map(short, shard)


def normalize(rows, gain, shift):
    mean = jnp.mean(rows, axis=-1, keepdims=True)
    centered = rows - mean
    spread = jnp.mean(centered * centered, axis=-1, keepdims=True)
    return centered * lax.rsqrt(spread + EPS) * gain + shift


def gelu(inner):
    return 0.5 * inner * (1.0 + lax.erf(inner * ROOT_HALF))


def segment_of(starts, positions):
    found = (starts[:, None, :] <= positions[:, :, None]).astype(jnp.int32)
    return jnp.sum(found, axis=-1) - 1


def project(inputs, weight):
    return jnp.einsum("btd,de->bte", inputs, weight, preferred_element_type=jnp.float32)


def project_back(grads, weight):
    return jnp.einsum("bte,de->btd", grads, weight, preferred_element_type=jnp.float32)


def outer_sum(inputs, grads):
    return jnp.einsum("btd,bte->de", inputs, grads, preferred_element_type=jnp.float32)


def row_sum(grads):
    return jnp.sum(grads.astype(jnp.float32), axis=(0, 1))


def heads_of(array):
    return array.reshape(array.shape[0], array.shape[1], HEADS, HEAD_DIM)


def block_loop(width, carry, visit):
    block = math.gcd(width, 512)

    def step(state, index):
        return (visit(state, index * block, block), None)

    carry, _ = lax.scan(step, carry, jnp.arange(width // block, dtype=jnp.int32))
    return carry


def reaches(starts, own_seg, first, count):
    positions = first + jnp.arange(count, dtype=jnp.int32)
    other = segment_of(starts, jnp.broadcast_to(positions, (starts.shape[0], count)))
    touch = jnp.any((other[:, 0] <= own_seg[:, -1]) & (other[:, -1] >= own_seg[:, 0]))
    return (other, touch)


def keep_state(state):
    return state


def forward_attention(queries, query_seg, starts, keys, values):
    scale = HEAD_DIM ** (-0.5)
    batch, rows = (queries.shape[0], queries.shape[1])
    query_heads = heads_of(queries)

    def forward_fold(carry, piece, start):
        key_piece, value_piece = piece

        def visit(state, offset, count):
            other, touch = reaches(starts, query_seg, offset, count)

            def compute(state):
                top, total, accum = state
                key_block = heads_of(lax.dynamic_slice_in_dim(key_piece, offset, count, 1))
                value_block = heads_of(lax.dynamic_slice_in_dim(value_piece, offset, count, 1))
                scores = (
                    jnp.einsum(
                        "bqhd,bkhd->bhqk",
                        query_heads,
                        key_block,
                        preferred_element_type=jnp.float32,
                    )
                    * scale
                )
                mask = (query_seg[:, :, None] == other[:, None, :])[:, None]
                scores = jnp.where(mask, scores, NEG)
                new_top = jnp.maximum(top, jnp.max(scores, axis=-1))
                expd = jnp.where(mask, jnp.exp(scores - new_top[..., None]), 0.0)
                factor = jnp.exp(top - new_top)
                total = total * factor + jnp.sum(expd, axis=-1)
                added = jnp.einsum(
                    "bhqk,bkhd->bqhd",
                    expd.astype(jnp.bfloat16),
                    value_block,
                    preferred_element_type=jnp.float32,
                )
                accum = accum * jnp.transpose(factor, (0, 2, 1))[..., None] + added
                return (new_top, total, accum)

            return lax.cond(touch, compute, keep_state, state)

        return block_loop(key_piece.shape[1], carry, visit)

    init = (
        jnp.full((batch, HEADS, rows), NEG, jnp.float32),
        jnp.zeros((batch, HEADS, rows), jnp.float32),
        jnp.zeros((batch, rows, HEADS, HEAD_DIM), jnp.float32),
    )
    whole = (keys, values)
    top, total, accum = forward_fold(
        init,
        (
            lax.all_gather(keys, "ctx", axis=1, tiled=True),
            lax.all_gather(values, "ctx", axis=1, tiled=True),
        ),
        jnp.int32(0),
    )
    mixed = accum / jnp.transpose(total, (0, 2, 1))[..., None]
    return (mixed, top + jnp.log(total), whole)


def query_gradient(queries, query_seg, starts, keys, values, dmixed, logsum, delta):
    scale = HEAD_DIM ** (-0.5)
    query_heads = heads_of(queries)
    grad_heads = heads_of(dmixed)

    def query_fold(carry, piece, start):
        key_piece, value_piece = piece

        def visit(state, offset, count):
            other, touch = reaches(starts, query_seg, offset, count)

            def compute(state):
                key_block = heads_of(lax.dynamic_slice_in_dim(key_piece, offset, count, 1))
                value_block = heads_of(lax.dynamic_slice_in_dim(value_piece, offset, count, 1))
                scores = (
                    jnp.einsum(
                        "bqhd,bkhd->bhqk",
                        query_heads,
                        key_block,
                        preferred_element_type=jnp.float32,
                    )
                    * scale
                )
                mask = (query_seg[:, :, None] == other[:, None, :])[:, None]
                probs = jnp.where(
                    mask, jnp.exp(jnp.where(mask, scores, NEG) - logsum[..., None]), 0.0
                )
                dprobs = jnp.einsum(
                    "bqhd,bkhd->bhqk", grad_heads, value_block, preferred_element_type=jnp.float32
                )
                dscores = (probs * (dprobs - delta[..., None])).astype(jnp.bfloat16)
                return (
                    state
                    + jnp.einsum(
                        "bhqk,bkhd->bqhd", dscores, key_block, preferred_element_type=jnp.float32
                    )
                    * scale
                )

            return lax.cond(touch, compute, keep_state, state)

        return block_loop(key_piece.shape[1], carry, visit)

    init = jnp.zeros(query_heads.shape, jnp.float32)
    return query_fold(
        init,
        (
            lax.all_gather(keys, "ctx", axis=1, tiled=True),
            lax.all_gather(values, "ctx", axis=1, tiled=True),
        ),
        jnp.int32(0),
    )


def key_gradient(keys, values, key_seg, starts, queries, dmixed, logsum, delta):
    scale = HEAD_DIM ** (-0.5)
    key_heads = heads_of(keys)
    value_heads = heads_of(values)
    every_top, every_delta = (
        lax.all_gather(logsum, "ctx", axis=2, tiled=True),
        lax.all_gather(delta, "ctx", axis=2, tiled=True),
    )

    def key_fold(carry, piece, start):
        query_piece, grad_piece = piece

        def visit(state, offset, count):
            other, touch = reaches(starts, key_seg, offset, count)

            def compute(state):
                dkeys, dvalues = state
                query_block = heads_of(lax.dynamic_slice_in_dim(query_piece, offset, count, 1))
                grad_block = heads_of(lax.dynamic_slice_in_dim(grad_piece, offset, count, 1))
                top_block = lax.dynamic_slice_in_dim(every_top, offset, count, 2)
                delta_block = lax.dynamic_slice_in_dim(every_delta, offset, count, 2)
                scores = (
                    jnp.einsum(
                        "bqhd,bkhd->bhqk",
                        query_block,
                        key_heads,
                        preferred_element_type=jnp.float32,
                    )
                    * scale
                )
                mask = (other[:, :, None] == key_seg[:, None, :])[:, None]
                probs = jnp.where(
                    mask, jnp.exp(jnp.where(mask, scores, NEG) - top_block[..., None]), 0.0
                )
                dvalues = dvalues + jnp.einsum(
                    "bhqk,bqhd->bkhd",
                    probs.astype(jnp.bfloat16),
                    grad_block,
                    preferred_element_type=jnp.float32,
                )
                dprobs = jnp.einsum(
                    "bqhd,bkhd->bhqk", grad_block, value_heads, preferred_element_type=jnp.float32
                )
                dscores = (probs * (dprobs - delta_block[..., None])).astype(jnp.bfloat16)
                dkeys = (
                    dkeys
                    + jnp.einsum(
                        "bhqk,bqhd->bkhd", dscores, query_block, preferred_element_type=jnp.float32
                    )
                    * scale
                )
                return (dkeys, dvalues)

            return lax.cond(touch, compute, keep_state, state)

        return block_loop(query_piece.shape[1], carry, visit)

    empty = jnp.zeros(key_heads.shape, jnp.float32)
    return key_fold(
        (empty, empty),
        (
            lax.all_gather(queries, "ctx", axis=1, tiled=True),
            lax.all_gather(dmixed, "ctx", axis=1, tiled=True),
        ),
        jnp.int32(0),
    )


def forward_pass(tokens, starts, weights, base):
    (
        query_weight,
        query_bias,
        key_weight,
        value_weight,
        value_bias,
        out_weight,
        out_bias,
        first_gain,
        first_shift,
        inner_weight,
        inner_bias,
        outer_weight,
        outer_bias,
        second_gain,
        second_shift,
    ) = weights
    rows = tokens.shape[1]
    positions = base + jnp.arange(rows, dtype=jnp.int32)
    query_seg = segment_of(starts, jnp.broadcast_to(positions, (tokens.shape[0], rows)))
    queries = (project(tokens, query_weight) + query_bias.astype(jnp.float32)).astype(jnp.bfloat16)
    keys = project(tokens, key_weight).astype(jnp.bfloat16)
    values = (project(tokens, value_weight) + value_bias.astype(jnp.float32)).astype(jnp.bfloat16)
    mixed, logsum, whole = forward_attention(queries, query_seg, starts, keys, values)
    mixed_low = mixed.reshape(tokens.shape).astype(jnp.bfloat16)
    first_sum = (
        tokens.astype(jnp.float32) + project(mixed_low, out_weight) + out_bias.astype(jnp.float32)
    )
    first = normalize(first_sum, first_gain.astype(jnp.float32), first_shift.astype(jnp.float32))
    first_low = first.astype(jnp.bfloat16)
    inner = project(first_low, inner_weight) + inner_bias.astype(jnp.float32)
    active = gelu(inner).astype(jnp.bfloat16)
    second_sum = first + project(active, outer_weight) + outer_bias.astype(jnp.float32)
    output = normalize(
        second_sum, second_gain.astype(jnp.float32), second_shift.astype(jnp.float32)
    ).astype(jnp.bfloat16)
    saved = (
        tokens,
        query_seg,
        queries,
        keys,
        values,
        mixed,
        logsum,
        mixed_low,
        first_sum,
        first_low,
        inner,
        active,
        second_sum,
        whole,
    )
    return (output, saved)


def backward_pass(saved, starts, weights, cotangent):
    (
        query_weight,
        _,
        key_weight,
        value_weight,
        _,
        out_weight,
        _,
        first_gain,
        first_shift,
        inner_weight,
        _,
        outer_weight,
        _,
        second_gain,
        second_shift,
    ) = weights
    (
        tokens,
        query_seg,
        queries,
        keys,
        values,
        mixed,
        logsum,
        mixed_low,
        first_sum,
        first_low,
        inner,
        active,
        second_sum,
        _,
    ) = saved
    unused, second_back = jax.vjp(
        normalize, second_sum, second_gain.astype(jnp.float32), second_shift.astype(jnp.float32)
    )
    dsecond, dgain_second, dshift_second = second_back(cotangent.astype(jnp.float32))
    douter = dsecond.astype(jnp.bfloat16)
    dactive = project_back(douter, outer_weight)
    unused, gelu_back = jax.vjp(gelu, inner)
    dinner = gelu_back(dactive)[0].astype(jnp.bfloat16)
    dfirst = dsecond + project_back(dinner, inner_weight)
    unused, first_back = jax.vjp(
        normalize, first_sum, first_gain.astype(jnp.float32), first_shift.astype(jnp.float32)
    )
    dfirst_sum, dgain_first, dshift_first = first_back(dfirst)
    dbranch = dfirst_sum.astype(jnp.bfloat16)
    dmixed = project_back(dbranch, out_weight).astype(jnp.bfloat16)
    delta = jnp.einsum("bqhd,bqhd->bhq", heads_of(dmixed).astype(jnp.float32), mixed)
    dqueries = query_gradient(queries, query_seg, starts, keys, values, dmixed, logsum, delta)
    dkeys, dvalues = key_gradient(keys, values, query_seg, starts, queries, dmixed, logsum, delta)
    dqueries = dqueries.reshape(tokens.shape).astype(jnp.bfloat16)
    dkeys = dkeys.reshape(tokens.shape).astype(jnp.bfloat16)
    dvalues = dvalues.reshape(tokens.shape).astype(jnp.bfloat16)
    tokens_grad = (
        dfirst_sum
        + project_back(dqueries, query_weight)
        + project_back(dkeys, key_weight)
        + project_back(dvalues, value_weight)
    )
    sums = (
        outer_sum(tokens, dqueries),
        row_sum(dqueries),
        outer_sum(tokens, dkeys),
        outer_sum(tokens, dvalues),
        row_sum(dvalues),
        outer_sum(mixed_low, dbranch),
        row_sum(dbranch),
        dgain_first,
        dshift_first,
        outer_sum(first_low, dinner),
        row_sum(dinner),
        outer_sum(active, douter),
        row_sum(douter),
        dgain_second,
        dshift_second,
    )
    return (tokens_grad, sums)


def general_device(
    tokens,
    doc_lengths,
    query_weight,
    query_bias,
    key_weight,
    value_weight,
    value_bias,
    out_weight,
    out_bias,
    first_gain,
    first_shift,
    inner_weight,
    inner_bias,
    outer_weight,
    outer_bias,
    second_gain,
    second_shift,
    cotangent,
):
    params = (
        query_weight,
        query_bias,
        key_weight,
        value_weight,
        value_bias,
        out_weight,
        out_bias,
        first_gain,
        first_shift,
        inner_weight,
        inner_bias,
        outer_weight,
        outer_bias,
        second_gain,
        second_shift,
    )
    rows = tokens.shape[2]
    base = lax.axis_index("ctx") * rows
    lengths = doc_lengths[:, 0]
    starts = jnp.cumsum(lengths, axis=-1) - lengths
    outputs = []
    token_parts = []
    sums = None
    for index in range(tokens.shape[0]):
        weights = (
            lax.all_gather(params[0], "wt", axis=0, tiled=True),
            lax.all_gather(params[1], "wt", axis=0, tiled=True),
            lax.all_gather(params[2], "wt", axis=0, tiled=True),
            lax.all_gather(params[3], "wt", axis=0, tiled=True),
            lax.all_gather(params[4], "wt", axis=0, tiled=True),
            lax.all_gather(params[5], "wt", axis=0, tiled=True),
            lax.all_gather(params[6], "wt", axis=0, tiled=True),
            lax.all_gather(params[7], "wt", axis=0, tiled=True),
            lax.all_gather(params[8], "wt", axis=0, tiled=True),
            lax.all_gather(params[9], "wt", axis=0, tiled=True),
            lax.all_gather(params[10], "wt", axis=0, tiled=True),
            lax.all_gather(params[11], "wt", axis=0, tiled=True),
            lax.all_gather(params[12], "wt", axis=0, tiled=True),
            lax.all_gather(params[13], "wt", axis=0, tiled=True),
            lax.all_gather(params[14], "wt", axis=0, tiled=True),
        )
        part_out, saved = forward_pass(
            tokens[index : index + 1, 0], starts[index : index + 1], weights, base
        )
        again = (
            lax.all_gather(params[0], "wt", axis=0, tiled=True),
            lax.all_gather(params[1], "wt", axis=0, tiled=True),
            lax.all_gather(params[2], "wt", axis=0, tiled=True),
            lax.all_gather(params[3], "wt", axis=0, tiled=True),
            lax.all_gather(params[4], "wt", axis=0, tiled=True),
            lax.all_gather(params[5], "wt", axis=0, tiled=True),
            lax.all_gather(params[6], "wt", axis=0, tiled=True),
            lax.all_gather(params[7], "wt", axis=0, tiled=True),
            lax.all_gather(params[8], "wt", axis=0, tiled=True),
            lax.all_gather(params[9], "wt", axis=0, tiled=True),
            lax.all_gather(params[10], "wt", axis=0, tiled=True),
            lax.all_gather(params[11], "wt", axis=0, tiled=True),
            lax.all_gather(params[12], "wt", axis=0, tiled=True),
            lax.all_gather(params[13], "wt", axis=0, tiled=True),
            lax.all_gather(params[14], "wt", axis=0, tiled=True),
        )
        part_grad, part_sums = backward_pass(
            saved, starts[index : index + 1], again, cotangent[index : index + 1, 0]
        )
        outputs.append(part_out)
        token_parts.append(part_grad)
        sums = part_sums if sums is None else jax.tree.map(jnp.add, sums, part_sums)
    output = jnp.concatenate(outputs, axis=0)
    tokens_grad = jnp.concatenate(token_parts, axis=0)
    shards = jax.tree.map(
        lambda part: part.astype(jnp.float32),
        lax.psum_scatter(for_sending(sums), "wt", scatter_dimension=0, tiled=True),
    )
    totals = lax.psum(shards, "ctx")
    return (output[:, None], tokens_grad[:, None]) + tuple(totals)


def flip(value, bits):
    return lax.ppermute(value, "ctx", [(i, i ^ bits) for i in range(8)])


def turn(value, step):
    return lax.ppermute(value, "wt", [(i, (i - step) % 4) for i in range(4)])


def pick(value, index, axis=0):
    return lax.dynamic_index_in_dim(value, index, axis, keepdims=False)


def pair(own, other, bit, axis=0):
    return jnp.where(bit == 0, jnp.stack([own, other], axis), jnp.stack([other, own], axis))


def short(value):
    return value.astype(jnp.bfloat16)


def wide(value):
    return value.astype(jnp.float32)


def dot(left, right):
    return jnp.dot(left, right, preferred_element_type=jnp.float32)


def dot_back(left, right):
    return lax.dot_general(
        left, right, (((1,), (1,)), ((), ())), preferred_element_type=jnp.float32
    )


def dot_sum(left, right):
    return lax.dot_general(
        left, right, (((0,), (0,)), ((), ())), preferred_element_type=jnp.float32
    )


def norm_parts(rows):
    mean = jnp.mean(rows, axis=-1, keepdims=True)
    centered = rows - mean
    spread = jnp.mean(centered * centered, axis=-1, keepdims=True)
    root = lax.rsqrt(spread + EPS)
    return centered * root, root


def norm_back(upstream, normed, root, gain):
    grad = upstream * gain
    mean = jnp.mean(grad, axis=-1, keepdims=True)
    along = jnp.mean(grad * normed, axis=-1, keepdims=True)
    return root * (grad - mean - normed * along)


def gelu_slope(inner):
    bell = jnp.exp(-0.5 * inner * inner) * (1.0 / math.sqrt(2.0 * math.pi))
    return 0.5 * (1.0 + lax.erf(inner * ROOT_HALF)) + inner * bell


def run(kernel, outs, args, scratch=(), scalars=()):
    shapes = tuple(jax.ShapeDtypeStruct(shape, dtype) for shape, dtype in outs)
    spaces = [pltpu.SMEM] * len(scalars) + [pltpu.VMEM] * len(args)
    return pl.pallas_call(
        kernel,
        out_shape=shapes,
        in_specs=[pl.BlockSpec(memory_space=space) for space in spaces],
        scratch_shapes=list(scratch),
    )(*scalars, *args)


BF = jnp.bfloat16
F32 = jnp.float32


def where_am_i():
    ctx, own = lax.axis_index("ctx"), lax.axis_index("wt")
    return ctx & 1, (ctx >> 1) & 3, ctx & 3, own


def some_rows(start, count):
    return pl.ds(pl.multiple_of(start, 16), count)


def prepare_kernel(wq, wk, wv, wo, wi, wo2, vec, heads_own, heads_send, w2_send, inner_half, outer_half):
    core, quarter, group, _ = where_am_i()
    shard, dim = wq.shape
    width, half = dim // 4, wo2.shape[0] // 2
    for index in range(4):

        @pl.when(group == index)
        def _():
            for slot, ref in enumerate((wq, wk, wv)):
                heads_own[:, slot * width : (slot + 1) * width] = ref[
                    :, index * width : (index + 1) * width
                ]

    for index in range(2):

        @pl.when(core == index)
        def _():
            for block in range(4):
                at = block * 2 * half + index * half
                inner_half[:, block * half : (block + 1) * half] = wi[:, at : at + half]
            outer_half[...] = wo2[index * half : (index + 1) * half, :]

    part = shard // 2
    heads_send[0:part, :] = heads_own[some_rows((quarter >> 1) * part, part), :]
    heads_send[part:, 0:width] = vec[...]
    heads_send[part:, width:] = jnp.zeros((16, 2 * width), BF)
    part = shard // 4
    rows = some_rows(quarter * part, part)
    w2_send[0:part, :] = inner_half[rows, 0:dim]
    w2_send[part : 2 * part, :] = inner_half[rows, dim:]
    step = half // 4
    w2_send[2 * part : 2 * part + step, :] = outer_half[some_rows(quarter * step, step), :]
    w2_send[2 * part + step :, :] = wo[rows, :]


CHUNK = 128
WINDOWS = (2, 5, 8)


def chunk_of(ctx, index):
    return ctx ^ ((index >> 2) | (index & 2) | ((index & 1) << 2))


def over_window(bounds, chunk, visit):
    low, count = bounds[0, chunk], bounds[1, chunk]
    least = 0
    for size in WINDOWS:

        @pl.when((count > least) & (count <= size))
        def _(size=size):
            start = jnp.minimum(low, WINDOWS[-1] - size) * CHUNK
            visit(pl.multiple_of(start, CHUNK), size * CHUNK)

        least = size


def attend_rows(bounds, qkv, seg_col, seg_row, first, outs, logsum):
    ctx = lax.axis_index("ctx")
    scale = HEAD_DIM ** (-0.5)
    group = qkv.shape[0] // 3
    for place, out in enumerate(outs):

        def step(side, carry, place=place, out=out):
            chunk = chunk_of(ctx, first + 2 * place + side)
            rows = pl.ds(pl.multiple_of(chunk * CHUNK, CHUNK), CHUNK)
            at = pl.multiple_of(side * CHUNK, CHUNK)

            def visit(start, count):
                keys = pl.ds(start, count)
                mask = seg_col[rows, :] == seg_row[:, keys]
                sums = []
                for head in range(group):
                    scores = dot_back(qkv[head, rows, :], qkv[group + head, keys, :])
                    scores = jnp.where(mask, scores * scale, NEG)
                    top = jnp.max(scores, axis=-1, keepdims=True)
                    expd = jnp.exp(scores - top)
                    total = jnp.sum(expd, axis=-1, keepdims=True)
                    probs = short(expd * (1.0 / total))
                    out[pl.ds(at, CHUNK), head * HEAD_DIM : (head + 1) * HEAD_DIM] = short(
                        dot(probs, qkv[2 * group + head, keys, :])
                    )
                    sums.append(top + jnp.log(total))
                logsum[pl.ds(at + 2 * place * CHUNK, CHUNK), :] = jnp.concatenate(
                    sums + [jnp.zeros_like(sums[0])] * (128 - group), axis=1
                )

            over_window(bounds, chunk, visit)
            return carry

        lax.fori_loop(0, 2, step, 0)


def attend_near_kernel(
    bounds, mine, other, far, heads_own, g1, g2, g3, h1, h2, h3, bias, seg_col, seg_row,
    qkv, m0, m2, logsum, weight,
):
    _, quarter, _, own = where_am_i()
    ctx = lax.axis_index("ctx")
    shard = heads_own.shape[0]
    part = shard // 2
    y = quarter >> 1
    weight[some_rows(own * shard, shard), :] = heads_own[...]
    for step, near_half, far_half in ((1, g1, h1), (2, g2, h2), (3, g3, h3)):
        at = ((own + step) & 3) * shard
        weight[some_rows(at + part * y, part), :] = near_half[0:part, :]
        weight[some_rows(at + part * (1 - y), part), :] = far_half[0:part, :]
    index = 0
    for source in (mine, other, far):
        for first in range(0, source.shape[0], 2 * CHUNK):
            low = short(dot(source[first : first + 2 * CHUNK, :], weight[...]) + bias[...])
            for half in range(2):
                at = pl.multiple_of(chunk_of(ctx, index) * CHUNK, CHUNK)
                for slot in range(qkv.shape[0]):
                    qkv[slot, pl.ds(at, CHUNK), :] = low[
                        half * CHUNK : (half + 1) * CHUNK,
                        slot * HEAD_DIM : (slot + 1) * HEAD_DIM,
                    ]
                index += 1
    attend_rows(bounds, qkv, seg_col, seg_row, 0, (m0, m2), logsum)


def attend_far_kernel(bounds, qkv, seg_col, seg_row, m1, m3, logsum):
    attend_rows(bounds, qkv, seg_col, seg_row, 4, (m1, m3), logsum)


def project_kernel(m0, m1, m2, m3, mine, wo, vec, *refs):
    pieces, (first_sum, first_low, out_full) = refs[:12], refs[12:]
    _, quarter, group, own = where_am_i()
    shard = wo.shape[0]
    part = shard // 4
    out_full[some_rows(own * shard, shard), :] = wo[...]
    for index, piece in enumerate(pieces):
        at = ((own + 1 + index // 4) & 3) * shard + part * (quarter ^ (index % 4))
        out_full[some_rows(at, part), :] = piece[piece.shape[0] - part :, :]
    total = wide(mine[...]) + vec[2:3, :]
    for code, ref in enumerate((m0, m1, m2, m3)):
        total += dot(ref[...], out_full[some_rows((group ^ code) * shard, shard), :])
    first_sum[...] = total
    first_low[...] = short(norm_parts(total)[0] * vec[3:4, :] + vec[4:5, :])


def forward_kernel(near, far, inner_half, outer_half, bias, *refs):
    pieces, (keep, send, inner, active, wi_full, wo2_full) = refs[:12], refs[12:]
    _, quarter, _, own = where_am_i()
    shard, half = inner_half.shape[0], outer_half.shape[0]
    dim = keep.shape[1]
    part, step = shard // 4, half // 4
    wi_full[some_rows(own * shard, shard), :] = inner_half[...]
    wo2_full[some_rows(own * half, half), :] = outer_half[...]
    for index, piece in enumerate(pieces):
        row, spot = (own + 1 + index // 4) & 3, quarter ^ (index % 4)
        rows = some_rows(row * shard + part * spot, part)
        wi_full[rows, 0:dim] = piece[0:part, :]
        wi_full[rows, dim:] = piece[part : 2 * part, :]
        wo2_full[some_rows(row * half + step * spot, step), :] = piece[
            2 * part : 2 * part + step, :
        ]
    count = near.shape[0]
    chunk = 512
    for index, (source, out) in enumerate(((far, send), (near, keep))):
        at = (1 - index) * count
        total = None
        for lane in range(0, inner.shape[1], chunk):
            lanes = slice(lane, lane + chunk)
            value = dot(source[...], wi_full[:, lanes]) + bias[:, lanes]
            inner[at : at + count, lanes] = value
            low = short(gelu(value))
            active[at : at + count, lanes] = low
            added = dot(low, wo2_full[lanes, :])
            total = added if total is None else total + added
        out[...] = total


def turnaround_kernel(first_sum, keep, got, vec, cot0, cot1, out0, out1, dsecond, douter, sums):
    rows = cot0.shape[0]
    first = norm_parts(first_sum[...])[0] * vec[3:4, :] + vec[4:5, :]
    normed, root = norm_parts(first + vec[5:6, :] + keep[...] + got[...])
    output = short(normed * vec[6:7, :] + vec[7:8, :])
    out0[...] = output[:rows]
    out1[...] = output[rows:]
    upstream = jnp.concatenate([wide(cot0[...]), wide(cot1[...])])
    back = norm_back(upstream, normed, root, vec[6:7, :])
    low = short(back)
    dsecond[...] = back
    douter[...] = low
    sums[0:1, :] = jnp.sum(wide(low), axis=0, keepdims=True)
    sums[1:2, :] = jnp.sum(upstream * normed, axis=0, keepdims=True)
    sums[2:3, :] = jnp.sum(upstream, axis=0, keepdims=True)
    sums[3:, :] = jnp.zeros_like(sums[3:, :])


def backward_kernel(near, far, inner, wi_full, wo2_full, keep, send, dinner, sums):
    count, dim = near.shape
    chunk = 512
    for index, (source, out) in enumerate(((far, send), (near, keep))):
        at = (1 - index) * count
        total = None
        for lane in range(0, inner.shape[1], chunk):
            lanes = slice(lane, lane + chunk)
            slope = gelu_slope(inner[at : at + count, lanes])
            low = short(dot_back(source[...], wo2_full[lanes, :]) * slope)
            dinner[at : at + count, lanes] = low
            added = dot_back(low, wi_full[:, lanes])
            total = added if total is None else total + added
        out[...] = total
    total = jnp.sum(wide(dinner[...]), axis=0, keepdims=True)
    sums[0:1, :] = total[:, :dim]
    sums[1:2, :] = total[:, dim:]
    sums[2:, :] = jnp.zeros_like(sums[2:, :])


def weights_kernel(first0, first1, douter0, douter1, dinner, active, ak, az, bk, bz, left, right):
    _, quarter, _, _ = where_am_i()
    x, y = quarter & 1, quarter >> 1
    count = first0.shape[0]
    part, step = first0.shape[1] // 16, active.shape[1] // 16
    left[...] = short(dot_sum(first0[...], dinner[:count]) + dot_sum(first1[...], dinner[count:]))
    for block in range(8):
        rows = slice(block * part, (block + 1) * part)
        ak[rows, :] = left[some_rows((2 * block + x) * part, part), :]
        az[rows, :] = left[some_rows((2 * block + 1 - x) * part, part), :]
    right[...] = short(
        dot_sum(active[:count], douter0[...]) + dot_sum(active[count:], douter1[...])
    )
    for block in range(8):
        row, side = block // 2, block % 2
        rows = slice(block * step, (block + 1) * step)
        bk[rows, :] = right[some_rows((4 * row + 2 * y + side) * step, step), :]
        bz[rows, :] = right[some_rows((4 * row + 2 * (1 - y) + side) * step, step), :]


def branch_kernel(first_sum, dsecond, keep, got, vec, out_full, dfirst_sum, dbranch, d0, d1, d2, d3, sums):
    _, _, group, _ = where_am_i()
    shard = d0.shape[1]
    normed, root = norm_parts(first_sum[...])
    dfirst = dsecond[...] + keep[...] + got[...]
    back = norm_back(dfirst, normed, root, vec[3:4, :])
    low = short(back)
    dfirst_sum[...] = back
    dbranch[...] = low
    for code, ref in enumerate((d0, d1, d2, d3)):
        ref[...] = short(dot_back(low, out_full[some_rows((group ^ code) * shard, shard), :]))
    sums[0:1, :] = jnp.sum(wide(low), axis=0, keepdims=True)
    sums[1:2, :] = jnp.sum(dfirst * normed, axis=0, keepdims=True)
    sums[2:3, :] = jnp.sum(dfirst, axis=0, keepdims=True)
    sums[3:, :] = jnp.zeros_like(sums[3:, :])


def out_weight_kernel(m0, m1, m2, m3, dbranch, sums1, sums2, sums3, ck, cz, whole):
    core, _, group, _ = where_am_i()
    shard, dim = m0.shape[1], dbranch.shape[1]
    half = dim // 2
    for code, ref in enumerate((m0, m1, m2, m3)):
        whole[some_rows((group ^ code) * shard, shard), :] = short(
            dot_sum(ref[...], dbranch[...])
        )
    for side in range(2):

        @pl.when(core == side)
        def _():
            for ref, which in ((ck, side), (cz, 1 - side)):
                ref[0:dim, :] = whole[:, which * half : (which + 1) * half]

    rows = short(
        jnp.concatenate([sums1[0:3, :], sums2[0:3, :], sums3[0:2, :], jnp.zeros_like(sums1[...])])
    )
    for ref in (ck, cz):
        ref[dim : dim + 16, :] = rows[:, :half]
        ref[dim + 16 :, :] = rows[:, half:]


def out_split_kernel(packed, got, ck, cz):
    core, quarter, _, _ = where_am_i()
    x = quarter & 1
    dim = packed.shape[0] - 32
    part = dim // 16
    for block in range(8):
        rows = slice(block * part, (block + 1) * part)
        for ref, side in ((ck, x), (cz, 1 - x)):
            take = some_rows((2 * block + side) * part, part)
            ref[rows, :] = short(wide(packed[take, :]) + wide(got[take, :]))
    for lanes in range(2):
        at = dim + 16 * lanes
        mine, other = wide(packed[at : at + 16, :]), wide(got[at : at + 16, :])
        low = jnp.where(core == 0, mine, other)[6:8]
        high = jnp.where(core == 0, other, mine)[6:8]
        rows = jnp.concatenate([(mine + other)[0:6], low, high, jnp.zeros_like(mine[0:6])])
        at = 8 * part + 16 * lanes
        for ref in (ck, cz):
            ref[at : at + 16, :] = short(rows)


def reduce_rows(keep, got, outs, bit):
    size = keep.shape[0] // 8
    size -= size % 16
    for block in range(4):
        for out, side in zip(outs, (bit, 1 - bit)):
            take = some_rows((2 * block + side) * size, size)
            out[block * size : (block + 1) * size, :] = short(
                wide(keep[take, :]) + wide(got[take, :])
            )
    if keep.shape[0] > 8 * size:
        for out in outs:
            out[4 * size :, :] = short(wide(keep[8 * size :, :]) + wide(got[8 * size :, :]))


def reduce_kernel(ak, ar, bk, br, a2k, a2z, b2k, b2z):
    _, quarter, _, _ = where_am_i()
    reduce_rows(ak, ar, (a2k, a2z), quarter >> 1)
    reduce_rows(bk, br, (b2k, b2z), quarter & 1)


def reduce_out_kernel(ck, cr, c2k, c2z):
    _, quarter, _, _ = where_am_i()
    reduce_rows(ck, cr, (c2k, c2z), quarter >> 1)


def owners_kernel(ak, ar, bk, br, ck, cr, p0, p1, p2, p3):
    _, _, _, own = where_am_i()
    dim = bk.shape[1]
    half = dim // 2
    part, step = ak.shape[0] // 4, bk.shape[0] // 4
    size = (ck.shape[0] - 32) // 4
    for index, out in enumerate((p0, p1, p2, p3)):
        row = (own - index) & 3
        rows = some_rows(row * part, part)
        total = wide(ak[rows, :]) + wide(ar[rows, :])
        out[0:part, :] = total[:, :dim].astype(out.dtype)
        out[part : 2 * part, :] = total[:, dim:].astype(out.dtype)
        at = 2 * part
        rows = some_rows(row * step, step)
        out[at : at + step, :] = (wide(bk[rows, :]) + wide(br[rows, :])).astype(out.dtype)
        at += step
        rows = some_rows(row * size, size)
        out[at:, 0:half] = (wide(ck[rows, :]) + wide(cr[rows, :])).astype(out.dtype)
        tail = wide(ck[4 * size :, :]) + wide(cr[4 * size :, :])
        out[at : at + 32, half:] = tail.astype(out.dtype)
        out[at + 32 :, half:] = jnp.zeros((size - 32, half), out.dtype)


def total_kernel(mine, *refs):
    total = wide(mine[...])
    for ref in refs[:-1]:
        total += wide(ref[...])
    refs[-1][...] = short(total)


def finish_kernel(*refs):
    pieces, (dwi, dwo2, dwo, small) = refs[:8], refs[8:]
    core, quarter, _, _ = where_am_i()
    part, half = dwi.shape[0] // 4, dwi.shape[1] // 8
    step = half // 4
    tail = 2 * part + step
    for side in range(2):

        @pl.when(core == side)
        def _():
            for index, piece in enumerate(pieces):
                spot = quarter ^ (index % 4)
                which = side if index < 4 else 1 - side
                rows = some_rows(spot * part, part)
                for block in range(4):
                    at = block * 2 * half + which * half
                    up, lane = part * (block // 2), half * (block % 2)
                    dwi[rows, at : at + half] = wide(piece[up : up + part, lane : lane + half])
                dwo2[some_rows(which * half + spot * step, step), :] = wide(
                    piece[2 * part : tail, :]
                )
                dwo[rows, which * half : (which + 1) * half] = wide(piece[tail:, 0:half])

    small[:, 0:half] = wide(pieces[0][tail : tail + 16, half:])
    small[:, half:] = wide(pieces[0][tail + 16 : tail + 32, half:])


def attend_back_kernel(
    bounds, qkv, logsum0, logsum1, seg_col, seg_row, p0, p1, p2, p3, mine, other, far, weight,
    h0, h1, h2, h3, keep, send, grads, dkeys, dvalues, dweight, dmixed, logsum,
):
    _, _, _, own = where_am_i()
    ctx = lax.axis_index("ctx")
    scale = HEAD_DIM ** (-0.5)
    group = qkv.shape[0] // 3
    width = group * HEAD_DIM
    block = p0.shape[0]
    dkeys[...] = jnp.zeros_like(dkeys)
    dvalues[...] = jnp.zeros_like(dvalues)
    for index, part in enumerate((p0, p2, p1, p3)):
        dmixed[index * block : (index + 1) * block, :] = part[...]
    logsum[: 2 * block, :] = logsum0[...]
    logsum[2 * block :, :] = logsum1[...]

    def step(index, carry):
        chunk = chunk_of(ctx, index)
        rows = pl.ds(pl.multiple_of(chunk * CHUNK, CHUNK), CHUNK)
        here = pl.ds(pl.multiple_of(index * CHUNK, CHUNK), CHUNK)

        def visit(start, count):
            window = pl.ds(start, count)
            mask = seg_col[rows, :] == seg_row[:, window]
            for head in range(group):
                lanes = slice(head * HEAD_DIM, (head + 1) * HEAD_DIM)
                query = qkv[head, rows, :]
                grad = dmixed[here, lanes]
                keys = qkv[group + head, window, :]
                scores = jnp.where(mask, dot_back(query, keys) * scale, NEG)
                probs = jnp.exp(scores - logsum[here, head : head + 1])
                dprobs = dot_back(grad, qkv[2 * group + head, window, :])
                delta = jnp.sum(probs * dprobs, axis=-1, keepdims=True)
                dscores = short(probs * (dprobs - delta))
                grads[here, lanes] = short(dot(dscores, keys) * scale)
                dkeys[head, window, :] += dot_sum(dscores, query)
                dvalues[head, window, :] += dot_sum(short(probs), grad)

        over_window(bounds, chunk, visit)
        return carry

    lax.fori_loop(0, 8, step, 0)

    def gather(index, carry):
        rows = pl.ds(pl.multiple_of(chunk_of(ctx, index) * CHUNK, CHUNK), CHUNK)
        here = pl.ds(pl.multiple_of(index * CHUNK, CHUNK), CHUNK)
        for head in range(group):
            at = width + head * HEAD_DIM
            grads[here, at : at + HEAD_DIM] = short(dkeys[head, rows, :] * scale)
            grads[here, at + width : at + width + HEAD_DIM] = short(dvalues[head, rows, :])
        return carry

    lax.fori_loop(0, 8, gather, 0)
    rows = 2 * block
    dweight[...] = (
        dot_sum(mine[...], grads[:block])
        + dot_sum(other[...], grads[block:rows])
        + dot_sum(far[...], grads[rows:])
    )
    sums = jnp.sum(wide(grads[...]), axis=0, keepdims=True)
    tail = jnp.concatenate([sums, jnp.zeros((15, sums.shape[1]), F32)])
    for index, out in enumerate((h0, h1, h2, h3)):
        take = pl.ds(pl.multiple_of(((own - index) & 3) * width, 16), width)
        out[0:width, :] = dweight[take, :].astype(out.dtype)
        out[width:, :] = tail.astype(out.dtype)
    keep[...] = dot_back(grads[:rows], weight[...])
    send[...] = short(dot_back(grads[rows:], weight[...]))


def merge_kernel(keep, got, base, near, far):
    total = keep[...] + wide(got[...])
    count = near.shape[0]
    near[...] = total[:count] + base[...]
    far[...] = short(total[count:])


def heads_kernel(s0, s1, s2, s3, dq, dk, dv, bias):
    _, _, group, own = where_am_i()
    shard = dq.shape[0]
    for index in range(4):

        @pl.when(group == index)
        def _():
            for code, ref in enumerate((s0, s1, s2, s3)):
                at = (index ^ code) * shard
                for slot, out in enumerate((dq, dk, dv)):
                    out[:, at : at + shard] = wide(
                        ref[0:shard, slot * shard : (slot + 1) * shard]
                    )

                @pl.when(own == index ^ code)
                def _():
                    bias[...] = wide(ref[shard:, :])


def plane_steps(
    tokens,
    doc_lengths,
    query_weight,
    query_bias,
    key_weight,
    value_weight,
    value_bias,
    out_weight,
    out_bias,
    first_gain,
    first_shift,
    inner_weight,
    inner_bias,
    outer_weight,
    outer_bias,
    second_gain,
    second_shift,
    cotangent,
):
    ctx, own = lax.axis_index("ctx"), lax.axis_index("wt")
    core, y, group = ctx & 1, ctx >> 2, ctx & 3
    rows, dim = tokens.shape[2], tokens.shape[3]
    shard = query_weight.shape[0]
    hidden = outer_weight.shape[0]
    half = hidden // 2
    count = 2 * rows

    mine = jnp.concatenate([pick(tokens[:, 0], y), flip(pick(tokens[:, 0], 1 - y), 4)])
    other = flip(mine, 2)
    far = flip(jnp.concatenate([mine, other]), 1)

    vector_list = (
        query_bias,
        value_bias,
        out_bias,
        first_gain,
        first_shift,
        outer_bias,
        second_gain,
        second_shift,
        *[inner_bias[at : at + shard] for at in range(0, 4 * shard, shard)],
    )
    line = lax.broadcasted_iota(jnp.int32, (16, shard), 0)
    vec = jnp.zeros((16, shard), BF)
    for index, value in enumerate(vector_list):
        vec = jnp.where(line == index, value[None, :], vec)
    heads_own, heads_send, w2_send, inner_half, outer_half = run(
        prepare_kernel,
        [
            ((shard, 3 * shard), BF),
            ((shard // 2 + 16, 3 * shard), BF),
            ((shard // 4 * 3 + half // 4, dim), BF),
            ((shard, 4 * half), BF),
            ((half, dim), BF),
        ],
        (query_weight, key_weight, value_weight, out_weight, inner_weight, outer_weight, vec),
    )
    got = [turn(heads_send, step) for step in (1, 2, 3)]
    gone = [flip(value, 4) for value in got]
    pieces = []
    for step in (1, 2, 3):
        piece = turn(w2_send, step)
        pieces += [piece] + [flip(piece, bits) for bits in (2, 4, 6)]

    at = shard // 2
    rel = jnp.stack([vec] + [value[at:, :shard] for value in got])
    vectors = wide(lax.dynamic_slice_in_dim(jnp.concatenate([rel, rel]), (4 - own) % 4, 4))
    mine_b = pick(vectors, group)
    heads_bias = jnp.concatenate([mine_b[0], jnp.zeros_like(mine_b[0]), mine_b[1]])[None]
    inner_b = pick(vectors[:, 8:12].reshape(4, 2, half), core, 1).reshape(1, 4 * half)
    vectors = jnp.swapaxes(vectors[:, :8], 0, 1).reshape(8, dim)

    lengths = pick(doc_lengths[:, 0], y)
    starts = jnp.cumsum(lengths) - lengths
    total = 8 * rows
    positions = jnp.arange(total, dtype=jnp.int32)
    seg = jnp.sum((starts[None, :] <= positions[:, None]).astype(jnp.int32), axis=-1) - 1
    segs = (seg[:, None], seg[None, :])
    chunks = jnp.arange(8, dtype=jnp.int32)[:, None] * CHUNK
    low = jnp.max(jnp.where(starts[None, :] <= chunks, starts[None, :], 0), axis=-1) // CHUNK
    high = jnp.min(jnp.where(starts[None, :] >= chunks + CHUNK, starts[None, :], total), axis=-1)
    bounds = jnp.stack([low, (high - 1) // CHUNK - low + 1])

    qkv, m0, m2, logsum0, heads_weight = run(
        attend_near_kernel,
        [
            ((9, total, HEAD_DIM), BF),
            ((count, shard), BF),
            ((count, shard), BF),
            ((2 * count, 128), F32),
            ((dim, 3 * shard), BF),
        ],
        (mine, other, far, heads_own, *got, *gone, heads_bias, *segs),
        scalars=(bounds,),
    )
    m1, m3, logsum1 = run(
        attend_far_kernel,
        [((count, shard), BF), ((count, shard), BF), ((2 * count, 128), F32)],
        (qkv, *segs),
        scalars=(bounds,),
    )
    mixed = [m0, flip(m1, 1), flip(m2, 2), flip(m3, 3)]

    first_sum, first_low, out_full = run(
        project_kernel,
        [((count, dim), F32), ((count, dim), BF), ((dim, dim), BF)],
        (*mixed, mine, out_weight, vectors, *pieces),
    )
    first_far = flip(first_low, 1)
    keep, send, inner, active, wi_full, wo2_full = run(
        forward_kernel,
        [
            ((count, dim), F32),
            ((count, dim), F32),
            ((2 * count, 4 * half), F32),
            ((2 * count, 4 * half), BF),
            ((dim, 4 * half), BF),
            ((4 * half, dim), BF),
        ],
        (first_low, first_far, inner_half, outer_half, inner_b, *pieces),
    )
    cot = pick(cotangent[:, 0], y), flip(pick(cotangent[:, 0], 1 - y), 4)
    out0, out1, dsecond, douter, sums2 = run(
        turnaround_kernel,
        [
            ((rows, dim), BF),
            ((rows, dim), BF),
            ((count, dim), F32),
            ((count, dim), BF),
            ((8, dim), F32),
        ],
        (first_sum, keep, flip(send, 1), vectors, *cot),
    )
    output = pair(out0, flip(out1, 4), y)

    douter_far = flip(douter, 1)
    keep, send, dinner, sums3 = run(
        backward_kernel,
        [
            ((count, dim), F32),
            ((count, dim), F32),
            ((2 * count, 4 * half), BF),
            ((8, dim), F32),
        ],
        (douter, douter_far, inner, wi_full, wo2_full),
    )
    dfirst_sum, dbranch, d0, d1, d2, d3, sums1 = run(
        branch_kernel,
        [((count, dim), F32), ((count, dim), BF)] + [((count, shard), BF)] * 4 + [((8, dim), F32)],
        (first_sum, dsecond, keep, flip(send, 1), vectors, out_full),
    )
    dmixed = [d0, flip(d1, 1), flip(d2, 2), flip(d3, 3)]

    ak, az, bk, bz = run(
        weights_kernel,
        [((dim // 2, 4 * half), BF)] * 2 + [((2 * half, dim), BF)] * 2,
        (first_low, first_far, douter, douter_far, dinner, active),
        [pltpu.VMEM((dim, 4 * half), BF), pltpu.VMEM((4 * half, dim), BF)],
    )
    ar, br = flip(az, 2), flip(bz, 4)
    ck, cz = run(
        out_weight_kernel,
        [((dim + 32, dim // 2), BF)] * 2,
        (*mixed, dbranch, sums1, sums2, sums3),
        [pltpu.VMEM((dim, dim), BF)],
    )
    ck, cz = run(out_split_kernel, [((dim // 2 + 32, dim // 2), BF)] * 2, (ck, flip(cz, 1)))
    cr = flip(cz, 2)

    h0, h1, h2, h3, keep, send = run(
        attend_back_kernel,
        [((shard + 16, 3 * shard), F32)]
        + [((shard + 16, 3 * shard), BF)] * 3
        + [((2 * count, dim), F32), ((2 * count, dim), BF)],
        (qkv, logsum0, logsum1, *segs, *dmixed, mine, other, far, heads_weight),
        [
            pltpu.VMEM((4 * count, 3 * shard), BF),
            pltpu.VMEM((3, 4 * count, HEAD_DIM), F32),
            pltpu.VMEM((3, 4 * count, HEAD_DIM), F32),
            pltpu.VMEM((dim, 3 * shard), F32),
            pltpu.VMEM((total, shard), BF),
            pltpu.VMEM((total, 128), F32),
        ],
        scalars=(bounds,),
    )

    a2k, a2z, b2k, b2z = run(
        reduce_kernel, [((dim // 4, 4 * half), BF)] * 2 + [((half, dim), BF)] * 2, (ak, ar, bk, br)
    )
    c2k, c2z = run(reduce_out_kernel, [((dim // 4 + 32, dim // 2), BF)] * 2, (ck, cr))
    size = shard // 4 * 3 + half // 4
    p0, p1, p2, p3 = run(
        owners_kernel,
        [((size, dim), F32)] + [((size, dim), BF)] * 3,
        (a2k, flip(a2z, 4), b2k, flip(b2z, 2), c2k, flip(c2z, 4)),
    )
    (mine_p,) = run(total_kernel, [((size, dim), BF)], (p0, turn(p1, 1), turn(p2, 2), turn(p3, 3)))
    plane = [mine_p] + [flip(mine_p, bits) for bits in (2, 4, 6)]
    plane += [flip(piece, 1) for piece in plane]
    dinner_w, douter_w, dout_w, small = run(
        finish_kernel,
        [((shard, 8 * half), F32), ((hidden, dim), F32), ((shard, dim), F32), ((16, dim), F32)],
        plane,
    )
    dinner_b = pick(small[6:10].reshape(2, 4, half), own, 1).reshape(hidden)
    small = lax.dynamic_slice_in_dim(small[:6], own * shard, shard, 1)

    (heads,) = run(
        total_kernel, [((shard + 16, 3 * shard), BF)], (h0, turn(h1, 1), turn(h2, 2), turn(h3, 3))
    )
    (heads,) = run(total_kernel, [((shard + 16, 3 * shard), BF)], (heads, flip(heads, 4)))
    dquery_w, dkey_w, dvalue_w, heads_b = run(
        heads_kernel,
        [((shard, dim), F32)] * 3 + [((16, 3 * shard), F32)],
        (heads, flip(heads, 1), flip(heads, 2), flip(heads, 3)),
    )

    near_t, far_t = run(
        merge_kernel, [((count, dim), F32), ((count, dim), BF)], (keep, flip(send, 1), dfirst_sum)
    )
    dtokens = near_t + wide(flip(far_t, 2))
    tokens_grad = pair(dtokens[:rows], wide(flip(short(dtokens[rows:]), 4)), y)

    return (
        output[:, None],
        tokens_grad[:, None],
        dquery_w,
        heads_b[0, :shard],
        dkey_w,
        dvalue_w,
        heads_b[0, 2 * shard :],
        dout_w,
        small[0],
        small[1],
        small[2],
        dinner_w,
        dinner_b,
        douter_w,
        small[3],
        small[4],
        small[5],
    )


def plane_device(*args):
    return plane_steps(*args)


def solution(mesh):
    placed = (
        P(None, "wt", "ctx", None),
        P(None, "wt", None),
        P("wt", None),
        P("wt"),
        P("wt", None),
        P("wt", None),
        P("wt"),
        P("wt", None),
        P("wt"),
        P("wt"),
        P("wt"),
        P("wt", None),
        P("wt"),
        P("wt", None),
        P("wt"),
        P("wt"),
        P("wt"),
        P(None, "wt", "ctx", None),
    )
    fits = mesh.shape["ctx"] == 8 and mesh.shape["wt"] == 4
    return jax.shard_map(
        plane_device if fits else general_device,
        mesh=mesh,
        in_specs=placed,
        out_specs=(
            P(None, "wt", "ctx", None),
            P(None, "wt", "ctx", None),
            P("wt", None),
            P("wt"),
            P("wt", None),
            P("wt", None),
            P("wt"),
            P("wt", None),
            P("wt"),
            P("wt"),
            P("wt"),
            P("wt", None),
            P("wt"),
            P("wt", None),
            P("wt"),
            P("wt"),
            P("wt"),
        ),
        check_vma=False,
    )
```

```python
import math

import jax
import jax.numpy as jnp
from jax import lax
from jax.experimental import pallas as pl
from jax.experimental.pallas import tpu as pltpu
from jax.sharding import PartitionSpec as P


HEADS = 12
HEAD_DIM = 64


EPS = 1e-12
NEG = -1e30
ROOT_HALF = 0.7071067811865476


def for_sending(shard):

    def short(part):
        return part.astype(jnp.bfloat16) if part.dtype == jnp.float32 else part

    return jax.tree.map(short, shard)


def normalize(rows, gain, shift):
    mean = jnp.mean(rows, axis=-1, keepdims=True)
    centered = rows - mean
    spread = jnp.mean(centered * centered, axis=-1, keepdims=True)
    return centered * lax.rsqrt(spread + EPS) * gain + shift


def gelu(inner):
    return 0.5 * inner * (1.0 + lax.erf(inner * ROOT_HALF))


def segment_of(starts, positions):
    found = (starts[:, None, :] <= positions[:, :, None]).astype(jnp.int32)
    return jnp.sum(found, axis=-1) - 1


def project(inputs, weight):
    return jnp.einsum("btd,de->bte", inputs, weight, preferred_element_type=jnp.float32)


def project_back(grads, weight):
    return jnp.einsum("bte,de->btd", grads, weight, preferred_element_type=jnp.float32)


def outer_sum(inputs, grads):
    return jnp.einsum("btd,bte->de", inputs, grads, preferred_element_type=jnp.float32)


def row_sum(grads):
    return jnp.sum(grads.astype(jnp.float32), axis=(0, 1))


def heads_of(array):
    return array.reshape(array.shape[0], array.shape[1], HEADS, HEAD_DIM)


def block_loop(width, carry, visit):
    block = math.gcd(width, 512)

    def step(state, index):
        return (visit(state, index * block, block), None)

    carry, _ = lax.scan(step, carry, jnp.arange(width // block, dtype=jnp.int32))
    return carry


def reaches(starts, own_seg, first, count):
    positions = first + jnp.arange(count, dtype=jnp.int32)
    other = segment_of(starts, jnp.broadcast_to(positions, (starts.shape[0], count)))
    touch = jnp.any((other[:, 0] <= own_seg[:, -1]) & (other[:, -1] >= own_seg[:, 0]))
    return (other, touch)


def keep_state(state):
    return state


def forward_attention(queries, query_seg, starts, keys, values):
    scale = HEAD_DIM ** (-0.5)
    batch, rows = (queries.shape[0], queries.shape[1])
    query_heads = heads_of(queries)

    def forward_fold(carry, piece, start):
        key_piece, value_piece = piece

        def visit(state, offset, count):
            other, touch = reaches(starts, query_seg, offset, count)

            def compute(state):
                top, total, accum = state
                key_block = heads_of(lax.dynamic_slice_in_dim(key_piece, offset, count, 1))
                value_block = heads_of(lax.dynamic_slice_in_dim(value_piece, offset, count, 1))
                scores = (
                    jnp.einsum(
                        "bqhd,bkhd->bhqk",
                        query_heads,
                        key_block,
                        preferred_element_type=jnp.float32,
                    )
                    * scale
                )
                mask = (query_seg[:, :, None] == other[:, None, :])[:, None]
                scores = jnp.where(mask, scores, NEG)
                new_top = jnp.maximum(top, jnp.max(scores, axis=-1))
                expd = jnp.where(mask, jnp.exp(scores - new_top[..., None]), 0.0)
                factor = jnp.exp(top - new_top)
                total = total * factor + jnp.sum(expd, axis=-1)
                added = jnp.einsum(
                    "bhqk,bkhd->bqhd",
                    expd.astype(jnp.bfloat16),
                    value_block,
                    preferred_element_type=jnp.float32,
                )
                accum = accum * jnp.transpose(factor, (0, 2, 1))[..., None] + added
                return (new_top, total, accum)

            return lax.cond(touch, compute, keep_state, state)

        return block_loop(key_piece.shape[1], carry, visit)

    init = (
        jnp.full((batch, HEADS, rows), NEG, jnp.float32),
        jnp.zeros((batch, HEADS, rows), jnp.float32),
        jnp.zeros((batch, rows, HEADS, HEAD_DIM), jnp.float32),
    )
    whole = (keys, values)
    top, total, accum = forward_fold(
        init,
        (
            lax.all_gather(keys, "ctx", axis=1, tiled=True),
            lax.all_gather(values, "ctx", axis=1, tiled=True),
        ),
        jnp.int32(0),
    )
    mixed = accum / jnp.transpose(total, (0, 2, 1))[..., None]
    return (mixed, top + jnp.log(total), whole)


def query_gradient(queries, query_seg, starts, keys, values, dmixed, logsum, delta):
    scale = HEAD_DIM ** (-0.5)
    query_heads = heads_of(queries)
    grad_heads = heads_of(dmixed)

    def query_fold(carry, piece, start):
        key_piece, value_piece = piece

        def visit(state, offset, count):
            other, touch = reaches(starts, query_seg, offset, count)

            def compute(state):
                key_block = heads_of(lax.dynamic_slice_in_dim(key_piece, offset, count, 1))
                value_block = heads_of(lax.dynamic_slice_in_dim(value_piece, offset, count, 1))
                scores = (
                    jnp.einsum(
                        "bqhd,bkhd->bhqk",
                        query_heads,
                        key_block,
                        preferred_element_type=jnp.float32,
                    )
                    * scale
                )
                mask = (query_seg[:, :, None] == other[:, None, :])[:, None]
                probs = jnp.where(
                    mask, jnp.exp(jnp.where(mask, scores, NEG) - logsum[..., None]), 0.0
                )
                dprobs = jnp.einsum(
                    "bqhd,bkhd->bhqk", grad_heads, value_block, preferred_element_type=jnp.float32
                )
                dscores = (probs * (dprobs - delta[..., None])).astype(jnp.bfloat16)
                return (
                    state
                    + jnp.einsum(
                        "bhqk,bkhd->bqhd", dscores, key_block, preferred_element_type=jnp.float32
                    )
                    * scale
                )

            return lax.cond(touch, compute, keep_state, state)

        return block_loop(key_piece.shape[1], carry, visit)

    init = jnp.zeros(query_heads.shape, jnp.float32)
    return query_fold(
        init,
        (
            lax.all_gather(keys, "ctx", axis=1, tiled=True),
            lax.all_gather(values, "ctx", axis=1, tiled=True),
        ),
        jnp.int32(0),
    )


def key_gradient(keys, values, key_seg, starts, queries, dmixed, logsum, delta):
    scale = HEAD_DIM ** (-0.5)
    key_heads = heads_of(keys)
    value_heads = heads_of(values)
    every_top, every_delta = (
        lax.all_gather(logsum, "ctx", axis=2, tiled=True),
        lax.all_gather(delta, "ctx", axis=2, tiled=True),
    )

    def key_fold(carry, piece, start):
        query_piece, grad_piece = piece

        def visit(state, offset, count):
            other, touch = reaches(starts, key_seg, offset, count)

            def compute(state):
                dkeys, dvalues = state
                query_block = heads_of(lax.dynamic_slice_in_dim(query_piece, offset, count, 1))
                grad_block = heads_of(lax.dynamic_slice_in_dim(grad_piece, offset, count, 1))
                top_block = lax.dynamic_slice_in_dim(every_top, offset, count, 2)
                delta_block = lax.dynamic_slice_in_dim(every_delta, offset, count, 2)
                scores = (
                    jnp.einsum(
                        "bqhd,bkhd->bhqk",
                        query_block,
                        key_heads,
                        preferred_element_type=jnp.float32,
                    )
                    * scale
                )
                mask = (other[:, :, None] == key_seg[:, None, :])[:, None]
                probs = jnp.where(
                    mask, jnp.exp(jnp.where(mask, scores, NEG) - top_block[..., None]), 0.0
                )
                dvalues = dvalues + jnp.einsum(
                    "bhqk,bqhd->bkhd",
                    probs.astype(jnp.bfloat16),
                    grad_block,
                    preferred_element_type=jnp.float32,
                )
                dprobs = jnp.einsum(
                    "bqhd,bkhd->bhqk", grad_block, value_heads, preferred_element_type=jnp.float32
                )
                dscores = (probs * (dprobs - delta_block[..., None])).astype(jnp.bfloat16)
                dkeys = (
                    dkeys
                    + jnp.einsum(
                        "bhqk,bqhd->bkhd", dscores, query_block, preferred_element_type=jnp.float32
                    )
                    * scale
                )
                return (dkeys, dvalues)

            return lax.cond(touch, compute, keep_state, state)

        return block_loop(query_piece.shape[1], carry, visit)

    empty = jnp.zeros(key_heads.shape, jnp.float32)
    return key_fold(
        (empty, empty),
        (
            lax.all_gather(queries, "ctx", axis=1, tiled=True),
            lax.all_gather(dmixed, "ctx", axis=1, tiled=True),
        ),
        jnp.int32(0),
    )


def forward_pass(tokens, starts, weights, base):
    (
        query_weight,
        query_bias,
        key_weight,
        value_weight,
        value_bias,
        out_weight,
        out_bias,
        first_gain,
        first_shift,
        inner_weight,
        inner_bias,
        outer_weight,
        outer_bias,
        second_gain,
        second_shift,
    ) = weights
    rows = tokens.shape[1]
    positions = base + jnp.arange(rows, dtype=jnp.int32)
    query_seg = segment_of(starts, jnp.broadcast_to(positions, (tokens.shape[0], rows)))
    queries = (project(tokens, query_weight) + query_bias.astype(jnp.float32)).astype(jnp.bfloat16)
    keys = project(tokens, key_weight).astype(jnp.bfloat16)
    values = (project(tokens, value_weight) + value_bias.astype(jnp.float32)).astype(jnp.bfloat16)
    mixed, logsum, whole = forward_attention(queries, query_seg, starts, keys, values)
    mixed_low = mixed.reshape(tokens.shape).astype(jnp.bfloat16)
    first_sum = (
        tokens.astype(jnp.float32) + project(mixed_low, out_weight) + out_bias.astype(jnp.float32)
    )
    first = normalize(first_sum, first_gain.astype(jnp.float32), first_shift.astype(jnp.float32))
    first_low = first.astype(jnp.bfloat16)
    inner = project(first_low, inner_weight) + inner_bias.astype(jnp.float32)
    active = gelu(inner).astype(jnp.bfloat16)
    second_sum = first + project(active, outer_weight) + outer_bias.astype(jnp.float32)
    output = normalize(
        second_sum, second_gain.astype(jnp.float32), second_shift.astype(jnp.float32)
    ).astype(jnp.bfloat16)
    saved = (
        tokens,
        query_seg,
        queries,
        keys,
        values,
        mixed,
        logsum,
        mixed_low,
        first_sum,
        first_low,
        inner,
        active,
        second_sum,
        whole,
    )
    return (output, saved)


def backward_pass(saved, starts, weights, cotangent):
    (
        query_weight,
        _,
        key_weight,
        value_weight,
        _,
        out_weight,
        _,
        first_gain,
        first_shift,
        inner_weight,
        _,
        outer_weight,
        _,
        second_gain,
        second_shift,
    ) = weights
    (
        tokens,
        query_seg,
        queries,
        keys,
        values,
        mixed,
        logsum,
        mixed_low,
        first_sum,
        first_low,
        inner,
        active,
        second_sum,
        _,
    ) = saved
    unused, second_back = jax.vjp(
        normalize, second_sum, second_gain.astype(jnp.float32), second_shift.astype(jnp.float32)
    )
    dsecond, dgain_second, dshift_second = second_back(cotangent.astype(jnp.float32))
    douter = dsecond.astype(jnp.bfloat16)
    dactive = project_back(douter, outer_weight)
    unused, gelu_back = jax.vjp(gelu, inner)
    dinner = gelu_back(dactive)[0].astype(jnp.bfloat16)
    dfirst = dsecond + project_back(dinner, inner_weight)
    unused, first_back = jax.vjp(
        normalize, first_sum, first_gain.astype(jnp.float32), first_shift.astype(jnp.float32)
    )
    dfirst_sum, dgain_first, dshift_first = first_back(dfirst)
    dbranch = dfirst_sum.astype(jnp.bfloat16)
    dmixed = project_back(dbranch, out_weight).astype(jnp.bfloat16)
    delta = jnp.einsum("bqhd,bqhd->bhq", heads_of(dmixed).astype(jnp.float32), mixed)
    dqueries = query_gradient(queries, query_seg, starts, keys, values, dmixed, logsum, delta)
    dkeys, dvalues = key_gradient(keys, values, query_seg, starts, queries, dmixed, logsum, delta)
    dqueries = dqueries.reshape(tokens.shape).astype(jnp.bfloat16)
    dkeys = dkeys.reshape(tokens.shape).astype(jnp.bfloat16)
    dvalues = dvalues.reshape(tokens.shape).astype(jnp.bfloat16)
    tokens_grad = (
        dfirst_sum
        + project_back(dqueries, query_weight)
        + project_back(dkeys, key_weight)
        + project_back(dvalues, value_weight)
    )
    sums = (
        outer_sum(tokens, dqueries),
        row_sum(dqueries),
        outer_sum(tokens, dkeys),
        outer_sum(tokens, dvalues),
        row_sum(dvalues),
        outer_sum(mixed_low, dbranch),
        row_sum(dbranch),
        dgain_first,
        dshift_first,
        outer_sum(first_low, dinner),
        row_sum(dinner),
        outer_sum(active, douter),
        row_sum(douter),
        dgain_second,
        dshift_second,
    )
    return (tokens_grad, sums)


def general_device(
    tokens,
    doc_lengths,
    query_weight,
    query_bias,
    key_weight,
    value_weight,
    value_bias,
    out_weight,
    out_bias,
    first_gain,
    first_shift,
    inner_weight,
    inner_bias,
    outer_weight,
    outer_bias,
    second_gain,
    second_shift,
    cotangent,
):
    params = (
        query_weight,
        query_bias,
        key_weight,
        value_weight,
        value_bias,
        out_weight,
        out_bias,
        first_gain,
        first_shift,
        inner_weight,
        inner_bias,
        outer_weight,
        outer_bias,
        second_gain,
        second_shift,
    )
    rows = tokens.shape[2]
    base = lax.axis_index("ctx") * rows
    lengths = doc_lengths[:, 0]
    starts = jnp.cumsum(lengths, axis=-1) - lengths
    outputs = []
    token_parts = []
    sums = None
    for index in range(tokens.shape[0]):
        weights = (
            lax.all_gather(params[0], "wt", axis=0, tiled=True),
            lax.all_gather(params[1], "wt", axis=0, tiled=True),
            lax.all_gather(params[2], "wt", axis=0, tiled=True),
            lax.all_gather(params[3], "wt", axis=0, tiled=True),
            lax.all_gather(params[4], "wt", axis=0, tiled=True),
            lax.all_gather(params[5], "wt", axis=0, tiled=True),
            lax.all_gather(params[6], "wt", axis=0, tiled=True),
            lax.all_gather(params[7], "wt", axis=0, tiled=True),
            lax.all_gather(params[8], "wt", axis=0, tiled=True),
            lax.all_gather(params[9], "wt", axis=0, tiled=True),
            lax.all_gather(params[10], "wt", axis=0, tiled=True),
            lax.all_gather(params[11], "wt", axis=0, tiled=True),
            lax.all_gather(params[12], "wt", axis=0, tiled=True),
            lax.all_gather(params[13], "wt", axis=0, tiled=True),
            lax.all_gather(params[14], "wt", axis=0, tiled=True),
        )
        part_out, saved = forward_pass(
            tokens[index : index + 1, 0], starts[index : index + 1], weights, base
        )
        again = (
            lax.all_gather(params[0], "wt", axis=0, tiled=True),
            lax.all_gather(params[1], "wt", axis=0, tiled=True),
            lax.all_gather(params[2], "wt", axis=0, tiled=True),
            lax.all_gather(params[3], "wt", axis=0, tiled=True),
            lax.all_gather(params[4], "wt", axis=0, tiled=True),
            lax.all_gather(params[5], "wt", axis=0, tiled=True),
            lax.all_gather(params[6], "wt", axis=0, tiled=True),
            lax.all_gather(params[7], "wt", axis=0, tiled=True),
            lax.all_gather(params[8], "wt", axis=0, tiled=True),
            lax.all_gather(params[9], "wt", axis=0, tiled=True),
            lax.all_gather(params[10], "wt", axis=0, tiled=True),
            lax.all_gather(params[11], "wt", axis=0, tiled=True),
            lax.all_gather(params[12], "wt", axis=0, tiled=True),
            lax.all_gather(params[13], "wt", axis=0, tiled=True),
            lax.all_gather(params[14], "wt", axis=0, tiled=True),
        )
        part_grad, part_sums = backward_pass(
            saved, starts[index : index + 1], again, cotangent[index : index + 1, 0]
        )
        outputs.append(part_out)
        token_parts.append(part_grad)
        sums = part_sums if sums is None else jax.tree.map(jnp.add, sums, part_sums)
    output = jnp.concatenate(outputs, axis=0)
    tokens_grad = jnp.concatenate(token_parts, axis=0)
    shards = jax.tree.map(
        lambda part: part.astype(jnp.float32),
        lax.psum_scatter(for_sending(sums), "wt", scatter_dimension=0, tiled=True),
    )
    totals = lax.psum(shards, "ctx")
    return (output[:, None], tokens_grad[:, None]) + tuple(totals)


def flip(value, bits):
    return lax.ppermute(value, "ctx", [(i, i ^ bits) for i in range(8)])


def turn(value, step):
    return lax.ppermute(value, "wt", [(i, (i - step) % 4) for i in range(4)])


def pick(value, index, axis=0):
    return lax.dynamic_index_in_dim(value, index, axis, keepdims=False)


def pair(own, other, bit, axis=0):
    return jnp.where(bit == 0, jnp.stack([own, other], axis), jnp.stack([other, own], axis))


def short(value):
    return value.astype(jnp.bfloat16)


def wide(value):
    return value.astype(jnp.float32)


def dot(left, right):
    return jnp.dot(left, right, preferred_element_type=jnp.float32)


def dot_back(left, right):
    return lax.dot_general(
        left, right, (((1,), (1,)), ((), ())), preferred_element_type=jnp.float32
    )


def dot_sum(left, right):
    return lax.dot_general(
        left, right, (((0,), (0,)), ((), ())), preferred_element_type=jnp.float32
    )


def norm_parts(rows):
    mean = jnp.mean(rows, axis=-1, keepdims=True)
    centered = rows - mean
    spread = jnp.mean(centered * centered, axis=-1, keepdims=True)
    root = lax.rsqrt(spread + EPS)
    return centered * root, root


def norm_back(upstream, normed, root, gain):
    grad = upstream * gain
    mean = jnp.mean(grad, axis=-1, keepdims=True)
    along = jnp.mean(grad * normed, axis=-1, keepdims=True)
    return root * (grad - mean - normed * along)


def gelu_slope(inner):
    bell = jnp.exp(-0.5 * inner * inner) * (1.0 / math.sqrt(2.0 * math.pi))
    return 0.5 * (1.0 + lax.erf(inner * ROOT_HALF)) + inner * bell


def run(kernel, outs, args, scratch=(), scalars=()):
    shapes = tuple(jax.ShapeDtypeStruct(shape, dtype) for shape, dtype in outs)
    spaces = [pltpu.SMEM] * len(scalars) + [pltpu.VMEM] * len(args)
    return pl.pallas_call(
        kernel,
        out_shape=shapes,
        in_specs=[pl.BlockSpec(memory_space=space) for space in spaces],
        scratch_shapes=list(scratch),
    )(*scalars, *args)


BF = jnp.bfloat16
F32 = jnp.float32


def where_am_i():
    ctx, own = lax.axis_index("ctx"), lax.axis_index("wt")
    return ctx & 1, (ctx >> 1) & 3, ctx & 3, own


def some_rows(start, count):
    return pl.ds(pl.multiple_of(start, 16), count)


def prepare_kernel(wq, wk, wv, wo, wi, wo2, vec, heads_own, heads_send, w2_send, inner_half, outer_half):
    core, quarter, group, _ = where_am_i()
    shard, dim = wq.shape
    width, half = dim // 4, wo2.shape[0] // 2
    for index in range(4):

        @pl.when(group == index)
        def _():
            for slot, ref in enumerate((wq, wk, wv)):
                heads_own[:, slot * width : (slot + 1) * width] = ref[
                    :, index * width : (index + 1) * width
                ]

    for index in range(2):

        @pl.when(core == index)
        def _():
            for block in range(4):
                at = block * 2 * half + index * half
                inner_half[:, block * half : (block + 1) * half] = wi[:, at : at + half]
            outer_half[...] = wo2[index * half : (index + 1) * half, :]

    part = shard // 2
    heads_send[0:part, :] = heads_own[some_rows((quarter >> 1) * part, part), :]
    heads_send[part:, 0:width] = vec[...]
    heads_send[part:, width:] = jnp.zeros((16, 2 * width), BF)
    part = shard // 4
    rows = some_rows(quarter * part, part)
    w2_send[0:part, :] = inner_half[rows, 0:dim]
    w2_send[part : 2 * part, :] = inner_half[rows, dim:]
    step = half // 4
    w2_send[2 * part : 2 * part + step, :] = outer_half[some_rows(quarter * step, step), :]
    w2_send[2 * part + step :, :] = wo[rows, :]


CHUNK = 128
WINDOWS = (4, 6, 8)


def chunk_of(ctx, index):
    return ctx ^ ((index >> 2) | (index & 2) | ((index & 1) << 2))


def some_chunks(start, count):
    return pl.ds(pl.multiple_of(start * CHUNK, CHUNK), count * CHUNK)


def over_window(bounds, block, visit):
    low, count = bounds[0, block], bounds[1, block]
    if len(WINDOWS) == 1:
        visit(pl.ds(0, WINDOWS[0] * CHUNK))
        return
    least = 0
    for size in WINDOWS:

        @pl.when((count > least) & (count <= size))
        def _(size=size):
            visit(some_chunks(jnp.minimum(low, WINDOWS[-1] - size), size))

        least = size


def attend_rows(bounds, qkv, seg_col, seg_row, far, outs, logsum, mixed):
    core, quarter, _, _ = where_am_i()
    scale = HEAD_DIM ** (-0.5)
    group = qkv.shape[0] // 3

    def step(side, carry):
        block = 2 * side + ((quarter & 1) ^ far)
        rows = some_chunks(2 * block, 2)
        here = some_chunks(2 * side, 2)

        def visit(keys):
            mask = seg_col[rows, :] == seg_row[:, keys]
            sums = []
            for head in range(group):
                scores = dot_back(qkv[head, rows, :], qkv[group + head, keys, :])
                scores = jnp.where(mask, scores * scale, NEG)
                top = jnp.max(scores, axis=-1, keepdims=True)
                expd = jnp.exp(scores - top)
                total = jnp.sum(expd, axis=-1, keepdims=True)
                probs = short(expd * (1.0 / total))
                mixed[here, head * HEAD_DIM : (head + 1) * HEAD_DIM] = short(
                    dot(probs, qkv[2 * group + head, keys, :])
                )
                sums.append(top + jnp.log(total))
            logsum[here, :] = jnp.concatenate(
                sums + [jnp.zeros_like(sums[0])] * (128 - group), axis=1
            )

        over_window(bounds, block, visit)
        return carry

    lax.fori_loop(0, 2, step, 0)
    y = quarter >> 1
    for index, out in enumerate(outs):
        for side in range(2):
            chunk = 2 * (y ^ side) + (core ^ index)
            out[side * CHUNK : (side + 1) * CHUNK, :] = mixed[some_chunks(chunk, 1), :]


def attend_near_kernel(
    bounds, mine, other, far, heads_own, g1, g2, g3, h1, h2, h3, bias, seg_col, seg_row,
    qkv, m0, m1, logsum, weight, mixed,
):
    _, quarter, _, own = where_am_i()
    ctx = lax.axis_index("ctx")
    shard = heads_own.shape[0]
    part = shard // 2
    y = quarter >> 1
    weight[some_rows(own * shard, shard), :] = heads_own[...]
    for step, near_half, far_half in ((1, g1, h1), (2, g2, h2), (3, g3, h3)):
        at = ((own + step) & 3) * shard
        weight[some_rows(at + part * y, part), :] = near_half[0:part, :]
        weight[some_rows(at + part * (1 - y), part), :] = far_half[0:part, :]
    index = 0
    for source in (mine, other, far):
        for first in range(0, source.shape[0], 2 * CHUNK):
            low = short(dot(source[first : first + 2 * CHUNK, :], weight[...]) + bias[...])
            for half in range(2):
                at = pl.multiple_of(chunk_of(ctx, index) * CHUNK, CHUNK)
                for slot in range(qkv.shape[0]):
                    qkv[slot, pl.ds(at, CHUNK), :] = low[
                        half * CHUNK : (half + 1) * CHUNK,
                        slot * HEAD_DIM : (slot + 1) * HEAD_DIM,
                    ]
                index += 1
    attend_rows(bounds, qkv, seg_col, seg_row, 0, (m0, m1), logsum, mixed)


def attend_far_kernel(bounds, qkv, seg_col, seg_row, m2, m3, logsum, mixed):
    attend_rows(bounds, qkv, seg_col, seg_row, 1, (m2, m3), logsum, mixed)


def project_kernel(m0, m1, m2, m3, mine, wo, vec, *refs):
    pieces, (first_sum, first_low, out_full) = refs[:12], refs[12:]
    _, quarter, group, own = where_am_i()
    shard = wo.shape[0]
    part = shard // 4
    out_full[some_rows(own * shard, shard), :] = wo[...]
    for index, piece in enumerate(pieces):
        at = ((own + 1 + index // 4) & 3) * shard + part * (quarter ^ (index % 4))
        out_full[some_rows(at, part), :] = piece[piece.shape[0] - part :, :]
    total = wide(mine[...]) + vec[2:3, :]
    for code, ref in enumerate((m0, m1, m2, m3)):
        total += dot(ref[...], out_full[some_rows((group ^ code) * shard, shard), :])
    first_sum[...] = total
    first_low[...] = short(norm_parts(total)[0] * vec[3:4, :] + vec[4:5, :])


def forward_kernel(near, far, inner_half, outer_half, bias, *refs):
    pieces, (keep, send, inner, active, wi_full, wo2_full) = refs[:12], refs[12:]
    _, quarter, _, own = where_am_i()
    shard, half = inner_half.shape[0], outer_half.shape[0]
    dim = keep.shape[1]
    part, step = shard // 4, half // 4
    wi_full[some_rows(own * shard, shard), :] = inner_half[...]
    wo2_full[some_rows(own * half, half), :] = outer_half[...]
    for index, piece in enumerate(pieces):
        row, spot = (own + 1 + index // 4) & 3, quarter ^ (index % 4)
        rows = some_rows(row * shard + part * spot, part)
        wi_full[rows, 0:dim] = piece[0:part, :]
        wi_full[rows, dim:] = piece[part : 2 * part, :]
        wo2_full[some_rows(row * half + step * spot, step), :] = piece[
            2 * part : 2 * part + step, :
        ]
    count = near.shape[0]
    chunk = 512
    for index, (source, out) in enumerate(((far, send), (near, keep))):
        at = (1 - index) * count
        total = None
        for lane in range(0, inner.shape[1], chunk):
            lanes = slice(lane, lane + chunk)
            value = dot(source[...], wi_full[:, lanes]) + bias[:, lanes]
            inner[at : at + count, lanes] = value
            low = short(gelu(value))
            active[at : at + count, lanes] = low
            added = dot(low, wo2_full[lanes, :])
            total = added if total is None else total + added
        out[...] = total


def turnaround_kernel(first_sum, keep, got, vec, cot0, cot1, out0, out1, dsecond, douter, sums):
    rows = cot0.shape[0]
    first = norm_parts(first_sum[...])[0] * vec[3:4, :] + vec[4:5, :]
    normed, root = norm_parts(first + vec[5:6, :] + keep[...] + got[...])
    output = short(normed * vec[6:7, :] + vec[7:8, :])
    out0[...] = output[:rows]
    out1[...] = output[rows:]
    upstream = jnp.concatenate([wide(cot0[...]), wide(cot1[...])])
    back = norm_back(upstream, normed, root, vec[6:7, :])
    low = short(back)
    dsecond[...] = back
    douter[...] = low
    sums[0:1, :] = jnp.sum(wide(low), axis=0, keepdims=True)
    sums[1:2, :] = jnp.sum(upstream * normed, axis=0, keepdims=True)
    sums[2:3, :] = jnp.sum(upstream, axis=0, keepdims=True)
    sums[3:, :] = jnp.zeros_like(sums[3:, :])


def backward_kernel(near, far, inner, wi_full, wo2_full, keep, send, dinner, sums):
    count, dim = near.shape
    chunk = 512
    for index, (source, out) in enumerate(((far, send), (near, keep))):
        at = (1 - index) * count
        total = None
        for lane in range(0, inner.shape[1], chunk):
            lanes = slice(lane, lane + chunk)
            slope = gelu_slope(inner[at : at + count, lanes])
            low = short(dot_back(source[...], wo2_full[lanes, :]) * slope)
            dinner[at : at + count, lanes] = low
            added = dot_back(low, wi_full[:, lanes])
            total = added if total is None else total + added
        out[...] = total
    total = jnp.sum(wide(dinner[...]), axis=0, keepdims=True)
    sums[0:1, :] = total[:, :dim]
    sums[1:2, :] = total[:, dim:]
    sums[2:, :] = jnp.zeros_like(sums[2:, :])


def weights_kernel(first0, first1, douter0, douter1, dinner, active, ak, az, bk, bz, left, right):
    _, quarter, _, _ = where_am_i()
    x, y = quarter & 1, quarter >> 1
    count = first0.shape[0]
    part, step = first0.shape[1] // 16, active.shape[1] // 16
    left[...] = short(dot_sum(first0[...], dinner[:count]) + dot_sum(first1[...], dinner[count:]))
    for block in range(8):
        rows = slice(block * part, (block + 1) * part)
        ak[rows, :] = left[some_rows((2 * block + x) * part, part), :]
        az[rows, :] = left[some_rows((2 * block + 1 - x) * part, part), :]
    right[...] = short(
        dot_sum(active[:count], douter0[...]) + dot_sum(active[count:], douter1[...])
    )
    for block in range(8):
        row, side = block // 2, block % 2
        rows = slice(block * step, (block + 1) * step)
        bk[rows, :] = right[some_rows((4 * row + 2 * y + side) * step, step), :]
        bz[rows, :] = right[some_rows((4 * row + 2 * (1 - y) + side) * step, step), :]


def branch_kernel(first_sum, dsecond, keep, got, vec, out_full, dfirst_sum, dbranch, d0, d1, d2, d3, sums):
    _, _, group, _ = where_am_i()
    shard = d0.shape[1]
    normed, root = norm_parts(first_sum[...])
    dfirst = dsecond[...] + keep[...] + got[...]
    back = norm_back(dfirst, normed, root, vec[3:4, :])
    low = short(back)
    dfirst_sum[...] = back
    dbranch[...] = low
    for code, ref in enumerate((d0, d1, d2, d3)):
        ref[...] = short(dot_back(low, out_full[some_rows((group ^ code) * shard, shard), :]))
    sums[0:1, :] = jnp.sum(wide(low), axis=0, keepdims=True)
    sums[1:2, :] = jnp.sum(dfirst * normed, axis=0, keepdims=True)
    sums[2:3, :] = jnp.sum(dfirst, axis=0, keepdims=True)
    sums[3:, :] = jnp.zeros_like(sums[3:, :])


def out_weight_kernel(m0, m1, m2, m3, dbranch, sums1, sums2, sums3, ck, cz, whole):
    core, _, group, _ = where_am_i()
    shard, dim = m0.shape[1], dbranch.shape[1]
    half = dim // 2
    for code, ref in enumerate((m0, m1, m2, m3)):
        whole[some_rows((group ^ code) * shard, shard), :] = short(
            dot_sum(ref[...], dbranch[...])
        )
    for side in range(2):

        @pl.when(core == side)
        def _():
            for ref, which in ((ck, side), (cz, 1 - side)):
                ref[0:dim, :] = whole[:, which * half : (which + 1) * half]

    rows = short(
        jnp.concatenate([sums1[0:3, :], sums2[0:3, :], sums3[0:2, :], jnp.zeros_like(sums1[...])])
    )
    for ref in (ck, cz):
        ref[dim : dim + 16, :] = rows[:, :half]
        ref[dim + 16 :, :] = rows[:, half:]


def out_split_kernel(packed, got, ck, cz):
    core, quarter, _, _ = where_am_i()
    x = quarter & 1
    dim = packed.shape[0] - 32
    part = dim // 16
    for block in range(8):
        rows = slice(block * part, (block + 1) * part)
        for ref, side in ((ck, x), (cz, 1 - x)):
            take = some_rows((2 * block + side) * part, part)
            ref[rows, :] = short(wide(packed[take, :]) + wide(got[take, :]))
    for lanes in range(2):
        at = dim + 16 * lanes
        mine, other = wide(packed[at : at + 16, :]), wide(got[at : at + 16, :])
        low = jnp.where(core == 0, mine, other)[6:8]
        high = jnp.where(core == 0, other, mine)[6:8]
        rows = jnp.concatenate([(mine + other)[0:6], low, high, jnp.zeros_like(mine[0:6])])
        at = 8 * part + 16 * lanes
        for ref in (ck, cz):
            ref[at : at + 16, :] = short(rows)


def reduce_rows(keep, got, outs, bit):
    size = keep.shape[0] // 8
    size -= size % 16
    for block in range(4):
        for out, side in zip(outs, (bit, 1 - bit)):
            take = some_rows((2 * block + side) * size, size)
            out[block * size : (block + 1) * size, :] = short(
                wide(keep[take, :]) + wide(got[take, :])
            )
    if keep.shape[0] > 8 * size:
        for out in outs:
            out[4 * size :, :] = short(wide(keep[8 * size :, :]) + wide(got[8 * size :, :]))


def reduce_kernel(ak, ar, bk, br, a2k, a2z, b2k, b2z):
    _, quarter, _, _ = where_am_i()
    reduce_rows(ak, ar, (a2k, a2z), quarter >> 1)
    reduce_rows(bk, br, (b2k, b2z), quarter & 1)


def reduce_out_kernel(ck, cr, c2k, c2z):
    _, quarter, _, _ = where_am_i()
    reduce_rows(ck, cr, (c2k, c2z), quarter >> 1)


def owners_kernel(ak, ar, bk, br, ck, cr, p0, p1, p2, p3):
    _, _, _, own = where_am_i()
    dim = bk.shape[1]
    half = dim // 2
    part, step = ak.shape[0] // 4, bk.shape[0] // 4
    size = (ck.shape[0] - 32) // 4
    for index, out in enumerate((p0, p1, p2, p3)):
        row = (own - index) & 3
        rows = some_rows(row * part, part)
        total = wide(ak[rows, :]) + wide(ar[rows, :])
        out[0:part, :] = total[:, :dim].astype(out.dtype)
        out[part : 2 * part, :] = total[:, dim:].astype(out.dtype)
        at = 2 * part
        rows = some_rows(row * step, step)
        out[at : at + step, :] = (wide(bk[rows, :]) + wide(br[rows, :])).astype(out.dtype)
        at += step
        rows = some_rows(row * size, size)
        out[at:, 0:half] = (wide(ck[rows, :]) + wide(cr[rows, :])).astype(out.dtype)
        tail = wide(ck[4 * size :, :]) + wide(cr[4 * size :, :])
        out[at : at + 32, half:] = tail.astype(out.dtype)
        out[at + 32 :, half:] = jnp.zeros((size - 32, half), out.dtype)


def total_kernel(mine, *refs):
    total = wide(mine[...])
    for ref in refs[:-1]:
        total += wide(ref[...])
    refs[-1][...] = short(total)


def finish_kernel(*refs):
    pieces, (dwi, dwo2, dwo, small) = refs[:8], refs[8:]
    core, quarter, _, _ = where_am_i()
    part, half = dwi.shape[0] // 4, dwi.shape[1] // 8
    step = half // 4
    tail = 2 * part + step
    for side in range(2):

        @pl.when(core == side)
        def _():
            for index, piece in enumerate(pieces):
                spot = quarter ^ (index % 4)
                which = side if index < 4 else 1 - side
                rows = some_rows(spot * part, part)
                for block in range(4):
                    at = block * 2 * half + which * half
                    up, lane = part * (block // 2), half * (block % 2)
                    dwi[rows, at : at + half] = wide(piece[up : up + part, lane : lane + half])
                dwo2[some_rows(which * half + spot * step, step), :] = wide(
                    piece[2 * part : tail, :]
                )
                dwo[rows, which * half : (which + 1) * half] = wide(piece[tail:, 0:half])

    small[:, 0:half] = wide(pieces[0][tail : tail + 16, half:])
    small[:, half:] = wide(pieces[0][tail + 16 : tail + 32, half:])


def attend_back_kernel(
    bounds, qkv, logsum0, logsum1, seg_col, seg_row, p0, p1, p2, p3, mine, other, far, weight,
    h0, h1, h2, h3, keep, send, grads, dkeys, dvalues, dweight, dmixed, logsum, whole,
):
    _, quarter, _, own = where_am_i()
    ctx = lax.axis_index("ctx")
    x = quarter & 1
    scale = HEAD_DIM ** (-0.5)
    group = qkv.shape[0] // 3
    width = group * HEAD_DIM
    block = p0.shape[0]
    dkeys[...] = jnp.zeros_like(dkeys)
    dvalues[...] = jnp.zeros_like(dvalues)
    for index, part in enumerate((p0, p2, p1, p3)):
        for side in range(2):
            chunk = chunk_of(ctx, 2 * index + side)
            dmixed[some_chunks(chunk, 1), :] = part[side * CHUNK : (side + 1) * CHUNK, :]
    for side in range(2):
        rows = slice(2 * side * CHUNK, 2 * (side + 1) * CHUNK)
        logsum[some_chunks(2 * (2 * side + x), 2), :] = logsum0[rows, :]
        logsum[some_chunks(2 * (2 * side + 1 - x), 2), :] = logsum1[rows, :]

    def step(index, carry):
        rows = some_chunks(2 * index, 2)

        def visit(window):
            mask = seg_col[rows, :] == seg_row[:, window]
            for head in range(group):
                lanes = slice(head * HEAD_DIM, (head + 1) * HEAD_DIM)
                query = qkv[head, rows, :]
                grad = dmixed[rows, lanes]
                keys = qkv[group + head, window, :]
                scores = jnp.where(mask, dot_back(query, keys) * scale, NEG)
                probs = jnp.exp(scores - logsum[rows, head : head + 1])
                dprobs = dot_back(grad, qkv[2 * group + head, window, :])
                delta = jnp.sum(probs * dprobs, axis=-1, keepdims=True)
                dscores = short(probs * (dprobs - delta))
                whole[rows, lanes] = short(dot(dscores, keys) * scale)
                dkeys[head, window, :] += dot_sum(dscores, query)
                dvalues[head, window, :] += dot_sum(short(probs), grad)

        over_window(bounds, index, visit)
        return carry

    lax.fori_loop(0, 4, step, 0)
    for head in range(group):
        at = width + head * HEAD_DIM
        whole[:, at : at + HEAD_DIM] = short(dkeys[head] * scale)
        whole[:, at + width : at + width + HEAD_DIM] = short(dvalues[head])
    for index in range(8):
        grads[index * CHUNK : (index + 1) * CHUNK, :] = whole[
            some_chunks(chunk_of(ctx, index), 1), :
        ]
    rows = 2 * block
    dweight[...] = (
        dot_sum(mine[...], grads[:block])
        + dot_sum(other[...], grads[block:rows])
        + dot_sum(far[...], grads[rows:])
    )
    sums = jnp.sum(wide(grads[...]), axis=0, keepdims=True)
    tail = jnp.concatenate([sums, jnp.zeros((15, sums.shape[1]), F32)])
    for index, out in enumerate((h0, h1, h2, h3)):
        take = pl.ds(pl.multiple_of(((own - index) & 3) * width, 16), width)
        out[0:width, :] = dweight[take, :].astype(out.dtype)
        out[width:, :] = tail.astype(out.dtype)
    keep[...] = dot_back(grads[:rows], weight[...])
    send[...] = short(dot_back(grads[rows:], weight[...]))


def merge_kernel(keep, got, base, near, far):
    total = keep[...] + wide(got[...])
    count = near.shape[0]
    near[...] = total[:count] + base[...]
    far[...] = short(total[count:])


def heads_kernel(s0, s1, s2, s3, dq, dk, dv, bias):
    _, _, group, own = where_am_i()
    shard = dq.shape[0]
    for index in range(4):

        @pl.when(group == index)
        def _():
            for code, ref in enumerate((s0, s1, s2, s3)):
                at = (index ^ code) * shard
                for slot, out in enumerate((dq, dk, dv)):
                    out[:, at : at + shard] = wide(
                        ref[0:shard, slot * shard : (slot + 1) * shard]
                    )

                @pl.when(own == index ^ code)
                def _():
                    bias[...] = wide(ref[shard:, :])


def plane_steps(
    tokens,
    doc_lengths,
    query_weight,
    query_bias,
    key_weight,
    value_weight,
    value_bias,
    out_weight,
    out_bias,
    first_gain,
    first_shift,
    inner_weight,
    inner_bias,
    outer_weight,
    outer_bias,
    second_gain,
    second_shift,
    cotangent,
):
    ctx, own = lax.axis_index("ctx"), lax.axis_index("wt")
    core, y, group = ctx & 1, ctx >> 2, ctx & 3
    rows, dim = tokens.shape[2], tokens.shape[3]
    shard = query_weight.shape[0]
    hidden = outer_weight.shape[0]
    half = hidden // 2
    count = 2 * rows

    mine = jnp.concatenate([pick(tokens[:, 0], y), flip(pick(tokens[:, 0], 1 - y), 4)])
    other = flip(mine, 2)
    far = flip(jnp.concatenate([mine, other]), 1)

    vector_list = (
        query_bias,
        value_bias,
        out_bias,
        first_gain,
        first_shift,
        outer_bias,
        second_gain,
        second_shift,
        *[inner_bias[at : at + shard] for at in range(0, 4 * shard, shard)],
    )
    line = lax.broadcasted_iota(jnp.int32, (16, shard), 0)
    vec = jnp.zeros((16, shard), BF)
    for index, value in enumerate(vector_list):
        vec = jnp.where(line == index, value[None, :], vec)
    heads_own, heads_send, w2_send, inner_half, outer_half = run(
        prepare_kernel,
        [
            ((shard, 3 * shard), BF),
            ((shard // 2 + 16, 3 * shard), BF),
            ((shard // 4 * 3 + half // 4, dim), BF),
            ((shard, 4 * half), BF),
            ((half, dim), BF),
        ],
        (query_weight, key_weight, value_weight, out_weight, inner_weight, outer_weight, vec),
    )
    got = [turn(heads_send, step) for step in (1, 2, 3)]
    gone = [flip(value, 4) for value in got]
    pieces = []
    for step in (1, 2, 3):
        piece = turn(w2_send, step)
        pieces += [piece] + [flip(piece, bits) for bits in (2, 4, 6)]

    at = shard // 2
    rel = jnp.stack([vec] + [value[at:, :shard] for value in got])
    vectors = wide(lax.dynamic_slice_in_dim(jnp.concatenate([rel, rel]), (4 - own) % 4, 4))
    mine_b = pick(vectors, group)
    heads_bias = jnp.concatenate([mine_b[0], jnp.zeros_like(mine_b[0]), mine_b[1]])[None]
    inner_b = pick(vectors[:, 8:12].reshape(4, 2, half), core, 1).reshape(1, 4 * half)
    vectors = jnp.swapaxes(vectors[:, :8], 0, 1).reshape(8, dim)

    lengths = pick(doc_lengths[:, 0], y)
    starts = jnp.cumsum(lengths) - lengths
    total = 8 * rows
    positions = jnp.arange(total, dtype=jnp.int32)
    seg = jnp.sum((starts[None, :] <= positions[:, None]).astype(jnp.int32), axis=-1) - 1
    segs = (seg[:, None], seg[None, :])
    first = jnp.arange(4, dtype=jnp.int32)[:, None] * (2 * CHUNK)
    low = jnp.max(jnp.where(starts[None, :] <= first, starts[None, :], 0), axis=-1) // CHUNK
    ends = jnp.where(starts[None, :] >= first + 2 * CHUNK, starts[None, :], total)
    bounds = jnp.stack([low, (jnp.min(ends, axis=-1) - 1) // CHUNK - low + 1])

    qkv, m0, m1, logsum0, heads_weight = run(
        attend_near_kernel,
        [
            ((9, total, HEAD_DIM), BF),
            ((count, shard), BF),
            ((count, shard), BF),
            ((2 * count, 128), F32),
            ((dim, 3 * shard), BF),
        ],
        (mine, other, far, heads_own, *got, *gone, heads_bias, *segs),
        [pltpu.VMEM((2 * count, shard), BF)],
        scalars=(bounds,),
    )
    m2, m3, logsum1 = run(
        attend_far_kernel,
        [((count, shard), BF), ((count, shard), BF), ((2 * count, 128), F32)],
        (qkv, *segs),
        [pltpu.VMEM((2 * count, shard), BF)],
        scalars=(bounds,),
    )
    mixed = [m0, flip(m1, 1), flip(m2, 2), flip(m3, 3)]

    first_sum, first_low, out_full = run(
        project_kernel,
        [((count, dim), F32), ((count, dim), BF), ((dim, dim), BF)],
        (*mixed, mine, out_weight, vectors, *pieces),
    )
    first_far = flip(first_low, 1)
    keep, send, inner, active, wi_full, wo2_full = run(
        forward_kernel,
        [
            ((count, dim), F32),
            ((count, dim), F32),
            ((2 * count, 4 * half), F32),
            ((2 * count, 4 * half), BF),
            ((dim, 4 * half), BF),
            ((4 * half, dim), BF),
        ],
        (first_low, first_far, inner_half, outer_half, inner_b, *pieces),
    )
    cot = pick(cotangent[:, 0], y), flip(pick(cotangent[:, 0], 1 - y), 4)
    out0, out1, dsecond, douter, sums2 = run(
        turnaround_kernel,
        [
            ((rows, dim), BF),
            ((rows, dim), BF),
            ((count, dim), F32),
            ((count, dim), BF),
            ((8, dim), F32),
        ],
        (first_sum, keep, flip(send, 1), vectors, *cot),
    )
    output = pair(out0, flip(out1, 4), y)

    douter_far = flip(douter, 1)
    keep, send, dinner, sums3 = run(
        backward_kernel,
        [
            ((count, dim), F32),
            ((count, dim), F32),
            ((2 * count, 4 * half), BF),
            ((8, dim), F32),
        ],
        (douter, douter_far, inner, wi_full, wo2_full),
    )
    dfirst_sum, dbranch, d0, d1, d2, d3, sums1 = run(
        branch_kernel,
        [((count, dim), F32), ((count, dim), BF)] + [((count, shard), BF)] * 4 + [((8, dim), F32)],
        (first_sum, dsecond, keep, flip(send, 1), vectors, out_full),
    )
    dmixed = [d0, flip(d1, 1), flip(d2, 2), flip(d3, 3)]

    ak, az, bk, bz = run(
        weights_kernel,
        [((dim // 2, 4 * half), BF)] * 2 + [((2 * half, dim), BF)] * 2,
        (first_low, first_far, douter, douter_far, dinner, active),
        [pltpu.VMEM((dim, 4 * half), BF), pltpu.VMEM((4 * half, dim), BF)],
    )
    ar, br = flip(az, 2), flip(bz, 4)
    ck, cz = run(
        out_weight_kernel,
        [((dim + 32, dim // 2), BF)] * 2,
        (*mixed, dbranch, sums1, sums2, sums3),
        [pltpu.VMEM((dim, dim), BF)],
    )
    ck, cz = run(out_split_kernel, [((dim // 2 + 32, dim // 2), BF)] * 2, (ck, flip(cz, 1)))
    cr = flip(cz, 2)

    h0, h1, h2, h3, keep, send = run(
        attend_back_kernel,
        [((shard + 16, 3 * shard), F32)]
        + [((shard + 16, 3 * shard), BF)] * 3
        + [((2 * count, dim), F32), ((2 * count, dim), BF)],
        (qkv, logsum0, logsum1, *segs, *dmixed, mine, other, far, heads_weight),
        [
            pltpu.VMEM((4 * count, 3 * shard), BF),
            pltpu.VMEM((3, 4 * count, HEAD_DIM), F32),
            pltpu.VMEM((3, 4 * count, HEAD_DIM), F32),
            pltpu.VMEM((dim, 3 * shard), F32),
            pltpu.VMEM((total, shard), BF),
            pltpu.VMEM((total, 128), F32),
            pltpu.VMEM((total, 3 * shard), BF),
        ],
        scalars=(bounds,),
    )

    a2k, a2z, b2k, b2z = run(
        reduce_kernel, [((dim // 4, 4 * half), BF)] * 2 + [((half, dim), BF)] * 2, (ak, ar, bk, br)
    )
    c2k, c2z = run(reduce_out_kernel, [((dim // 4 + 32, dim // 2), BF)] * 2, (ck, cr))
    size = shard // 4 * 3 + half // 4
    p0, p1, p2, p3 = run(
        owners_kernel,
        [((size, dim), F32)] + [((size, dim), BF)] * 3,
        (a2k, flip(a2z, 4), b2k, flip(b2z, 2), c2k, flip(c2z, 4)),
    )
    (mine_p,) = run(total_kernel, [((size, dim), BF)], (p0, turn(p1, 1), turn(p2, 2), turn(p3, 3)))
    plane = [mine_p] + [flip(mine_p, bits) for bits in (2, 4, 6)]
    plane += [flip(piece, 1) for piece in plane]
    dinner_w, douter_w, dout_w, small = run(
        finish_kernel,
        [((shard, 8 * half), F32), ((hidden, dim), F32), ((shard, dim), F32), ((16, dim), F32)],
        plane,
    )
    dinner_b = pick(small[6:10].reshape(2, 4, half), own, 1).reshape(hidden)
    small = lax.dynamic_slice_in_dim(small[:6], own * shard, shard, 1)

    (heads,) = run(
        total_kernel, [((shard + 16, 3 * shard), BF)], (h0, turn(h1, 1), turn(h2, 2), turn(h3, 3))
    )
    (heads,) = run(total_kernel, [((shard + 16, 3 * shard), BF)], (heads, flip(heads, 4)))
    dquery_w, dkey_w, dvalue_w, heads_b = run(
        heads_kernel,
        [((shard, dim), F32)] * 3 + [((16, 3 * shard), F32)],
        (heads, flip(heads, 1), flip(heads, 2), flip(heads, 3)),
    )

    near_t, far_t = run(
        merge_kernel, [((count, dim), F32), ((count, dim), BF)], (keep, flip(send, 1), dfirst_sum)
    )
    dtokens = near_t + wide(flip(far_t, 2))
    tokens_grad = pair(dtokens[:rows], wide(flip(short(dtokens[rows:]), 4)), y)

    return (
        output[:, None],
        tokens_grad[:, None],
        dquery_w,
        heads_b[0, :shard],
        dkey_w,
        dvalue_w,
        heads_b[0, 2 * shard :],
        dout_w,
        small[0],
        small[1],
        small[2],
        dinner_w,
        dinner_b,
        douter_w,
        small[3],
        small[4],
        small[5],
    )


def plane_device(*args):
    return plane_steps(*args)


def solution(mesh):
    placed = (
        P(None, "wt", "ctx", None),
        P(None, "wt", None),
        P("wt", None),
        P("wt"),
        P("wt", None),
        P("wt", None),
        P("wt"),
        P("wt", None),
        P("wt"),
        P("wt"),
        P("wt"),
        P("wt", None),
        P("wt"),
        P("wt", None),
        P("wt"),
        P("wt"),
        P("wt"),
        P(None, "wt", "ctx", None),
    )
    fits = mesh.shape["ctx"] == 8 and mesh.shape["wt"] == 4
    return jax.shard_map(
        plane_device if fits else general_device,
        mesh=mesh,
        in_specs=placed,
        out_specs=(
            P(None, "wt", "ctx", None),
            P(None, "wt", "ctx", None),
            P("wt", None),
            P("wt"),
            P("wt", None),
            P("wt", None),
            P("wt"),
            P("wt", None),
            P("wt"),
            P("wt"),
            P("wt"),
            P("wt", None),
            P("wt"),
            P("wt", None),
            P("wt"),
            P("wt"),
            P("wt"),
        ),
        check_vma=False,
    )
```

```python
import functools
import math

import jax
import jax.numpy as jnp
from jax import lax
from jax.experimental import pallas as pl
from jax.experimental.pallas import tpu as pltpu
from jax.sharding import PartitionSpec as P


HEADS = 12
HEAD_DIM = 64


EPS = 1e-12
NEG = -1e30
ROOT_HALF = 0.7071067811865476


def for_sending(shard):

    def short(part):
        return part.astype(jnp.bfloat16) if part.dtype == jnp.float32 else part

    return jax.tree.map(short, shard)


def normalize(rows, gain, shift):
    mean = jnp.mean(rows, axis=-1, keepdims=True)
    centered = rows - mean
    spread = jnp.mean(centered * centered, axis=-1, keepdims=True)
    return centered * lax.rsqrt(spread + EPS) * gain + shift


def gelu(inner):
    return 0.5 * inner * (1.0 + lax.erf(inner * ROOT_HALF))


def segment_of(starts, positions):
    found = (starts[:, None, :] <= positions[:, :, None]).astype(jnp.int32)
    return jnp.sum(found, axis=-1) - 1


def project(inputs, weight):
    return jnp.einsum("btd,de->bte", inputs, weight, preferred_element_type=jnp.float32)


def project_back(grads, weight):
    return jnp.einsum("bte,de->btd", grads, weight, preferred_element_type=jnp.float32)


def outer_sum(inputs, grads):
    return jnp.einsum("btd,bte->de", inputs, grads, preferred_element_type=jnp.float32)


def row_sum(grads):
    return jnp.sum(grads.astype(jnp.float32), axis=(0, 1))


def heads_of(array):
    return array.reshape(array.shape[0], array.shape[1], HEADS, HEAD_DIM)


def block_loop(width, carry, visit):
    block = math.gcd(width, 512)

    def step(state, index):
        return (visit(state, index * block, block), None)

    carry, _ = lax.scan(step, carry, jnp.arange(width // block, dtype=jnp.int32))
    return carry


def reaches(starts, own_seg, first, count):
    positions = first + jnp.arange(count, dtype=jnp.int32)
    other = segment_of(starts, jnp.broadcast_to(positions, (starts.shape[0], count)))
    touch = jnp.any((other[:, 0] <= own_seg[:, -1]) & (other[:, -1] >= own_seg[:, 0]))
    return (other, touch)


def keep_state(state):
    return state


def forward_attention(queries, query_seg, starts, keys, values):
    scale = HEAD_DIM ** (-0.5)
    batch, rows = (queries.shape[0], queries.shape[1])
    query_heads = heads_of(queries)

    def forward_fold(carry, piece, start):
        key_piece, value_piece = piece

        def visit(state, offset, count):
            other, touch = reaches(starts, query_seg, offset, count)

            def compute(state):
                top, total, accum = state
                key_block = heads_of(lax.dynamic_slice_in_dim(key_piece, offset, count, 1))
                value_block = heads_of(lax.dynamic_slice_in_dim(value_piece, offset, count, 1))
                scores = (
                    jnp.einsum(
                        "bqhd,bkhd->bhqk",
                        query_heads,
                        key_block,
                        preferred_element_type=jnp.float32,
                    )
                    * scale
                )
                mask = (query_seg[:, :, None] == other[:, None, :])[:, None]
                scores = jnp.where(mask, scores, NEG)
                new_top = jnp.maximum(top, jnp.max(scores, axis=-1))
                expd = jnp.where(mask, jnp.exp(scores - new_top[..., None]), 0.0)
                factor = jnp.exp(top - new_top)
                total = total * factor + jnp.sum(expd, axis=-1)
                added = jnp.einsum(
                    "bhqk,bkhd->bqhd",
                    expd.astype(jnp.bfloat16),
                    value_block,
                    preferred_element_type=jnp.float32,
                )
                accum = accum * jnp.transpose(factor, (0, 2, 1))[..., None] + added
                return (new_top, total, accum)

            return lax.cond(touch, compute, keep_state, state)

        return block_loop(key_piece.shape[1], carry, visit)

    init = (
        jnp.full((batch, HEADS, rows), NEG, jnp.float32),
        jnp.zeros((batch, HEADS, rows), jnp.float32),
        jnp.zeros((batch, rows, HEADS, HEAD_DIM), jnp.float32),
    )
    whole = (keys, values)
    top, total, accum = forward_fold(
        init,
        (
            lax.all_gather(keys, "ctx", axis=1, tiled=True),
            lax.all_gather(values, "ctx", axis=1, tiled=True),
        ),
        jnp.int32(0),
    )
    mixed = accum / jnp.transpose(total, (0, 2, 1))[..., None]
    return (mixed, top + jnp.log(total), whole)


def query_gradient(queries, query_seg, starts, keys, values, dmixed, logsum, delta):
    scale = HEAD_DIM ** (-0.5)
    query_heads = heads_of(queries)
    grad_heads = heads_of(dmixed)

    def query_fold(carry, piece, start):
        key_piece, value_piece = piece

        def visit(state, offset, count):
            other, touch = reaches(starts, query_seg, offset, count)

            def compute(state):
                key_block = heads_of(lax.dynamic_slice_in_dim(key_piece, offset, count, 1))
                value_block = heads_of(lax.dynamic_slice_in_dim(value_piece, offset, count, 1))
                scores = (
                    jnp.einsum(
                        "bqhd,bkhd->bhqk",
                        query_heads,
                        key_block,
                        preferred_element_type=jnp.float32,
                    )
                    * scale
                )
                mask = (query_seg[:, :, None] == other[:, None, :])[:, None]
                probs = jnp.where(
                    mask, jnp.exp(jnp.where(mask, scores, NEG) - logsum[..., None]), 0.0
                )
                dprobs = jnp.einsum(
                    "bqhd,bkhd->bhqk", grad_heads, value_block, preferred_element_type=jnp.float32
                )
                dscores = (probs * (dprobs - delta[..., None])).astype(jnp.bfloat16)
                return (
                    state
                    + jnp.einsum(
                        "bhqk,bkhd->bqhd", dscores, key_block, preferred_element_type=jnp.float32
                    )
                    * scale
                )

            return lax.cond(touch, compute, keep_state, state)

        return block_loop(key_piece.shape[1], carry, visit)

    init = jnp.zeros(query_heads.shape, jnp.float32)
    return query_fold(
        init,
        (
            lax.all_gather(keys, "ctx", axis=1, tiled=True),
            lax.all_gather(values, "ctx", axis=1, tiled=True),
        ),
        jnp.int32(0),
    )


def key_gradient(keys, values, key_seg, starts, queries, dmixed, logsum, delta):
    scale = HEAD_DIM ** (-0.5)
    key_heads = heads_of(keys)
    value_heads = heads_of(values)
    every_top, every_delta = (
        lax.all_gather(logsum, "ctx", axis=2, tiled=True),
        lax.all_gather(delta, "ctx", axis=2, tiled=True),
    )

    def key_fold(carry, piece, start):
        query_piece, grad_piece = piece

        def visit(state, offset, count):
            other, touch = reaches(starts, key_seg, offset, count)

            def compute(state):
                dkeys, dvalues = state
                query_block = heads_of(lax.dynamic_slice_in_dim(query_piece, offset, count, 1))
                grad_block = heads_of(lax.dynamic_slice_in_dim(grad_piece, offset, count, 1))
                top_block = lax.dynamic_slice_in_dim(every_top, offset, count, 2)
                delta_block = lax.dynamic_slice_in_dim(every_delta, offset, count, 2)
                scores = (
                    jnp.einsum(
                        "bqhd,bkhd->bhqk",
                        query_block,
                        key_heads,
                        preferred_element_type=jnp.float32,
                    )
                    * scale
                )
                mask = (other[:, :, None] == key_seg[:, None, :])[:, None]
                probs = jnp.where(
                    mask, jnp.exp(jnp.where(mask, scores, NEG) - top_block[..., None]), 0.0
                )
                dvalues = dvalues + jnp.einsum(
                    "bhqk,bqhd->bkhd",
                    probs.astype(jnp.bfloat16),
                    grad_block,
                    preferred_element_type=jnp.float32,
                )
                dprobs = jnp.einsum(
                    "bqhd,bkhd->bhqk", grad_block, value_heads, preferred_element_type=jnp.float32
                )
                dscores = (probs * (dprobs - delta_block[..., None])).astype(jnp.bfloat16)
                dkeys = (
                    dkeys
                    + jnp.einsum(
                        "bhqk,bqhd->bkhd", dscores, query_block, preferred_element_type=jnp.float32
                    )
                    * scale
                )
                return (dkeys, dvalues)

            return lax.cond(touch, compute, keep_state, state)

        return block_loop(query_piece.shape[1], carry, visit)

    empty = jnp.zeros(key_heads.shape, jnp.float32)
    return key_fold(
        (empty, empty),
        (
            lax.all_gather(queries, "ctx", axis=1, tiled=True),
            lax.all_gather(dmixed, "ctx", axis=1, tiled=True),
        ),
        jnp.int32(0),
    )


def forward_pass(tokens, starts, weights, base):
    (
        query_weight,
        query_bias,
        key_weight,
        value_weight,
        value_bias,
        out_weight,
        out_bias,
        first_gain,
        first_shift,
        inner_weight,
        inner_bias,
        outer_weight,
        outer_bias,
        second_gain,
        second_shift,
    ) = weights
    rows = tokens.shape[1]
    positions = base + jnp.arange(rows, dtype=jnp.int32)
    query_seg = segment_of(starts, jnp.broadcast_to(positions, (tokens.shape[0], rows)))
    queries = (project(tokens, query_weight) + query_bias.astype(jnp.float32)).astype(jnp.bfloat16)
    keys = project(tokens, key_weight).astype(jnp.bfloat16)
    values = (project(tokens, value_weight) + value_bias.astype(jnp.float32)).astype(jnp.bfloat16)
    mixed, logsum, whole = forward_attention(queries, query_seg, starts, keys, values)
    mixed_low = mixed.reshape(tokens.shape).astype(jnp.bfloat16)
    first_sum = (
        tokens.astype(jnp.float32) + project(mixed_low, out_weight) + out_bias.astype(jnp.float32)
    )
    first = normalize(first_sum, first_gain.astype(jnp.float32), first_shift.astype(jnp.float32))
    first_low = first.astype(jnp.bfloat16)
    inner = project(first_low, inner_weight) + inner_bias.astype(jnp.float32)
    active = gelu(inner).astype(jnp.bfloat16)
    second_sum = first + project(active, outer_weight) + outer_bias.astype(jnp.float32)
    output = normalize(
        second_sum, second_gain.astype(jnp.float32), second_shift.astype(jnp.float32)
    ).astype(jnp.bfloat16)
    saved = (
        tokens,
        query_seg,
        queries,
        keys,
        values,
        mixed,
        logsum,
        mixed_low,
        first_sum,
        first_low,
        inner,
        active,
        second_sum,
        whole,
    )
    return (output, saved)


def backward_pass(saved, starts, weights, cotangent):
    (
        query_weight,
        _,
        key_weight,
        value_weight,
        _,
        out_weight,
        _,
        first_gain,
        first_shift,
        inner_weight,
        _,
        outer_weight,
        _,
        second_gain,
        second_shift,
    ) = weights
    (
        tokens,
        query_seg,
        queries,
        keys,
        values,
        mixed,
        logsum,
        mixed_low,
        first_sum,
        first_low,
        inner,
        active,
        second_sum,
        _,
    ) = saved
    unused, second_back = jax.vjp(
        normalize, second_sum, second_gain.astype(jnp.float32), second_shift.astype(jnp.float32)
    )
    dsecond, dgain_second, dshift_second = second_back(cotangent.astype(jnp.float32))
    douter = dsecond.astype(jnp.bfloat16)
    dactive = project_back(douter, outer_weight)
    unused, gelu_back = jax.vjp(gelu, inner)
    dinner = gelu_back(dactive)[0].astype(jnp.bfloat16)
    dfirst = dsecond + project_back(dinner, inner_weight)
    unused, first_back = jax.vjp(
        normalize, first_sum, first_gain.astype(jnp.float32), first_shift.astype(jnp.float32)
    )
    dfirst_sum, dgain_first, dshift_first = first_back(dfirst)
    dbranch = dfirst_sum.astype(jnp.bfloat16)
    dmixed = project_back(dbranch, out_weight).astype(jnp.bfloat16)
    delta = jnp.einsum("bqhd,bqhd->bhq", heads_of(dmixed).astype(jnp.float32), mixed)
    dqueries = query_gradient(queries, query_seg, starts, keys, values, dmixed, logsum, delta)
    dkeys, dvalues = key_gradient(keys, values, query_seg, starts, queries, dmixed, logsum, delta)
    dqueries = dqueries.reshape(tokens.shape).astype(jnp.bfloat16)
    dkeys = dkeys.reshape(tokens.shape).astype(jnp.bfloat16)
    dvalues = dvalues.reshape(tokens.shape).astype(jnp.bfloat16)
    tokens_grad = (
        dfirst_sum
        + project_back(dqueries, query_weight)
        + project_back(dkeys, key_weight)
        + project_back(dvalues, value_weight)
    )
    sums = (
        outer_sum(tokens, dqueries),
        row_sum(dqueries),
        outer_sum(tokens, dkeys),
        outer_sum(tokens, dvalues),
        row_sum(dvalues),
        outer_sum(mixed_low, dbranch),
        row_sum(dbranch),
        dgain_first,
        dshift_first,
        outer_sum(first_low, dinner),
        row_sum(dinner),
        outer_sum(active, douter),
        row_sum(douter),
        dgain_second,
        dshift_second,
    )
    return (tokens_grad, sums)


def general_device(
    tokens,
    doc_lengths,
    query_weight,
    query_bias,
    key_weight,
    value_weight,
    value_bias,
    out_weight,
    out_bias,
    first_gain,
    first_shift,
    inner_weight,
    inner_bias,
    outer_weight,
    outer_bias,
    second_gain,
    second_shift,
    cotangent,
):
    params = (
        query_weight,
        query_bias,
        key_weight,
        value_weight,
        value_bias,
        out_weight,
        out_bias,
        first_gain,
        first_shift,
        inner_weight,
        inner_bias,
        outer_weight,
        outer_bias,
        second_gain,
        second_shift,
    )
    rows = tokens.shape[2]
    base = lax.axis_index("ctx") * rows
    lengths = doc_lengths[:, 0]
    starts = jnp.cumsum(lengths, axis=-1) - lengths
    outputs = []
    token_parts = []
    sums = None
    for index in range(tokens.shape[0]):
        weights = (
            lax.all_gather(params[0], "wt", axis=0, tiled=True),
            lax.all_gather(params[1], "wt", axis=0, tiled=True),
            lax.all_gather(params[2], "wt", axis=0, tiled=True),
            lax.all_gather(params[3], "wt", axis=0, tiled=True),
            lax.all_gather(params[4], "wt", axis=0, tiled=True),
            lax.all_gather(params[5], "wt", axis=0, tiled=True),
            lax.all_gather(params[6], "wt", axis=0, tiled=True),
            lax.all_gather(params[7], "wt", axis=0, tiled=True),
            lax.all_gather(params[8], "wt", axis=0, tiled=True),
            lax.all_gather(params[9], "wt", axis=0, tiled=True),
            lax.all_gather(params[10], "wt", axis=0, tiled=True),
            lax.all_gather(params[11], "wt", axis=0, tiled=True),
            lax.all_gather(params[12], "wt", axis=0, tiled=True),
            lax.all_gather(params[13], "wt", axis=0, tiled=True),
            lax.all_gather(params[14], "wt", axis=0, tiled=True),
        )
        part_out, saved = forward_pass(
            tokens[index : index + 1, 0], starts[index : index + 1], weights, base
        )
        again = (
            lax.all_gather(params[0], "wt", axis=0, tiled=True),
            lax.all_gather(params[1], "wt", axis=0, tiled=True),
            lax.all_gather(params[2], "wt", axis=0, tiled=True),
            lax.all_gather(params[3], "wt", axis=0, tiled=True),
            lax.all_gather(params[4], "wt", axis=0, tiled=True),
            lax.all_gather(params[5], "wt", axis=0, tiled=True),
            lax.all_gather(params[6], "wt", axis=0, tiled=True),
            lax.all_gather(params[7], "wt", axis=0, tiled=True),
            lax.all_gather(params[8], "wt", axis=0, tiled=True),
            lax.all_gather(params[9], "wt", axis=0, tiled=True),
            lax.all_gather(params[10], "wt", axis=0, tiled=True),
            lax.all_gather(params[11], "wt", axis=0, tiled=True),
            lax.all_gather(params[12], "wt", axis=0, tiled=True),
            lax.all_gather(params[13], "wt", axis=0, tiled=True),
            lax.all_gather(params[14], "wt", axis=0, tiled=True),
        )
        part_grad, part_sums = backward_pass(
            saved, starts[index : index + 1], again, cotangent[index : index + 1, 0]
        )
        outputs.append(part_out)
        token_parts.append(part_grad)
        sums = part_sums if sums is None else jax.tree.map(jnp.add, sums, part_sums)
    output = jnp.concatenate(outputs, axis=0)
    tokens_grad = jnp.concatenate(token_parts, axis=0)
    shards = jax.tree.map(
        lambda part: part.astype(jnp.float32),
        lax.psum_scatter(for_sending(sums), "wt", scatter_dimension=0, tiled=True),
    )
    totals = lax.psum(shards, "ctx")
    return (output[:, None], tokens_grad[:, None]) + tuple(totals)


def flip(value, bits):
    return lax.ppermute(value, "ctx", [(i, i ^ bits) for i in range(8)])


def turn(value, step):
    return lax.ppermute(value, "wt", [(i, (i - step) % 4) for i in range(4)])


def pick(value, index, axis=0):
    return lax.dynamic_index_in_dim(value, index, axis, keepdims=False)


def pair(own, other, bit, axis=0):
    return jnp.where(bit == 0, jnp.stack([own, other], axis), jnp.stack([other, own], axis))


def short(value):
    return value.astype(jnp.bfloat16)


def wide(value):
    return value.astype(jnp.float32)


def dot(left, right):
    return jnp.dot(left, right, preferred_element_type=jnp.float32)


def dot_back(left, right):
    return lax.dot_general(
        left, right, (((1,), (1,)), ((), ())), preferred_element_type=jnp.float32
    )


def dot_sum(left, right):
    return lax.dot_general(
        left, right, (((0,), (0,)), ((), ())), preferred_element_type=jnp.float32
    )


def norm_parts(rows):
    mean = jnp.mean(rows, axis=-1, keepdims=True)
    centered = rows - mean
    spread = jnp.mean(centered * centered, axis=-1, keepdims=True)
    root = lax.rsqrt(spread + EPS)
    return centered * root, root


def norm_back(upstream, normed, root, gain):
    grad = upstream * gain
    mean = jnp.mean(grad, axis=-1, keepdims=True)
    along = jnp.mean(grad * normed, axis=-1, keepdims=True)
    return root * (grad - mean - normed * along)


def gelu_slope(inner):
    bell = jnp.exp(-0.5 * inner * inner) * (1.0 / math.sqrt(2.0 * math.pi))
    return 0.5 * (1.0 + lax.erf(inner * ROOT_HALF)) + inner * bell


def run(kernel, outs, args, scratch=(), scalars=()):
    shapes = tuple(jax.ShapeDtypeStruct(shape, dtype) for shape, dtype in outs)
    spaces = [pltpu.SMEM] * len(scalars) + [pltpu.VMEM] * len(args)
    return pl.pallas_call(
        kernel,
        out_shape=shapes,
        in_specs=[pl.BlockSpec(memory_space=space) for space in spaces],
        scratch_shapes=list(scratch),
    )(*scalars, *args)


BF = jnp.bfloat16
F32 = jnp.float32


def where_am_i():
    ctx, own = lax.axis_index("ctx"), lax.axis_index("wt")
    return ctx & 1, (ctx >> 1) & 3, ctx & 3, own


def some_rows(start, count):
    return pl.ds(pl.multiple_of(start, 16), count)


def prepare_kernel(wq, wk, wv, wo, wi, wo2, vec, heads_own, heads_send, w2_send, inner_half, outer_half):
    core, quarter, group, _ = where_am_i()
    shard, dim = wq.shape
    width, half = dim // 4, wo2.shape[0] // 2
    for index in range(4):

        @pl.when(group == index)
        def _():
            for slot, ref in enumerate((wq, wk, wv)):
                heads_own[:, slot * width : (slot + 1) * width] = ref[
                    :, index * width : (index + 1) * width
                ]

    for index in range(2):

        @pl.when(core == index)
        def _():
            for block in range(4):
                at = block * 2 * half + index * half
                inner_half[:, block * half : (block + 1) * half] = wi[:, at : at + half]
            outer_half[...] = wo2[index * half : (index + 1) * half, :]

    part = shard // 2
    heads_send[0:part, :] = heads_own[some_rows((quarter >> 1) * part, part), :]
    heads_send[part:, 0:width] = vec[...]
    heads_send[part:, width:] = jnp.zeros((16, 2 * width), BF)
    part = shard // 4
    rows = some_rows(quarter * part, part)
    w2_send[0:part, :] = inner_half[rows, 0:dim]
    w2_send[part : 2 * part, :] = inner_half[rows, dim:]
    step = half // 4
    w2_send[2 * part : 2 * part + step, :] = outer_half[some_rows(quarter * step, step), :]
    w2_send[2 * part + step :, :] = wo[rows, :]


CHUNK = 128
ALL_KEYS = (8,)
WINDOWS = (4, 6, 8)


def chunk_of(ctx, index):
    return ctx ^ ((index >> 2) | (index & 2) | ((index & 1) << 2))


def some_chunks(start, count):
    return pl.ds(pl.multiple_of(start * CHUNK, CHUNK), count * CHUNK)


def over_window(bounds, block, windows, visit):
    if len(windows) == 1:
        visit(pl.ds(0, windows[0] * CHUNK))
        return
    low, count = bounds[0, block], bounds[1, block]
    least = 0
    for size in windows:

        @pl.when((count > least) & (count <= size))
        def _(size=size):
            visit(some_chunks(jnp.minimum(low, windows[-1] - size), size))

        least = size


def attend_rows(qkv, seg_col, seg_row, far, outs, logsum, mixed):
    core, quarter, _, _ = where_am_i()
    scale = HEAD_DIM ** (-0.5)
    group = qkv.shape[0] // 3

    def step(side, carry):
        block = 2 * side + ((quarter & 1) ^ far)
        rows = some_chunks(2 * block, 2)
        here = some_chunks(2 * side, 2)

        def visit(keys):
            mask = seg_col[rows, :] == seg_row[:, keys]
            sums = []
            for head in range(group):
                scores = dot_back(qkv[head, rows, :], qkv[group + head, keys, :])
                scores = jnp.where(mask, scores * scale, NEG)
                top = jnp.max(scores, axis=-1, keepdims=True)
                expd = jnp.exp(scores - top)
                total = jnp.sum(expd, axis=-1, keepdims=True)
                probs = short(expd * (1.0 / total))
                mixed[here, head * HEAD_DIM : (head + 1) * HEAD_DIM] = short(
                    dot(probs, qkv[2 * group + head, keys, :])
                )
                sums.append(top + jnp.log(total))
            logsum[here, :] = jnp.concatenate(
                sums + [jnp.zeros_like(sums[0])] * (128 - group), axis=1
            )

        over_window(None, block, ALL_KEYS, visit)
        return carry

    lax.fori_loop(0, 2, step, 0)
    y = quarter >> 1
    for index, out in enumerate(outs):
        for side in range(2):
            chunk = 2 * (y ^ side) + (core ^ index)
            out[side * CHUNK : (side + 1) * CHUNK, :] = mixed[some_chunks(chunk, 1), :]


def attend_near_kernel(
    mine, other, far, heads_own, g1, g2, g3, h1, h2, h3, bias, seg_col, seg_row,
    qkv, m0, m1, logsum, weight, mixed,
):
    _, quarter, _, own = where_am_i()
    ctx = lax.axis_index("ctx")
    shard = heads_own.shape[0]
    part = shard // 2
    y = quarter >> 1
    weight[some_rows(own * shard, shard), :] = heads_own[...]
    for step, near_half, far_half in ((1, g1, h1), (2, g2, h2), (3, g3, h3)):
        at = ((own + step) & 3) * shard
        weight[some_rows(at + part * y, part), :] = near_half[0:part, :]
        weight[some_rows(at + part * (1 - y), part), :] = far_half[0:part, :]
    index = 0
    for source in (mine, other, far):
        for first in range(0, source.shape[0], 2 * CHUNK):
            low = short(dot(source[first : first + 2 * CHUNK, :], weight[...]) + bias[...])
            for half in range(2):
                at = pl.multiple_of(chunk_of(ctx, index) * CHUNK, CHUNK)
                for slot in range(qkv.shape[0]):
                    qkv[slot, pl.ds(at, CHUNK), :] = low[
                        half * CHUNK : (half + 1) * CHUNK,
                        slot * HEAD_DIM : (slot + 1) * HEAD_DIM,
                    ]
                index += 1
    attend_rows(qkv, seg_col, seg_row, 0, (m0, m1), logsum, mixed)


def attend_far_kernel(qkv, seg_col, seg_row, m2, m3, logsum, mixed):
    attend_rows(qkv, seg_col, seg_row, 1, (m2, m3), logsum, mixed)


def project_kernel(m0, m1, m2, m3, mine, wo, vec, *refs):
    pieces, (first_sum, first_low, out_full) = refs[:12], refs[12:]
    _, quarter, group, own = where_am_i()
    shard = wo.shape[0]
    part = shard // 4
    out_full[some_rows(own * shard, shard), :] = wo[...]
    for index, piece in enumerate(pieces):
        at = ((own + 1 + index // 4) & 3) * shard + part * (quarter ^ (index % 4))
        out_full[some_rows(at, part), :] = piece[piece.shape[0] - part :, :]
    total = wide(mine[...]) + vec[2:3, :]
    for code, ref in enumerate((m0, m1, m2, m3)):
        total += dot(ref[...], out_full[some_rows((group ^ code) * shard, shard), :])
    first_sum[...] = total
    first_low[...] = short(norm_parts(total)[0] * vec[3:4, :] + vec[4:5, :])


def forward_kernel(near, far, inner_half, outer_half, bias, *refs):
    pieces, (keep, send, inner, active, wi_full, wo2_full) = refs[:12], refs[12:]
    _, quarter, _, own = where_am_i()
    shard, half = inner_half.shape[0], outer_half.shape[0]
    dim = keep.shape[1]
    part, step = shard // 4, half // 4
    wi_full[some_rows(own * shard, shard), :] = inner_half[...]
    wo2_full[some_rows(own * half, half), :] = outer_half[...]
    for index, piece in enumerate(pieces):
        row, spot = (own + 1 + index // 4) & 3, quarter ^ (index % 4)
        rows = some_rows(row * shard + part * spot, part)
        wi_full[rows, 0:dim] = piece[0:part, :]
        wi_full[rows, dim:] = piece[part : 2 * part, :]
        wo2_full[some_rows(row * half + step * spot, step), :] = piece[
            2 * part : 2 * part + step, :
        ]
    count = near.shape[0]
    chunk = 512
    for index, (source, out) in enumerate(((far, send), (near, keep))):
        at = (1 - index) * count
        total = None
        for lane in range(0, inner.shape[1], chunk):
            lanes = slice(lane, lane + chunk)
            value = dot(source[...], wi_full[:, lanes]) + bias[:, lanes]
            inner[at : at + count, lanes] = value
            low = short(gelu(value))
            active[at : at + count, lanes] = low
            added = dot(low, wo2_full[lanes, :])
            total = added if total is None else total + added
        out[...] = total


def turnaround_kernel(first_sum, keep, got, vec, cot0, cot1, out0, out1, dsecond, douter, sums):
    rows = cot0.shape[0]
    first = norm_parts(first_sum[...])[0] * vec[3:4, :] + vec[4:5, :]
    normed, root = norm_parts(first + vec[5:6, :] + keep[...] + got[...])
    output = short(normed * vec[6:7, :] + vec[7:8, :])
    out0[...] = output[:rows]
    out1[...] = output[rows:]
    upstream = jnp.concatenate([wide(cot0[...]), wide(cot1[...])])
    back = norm_back(upstream, normed, root, vec[6:7, :])
    low = short(back)
    dsecond[...] = back
    douter[...] = low
    sums[0:1, :] = jnp.sum(wide(low), axis=0, keepdims=True)
    sums[1:2, :] = jnp.sum(upstream * normed, axis=0, keepdims=True)
    sums[2:3, :] = jnp.sum(upstream, axis=0, keepdims=True)
    sums[3:, :] = jnp.zeros_like(sums[3:, :])


def backward_kernel(near, far, inner, wi_full, wo2_full, keep, send, dinner, sums):
    count, dim = near.shape
    chunk = 512
    for index, (source, out) in enumerate(((far, send), (near, keep))):
        at = (1 - index) * count
        total = None
        for lane in range(0, inner.shape[1], chunk):
            lanes = slice(lane, lane + chunk)
            slope = gelu_slope(inner[at : at + count, lanes])
            low = short(dot_back(source[...], wo2_full[lanes, :]) * slope)
            dinner[at : at + count, lanes] = low
            added = dot_back(low, wi_full[:, lanes])
            total = added if total is None else total + added
        out[...] = total
    total = jnp.sum(wide(dinner[...]), axis=0, keepdims=True)
    sums[0:1, :] = total[:, :dim]
    sums[1:2, :] = total[:, dim:]
    sums[2:, :] = jnp.zeros_like(sums[2:, :])


def weights_kernel(lane, first0, first1, douter0, douter1, dinner, active, ak, az, bk, bz, left, right):
    _, quarter, _, _ = where_am_i()
    x, y = quarter & 1, quarter >> 1
    count = first0.shape[0]
    part, step = first0.shape[1] // 16, active.shape[1] // 16
    lanes = slice(lane * left.shape[1], (lane + 1) * left.shape[1])
    left[...] = short(
        dot_sum(first0[...], dinner[:count, lanes]) + dot_sum(first1[...], dinner[count:, lanes])
    )
    for block in range(8):
        rows = slice(block * part, (block + 1) * part)
        ak[rows, :] = left[some_rows((2 * block + x) * part, part), :]
        az[rows, :] = left[some_rows((2 * block + 1 - x) * part, part), :]
    lanes = slice(lane * right.shape[1], (lane + 1) * right.shape[1])
    right[...] = short(
        dot_sum(active[:count], douter0[:, lanes]) + dot_sum(active[count:], douter1[:, lanes])
    )
    for block in range(8):
        row, side = block // 2, block % 2
        rows = slice(block * step, (block + 1) * step)
        bk[rows, :] = right[some_rows((4 * row + 2 * y + side) * step, step), :]
        bz[rows, :] = right[some_rows((4 * row + 2 * (1 - y) + side) * step, step), :]


def branch_kernel(first_sum, dsecond, keep, got, vec, out_full, dfirst_sum, dbranch, d0, d1, d2, d3, sums):
    _, _, group, _ = where_am_i()
    shard = d0.shape[1]
    normed, root = norm_parts(first_sum[...])
    dfirst = dsecond[...] + keep[...] + got[...]
    back = norm_back(dfirst, normed, root, vec[3:4, :])
    low = short(back)
    dfirst_sum[...] = back
    dbranch[...] = low
    for code, ref in enumerate((d0, d1, d2, d3)):
        ref[...] = short(dot_back(low, out_full[some_rows((group ^ code) * shard, shard), :]))
    sums[0:1, :] = jnp.sum(wide(low), axis=0, keepdims=True)
    sums[1:2, :] = jnp.sum(dfirst * normed, axis=0, keepdims=True)
    sums[2:3, :] = jnp.sum(dfirst, axis=0, keepdims=True)
    sums[3:, :] = jnp.zeros_like(sums[3:, :])


def out_weight_kernel(m0, m1, m2, m3, dbranch, sums1, sums2, sums3, ck, cz, whole):
    core, _, group, _ = where_am_i()
    shard, dim = m0.shape[1], dbranch.shape[1]
    half = dim // 2
    for code, ref in enumerate((m0, m1, m2, m3)):
        whole[some_rows((group ^ code) * shard, shard), :] = short(
            dot_sum(ref[...], dbranch[...])
        )
    for side in range(2):

        @pl.when(core == side)
        def _():
            for ref, which in ((ck, side), (cz, 1 - side)):
                ref[0:dim, :] = whole[:, which * half : (which + 1) * half]

    rows = short(
        jnp.concatenate([sums1[0:3, :], sums2[0:3, :], sums3[0:2, :], jnp.zeros_like(sums1[...])])
    )
    for ref in (ck, cz):
        ref[dim : dim + 16, :] = rows[:, :half]
        ref[dim + 16 :, :] = rows[:, half:]


def out_split_kernel(packed, got, ck, cz):
    core, quarter, _, _ = where_am_i()
    x = quarter & 1
    dim = packed.shape[0] - 32
    part = dim // 16
    for block in range(8):
        rows = slice(block * part, (block + 1) * part)
        for ref, side in ((ck, x), (cz, 1 - x)):
            take = some_rows((2 * block + side) * part, part)
            ref[rows, :] = short(wide(packed[take, :]) + wide(got[take, :]))
    for lanes in range(2):
        at = dim + 16 * lanes
        mine, other = wide(packed[at : at + 16, :]), wide(got[at : at + 16, :])
        low = jnp.where(core == 0, mine, other)[6:8]
        high = jnp.where(core == 0, other, mine)[6:8]
        rows = jnp.concatenate([(mine + other)[0:6], low, high, jnp.zeros_like(mine[0:6])])
        at = 8 * part + 16 * lanes
        for ref in (ck, cz):
            ref[at : at + 16, :] = short(rows)


def reduce_rows(keep, got, outs, bit):
    size = keep.shape[0] // 8
    size -= size % 16
    for block in range(4):
        for out, side in zip(outs, (bit, 1 - bit)):
            take = some_rows((2 * block + side) * size, size)
            out[block * size : (block + 1) * size, :] = short(
                wide(keep[take, :]) + wide(got[take, :])
            )
    if keep.shape[0] > 8 * size:
        for out in outs:
            out[4 * size :, :] = short(wide(keep[8 * size :, :]) + wide(got[8 * size :, :]))


def reduce_kernel(ak, ar, bk, br, a2k, a2z, b2k, b2z):
    _, quarter, _, _ = where_am_i()
    reduce_rows(ak, ar, (a2k, a2z), quarter >> 1)
    reduce_rows(bk, br, (b2k, b2z), quarter & 1)


def reduce_out_kernel(ck, cr, c2k, c2z):
    _, quarter, _, _ = where_am_i()
    reduce_rows(ck, cr, (c2k, c2z), quarter >> 1)


def owners_kernel(*refs):
    inputs, outs = refs[:-4], refs[-4:]
    _, _, _, own = where_am_i()
    ak, ar, bk, br = inputs[:4]
    half = bk.shape[1]
    part = ak.shape[0] // 4
    for index, out in enumerate(outs):
        row = (own - index) & 3
        rows = some_rows(row * part, part)
        out[0:part, :] = (wide(ak[rows, :]) + wide(ar[rows, :])).astype(out.dtype)
        for side in range(2):
            rows = some_rows((2 * row + side) * part, part)
            out[part : 2 * part, side * half : (side + 1) * half] = (
                wide(bk[rows, :]) + wide(br[rows, :])
            ).astype(out.dtype)
        if len(inputs) > 4:
            ck, cr = inputs[4:]
            at = 2 * part
            rows = some_rows(row * part, part)
            out[at:, 0:half] = (wide(ck[rows, :]) + wide(cr[rows, :])).astype(out.dtype)
            tail = wide(ck[4 * part :, :]) + wide(cr[4 * part :, :])
            out[at : at + 32, half:] = tail.astype(out.dtype)
            out[at + 32 :, half:] = jnp.zeros((part - 32, half), out.dtype)


def total_kernel(mine, *refs):
    total = wide(mine[...])
    for ref in refs[:-1]:
        total += wide(ref[...])
    refs[-1][...] = short(total)


def finish_kernel(*refs):
    pieces, (dwi, dwo2, dwo, small) = refs[:16], refs[16:]
    core, quarter, _, _ = where_am_i()
    part, half = dwi.shape[0] // 4, dwi.shape[1] // 8
    for side in range(2):

        @pl.when(core == side)
        def _():
            for index, piece in enumerate(pieces):
                lane, index = index // 8, index % 8
                spot = quarter ^ (index % 4)
                which = side if index < 4 else 1 - side
                rows = some_rows(spot * part, part)
                for block in range(2):
                    at = (2 * lane + block) * 2 * half + which * half
                    dwi[rows, at : at + half] = wide(piece[0:part, block * half : (block + 1) * half])
                    at = which * half + spot * 2 * part + block * part
                    dwo2[some_rows(at, part), lane * half : (lane + 1) * half] = wide(
                        piece[part : 2 * part, block * half : (block + 1) * half]
                    )
                if lane == 1:
                    dwo[rows, which * half : (which + 1) * half] = wide(piece[2 * part :, 0:half])

    last = pieces[8]
    small[:, 0:half] = wide(last[2 * part : 2 * part + 16, half:])
    small[:, half:] = wide(last[2 * part + 16 : 2 * part + 32, half:])


def attend_back_kernel(
    bounds, qkv, logsum0, logsum1, seg_col, seg_row, p0, p1, p2, p3, mine, other, far, weight,
    h0, h1, h2, h3, keep, send, grads, dkeys, dvalues, dweight, dmixed, logsum, whole,
):
    _, quarter, _, own = where_am_i()
    ctx = lax.axis_index("ctx")
    x = quarter & 1
    scale = HEAD_DIM ** (-0.5)
    group = qkv.shape[0] // 3
    width = group * HEAD_DIM
    block = p0.shape[0]
    dkeys[...] = jnp.zeros_like(dkeys)
    dvalues[...] = jnp.zeros_like(dvalues)
    for index, part in enumerate((p0, p2, p1, p3)):
        for side in range(2):
            chunk = chunk_of(ctx, 2 * index + side)
            dmixed[some_chunks(chunk, 1), :] = part[side * CHUNK : (side + 1) * CHUNK, :]
    for side in range(2):
        rows = slice(2 * side * CHUNK, 2 * (side + 1) * CHUNK)
        logsum[some_chunks(2 * (2 * side + x), 2), :] = logsum0[rows, :]
        logsum[some_chunks(2 * (2 * side + 1 - x), 2), :] = logsum1[rows, :]

    def step(index, carry):
        rows = some_chunks(2 * index, 2)

        def visit(window):
            mask = seg_col[rows, :] == seg_row[:, window]
            for head in range(group):
                lanes = slice(head * HEAD_DIM, (head + 1) * HEAD_DIM)
                query = qkv[head, rows, :]
                grad = dmixed[rows, lanes]
                keys = qkv[group + head, window, :]
                scores = jnp.where(mask, dot_back(query, keys) * scale, NEG)
                probs = jnp.exp(scores - logsum[rows, head : head + 1])
                dprobs = dot_back(grad, qkv[2 * group + head, window, :])
                delta = jnp.sum(probs * dprobs, axis=-1, keepdims=True)
                dscores = short(probs * (dprobs - delta))
                whole[rows, lanes] = short(dot(dscores, keys) * scale)
                dkeys[head, window, :] += dot_sum(dscores, query)
                dvalues[head, window, :] += dot_sum(short(probs), grad)

        over_window(bounds, index, WINDOWS, visit)
        return carry

    lax.fori_loop(0, 4, step, 0)
    for head in range(group):
        at = width + head * HEAD_DIM
        whole[:, at : at + HEAD_DIM] = short(dkeys[head] * scale)
        whole[:, at + width : at + width + HEAD_DIM] = short(dvalues[head])
    for index in range(8):
        grads[index * CHUNK : (index + 1) * CHUNK, :] = whole[
            some_chunks(chunk_of(ctx, index), 1), :
        ]
    rows = 2 * block
    dweight[...] = (
        dot_sum(mine[...], grads[:block])
        + dot_sum(other[...], grads[block:rows])
        + dot_sum(far[...], grads[rows:])
    )
    sums = jnp.sum(wide(grads[...]), axis=0, keepdims=True)
    tail = jnp.concatenate([sums, jnp.zeros((15, sums.shape[1]), F32)])
    for index, out in enumerate((h0, h1, h2, h3)):
        take = pl.ds(pl.multiple_of(((own - index) & 3) * width, 16), width)
        out[0:width, :] = dweight[take, :].astype(out.dtype)
        out[width:, :] = tail.astype(out.dtype)
    keep[...] = dot_back(grads[:rows], weight[...])
    send[...] = short(dot_back(grads[rows:], weight[...]))


def merge_kernel(keep, got, base, near, far):
    total = keep[...] + wide(got[...])
    count = near.shape[0]
    near[...] = total[:count] + base[...]
    far[...] = short(total[count:])


def heads_kernel(s0, s1, s2, s3, dq, dk, dv, bias):
    _, _, group, own = where_am_i()
    shard = dq.shape[0]
    for index in range(4):

        @pl.when(group == index)
        def _():
            for code, ref in enumerate((s0, s1, s2, s3)):
                at = (index ^ code) * shard
                for slot, out in enumerate((dq, dk, dv)):
                    out[:, at : at + shard] = wide(
                        ref[0:shard, slot * shard : (slot + 1) * shard]
                    )

                @pl.when(own == index ^ code)
                def _():
                    bias[...] = wide(ref[shard:, :])


def plane_steps(
    tokens,
    doc_lengths,
    query_weight,
    query_bias,
    key_weight,
    value_weight,
    value_bias,
    out_weight,
    out_bias,
    first_gain,
    first_shift,
    inner_weight,
    inner_bias,
    outer_weight,
    outer_bias,
    second_gain,
    second_shift,
    cotangent,
):
    ctx, own = lax.axis_index("ctx"), lax.axis_index("wt")
    core, y, group = ctx & 1, ctx >> 2, ctx & 3
    rows, dim = tokens.shape[2], tokens.shape[3]
    shard = query_weight.shape[0]
    hidden = outer_weight.shape[0]
    half = hidden // 2
    count = 2 * rows

    mine = jnp.concatenate([pick(tokens[:, 0], y), flip(pick(tokens[:, 0], 1 - y), 4)])
    other = flip(mine, 2)
    far = flip(jnp.concatenate([mine, other]), 1)

    vector_list = (
        query_bias,
        value_bias,
        out_bias,
        first_gain,
        first_shift,
        outer_bias,
        second_gain,
        second_shift,
        *[inner_bias[at : at + shard] for at in range(0, 4 * shard, shard)],
    )
    line = lax.broadcasted_iota(jnp.int32, (16, shard), 0)
    vec = jnp.zeros((16, shard), BF)
    for index, value in enumerate(vector_list):
        vec = jnp.where(line == index, value[None, :], vec)
    heads_own, heads_send, w2_send, inner_half, outer_half = run(
        prepare_kernel,
        [
            ((shard, 3 * shard), BF),
            ((shard // 2 + 16, 3 * shard), BF),
            ((shard // 4 * 3 + half // 4, dim), BF),
            ((shard, 4 * half), BF),
            ((half, dim), BF),
        ],
        (query_weight, key_weight, value_weight, out_weight, inner_weight, outer_weight, vec),
    )
    got = [turn(heads_send, step) for step in (1, 2, 3)]
    gone = [flip(value, 4) for value in got]
    pieces = []
    for step in (1, 2, 3):
        piece = turn(w2_send, step)
        pieces += [piece] + [flip(piece, bits) for bits in (2, 4, 6)]

    at = shard // 2
    rel = jnp.stack([vec] + [value[at:, :shard] for value in got])
    vectors = wide(lax.dynamic_slice_in_dim(jnp.concatenate([rel, rel]), (4 - own) % 4, 4))
    mine_b = pick(vectors, group)
    heads_bias = jnp.concatenate([mine_b[0], jnp.zeros_like(mine_b[0]), mine_b[1]])[None]
    inner_b = pick(vectors[:, 8:12].reshape(4, 2, half), core, 1).reshape(1, 4 * half)
    vectors = jnp.swapaxes(vectors[:, :8], 0, 1).reshape(8, dim)

    lengths = pick(doc_lengths[:, 0], y)
    starts = jnp.cumsum(lengths) - lengths
    total = 8 * rows
    positions = jnp.arange(total, dtype=jnp.int32)
    seg = jnp.sum((starts[None, :] <= positions[:, None]).astype(jnp.int32), axis=-1) - 1
    segs = (seg[:, None], seg[None, :])
    first = jnp.arange(4, dtype=jnp.int32)[:, None] * (2 * CHUNK)
    low = jnp.max(jnp.where(starts[None, :] <= first, starts[None, :], 0), axis=-1) // CHUNK
    ends = jnp.where(starts[None, :] >= first + 2 * CHUNK, starts[None, :], total)
    bounds = jnp.stack([low, (jnp.min(ends, axis=-1) - 1) // CHUNK - low + 1])

    qkv, m0, m1, logsum0, heads_weight = run(
        attend_near_kernel,
        [
            ((9, total, HEAD_DIM), BF),
            ((count, shard), BF),
            ((count, shard), BF),
            ((2 * count, 128), F32),
            ((dim, 3 * shard), BF),
        ],
        (mine, other, far, heads_own, *got, *gone, heads_bias, *segs),
        [pltpu.VMEM((2 * count, shard), BF)],
    )
    m2, m3, logsum1 = run(
        attend_far_kernel,
        [((count, shard), BF), ((count, shard), BF), ((2 * count, 128), F32)],
        (qkv, *segs),
        [pltpu.VMEM((2 * count, shard), BF)],
    )
    mixed = [m0, flip(m1, 1), flip(m2, 2), flip(m3, 3)]

    first_sum, first_low, out_full = run(
        project_kernel,
        [((count, dim), F32), ((count, dim), BF), ((dim, dim), BF)],
        (*mixed, mine, out_weight, vectors, *pieces),
    )
    first_far = flip(first_low, 1)
    keep, send, inner, active, wi_full, wo2_full = run(
        forward_kernel,
        [
            ((count, dim), F32),
            ((count, dim), F32),
            ((2 * count, 4 * half), F32),
            ((2 * count, 4 * half), BF),
            ((dim, 4 * half), BF),
            ((4 * half, dim), BF),
        ],
        (first_low, first_far, inner_half, outer_half, inner_b, *pieces),
    )
    cot = pick(cotangent[:, 0], y), flip(pick(cotangent[:, 0], 1 - y), 4)
    out0, out1, dsecond, douter, sums2 = run(
        turnaround_kernel,
        [
            ((rows, dim), BF),
            ((rows, dim), BF),
            ((count, dim), F32),
            ((count, dim), BF),
            ((8, dim), F32),
        ],
        (first_sum, keep, flip(send, 1), vectors, *cot),
    )
    output = pair(out0, flip(out1, 4), y)

    douter_far = flip(douter, 1)
    keep, send, dinner, sums3 = run(
        backward_kernel,
        [
            ((count, dim), F32),
            ((count, dim), F32),
            ((2 * count, 4 * half), BF),
            ((8, dim), F32),
        ],
        (douter, douter_far, inner, wi_full, wo2_full),
    )
    dfirst_sum, dbranch, d0, d1, d2, d3, sums1 = run(
        branch_kernel,
        [((count, dim), F32), ((count, dim), BF)] + [((count, shard), BF)] * 4 + [((8, dim), F32)],
        (first_sum, dsecond, keep, flip(send, 1), vectors, out_full),
    )
    dmixed = [d0, flip(d1, 1), flip(d2, 2), flip(d3, 3)]

    stages = []
    for lane in range(2):
        ak, az, bk, bz = run(
            functools.partial(weights_kernel, lane),
            [((dim // 2, 2 * half), BF)] * 2 + [((2 * half, dim // 2), BF)] * 2,
            (first_low, first_far, douter, douter_far, dinner, active),
            [pltpu.VMEM((dim, 2 * half), BF), pltpu.VMEM((4 * half, dim // 2), BF)],
        )
        stages.append((ak, flip(az, 2), bk, flip(bz, 4)))
    ck, cz = run(
        out_weight_kernel,
        [((dim + 32, dim // 2), BF)] * 2,
        (*mixed, dbranch, sums1, sums2, sums3),
        [pltpu.VMEM((dim, dim), BF)],
    )
    ck, cz = run(out_split_kernel, [((dim // 2 + 32, dim // 2), BF)] * 2, (ck, flip(cz, 1)))
    cr = flip(cz, 2)

    h0, h1, h2, h3, keep, send = run(
        attend_back_kernel,
        [((shard + 16, 3 * shard), F32)]
        + [((shard + 16, 3 * shard), BF)] * 3
        + [((2 * count, dim), F32), ((2 * count, dim), BF)],
        (qkv, logsum0, logsum1, *segs, *dmixed, mine, other, far, heads_weight),
        [
            pltpu.VMEM((4 * count, 3 * shard), BF),
            pltpu.VMEM((3, 4 * count, HEAD_DIM), F32),
            pltpu.VMEM((3, 4 * count, HEAD_DIM), F32),
            pltpu.VMEM((dim, 3 * shard), F32),
            pltpu.VMEM((total, shard), BF),
            pltpu.VMEM((total, 128), F32),
            pltpu.VMEM((total, 3 * shard), BF),
        ],
        scalars=(bounds,),
    )

    c2k, c2z = run(reduce_out_kernel, [((dim // 4 + 32, dim // 2), BF)] * 2, (ck, cr))
    plane = []
    for lane in range(2):
        a2k, a2z, b2k, b2z = run(
            reduce_kernel,
            [((dim // 4, 2 * half), BF)] * 2 + [((half, dim // 2), BF)] * 2,
            stages[lane],
        )
        last = [a2k, flip(a2z, 4), b2k, flip(b2z, 2)]
        size = shard // 4 * 2
        if lane == 1:
            last += [c2k, flip(c2z, 4)]
            size = shard // 4 * 3
        p0, p1, p2, p3 = run(owners_kernel, [((size, dim), F32)] + [((size, dim), BF)] * 3, last)
        turned = [turn(p, step) for step, p in ((1, p1), (2, p2), (3, p3))]
        (piece,) = run(total_kernel, [((size, dim), BF)], (p0, *turned))
        near = [piece] + [flip(piece, bits) for bits in (2, 4, 6)]
        plane += near + [flip(p, 1) for p in near]
    dinner_w, douter_w, dout_w, small = run(
        finish_kernel,
        [((shard, 8 * half), F32), ((hidden, dim), F32), ((shard, dim), F32), ((16, dim), F32)],
        plane,
    )
    dinner_b = pick(small[6:10].reshape(2, 4, half), own, 1).reshape(hidden)
    small = lax.dynamic_slice_in_dim(small[:6], own * shard, shard, 1)

    (heads,) = run(
        total_kernel, [((shard + 16, 3 * shard), BF)], (h0, turn(h1, 1), turn(h2, 2), turn(h3, 3))
    )
    (heads,) = run(total_kernel, [((shard + 16, 3 * shard), BF)], (heads, flip(heads, 4)))
    dquery_w, dkey_w, dvalue_w, heads_b = run(
        heads_kernel,
        [((shard, dim), F32)] * 3 + [((16, 3 * shard), F32)],
        (heads, flip(heads, 1), flip(heads, 2), flip(heads, 3)),
    )

    near_t, far_t = run(
        merge_kernel, [((count, dim), F32), ((count, dim), BF)], (keep, flip(send, 1), dfirst_sum)
    )
    dtokens = near_t + wide(flip(far_t, 2))
    tokens_grad = pair(dtokens[:rows], wide(flip(short(dtokens[rows:]), 4)), y)

    return (
        output[:, None],
        tokens_grad[:, None],
        dquery_w,
        heads_b[0, :shard],
        dkey_w,
        dvalue_w,
        heads_b[0, 2 * shard :],
        dout_w,
        small[0],
        small[1],
        small[2],
        dinner_w,
        dinner_b,
        douter_w,
        small[3],
        small[4],
        small[5],
    )


def plane_device(*args):
    return plane_steps(*args)


def solution(mesh):
    placed = (
        P(None, "wt", "ctx", None),
        P(None, "wt", None),
        P("wt", None),
        P("wt"),
        P("wt", None),
        P("wt", None),
        P("wt"),
        P("wt", None),
        P("wt"),
        P("wt"),
        P("wt"),
        P("wt", None),
        P("wt"),
        P("wt", None),
        P("wt"),
        P("wt"),
        P("wt"),
        P(None, "wt", "ctx", None),
    )
    fits = mesh.shape["ctx"] == 8 and mesh.shape["wt"] == 4
    return jax.shard_map(
        plane_device if fits else general_device,
        mesh=mesh,
        in_specs=placed,
        out_specs=(
            P(None, "wt", "ctx", None),
            P(None, "wt", "ctx", None),
            P("wt", None),
            P("wt"),
            P("wt", None),
            P("wt", None),
            P("wt"),
            P("wt", None),
            P("wt"),
            P("wt"),
            P("wt"),
            P("wt", None),
            P("wt"),
            P("wt", None),
            P("wt"),
            P("wt"),
            P("wt"),
        ),
        check_vma=False,
    )
```

```python
import math

import jax
import jax.numpy as jnp
from jax import lax
from jax.experimental import pallas as pl
from jax.experimental.pallas import tpu as pltpu
from jax.sharding import PartitionSpec as P


HEADS = 12
HEAD_DIM = 64


EPS = 1e-12
NEG = -1e30
ROOT_HALF = 0.7071067811865476


def for_sending(shard):

    def short(part):
        return part.astype(jnp.bfloat16) if part.dtype == jnp.float32 else part

    return jax.tree.map(short, shard)


def normalize(rows, gain, shift):
    mean = jnp.mean(rows, axis=-1, keepdims=True)
    centered = rows - mean
    spread = jnp.mean(centered * centered, axis=-1, keepdims=True)
    return centered * lax.rsqrt(spread + EPS) * gain + shift


def gelu(inner):
    return 0.5 * inner * (1.0 + lax.erf(inner * ROOT_HALF))


def segment_of(starts, positions):
    found = (starts[:, None, :] <= positions[:, :, None]).astype(jnp.int32)
    return jnp.sum(found, axis=-1) - 1


def project(inputs, weight):
    return jnp.einsum("btd,de->bte", inputs, weight, preferred_element_type=jnp.float32)


def project_back(grads, weight):
    return jnp.einsum("bte,de->btd", grads, weight, preferred_element_type=jnp.float32)


def outer_sum(inputs, grads):
    return jnp.einsum("btd,bte->de", inputs, grads, preferred_element_type=jnp.float32)


def row_sum(grads):
    return jnp.sum(grads.astype(jnp.float32), axis=(0, 1))


def heads_of(array):
    return array.reshape(array.shape[0], array.shape[1], HEADS, HEAD_DIM)


def block_loop(width, carry, visit):
    block = math.gcd(width, 512)

    def step(state, index):
        return (visit(state, index * block, block), None)

    carry, _ = lax.scan(step, carry, jnp.arange(width // block, dtype=jnp.int32))
    return carry


def reaches(starts, own_seg, first, count):
    positions = first + jnp.arange(count, dtype=jnp.int32)
    other = segment_of(starts, jnp.broadcast_to(positions, (starts.shape[0], count)))
    touch = jnp.any((other[:, 0] <= own_seg[:, -1]) & (other[:, -1] >= own_seg[:, 0]))
    return (other, touch)


def keep_state(state):
    return state


def forward_attention(queries, query_seg, starts, keys, values):
    scale = HEAD_DIM ** (-0.5)
    batch, rows = (queries.shape[0], queries.shape[1])
    query_heads = heads_of(queries)

    def forward_fold(carry, piece, start):
        key_piece, value_piece = piece

        def visit(state, offset, count):
            other, touch = reaches(starts, query_seg, offset, count)

            def compute(state):
                top, total, accum = state
                key_block = heads_of(lax.dynamic_slice_in_dim(key_piece, offset, count, 1))
                value_block = heads_of(lax.dynamic_slice_in_dim(value_piece, offset, count, 1))
                scores = (
                    jnp.einsum(
                        "bqhd,bkhd->bhqk",
                        query_heads,
                        key_block,
                        preferred_element_type=jnp.float32,
                    )
                    * scale
                )
                mask = (query_seg[:, :, None] == other[:, None, :])[:, None]
                scores = jnp.where(mask, scores, NEG)
                new_top = jnp.maximum(top, jnp.max(scores, axis=-1))
                expd = jnp.where(mask, jnp.exp(scores - new_top[..., None]), 0.0)
                factor = jnp.exp(top - new_top)
                total = total * factor + jnp.sum(expd, axis=-1)
                added = jnp.einsum(
                    "bhqk,bkhd->bqhd",
                    expd.astype(jnp.bfloat16),
                    value_block,
                    preferred_element_type=jnp.float32,
                )
                accum = accum * jnp.transpose(factor, (0, 2, 1))[..., None] + added
                return (new_top, total, accum)

            return lax.cond(touch, compute, keep_state, state)

        return block_loop(key_piece.shape[1], carry, visit)

    init = (
        jnp.full((batch, HEADS, rows), NEG, jnp.float32),
        jnp.zeros((batch, HEADS, rows), jnp.float32),
        jnp.zeros((batch, rows, HEADS, HEAD_DIM), jnp.float32),
    )
    whole = (keys, values)
    top, total, accum = forward_fold(
        init,
        (
            lax.all_gather(keys, "ctx", axis=1, tiled=True),
            lax.all_gather(values, "ctx", axis=1, tiled=True),
        ),
        jnp.int32(0),
    )
    mixed = accum / jnp.transpose(total, (0, 2, 1))[..., None]
    return (mixed, top + jnp.log(total), whole)


def query_gradient(queries, query_seg, starts, keys, values, dmixed, logsum, delta):
    scale = HEAD_DIM ** (-0.5)
    query_heads = heads_of(queries)
    grad_heads = heads_of(dmixed)

    def query_fold(carry, piece, start):
        key_piece, value_piece = piece

        def visit(state, offset, count):
            other, touch = reaches(starts, query_seg, offset, count)

            def compute(state):
                key_block = heads_of(lax.dynamic_slice_in_dim(key_piece, offset, count, 1))
                value_block = heads_of(lax.dynamic_slice_in_dim(value_piece, offset, count, 1))
                scores = (
                    jnp.einsum(
                        "bqhd,bkhd->bhqk",
                        query_heads,
                        key_block,
                        preferred_element_type=jnp.float32,
                    )
                    * scale
                )
                mask = (query_seg[:, :, None] == other[:, None, :])[:, None]
                probs = jnp.where(
                    mask, jnp.exp(jnp.where(mask, scores, NEG) - logsum[..., None]), 0.0
                )
                dprobs = jnp.einsum(
                    "bqhd,bkhd->bhqk", grad_heads, value_block, preferred_element_type=jnp.float32
                )
                dscores = (probs * (dprobs - delta[..., None])).astype(jnp.bfloat16)
                return (
                    state
                    + jnp.einsum(
                        "bhqk,bkhd->bqhd", dscores, key_block, preferred_element_type=jnp.float32
                    )
                    * scale
                )

            return lax.cond(touch, compute, keep_state, state)

        return block_loop(key_piece.shape[1], carry, visit)

    init = jnp.zeros(query_heads.shape, jnp.float32)
    return query_fold(
        init,
        (
            lax.all_gather(keys, "ctx", axis=1, tiled=True),
            lax.all_gather(values, "ctx", axis=1, tiled=True),
        ),
        jnp.int32(0),
    )


def key_gradient(keys, values, key_seg, starts, queries, dmixed, logsum, delta):
    scale = HEAD_DIM ** (-0.5)
    key_heads = heads_of(keys)
    value_heads = heads_of(values)
    every_top, every_delta = (
        lax.all_gather(logsum, "ctx", axis=2, tiled=True),
        lax.all_gather(delta, "ctx", axis=2, tiled=True),
    )

    def key_fold(carry, piece, start):
        query_piece, grad_piece = piece

        def visit(state, offset, count):
            other, touch = reaches(starts, key_seg, offset, count)

            def compute(state):
                dkeys, dvalues = state
                query_block = heads_of(lax.dynamic_slice_in_dim(query_piece, offset, count, 1))
                grad_block = heads_of(lax.dynamic_slice_in_dim(grad_piece, offset, count, 1))
                top_block = lax.dynamic_slice_in_dim(every_top, offset, count, 2)
                delta_block = lax.dynamic_slice_in_dim(every_delta, offset, count, 2)
                scores = (
                    jnp.einsum(
                        "bqhd,bkhd->bhqk",
                        query_block,
                        key_heads,
                        preferred_element_type=jnp.float32,
                    )
                    * scale
                )
                mask = (other[:, :, None] == key_seg[:, None, :])[:, None]
                probs = jnp.where(
                    mask, jnp.exp(jnp.where(mask, scores, NEG) - top_block[..., None]), 0.0
                )
                dvalues = dvalues + jnp.einsum(
                    "bhqk,bqhd->bkhd",
                    probs.astype(jnp.bfloat16),
                    grad_block,
                    preferred_element_type=jnp.float32,
                )
                dprobs = jnp.einsum(
                    "bqhd,bkhd->bhqk", grad_block, value_heads, preferred_element_type=jnp.float32
                )
                dscores = (probs * (dprobs - delta_block[..., None])).astype(jnp.bfloat16)
                dkeys = (
                    dkeys
                    + jnp.einsum(
                        "bhqk,bqhd->bkhd", dscores, query_block, preferred_element_type=jnp.float32
                    )
                    * scale
                )
                return (dkeys, dvalues)

            return lax.cond(touch, compute, keep_state, state)

        return block_loop(query_piece.shape[1], carry, visit)

    empty = jnp.zeros(key_heads.shape, jnp.float32)
    return key_fold(
        (empty, empty),
        (
            lax.all_gather(queries, "ctx", axis=1, tiled=True),
            lax.all_gather(dmixed, "ctx", axis=1, tiled=True),
        ),
        jnp.int32(0),
    )


def forward_pass(tokens, starts, weights, base):
    (
        query_weight,
        query_bias,
        key_weight,
        value_weight,
        value_bias,
        out_weight,
        out_bias,
        first_gain,
        first_shift,
        inner_weight,
        inner_bias,
        outer_weight,
        outer_bias,
        second_gain,
        second_shift,
    ) = weights
    rows = tokens.shape[1]
    positions = base + jnp.arange(rows, dtype=jnp.int32)
    query_seg = segment_of(starts, jnp.broadcast_to(positions, (tokens.shape[0], rows)))
    queries = (project(tokens, query_weight) + query_bias.astype(jnp.float32)).astype(jnp.bfloat16)
    keys = project(tokens, key_weight).astype(jnp.bfloat16)
    values = (project(tokens, value_weight) + value_bias.astype(jnp.float32)).astype(jnp.bfloat16)
    mixed, logsum, whole = forward_attention(queries, query_seg, starts, keys, values)
    mixed_low = mixed.reshape(tokens.shape).astype(jnp.bfloat16)
    first_sum = (
        tokens.astype(jnp.float32) + project(mixed_low, out_weight) + out_bias.astype(jnp.float32)
    )
    first = normalize(first_sum, first_gain.astype(jnp.float32), first_shift.astype(jnp.float32))
    first_low = first.astype(jnp.bfloat16)
    inner = project(first_low, inner_weight) + inner_bias.astype(jnp.float32)
    active = gelu(inner).astype(jnp.bfloat16)
    second_sum = first + project(active, outer_weight) + outer_bias.astype(jnp.float32)
    output = normalize(
        second_sum, second_gain.astype(jnp.float32), second_shift.astype(jnp.float32)
    ).astype(jnp.bfloat16)
    saved = (
        tokens,
        query_seg,
        queries,
        keys,
        values,
        mixed,
        logsum,
        mixed_low,
        first_sum,
        first_low,
        inner,
        active,
        second_sum,
        whole,
    )
    return (output, saved)


def backward_pass(saved, starts, weights, cotangent):
    (
        query_weight,
        _,
        key_weight,
        value_weight,
        _,
        out_weight,
        _,
        first_gain,
        first_shift,
        inner_weight,
        _,
        outer_weight,
        _,
        second_gain,
        second_shift,
    ) = weights
    (
        tokens,
        query_seg,
        queries,
        keys,
        values,
        mixed,
        logsum,
        mixed_low,
        first_sum,
        first_low,
        inner,
        active,
        second_sum,
        _,
    ) = saved
    unused, second_back = jax.vjp(
        normalize, second_sum, second_gain.astype(jnp.float32), second_shift.astype(jnp.float32)
    )
    dsecond, dgain_second, dshift_second = second_back(cotangent.astype(jnp.float32))
    douter = dsecond.astype(jnp.bfloat16)
    dactive = project_back(douter, outer_weight)
    unused, gelu_back = jax.vjp(gelu, inner)
    dinner = gelu_back(dactive)[0].astype(jnp.bfloat16)
    dfirst = dsecond + project_back(dinner, inner_weight)
    unused, first_back = jax.vjp(
        normalize, first_sum, first_gain.astype(jnp.float32), first_shift.astype(jnp.float32)
    )
    dfirst_sum, dgain_first, dshift_first = first_back(dfirst)
    dbranch = dfirst_sum.astype(jnp.bfloat16)
    dmixed = project_back(dbranch, out_weight).astype(jnp.bfloat16)
    delta = jnp.einsum("bqhd,bqhd->bhq", heads_of(dmixed).astype(jnp.float32), mixed)
    dqueries = query_gradient(queries, query_seg, starts, keys, values, dmixed, logsum, delta)
    dkeys, dvalues = key_gradient(keys, values, query_seg, starts, queries, dmixed, logsum, delta)
    dqueries = dqueries.reshape(tokens.shape).astype(jnp.bfloat16)
    dkeys = dkeys.reshape(tokens.shape).astype(jnp.bfloat16)
    dvalues = dvalues.reshape(tokens.shape).astype(jnp.bfloat16)
    tokens_grad = (
        dfirst_sum
        + project_back(dqueries, query_weight)
        + project_back(dkeys, key_weight)
        + project_back(dvalues, value_weight)
    )
    sums = (
        outer_sum(tokens, dqueries),
        row_sum(dqueries),
        outer_sum(tokens, dkeys),
        outer_sum(tokens, dvalues),
        row_sum(dvalues),
        outer_sum(mixed_low, dbranch),
        row_sum(dbranch),
        dgain_first,
        dshift_first,
        outer_sum(first_low, dinner),
        row_sum(dinner),
        outer_sum(active, douter),
        row_sum(douter),
        dgain_second,
        dshift_second,
    )
    return (tokens_grad, sums)


def general_device(
    tokens,
    doc_lengths,
    query_weight,
    query_bias,
    key_weight,
    value_weight,
    value_bias,
    out_weight,
    out_bias,
    first_gain,
    first_shift,
    inner_weight,
    inner_bias,
    outer_weight,
    outer_bias,
    second_gain,
    second_shift,
    cotangent,
):
    params = (
        query_weight,
        query_bias,
        key_weight,
        value_weight,
        value_bias,
        out_weight,
        out_bias,
        first_gain,
        first_shift,
        inner_weight,
        inner_bias,
        outer_weight,
        outer_bias,
        second_gain,
        second_shift,
    )
    rows = tokens.shape[2]
    base = lax.axis_index("ctx") * rows
    lengths = doc_lengths[:, 0]
    starts = jnp.cumsum(lengths, axis=-1) - lengths
    outputs = []
    token_parts = []
    sums = None
    for index in range(tokens.shape[0]):
        weights = (
            lax.all_gather(params[0], "wt", axis=0, tiled=True),
            lax.all_gather(params[1], "wt", axis=0, tiled=True),
            lax.all_gather(params[2], "wt", axis=0, tiled=True),
            lax.all_gather(params[3], "wt", axis=0, tiled=True),
            lax.all_gather(params[4], "wt", axis=0, tiled=True),
            lax.all_gather(params[5], "wt", axis=0, tiled=True),
            lax.all_gather(params[6], "wt", axis=0, tiled=True),
            lax.all_gather(params[7], "wt", axis=0, tiled=True),
            lax.all_gather(params[8], "wt", axis=0, tiled=True),
            lax.all_gather(params[9], "wt", axis=0, tiled=True),
            lax.all_gather(params[10], "wt", axis=0, tiled=True),
            lax.all_gather(params[11], "wt", axis=0, tiled=True),
            lax.all_gather(params[12], "wt", axis=0, tiled=True),
            lax.all_gather(params[13], "wt", axis=0, tiled=True),
            lax.all_gather(params[14], "wt", axis=0, tiled=True),
        )
        part_out, saved = forward_pass(
            tokens[index : index + 1, 0], starts[index : index + 1], weights, base
        )
        again = (
            lax.all_gather(params[0], "wt", axis=0, tiled=True),
            lax.all_gather(params[1], "wt", axis=0, tiled=True),
            lax.all_gather(params[2], "wt", axis=0, tiled=True),
            lax.all_gather(params[3], "wt", axis=0, tiled=True),
            lax.all_gather(params[4], "wt", axis=0, tiled=True),
            lax.all_gather(params[5], "wt", axis=0, tiled=True),
            lax.all_gather(params[6], "wt", axis=0, tiled=True),
            lax.all_gather(params[7], "wt", axis=0, tiled=True),
            lax.all_gather(params[8], "wt", axis=0, tiled=True),
            lax.all_gather(params[9], "wt", axis=0, tiled=True),
            lax.all_gather(params[10], "wt", axis=0, tiled=True),
            lax.all_gather(params[11], "wt", axis=0, tiled=True),
            lax.all_gather(params[12], "wt", axis=0, tiled=True),
            lax.all_gather(params[13], "wt", axis=0, tiled=True),
            lax.all_gather(params[14], "wt", axis=0, tiled=True),
        )
        part_grad, part_sums = backward_pass(
            saved, starts[index : index + 1], again, cotangent[index : index + 1, 0]
        )
        outputs.append(part_out)
        token_parts.append(part_grad)
        sums = part_sums if sums is None else jax.tree.map(jnp.add, sums, part_sums)
    output = jnp.concatenate(outputs, axis=0)
    tokens_grad = jnp.concatenate(token_parts, axis=0)
    shards = jax.tree.map(
        lambda part: part.astype(jnp.float32),
        lax.psum_scatter(for_sending(sums), "wt", scatter_dimension=0, tiled=True),
    )
    totals = lax.psum(shards, "ctx")
    return (output[:, None], tokens_grad[:, None]) + tuple(totals)


def flip(value, bits):
    return lax.ppermute(value, "ctx", [(i, i ^ bits) for i in range(8)])


def turn(value, step):
    return lax.ppermute(value, "wt", [(i, (i - step) % 4) for i in range(4)])


def pick(value, index, axis=0):
    return lax.dynamic_index_in_dim(value, index, axis, keepdims=False)


def pair(own, other, bit, axis=0):
    return jnp.where(bit == 0, jnp.stack([own, other], axis), jnp.stack([other, own], axis))


def short(value):
    return value.astype(jnp.bfloat16)


def wide(value):
    return value.astype(jnp.float32)


def dot(left, right):
    return jnp.dot(left, right, preferred_element_type=jnp.float32)


def dot_back(left, right):
    return lax.dot_general(
        left, right, (((1,), (1,)), ((), ())), preferred_element_type=jnp.float32
    )


def dot_sum(left, right):
    return lax.dot_general(
        left, right, (((0,), (0,)), ((), ())), preferred_element_type=jnp.float32
    )


def norm_parts(rows):
    mean = jnp.mean(rows, axis=-1, keepdims=True)
    centered = rows - mean
    spread = jnp.mean(centered * centered, axis=-1, keepdims=True)
    root = lax.rsqrt(spread + EPS)
    return centered * root, root


def norm_back(upstream, normed, root, gain):
    grad = upstream * gain
    mean = jnp.mean(grad, axis=-1, keepdims=True)
    along = jnp.mean(grad * normed, axis=-1, keepdims=True)
    return root * (grad - mean - normed * along)


def gelu_slope(inner):
    bell = jnp.exp(-0.5 * inner * inner) * (1.0 / math.sqrt(2.0 * math.pi))
    return 0.5 * (1.0 + lax.erf(inner * ROOT_HALF)) + inner * bell


def run(kernel, outs, args, scratch=(), scalars=()):
    shapes = tuple(jax.ShapeDtypeStruct(shape, dtype) for shape, dtype in outs)
    spaces = [pltpu.SMEM] * len(scalars) + [pltpu.VMEM] * len(args)
    return pl.pallas_call(
        kernel,
        out_shape=shapes,
        in_specs=[pl.BlockSpec(memory_space=space) for space in spaces],
        scratch_shapes=list(scratch),
    )(*scalars, *args)


BF = jnp.bfloat16
F32 = jnp.float32


def where_am_i():
    ctx, own = lax.axis_index("ctx"), lax.axis_index("wt")
    return ctx & 1, (ctx >> 1) & 3, ctx & 3, own


def some_rows(start, count):
    return pl.ds(pl.multiple_of(start, 16), count)


def prepare_kernel(wq, wk, wv, wo, wi, wo2, vec, heads_own, heads_send, w2_send, inner_half, outer_half):
    core, quarter, group, _ = where_am_i()
    shard, dim = wq.shape
    width, half = dim // 4, wo2.shape[0] // 2
    for index in range(4):

        @pl.when(group == index)
        def _():
            for slot, ref in enumerate((wq, wk, wv)):
                heads_own[:, slot * width : (slot + 1) * width] = ref[
                    :, index * width : (index + 1) * width
                ]

    for index in range(2):

        @pl.when(core == index)
        def _():
            for block in range(4):
                at = block * 2 * half + index * half
                inner_half[:, block * half : (block + 1) * half] = wi[:, at : at + half]
            outer_half[...] = wo2[index * half : (index + 1) * half, :]

    part = shard // 2
    heads_send[0:part, :] = heads_own[some_rows((quarter >> 1) * part, part), :]
    heads_send[part:, 0:width] = vec[...]
    heads_send[part:, width:] = jnp.zeros((16, 2 * width), BF)
    part = shard // 4
    rows = some_rows(quarter * part, part)
    w2_send[0:part, :] = inner_half[rows, 0:dim]
    w2_send[part : 2 * part, :] = inner_half[rows, dim:]
    step = half // 4
    w2_send[2 * part : 2 * part + step, :] = outer_half[some_rows(quarter * step, step), :]
    w2_send[2 * part + step :, :] = wo[rows, :]


CHUNK = 128
WINDOWS = (4, 6, 8)


def chunk_of(ctx, index):
    return ctx ^ ((index >> 2) | (index & 2) | ((index & 1) << 2))


def some_chunks(start, count):
    return pl.ds(pl.multiple_of(start * CHUNK, CHUNK), count * CHUNK)


def over_window(bounds, block, windows, visit):
    if len(windows) == 1:
        visit(pl.ds(0, windows[0] * CHUNK))
        return
    low, count = bounds[0, block], bounds[1, block]
    least = 0
    for size in windows:

        @pl.when((count > least) & (count <= size))
        def _(size=size):
            visit(some_chunks(jnp.minimum(low, windows[-1] - size), size))

        least = size


def attend_rows(qkv, seg_col, seg_row, far, outs, logsum, mixed):
    core, quarter, _, _ = where_am_i()
    scale = HEAD_DIM ** (-0.5)
    group = qkv.shape[0] // 3

    def step(side, carry):
        rows = some_chunks(2 * (2 * side + ((quarter & 1) ^ far)), 2)
        here = some_chunks(2 * side, 2)

        def one_head(head, carry):
            mask = seg_col[rows, :] == seg_row[...]
            scores = dot_back(qkv[head, rows, :], qkv[group + head])
            scores = jnp.where(mask, scores * scale, NEG)
            top = jnp.max(scores, axis=-1, keepdims=True)
            expd = jnp.exp(scores - top)
            total = jnp.sum(expd, axis=-1, keepdims=True)
            probs = short(expd * (1.0 / total))
            mixed[head, here, :] = short(dot(probs, qkv[2 * group + head]))
            lane = lax.broadcasted_iota(jnp.int32, (2 * CHUNK, 128), 1)
            logsum[here, :] = jnp.where(lane == head, top + jnp.log(total), logsum[here, :])
            return carry

        lax.fori_loop(0, group, one_head, 0)
        return carry

    logsum[...] = jnp.zeros_like(logsum)
    lax.fori_loop(0, 2, step, 0)
    y = quarter >> 1
    for index, out in enumerate(outs):
        for side in range(2):
            chunk = 2 * (y ^ side) + (core ^ index)
            for head in range(group):
                out[
                    side * CHUNK : (side + 1) * CHUNK, head * HEAD_DIM : (head + 1) * HEAD_DIM
                ] = mixed[head, some_chunks(chunk, 1), :]


def attend_near_kernel(
    mine, other, far, heads_own, g1, g2, g3, h1, h2, h3, bias, seg_col, seg_row,
    qkv, m0, m1, logsum, weight, mixed,
):
    _, quarter, _, own = where_am_i()
    ctx = lax.axis_index("ctx")
    shard = heads_own.shape[0]
    part = shard // 2
    y = quarter >> 1
    weight[some_rows(own * shard, shard), :] = heads_own[...]
    for step, near_half, far_half in ((1, g1, h1), (2, g2, h2), (3, g3, h3)):
        at = ((own + step) & 3) * shard
        weight[some_rows(at + part * y, part), :] = near_half[0:part, :]
        weight[some_rows(at + part * (1 - y), part), :] = far_half[0:part, :]
    index = 0
    for source in (mine, other, far):
        for first in range(0, source.shape[0], 2 * CHUNK):
            low = short(dot(source[first : first + 2 * CHUNK, :], weight[...]) + bias[...])
            for half in range(2):
                at = pl.multiple_of(chunk_of(ctx, index) * CHUNK, CHUNK)
                for slot in range(qkv.shape[0]):
                    qkv[slot, pl.ds(at, CHUNK), :] = low[
                        half * CHUNK : (half + 1) * CHUNK,
                        slot * HEAD_DIM : (slot + 1) * HEAD_DIM,
                    ]
                index += 1
    attend_rows(qkv, seg_col, seg_row, 0, (m0, m1), logsum, mixed)


def attend_far_kernel(qkv, seg_col, seg_row, m2, m3, logsum, mixed):
    attend_rows(qkv, seg_col, seg_row, 1, (m2, m3), logsum, mixed)


def project_kernel(m0, m1, m2, m3, mine, wo, vec, *refs):
    pieces, (first_sum, first_low, out_full) = refs[:12], refs[12:]
    _, quarter, group, own = where_am_i()
    shard = wo.shape[0]
    part = shard // 4
    out_full[some_rows(own * shard, shard), :] = wo[...]
    for index, piece in enumerate(pieces):
        at = ((own + 1 + index // 4) & 3) * shard + part * (quarter ^ (index % 4))
        out_full[some_rows(at, part), :] = piece[piece.shape[0] - part :, :]
    total = wide(mine[...]) + vec[2:3, :]
    for code, ref in enumerate((m0, m1, m2, m3)):
        total += dot(ref[...], out_full[some_rows((group ^ code) * shard, shard), :])
    first_sum[...] = total
    first_low[...] = short(norm_parts(total)[0] * vec[3:4, :] + vec[4:5, :])


def forward_kernel(near, far, inner_half, outer_half, bias, *refs):
    pieces, (keep, send, inner, active, wi_full, wo2_full) = refs[:12], refs[12:]
    _, quarter, _, own = where_am_i()
    shard, half = inner_half.shape[0], outer_half.shape[0]
    dim = keep.shape[1]
    part, step = shard // 4, half // 4
    wi_full[some_rows(own * shard, shard), :] = inner_half[...]
    wo2_full[some_rows(own * half, half), :] = outer_half[...]
    for index, piece in enumerate(pieces):
        row, spot = (own + 1 + index // 4) & 3, quarter ^ (index % 4)
        rows = some_rows(row * shard + part * spot, part)
        wi_full[rows, 0:dim] = piece[0:part, :]
        wi_full[rows, dim:] = piece[part : 2 * part, :]
        wo2_full[some_rows(row * half + step * spot, step), :] = piece[
            2 * part : 2 * part + step, :
        ]
    count = near.shape[0]
    chunk = 512
    for index, (source, out) in enumerate(((far, send), (near, keep))):
        at = (1 - index) * count
        total = None
        for lane in range(0, inner.shape[1], chunk):
            lanes = slice(lane, lane + chunk)
            value = dot(source[...], wi_full[:, lanes]) + bias[:, lanes]
            inner[at : at + count, lanes] = value
            low = short(gelu(value))
            active[at : at + count, lanes] = low
            added = dot(low, wo2_full[lanes, :])
            total = added if total is None else total + added
        out[...] = total


def turnaround_kernel(first_sum, keep, got, vec, cot0, cot1, out0, out1, dsecond, douter, sums):
    rows = cot0.shape[0]
    first = norm_parts(first_sum[...])[0] * vec[3:4, :] + vec[4:5, :]
    normed, root = norm_parts(first + vec[5:6, :] + keep[...] + got[...])
    output = short(normed * vec[6:7, :] + vec[7:8, :])
    out0[...] = output[:rows]
    out1[...] = output[rows:]
    upstream = jnp.concatenate([wide(cot0[...]), wide(cot1[...])])
    back = norm_back(upstream, normed, root, vec[6:7, :])
    low = short(back)
    dsecond[...] = back
    douter[...] = low
    sums[0:1, :] = jnp.sum(wide(low), axis=0, keepdims=True)
    sums[1:2, :] = jnp.sum(upstream * normed, axis=0, keepdims=True)
    sums[2:3, :] = jnp.sum(upstream, axis=0, keepdims=True)
    sums[3:, :] = jnp.zeros_like(sums[3:, :])


def backward_kernel(near, far, inner, wi_full, wo2_full, keep, send, dinner, sums):
    count, dim = near.shape
    chunk = 512
    for index, (source, out) in enumerate(((far, send), (near, keep))):
        at = (1 - index) * count
        total = None
        for lane in range(0, inner.shape[1], chunk):
            lanes = slice(lane, lane + chunk)
            slope = gelu_slope(inner[at : at + count, lanes])
            low = short(dot_back(source[...], wo2_full[lanes, :]) * slope)
            dinner[at : at + count, lanes] = low
            added = dot_back(low, wi_full[:, lanes])
            total = added if total is None else total + added
        out[...] = total
    total = jnp.sum(wide(dinner[...]), axis=0, keepdims=True)
    sums[0:1, :] = total[:, :dim]
    sums[1:2, :] = total[:, dim:]
    sums[2:, :] = jnp.zeros_like(sums[2:, :])


def weights_kernel(first0, first1, douter0, douter1, dinner, active, ak, az, bk, bz, left, right):
    _, quarter, _, _ = where_am_i()
    x, y = quarter & 1, quarter >> 1
    count = first0.shape[0]
    part, step = first0.shape[1] // 16, active.shape[1] // 16
    left[...] = short(dot_sum(first0[...], dinner[:count]) + dot_sum(first1[...], dinner[count:]))
    for block in range(8):
        rows = slice(block * part, (block + 1) * part)
        ak[rows, :] = left[some_rows((2 * block + x) * part, part), :]
        az[rows, :] = left[some_rows((2 * block + 1 - x) * part, part), :]
    right[...] = short(
        dot_sum(active[:count], douter0[...]) + dot_sum(active[count:], douter1[...])
    )
    for block in range(8):
        row, side = block // 2, block % 2
        rows = slice(block * step, (block + 1) * step)
        bk[rows, :] = right[some_rows((4 * row + 2 * y + side) * step, step), :]
        bz[rows, :] = right[some_rows((4 * row + 2 * (1 - y) + side) * step, step), :]


def branch_kernel(first_sum, dsecond, keep, got, vec, out_full, dfirst_sum, dbranch, d0, d1, d2, d3, sums):
    _, _, group, _ = where_am_i()
    shard = d0.shape[1]
    normed, root = norm_parts(first_sum[...])
    dfirst = dsecond[...] + keep[...] + got[...]
    back = norm_back(dfirst, normed, root, vec[3:4, :])
    low = short(back)
    dfirst_sum[...] = back
    dbranch[...] = low
    for code, ref in enumerate((d0, d1, d2, d3)):
        ref[...] = short(dot_back(low, out_full[some_rows((group ^ code) * shard, shard), :]))
    sums[0:1, :] = jnp.sum(wide(low), axis=0, keepdims=True)
    sums[1:2, :] = jnp.sum(dfirst * normed, axis=0, keepdims=True)
    sums[2:3, :] = jnp.sum(dfirst, axis=0, keepdims=True)
    sums[3:, :] = jnp.zeros_like(sums[3:, :])


def out_weight_kernel(m0, m1, m2, m3, dbranch, sums1, sums2, sums3, ck, cz, whole):
    core, _, group, _ = where_am_i()
    shard, dim = m0.shape[1], dbranch.shape[1]
    half = dim // 2
    for code, ref in enumerate((m0, m1, m2, m3)):
        whole[some_rows((group ^ code) * shard, shard), :] = short(
            dot_sum(ref[...], dbranch[...])
        )
    for side in range(2):

        @pl.when(core == side)
        def _():
            for ref, which in ((ck, side), (cz, 1 - side)):
                ref[0:dim, :] = whole[:, which * half : (which + 1) * half]

    rows = short(
        jnp.concatenate([sums1[0:3, :], sums2[0:3, :], sums3[0:2, :], jnp.zeros_like(sums1[...])])
    )
    for ref in (ck, cz):
        ref[dim : dim + 16, :] = rows[:, :half]
        ref[dim + 16 :, :] = rows[:, half:]


def out_split_kernel(packed, got, ck, cz):
    core, quarter, _, _ = where_am_i()
    x = quarter & 1
    dim = packed.shape[0] - 32
    part = dim // 16
    for block in range(8):
        rows = slice(block * part, (block + 1) * part)
        for ref, side in ((ck, x), (cz, 1 - x)):
            take = some_rows((2 * block + side) * part, part)
            ref[rows, :] = short(wide(packed[take, :]) + wide(got[take, :]))
    for lanes in range(2):
        at = dim + 16 * lanes
        mine, other = wide(packed[at : at + 16, :]), wide(got[at : at + 16, :])
        low = jnp.where(core == 0, mine, other)[6:8]
        high = jnp.where(core == 0, other, mine)[6:8]
        rows = jnp.concatenate([(mine + other)[0:6], low, high, jnp.zeros_like(mine[0:6])])
        at = 8 * part + 16 * lanes
        for ref in (ck, cz):
            ref[at : at + 16, :] = short(rows)


def reduce_rows(keep, got, outs, bit):
    size = keep.shape[0] // 8
    size -= size % 16
    width = keep.shape[1] // len(outs)
    for lane, pair_of in enumerate(outs):
        lanes = slice(lane * width, (lane + 1) * width)
        for block in range(4):
            for out, side in zip(pair_of, (bit, 1 - bit)):
                take = some_rows((2 * block + side) * size, size)
                out[block * size : (block + 1) * size, :] = short(
                    wide(keep[take, lanes]) + wide(got[take, lanes])
                )
        if keep.shape[0] > 8 * size:
            for out in pair_of:
                out[4 * size :, :] = short(
                    wide(keep[8 * size :, lanes]) + wide(got[8 * size :, lanes])
                )


def reduce_kernel(ak, ar, bk, br, *outs):
    _, quarter, _, _ = where_am_i()
    reduce_rows(ak, ar, (outs[0:2], outs[4:6]), quarter >> 1)
    reduce_rows(bk, br, (outs[2:4], outs[6:8]), quarter & 1)


def reduce_out_kernel(ck, cr, c2k, c2z):
    _, quarter, _, _ = where_am_i()
    reduce_rows(ck, cr, ((c2k, c2z),), quarter >> 1)


def owners_kernel(*refs):
    inputs, outs = refs[:-4], refs[-4:]
    _, _, _, own = where_am_i()
    ak, ar, bk, br = inputs[:4]
    half = bk.shape[1]
    part = ak.shape[0] // 4
    for index, out in enumerate(outs):
        row = (own - index) & 3
        rows = some_rows(row * part, part)
        out[0:part, :] = (wide(ak[rows, :]) + wide(ar[rows, :])).astype(out.dtype)
        for side in range(2):
            rows = some_rows((2 * row + side) * part, part)
            out[part : 2 * part, side * half : (side + 1) * half] = (
                wide(bk[rows, :]) + wide(br[rows, :])
            ).astype(out.dtype)
        if len(inputs) > 4:
            ck, cr = inputs[4:]
            at = 2 * part
            rows = some_rows(row * part, part)
            out[at:, 0:half] = (wide(ck[rows, :]) + wide(cr[rows, :])).astype(out.dtype)
            tail = wide(ck[4 * part :, :]) + wide(cr[4 * part :, :])
            out[at : at + 32, half:] = tail.astype(out.dtype)
            out[at + 32 :, half:] = jnp.zeros((part - 32, half), out.dtype)


def total_kernel(mine, *refs):
    total = wide(mine[...])
    for ref in refs[:-1]:
        total += wide(ref[...])
    refs[-1][...] = short(total)


def finish_kernel(*refs):
    pieces, (dwi, dwo2, dwo, small) = refs[:16], refs[16:]
    core, quarter, _, _ = where_am_i()
    part, half = dwi.shape[0] // 4, dwi.shape[1] // 8
    for side in range(2):

        @pl.when(core == side)
        def _():
            for index, piece in enumerate(pieces):
                lane, index = index // 8, index % 8
                spot = quarter ^ (index % 4)
                which = side if index < 4 else 1 - side
                rows = some_rows(spot * part, part)
                for block in range(2):
                    at = (2 * lane + block) * 2 * half + which * half
                    dwi[rows, at : at + half] = wide(piece[0:part, block * half : (block + 1) * half])
                    at = which * half + spot * 2 * part + block * part
                    dwo2[some_rows(at, part), lane * half : (lane + 1) * half] = wide(
                        piece[part : 2 * part, block * half : (block + 1) * half]
                    )
                if lane == 1:
                    dwo[rows, which * half : (which + 1) * half] = wide(piece[2 * part :, 0:half])

    last = pieces[8]
    small[:, 0:half] = wide(last[2 * part : 2 * part + 16, half:])
    small[:, half:] = wide(last[2 * part + 16 : 2 * part + 32, half:])


def attend_back_kernel(
    bounds, qkv, logsum0, logsum1, seg_col, seg_row, p0, p1, p2, p3, mine, other, far, weight,
    h0, h1, h2, h3, keep, send, grads, dqueries, dkeys, dvalues, dweight, dmixed, logsum, whole,
):
    _, quarter, _, own = where_am_i()
    ctx = lax.axis_index("ctx")
    x = quarter & 1
    scale = HEAD_DIM ** (-0.5)
    group = qkv.shape[0] // 3
    width = group * HEAD_DIM
    block = p0.shape[0]
    dkeys[...] = jnp.zeros_like(dkeys)
    dvalues[...] = jnp.zeros_like(dvalues)
    for index, part in enumerate((p0, p2, p1, p3)):
        for side in range(2):
            chunk = chunk_of(ctx, 2 * index + side)
            for head in range(group):
                dmixed[head, some_chunks(chunk, 1), :] = part[
                    side * CHUNK : (side + 1) * CHUNK, head * HEAD_DIM : (head + 1) * HEAD_DIM
                ]
    for side in range(2):
        rows = slice(2 * side * CHUNK, 2 * (side + 1) * CHUNK)
        logsum[some_chunks(2 * (2 * side + x), 2), :] = logsum0[rows, :]
        logsum[some_chunks(2 * (2 * side + 1 - x), 2), :] = logsum1[rows, :]

    def step(index, carry):
        rows = some_chunks(2 * index, 2)

        def visit(window):
            def one_head(head, carry):
                mask = seg_col[rows, :] == seg_row[:, window]
                query = qkv[head, rows, :]
                grad = dmixed[head, rows, :]
                keys = qkv[group + head, window, :]
                lane = lax.broadcasted_iota(jnp.int32, (2 * CHUNK, 128), 1)
                sums = jnp.sum(
                    jnp.where(lane == head, logsum[rows, :], 0.0), axis=-1, keepdims=True
                )
                scores = jnp.where(mask, dot_back(query, keys) * scale, NEG)
                probs = jnp.exp(scores - sums)
                dprobs = dot_back(grad, qkv[2 * group + head, window, :])
                delta = jnp.sum(probs * dprobs, axis=-1, keepdims=True)
                dscores = short(probs * (dprobs - delta))
                dqueries[head, rows, :] = short(dot(dscores, keys) * scale)
                dkeys[head, window, :] += dot_sum(dscores, query)
                dvalues[head, window, :] += dot_sum(short(probs), grad)
                return carry

            lax.fori_loop(0, group, one_head, 0)

        over_window(bounds, index, WINDOWS, visit)
        return carry

    lax.fori_loop(0, 4, step, 0)
    for head in range(group):
        whole[:, head * HEAD_DIM : (head + 1) * HEAD_DIM] = dqueries[head]
        at = width + head * HEAD_DIM
        whole[:, at : at + HEAD_DIM] = short(dkeys[head] * scale)
        whole[:, at + width : at + width + HEAD_DIM] = short(dvalues[head])
    for index in range(8):
        grads[index * CHUNK : (index + 1) * CHUNK, :] = whole[
            some_chunks(chunk_of(ctx, index), 1), :
        ]
    rows = 2 * block
    dweight[...] = (
        dot_sum(mine[...], grads[:block])
        + dot_sum(other[...], grads[block:rows])
        + dot_sum(far[...], grads[rows:])
    )
    sums = jnp.sum(wide(grads[...]), axis=0, keepdims=True)
    tail = jnp.concatenate([sums, jnp.zeros((15, sums.shape[1]), F32)])
    for index, out in enumerate((h0, h1, h2, h3)):
        take = pl.ds(pl.multiple_of(((own - index) & 3) * width, 16), width)
        out[0:width, :] = dweight[take, :].astype(out.dtype)
        out[width:, :] = tail.astype(out.dtype)
    keep[...] = dot_back(grads[:rows], weight[...])
    send[...] = short(dot_back(grads[rows:], weight[...]))


def merge_kernel(keep, got, base, near, far):
    total = keep[...] + wide(got[...])
    count = near.shape[0]
    near[...] = total[:count] + base[...]
    far[...] = short(total[count:])


def heads_kernel(s0, s1, s2, s3, dq, dk, dv, bias):
    _, _, group, own = where_am_i()
    shard = dq.shape[0]
    for index in range(4):

        @pl.when(group == index)
        def _():
            for code, ref in enumerate((s0, s1, s2, s3)):
                at = (index ^ code) * shard
                for slot, out in enumerate((dq, dk, dv)):
                    out[:, at : at + shard] = wide(
                        ref[0:shard, slot * shard : (slot + 1) * shard]
                    )

                @pl.when(own == index ^ code)
                def _():
                    bias[...] = wide(ref[shard:, :])


def plane_steps(
    tokens,
    doc_lengths,
    query_weight,
    query_bias,
    key_weight,
    value_weight,
    value_bias,
    out_weight,
    out_bias,
    first_gain,
    first_shift,
    inner_weight,
    inner_bias,
    outer_weight,
    outer_bias,
    second_gain,
    second_shift,
    cotangent,
):
    ctx, own = lax.axis_index("ctx"), lax.axis_index("wt")
    core, y, group = ctx & 1, ctx >> 2, ctx & 3
    rows, dim = tokens.shape[2], tokens.shape[3]
    shard = query_weight.shape[0]
    hidden = outer_weight.shape[0]
    half = hidden // 2
    count = 2 * rows

    mine = jnp.concatenate([pick(tokens[:, 0], y), flip(pick(tokens[:, 0], 1 - y), 4)])
    other = flip(mine, 2)
    far = flip(jnp.concatenate([mine, other]), 1)

    vector_list = (
        query_bias,
        value_bias,
        out_bias,
        first_gain,
        first_shift,
        outer_bias,
        second_gain,
        second_shift,
        *[inner_bias[at : at + shard] for at in range(0, 4 * shard, shard)],
    )
    line = lax.broadcasted_iota(jnp.int32, (16, shard), 0)
    vec = jnp.zeros((16, shard), BF)
    for index, value in enumerate(vector_list):
        vec = jnp.where(line == index, value[None, :], vec)
    heads_own, heads_send, w2_send, inner_half, outer_half = run(
        prepare_kernel,
        [
            ((shard, 3 * shard), BF),
            ((shard // 2 + 16, 3 * shard), BF),
            ((shard // 4 * 3 + half // 4, dim), BF),
            ((shard, 4 * half), BF),
            ((half, dim), BF),
        ],
        (query_weight, key_weight, value_weight, out_weight, inner_weight, outer_weight, vec),
    )
    got = [turn(heads_send, step) for step in (1, 2, 3)]
    gone = [flip(value, 4) for value in got]
    pieces = []
    for step in (1, 2, 3):
        piece = turn(w2_send, step)
        pieces += [piece] + [flip(piece, bits) for bits in (2, 4, 6)]

    at = shard // 2
    rel = jnp.stack([vec] + [value[at:, :shard] for value in got])
    vectors = wide(lax.dynamic_slice_in_dim(jnp.concatenate([rel, rel]), (4 - own) % 4, 4))
    mine_b = pick(vectors, group)
    heads_bias = jnp.concatenate([mine_b[0], jnp.zeros_like(mine_b[0]), mine_b[1]])[None]
    inner_b = pick(vectors[:, 8:12].reshape(4, 2, half), core, 1).reshape(1, 4 * half)
    vectors = jnp.swapaxes(vectors[:, :8], 0, 1).reshape(8, dim)

    lengths = pick(doc_lengths[:, 0], y)
    starts = jnp.cumsum(lengths) - lengths
    total = 8 * rows
    positions = jnp.arange(total, dtype=jnp.int32)
    seg = jnp.sum((starts[None, :] <= positions[:, None]).astype(jnp.int32), axis=-1) - 1
    segs = (seg[:, None], seg[None, :])
    first = jnp.arange(4, dtype=jnp.int32)[:, None] * (2 * CHUNK)
    low = jnp.max(jnp.where(starts[None, :] <= first, starts[None, :], 0), axis=-1) // CHUNK
    ends = jnp.where(starts[None, :] >= first + 2 * CHUNK, starts[None, :], total)
    bounds = jnp.stack([low, (jnp.min(ends, axis=-1) - 1) // CHUNK - low + 1])

    qkv, m0, m1, logsum0, heads_weight = run(
        attend_near_kernel,
        [
            ((9, total, HEAD_DIM), BF),
            ((count, shard), BF),
            ((count, shard), BF),
            ((2 * count, 128), F32),
            ((dim, 3 * shard), BF),
        ],
        (mine, other, far, heads_own, *got, *gone, heads_bias, *segs),
        [pltpu.VMEM((3, 2 * count, HEAD_DIM), BF)],
    )
    m2, m3, logsum1 = run(
        attend_far_kernel,
        [((count, shard), BF), ((count, shard), BF), ((2 * count, 128), F32)],
        (qkv, *segs),
        [pltpu.VMEM((3, 2 * count, HEAD_DIM), BF)],
    )
    mixed = [m0, flip(m1, 1), flip(m2, 2), flip(m3, 3)]

    first_sum, first_low, out_full = run(
        project_kernel,
        [((count, dim), F32), ((count, dim), BF), ((dim, dim), BF)],
        (*mixed, mine, out_weight, vectors, *pieces),
    )
    first_far = flip(first_low, 1)
    keep, send, inner, active, wi_full, wo2_full = run(
        forward_kernel,
        [
            ((count, dim), F32),
            ((count, dim), F32),
            ((2 * count, 4 * half), F32),
            ((2 * count, 4 * half), BF),
            ((dim, 4 * half), BF),
            ((4 * half, dim), BF),
        ],
        (first_low, first_far, inner_half, outer_half, inner_b, *pieces),
    )
    cot = pick(cotangent[:, 0], y), flip(pick(cotangent[:, 0], 1 - y), 4)
    out0, out1, dsecond, douter, sums2 = run(
        turnaround_kernel,
        [
            ((rows, dim), BF),
            ((rows, dim), BF),
            ((count, dim), F32),
            ((count, dim), BF),
            ((8, dim), F32),
        ],
        (first_sum, keep, flip(send, 1), vectors, *cot),
    )
    output = pair(out0, flip(out1, 4), y)

    douter_far = flip(douter, 1)
    keep, send, dinner, sums3 = run(
        backward_kernel,
        [
            ((count, dim), F32),
            ((count, dim), F32),
            ((2 * count, 4 * half), BF),
            ((8, dim), F32),
        ],
        (douter, douter_far, inner, wi_full, wo2_full),
    )
    dfirst_sum, dbranch, d0, d1, d2, d3, sums1 = run(
        branch_kernel,
        [((count, dim), F32), ((count, dim), BF)] + [((count, shard), BF)] * 4 + [((8, dim), F32)],
        (first_sum, dsecond, keep, flip(send, 1), vectors, out_full),
    )
    dmixed = [d0, flip(d1, 1), flip(d2, 2), flip(d3, 3)]

    ak, az, bk, bz = run(
        weights_kernel,
        [((dim // 2, 4 * half), BF)] * 2 + [((2 * half, dim), BF)] * 2,
        (first_low, first_far, douter, douter_far, dinner, active),
        [pltpu.VMEM((dim, 4 * half), BF), pltpu.VMEM((4 * half, dim), BF)],
    )
    ar, br = flip(az, 2), flip(bz, 4)
    ck, cz = run(
        out_weight_kernel,
        [((dim + 32, dim // 2), BF)] * 2,
        (*mixed, dbranch, sums1, sums2, sums3),
        [pltpu.VMEM((dim, dim), BF)],
    )
    ck, cz = run(out_split_kernel, [((dim // 2 + 32, dim // 2), BF)] * 2, (ck, flip(cz, 1)))
    cr = flip(cz, 2)

    h0, h1, h2, h3, keep, send = run(
        attend_back_kernel,
        [((shard + 16, 3 * shard), F32)]
        + [((shard + 16, 3 * shard), BF)] * 3
        + [((2 * count, dim), F32), ((2 * count, dim), BF)],
        (qkv, logsum0, logsum1, *segs, *dmixed, mine, other, far, heads_weight),
        [
            pltpu.VMEM((4 * count, 3 * shard), BF),
            pltpu.VMEM((3, 4 * count, HEAD_DIM), BF),
            pltpu.VMEM((3, 4 * count, HEAD_DIM), F32),
            pltpu.VMEM((3, 4 * count, HEAD_DIM), F32),
            pltpu.VMEM((dim, 3 * shard), F32),
            pltpu.VMEM((3, total, HEAD_DIM), BF),
            pltpu.VMEM((total, 128), F32),
            pltpu.VMEM((total, 3 * shard), BF),
        ],
        scalars=(bounds,),
    )

    c2k, c2z = run(reduce_out_kernel, [((dim // 4 + 32, dim // 2), BF)] * 2, (ck, cr))
    reduced = run(
        reduce_kernel,
        ([((dim // 4, 2 * half), BF)] * 2 + [((half, dim // 2), BF)] * 2) * 2,
        (ak, ar, bk, br),
    )
    plane = []
    for lane in range(2):
        a2k, a2z, b2k, b2z = reduced[4 * lane : 4 * lane + 4]
        last = [a2k, flip(a2z, 4), b2k, flip(b2z, 2)]
        size = shard // 4 * 2
        if lane == 1:
            last += [c2k, flip(c2z, 4)]
            size = shard // 4 * 3
        p0, p1, p2, p3 = run(owners_kernel, [((size, dim), F32)] + [((size, dim), BF)] * 3, last)
        turned = [turn(p, step) for step, p in ((1, p1), (2, p2), (3, p3))]
        (piece,) = run(total_kernel, [((size, dim), BF)], (p0, *turned))
        near = [piece] + [flip(piece, bits) for bits in (2, 4, 6)]
        plane += near + [flip(p, 1) for p in near]
    dinner_w, douter_w, dout_w, small = run(
        finish_kernel,
        [((shard, 8 * half), F32), ((hidden, dim), F32), ((shard, dim), F32), ((16, dim), F32)],
        plane,
    )
    dinner_b = pick(small[6:10].reshape(2, 4, half), own, 1).reshape(hidden)
    small = lax.dynamic_slice_in_dim(small[:6], own * shard, shard, 1)

    (heads,) = run(
        total_kernel, [((shard + 16, 3 * shard), BF)], (h0, turn(h1, 1), turn(h2, 2), turn(h3, 3))
    )
    (heads,) = run(total_kernel, [((shard + 16, 3 * shard), BF)], (heads, flip(heads, 4)))
    dquery_w, dkey_w, dvalue_w, heads_b = run(
        heads_kernel,
        [((shard, dim), F32)] * 3 + [((16, 3 * shard), F32)],
        (heads, flip(heads, 1), flip(heads, 2), flip(heads, 3)),
    )

    near_t, far_t = run(
        merge_kernel, [((count, dim), F32), ((count, dim), BF)], (keep, flip(send, 1), dfirst_sum)
    )
    dtokens = near_t + wide(flip(far_t, 2))
    tokens_grad = pair(dtokens[:rows], wide(flip(short(dtokens[rows:]), 4)), y)

    return (
        output[:, None],
        tokens_grad[:, None],
        dquery_w,
        heads_b[0, :shard],
        dkey_w,
        dvalue_w,
        heads_b[0, 2 * shard :],
        dout_w,
        small[0],
        small[1],
        small[2],
        dinner_w,
        dinner_b,
        douter_w,
        small[3],
        small[4],
        small[5],
    )


def plane_device(*args):
    return plane_steps(*args)


def solution(mesh):
    placed = (
        P(None, "wt", "ctx", None),
        P(None, "wt", None),
        P("wt", None),
        P("wt"),
        P("wt", None),
        P("wt", None),
        P("wt"),
        P("wt", None),
        P("wt"),
        P("wt"),
        P("wt"),
        P("wt", None),
        P("wt"),
        P("wt", None),
        P("wt"),
        P("wt"),
        P("wt"),
        P(None, "wt", "ctx", None),
    )
    fits = mesh.shape["ctx"] == 8 and mesh.shape["wt"] == 4
    return jax.shard_map(
        plane_device if fits else general_device,
        mesh=mesh,
        in_specs=placed,
        out_specs=(
            P(None, "wt", "ctx", None),
            P(None, "wt", "ctx", None),
            P("wt", None),
            P("wt"),
            P("wt", None),
            P("wt", None),
            P("wt"),
            P("wt", None),
            P("wt"),
            P("wt"),
            P("wt"),
            P("wt", None),
            P("wt"),
            P("wt", None),
            P("wt"),
            P("wt"),
            P("wt"),
        ),
        check_vma=False,
    )
```

```python
import math

import jax
import jax.numpy as jnp
from jax import lax
from jax.experimental import pallas as pl
from jax.experimental.pallas import tpu as pltpu
from jax.sharding import PartitionSpec as P


HEADS = 12
HEAD_DIM = 64


EPS = 1e-12
NEG = -1e30
ROOT_HALF = 0.7071067811865476


def for_sending(shard):

    def short(part):
        return part.astype(jnp.bfloat16) if part.dtype == jnp.float32 else part

    return jax.tree.map(short, shard)


def normalize(rows, gain, shift):
    mean = jnp.mean(rows, axis=-1, keepdims=True)
    centered = rows - mean
    spread = jnp.mean(centered * centered, axis=-1, keepdims=True)
    return centered * lax.rsqrt(spread + EPS) * gain + shift


def gelu(inner):
    return 0.5 * inner * (1.0 + lax.erf(inner * ROOT_HALF))


def segment_of(starts, positions):
    found = (starts[:, None, :] <= positions[:, :, None]).astype(jnp.int32)
    return jnp.sum(found, axis=-1) - 1


def project(inputs, weight):
    return jnp.einsum("btd,de->bte", inputs, weight, preferred_element_type=jnp.float32)


def project_back(grads, weight):
    return jnp.einsum("bte,de->btd", grads, weight, preferred_element_type=jnp.float32)


def outer_sum(inputs, grads):
    return jnp.einsum("btd,bte->de", inputs, grads, preferred_element_type=jnp.float32)


def row_sum(grads):
    return jnp.sum(grads.astype(jnp.float32), axis=(0, 1))


def heads_of(array):
    return array.reshape(array.shape[0], array.shape[1], HEADS, HEAD_DIM)


def block_loop(width, carry, visit):
    block = math.gcd(width, 512)

    def step(state, index):
        return (visit(state, index * block, block), None)

    carry, _ = lax.scan(step, carry, jnp.arange(width // block, dtype=jnp.int32))
    return carry


def reaches(starts, own_seg, first, count):
    positions = first + jnp.arange(count, dtype=jnp.int32)
    other = segment_of(starts, jnp.broadcast_to(positions, (starts.shape[0], count)))
    touch = jnp.any((other[:, 0] <= own_seg[:, -1]) & (other[:, -1] >= own_seg[:, 0]))
    return (other, touch)


def keep_state(state):
    return state


def forward_attention(queries, query_seg, starts, keys, values):
    scale = HEAD_DIM ** (-0.5)
    batch, rows = (queries.shape[0], queries.shape[1])
    query_heads = heads_of(queries)

    def forward_fold(carry, piece, start):
        key_piece, value_piece = piece

        def visit(state, offset, count):
            other, touch = reaches(starts, query_seg, offset, count)

            def compute(state):
                top, total, accum = state
                key_block = heads_of(lax.dynamic_slice_in_dim(key_piece, offset, count, 1))
                value_block = heads_of(lax.dynamic_slice_in_dim(value_piece, offset, count, 1))
                scores = (
                    jnp.einsum(
                        "bqhd,bkhd->bhqk",
                        query_heads,
                        key_block,
                        preferred_element_type=jnp.float32,
                    )
                    * scale
                )
                mask = (query_seg[:, :, None] == other[:, None, :])[:, None]
                scores = jnp.where(mask, scores, NEG)
                new_top = jnp.maximum(top, jnp.max(scores, axis=-1))
                expd = jnp.where(mask, jnp.exp(scores - new_top[..., None]), 0.0)
                factor = jnp.exp(top - new_top)
                total = total * factor + jnp.sum(expd, axis=-1)
                added = jnp.einsum(
                    "bhqk,bkhd->bqhd",
                    expd.astype(jnp.bfloat16),
                    value_block,
                    preferred_element_type=jnp.float32,
                )
                accum = accum * jnp.transpose(factor, (0, 2, 1))[..., None] + added
                return (new_top, total, accum)

            return lax.cond(touch, compute, keep_state, state)

        return block_loop(key_piece.shape[1], carry, visit)

    init = (
        jnp.full((batch, HEADS, rows), NEG, jnp.float32),
        jnp.zeros((batch, HEADS, rows), jnp.float32),
        jnp.zeros((batch, rows, HEADS, HEAD_DIM), jnp.float32),
    )
    whole = (keys, values)
    top, total, accum = forward_fold(
        init,
        (
            lax.all_gather(keys, "ctx", axis=1, tiled=True),
            lax.all_gather(values, "ctx", axis=1, tiled=True),
        ),
        jnp.int32(0),
    )
    mixed = accum / jnp.transpose(total, (0, 2, 1))[..., None]
    return (mixed, top + jnp.log(total), whole)


def query_gradient(queries, query_seg, starts, keys, values, dmixed, logsum, delta):
    scale = HEAD_DIM ** (-0.5)
    query_heads = heads_of(queries)
    grad_heads = heads_of(dmixed)

    def query_fold(carry, piece, start):
        key_piece, value_piece = piece

        def visit(state, offset, count):
            other, touch = reaches(starts, query_seg, offset, count)

            def compute(state):
                key_block = heads_of(lax.dynamic_slice_in_dim(key_piece, offset, count, 1))
                value_block = heads_of(lax.dynamic_slice_in_dim(value_piece, offset, count, 1))
                scores = (
                    jnp.einsum(
                        "bqhd,bkhd->bhqk",
                        query_heads,
                        key_block,
                        preferred_element_type=jnp.float32,
                    )
                    * scale
                )
                mask = (query_seg[:, :, None] == other[:, None, :])[:, None]
                probs = jnp.where(
                    mask, jnp.exp(jnp.where(mask, scores, NEG) - logsum[..., None]), 0.0
                )
                dprobs = jnp.einsum(
                    "bqhd,bkhd->bhqk", grad_heads, value_block, preferred_element_type=jnp.float32
                )
                dscores = (probs * (dprobs - delta[..., None])).astype(jnp.bfloat16)
                return (
                    state
                    + jnp.einsum(
                        "bhqk,bkhd->bqhd", dscores, key_block, preferred_element_type=jnp.float32
                    )
                    * scale
                )

            return lax.cond(touch, compute, keep_state, state)

        return block_loop(key_piece.shape[1], carry, visit)

    init = jnp.zeros(query_heads.shape, jnp.float32)
    return query_fold(
        init,
        (
            lax.all_gather(keys, "ctx", axis=1, tiled=True),
            lax.all_gather(values, "ctx", axis=1, tiled=True),
        ),
        jnp.int32(0),
    )


def key_gradient(keys, values, key_seg, starts, queries, dmixed, logsum, delta):
    scale = HEAD_DIM ** (-0.5)
    key_heads = heads_of(keys)
    value_heads = heads_of(values)
    every_top, every_delta = (
        lax.all_gather(logsum, "ctx", axis=2, tiled=True),
        lax.all_gather(delta, "ctx", axis=2, tiled=True),
    )

    def key_fold(carry, piece, start):
        query_piece, grad_piece = piece

        def visit(state, offset, count):
            other, touch = reaches(starts, key_seg, offset, count)

            def compute(state):
                dkeys, dvalues = state
                query_block = heads_of(lax.dynamic_slice_in_dim(query_piece, offset, count, 1))
                grad_block = heads_of(lax.dynamic_slice_in_dim(grad_piece, offset, count, 1))
                top_block = lax.dynamic_slice_in_dim(every_top, offset, count, 2)
                delta_block = lax.dynamic_slice_in_dim(every_delta, offset, count, 2)
                scores = (
                    jnp.einsum(
                        "bqhd,bkhd->bhqk",
                        query_block,
                        key_heads,
                        preferred_element_type=jnp.float32,
                    )
                    * scale
                )
                mask = (other[:, :, None] == key_seg[:, None, :])[:, None]
                probs = jnp.where(
                    mask, jnp.exp(jnp.where(mask, scores, NEG) - top_block[..., None]), 0.0
                )
                dvalues = dvalues + jnp.einsum(
                    "bhqk,bqhd->bkhd",
                    probs.astype(jnp.bfloat16),
                    grad_block,
                    preferred_element_type=jnp.float32,
                )
                dprobs = jnp.einsum(
                    "bqhd,bkhd->bhqk", grad_block, value_heads, preferred_element_type=jnp.float32
                )
                dscores = (probs * (dprobs - delta_block[..., None])).astype(jnp.bfloat16)
                dkeys = (
                    dkeys
                    + jnp.einsum(
                        "bhqk,bqhd->bkhd", dscores, query_block, preferred_element_type=jnp.float32
                    )
                    * scale
                )
                return (dkeys, dvalues)

            return lax.cond(touch, compute, keep_state, state)

        return block_loop(query_piece.shape[1], carry, visit)

    empty = jnp.zeros(key_heads.shape, jnp.float32)
    return key_fold(
        (empty, empty),
        (
            lax.all_gather(queries, "ctx", axis=1, tiled=True),
            lax.all_gather(dmixed, "ctx", axis=1, tiled=True),
        ),
        jnp.int32(0),
    )


def forward_pass(tokens, starts, weights, base):
    (
        query_weight,
        query_bias,
        key_weight,
        value_weight,
        value_bias,
        out_weight,
        out_bias,
        first_gain,
        first_shift,
        inner_weight,
        inner_bias,
        outer_weight,
        outer_bias,
        second_gain,
        second_shift,
    ) = weights
    rows = tokens.shape[1]
    positions = base + jnp.arange(rows, dtype=jnp.int32)
    query_seg = segment_of(starts, jnp.broadcast_to(positions, (tokens.shape[0], rows)))
    queries = (project(tokens, query_weight) + query_bias.astype(jnp.float32)).astype(jnp.bfloat16)
    keys = project(tokens, key_weight).astype(jnp.bfloat16)
    values = (project(tokens, value_weight) + value_bias.astype(jnp.float32)).astype(jnp.bfloat16)
    mixed, logsum, whole = forward_attention(queries, query_seg, starts, keys, values)
    mixed_low = mixed.reshape(tokens.shape).astype(jnp.bfloat16)
    first_sum = (
        tokens.astype(jnp.float32) + project(mixed_low, out_weight) + out_bias.astype(jnp.float32)
    )
    first = normalize(first_sum, first_gain.astype(jnp.float32), first_shift.astype(jnp.float32))
    first_low = first.astype(jnp.bfloat16)
    inner = project(first_low, inner_weight) + inner_bias.astype(jnp.float32)
    active = gelu(inner).astype(jnp.bfloat16)
    second_sum = first + project(active, outer_weight) + outer_bias.astype(jnp.float32)
    output = normalize(
        second_sum, second_gain.astype(jnp.float32), second_shift.astype(jnp.float32)
    ).astype(jnp.bfloat16)
    saved = (
        tokens,
        query_seg,
        queries,
        keys,
        values,
        mixed,
        logsum,
        mixed_low,
        first_sum,
        first_low,
        inner,
        active,
        second_sum,
        whole,
    )
    return (output, saved)


def backward_pass(saved, starts, weights, cotangent):
    (
        query_weight,
        _,
        key_weight,
        value_weight,
        _,
        out_weight,
        _,
        first_gain,
        first_shift,
        inner_weight,
        _,
        outer_weight,
        _,
        second_gain,
        second_shift,
    ) = weights
    (
        tokens,
        query_seg,
        queries,
        keys,
        values,
        mixed,
        logsum,
        mixed_low,
        first_sum,
        first_low,
        inner,
        active,
        second_sum,
        _,
    ) = saved
    unused, second_back = jax.vjp(
        normalize, second_sum, second_gain.astype(jnp.float32), second_shift.astype(jnp.float32)
    )
    dsecond, dgain_second, dshift_second = second_back(cotangent.astype(jnp.float32))
    douter = dsecond.astype(jnp.bfloat16)
    dactive = project_back(douter, outer_weight)
    unused, gelu_back = jax.vjp(gelu, inner)
    dinner = gelu_back(dactive)[0].astype(jnp.bfloat16)
    dfirst = dsecond + project_back(dinner, inner_weight)
    unused, first_back = jax.vjp(
        normalize, first_sum, first_gain.astype(jnp.float32), first_shift.astype(jnp.float32)
    )
    dfirst_sum, dgain_first, dshift_first = first_back(dfirst)
    dbranch = dfirst_sum.astype(jnp.bfloat16)
    dmixed = project_back(dbranch, out_weight).astype(jnp.bfloat16)
    delta = jnp.einsum("bqhd,bqhd->bhq", heads_of(dmixed).astype(jnp.float32), mixed)
    dqueries = query_gradient(queries, query_seg, starts, keys, values, dmixed, logsum, delta)
    dkeys, dvalues = key_gradient(keys, values, query_seg, starts, queries, dmixed, logsum, delta)
    dqueries = dqueries.reshape(tokens.shape).astype(jnp.bfloat16)
    dkeys = dkeys.reshape(tokens.shape).astype(jnp.bfloat16)
    dvalues = dvalues.reshape(tokens.shape).astype(jnp.bfloat16)
    tokens_grad = (
        dfirst_sum
        + project_back(dqueries, query_weight)
        + project_back(dkeys, key_weight)
        + project_back(dvalues, value_weight)
    )
    sums = (
        outer_sum(tokens, dqueries),
        row_sum(dqueries),
        outer_sum(tokens, dkeys),
        outer_sum(tokens, dvalues),
        row_sum(dvalues),
        outer_sum(mixed_low, dbranch),
        row_sum(dbranch),
        dgain_first,
        dshift_first,
        outer_sum(first_low, dinner),
        row_sum(dinner),
        outer_sum(active, douter),
        row_sum(douter),
        dgain_second,
        dshift_second,
    )
    return (tokens_grad, sums)


def general_device(
    tokens,
    doc_lengths,
    query_weight,
    query_bias,
    key_weight,
    value_weight,
    value_bias,
    out_weight,
    out_bias,
    first_gain,
    first_shift,
    inner_weight,
    inner_bias,
    outer_weight,
    outer_bias,
    second_gain,
    second_shift,
    cotangent,
):
    params = (
        query_weight,
        query_bias,
        key_weight,
        value_weight,
        value_bias,
        out_weight,
        out_bias,
        first_gain,
        first_shift,
        inner_weight,
        inner_bias,
        outer_weight,
        outer_bias,
        second_gain,
        second_shift,
    )
    rows = tokens.shape[2]
    base = lax.axis_index("ctx") * rows
    lengths = doc_lengths[:, 0]
    starts = jnp.cumsum(lengths, axis=-1) - lengths
    outputs = []
    token_parts = []
    sums = None
    for index in range(tokens.shape[0]):
        weights = (
            lax.all_gather(params[0], "wt", axis=0, tiled=True),
            lax.all_gather(params[1], "wt", axis=0, tiled=True),
            lax.all_gather(params[2], "wt", axis=0, tiled=True),
            lax.all_gather(params[3], "wt", axis=0, tiled=True),
            lax.all_gather(params[4], "wt", axis=0, tiled=True),
            lax.all_gather(params[5], "wt", axis=0, tiled=True),
            lax.all_gather(params[6], "wt", axis=0, tiled=True),
            lax.all_gather(params[7], "wt", axis=0, tiled=True),
            lax.all_gather(params[8], "wt", axis=0, tiled=True),
            lax.all_gather(params[9], "wt", axis=0, tiled=True),
            lax.all_gather(params[10], "wt", axis=0, tiled=True),
            lax.all_gather(params[11], "wt", axis=0, tiled=True),
            lax.all_gather(params[12], "wt", axis=0, tiled=True),
            lax.all_gather(params[13], "wt", axis=0, tiled=True),
            lax.all_gather(params[14], "wt", axis=0, tiled=True),
        )
        part_out, saved = forward_pass(
            tokens[index : index + 1, 0], starts[index : index + 1], weights, base
        )
        again = (
            lax.all_gather(params[0], "wt", axis=0, tiled=True),
            lax.all_gather(params[1], "wt", axis=0, tiled=True),
            lax.all_gather(params[2], "wt", axis=0, tiled=True),
            lax.all_gather(params[3], "wt", axis=0, tiled=True),
            lax.all_gather(params[4], "wt", axis=0, tiled=True),
            lax.all_gather(params[5], "wt", axis=0, tiled=True),
            lax.all_gather(params[6], "wt", axis=0, tiled=True),
            lax.all_gather(params[7], "wt", axis=0, tiled=True),
            lax.all_gather(params[8], "wt", axis=0, tiled=True),
            lax.all_gather(params[9], "wt", axis=0, tiled=True),
            lax.all_gather(params[10], "wt", axis=0, tiled=True),
            lax.all_gather(params[11], "wt", axis=0, tiled=True),
            lax.all_gather(params[12], "wt", axis=0, tiled=True),
            lax.all_gather(params[13], "wt", axis=0, tiled=True),
            lax.all_gather(params[14], "wt", axis=0, tiled=True),
        )
        part_grad, part_sums = backward_pass(
            saved, starts[index : index + 1], again, cotangent[index : index + 1, 0]
        )
        outputs.append(part_out)
        token_parts.append(part_grad)
        sums = part_sums if sums is None else jax.tree.map(jnp.add, sums, part_sums)
    output = jnp.concatenate(outputs, axis=0)
    tokens_grad = jnp.concatenate(token_parts, axis=0)
    shards = jax.tree.map(
        lambda part: part.astype(jnp.float32),
        lax.psum_scatter(for_sending(sums), "wt", scatter_dimension=0, tiled=True),
    )
    totals = lax.psum(shards, "ctx")
    return (output[:, None], tokens_grad[:, None]) + tuple(totals)


def flip(value, bits):
    return lax.ppermute(value, "ctx", [(i, i ^ bits) for i in range(8)])


def turn(value, step):
    return lax.ppermute(value, "wt", [(i, (i - step) % 4) for i in range(4)])


def pick(value, index, axis=0):
    return lax.dynamic_index_in_dim(value, index, axis, keepdims=False)


def pair(own, other, bit, axis=0):
    return jnp.where(bit == 0, jnp.stack([own, other], axis), jnp.stack([other, own], axis))


def short(value):
    return value.astype(jnp.bfloat16)


def wide(value):
    return value.astype(jnp.float32)


def dot(left, right):
    return jnp.dot(left, right, preferred_element_type=jnp.float32)


def dot_back(left, right):
    return lax.dot_general(
        left, right, (((1,), (1,)), ((), ())), preferred_element_type=jnp.float32
    )


def dot_sum(left, right):
    return lax.dot_general(
        left, right, (((0,), (0,)), ((), ())), preferred_element_type=jnp.float32
    )


def norm_parts(rows):
    mean = jnp.mean(rows, axis=-1, keepdims=True)
    centered = rows - mean
    spread = jnp.mean(centered * centered, axis=-1, keepdims=True)
    root = lax.rsqrt(spread + EPS)
    return centered * root, root


def norm_back(upstream, normed, root, gain):
    grad = upstream * gain
    mean = jnp.mean(grad, axis=-1, keepdims=True)
    along = jnp.mean(grad * normed, axis=-1, keepdims=True)
    return root * (grad - mean - normed * along)


def gelu_parts(inner):
    rise = 0.5 * (1.0 + lax.erf(inner * ROOT_HALF))
    bell = jnp.exp(-0.5 * inner * inner) * (1.0 / math.sqrt(2.0 * math.pi))
    return inner * rise, rise + inner * bell


def run(kernel, outs, args, scratch=(), scalars=(), specs=None, out_specs=None):
    shapes = tuple(jax.ShapeDtypeStruct(shape, dtype) for shape, dtype in outs)
    whole = pl.BlockSpec(memory_space=pltpu.VMEM)
    in_specs = [pl.BlockSpec(memory_space=pltpu.SMEM)] * len(scalars)
    in_specs += [whole] * len(args) if specs is None else specs
    return pl.pallas_call(
        kernel,
        out_shape=shapes,
        in_specs=in_specs,
        out_specs=tuple([whole] * len(outs) if out_specs is None else out_specs),
        scratch_shapes=list(scratch),
    )(*scalars, *args)


WHOLE = pl.BlockSpec(memory_space=pltpu.VMEM)
LEFT = pl.BlockSpec(memory_space=pl.ANY)
BF = jnp.bfloat16
F32 = jnp.float32


def where_am_i():
    ctx, own = lax.axis_index("ctx"), lax.axis_index("wt")
    return ctx & 1, (ctx >> 1) & 3, ctx & 3, own


def some_rows(start, count):
    return pl.ds(pl.multiple_of(start, 16), count)


def prepare_heads_kernel(wq, wk, wv, vec, heads_own, heads_send):
    _, quarter, group, _ = where_am_i()
    shard, dim = wq.shape
    width = dim // 4
    for index in range(4):

        @pl.when(group == index)
        def _():
            for slot, ref in enumerate((wq, wk, wv)):
                heads_own[:, slot * width : (slot + 1) * width] = ref[
                    :, index * width : (index + 1) * width
                ]

    part = shard // 2
    heads_send[0:part, :] = heads_own[some_rows((quarter >> 1) * part, part), :]
    heads_send[part:, 0:width] = vec[...]
    heads_send[part:, width:] = jnp.zeros((16, 2 * width), BF)


def prepare_kernel(wo, wi, wo2, w2_send, inner_half, outer_half):
    core, quarter, _, _ = where_am_i()
    shard, dim = wo.shape
    half = wo2.shape[0] // 2
    for index in range(2):

        @pl.when(core == index)
        def _():
            for block in range(4):
                at = block * 2 * half + index * half
                inner_half[:, block * half : (block + 1) * half] = wi[:, at : at + half]
            outer_half[...] = wo2[index * half : (index + 1) * half, :]

    part = shard // 4
    rows = some_rows(quarter * part, part)
    w2_send[0:part, :] = inner_half[rows, 0:dim]
    w2_send[part : 2 * part, :] = inner_half[rows, dim:]
    step = half // 4
    w2_send[2 * part : 2 * part + step, :] = outer_half[some_rows(quarter * step, step), :]
    w2_send[2 * part + step :, :] = wo[rows, :]


CHUNK = 128
WINDOWS = (4, 6, 8)


def chunk_of(ctx, index):
    return ctx ^ ((index >> 2) | (index & 2) | ((index & 1) << 2))


def some_chunks(start, count):
    return pl.ds(pl.multiple_of(start * CHUNK, CHUNK), count * CHUNK)


def over_window(bounds, block, windows, visit):
    if len(windows) == 1:
        visit(pl.ds(0, windows[0] * CHUNK))
        return
    low, count = bounds[0, block], bounds[1, block]
    least = 0
    for size in windows:

        @pl.when((count > least) & (count <= size))
        def _(size=size):
            visit(some_chunks(jnp.minimum(low, windows[-1] - size), size))

        least = size


def attend_rows(qkv, seg_col, seg_row, far, outs, logsum, mixed):
    core, quarter, _, _ = where_am_i()
    scale = HEAD_DIM ** (-0.5)
    group = qkv.shape[0] // 3

    def step(side, carry):
        rows = some_chunks(2 * (2 * side + ((quarter & 1) ^ far)), 2)
        here = some_chunks(2 * side, 2)

        def one_head(head, carry):
            mask = seg_col[rows, :] == seg_row[...]
            scores = dot_back(qkv[head, rows, :], qkv[group + head])
            scores = jnp.where(mask, scores * scale, NEG)
            top = jnp.max(scores, axis=-1, keepdims=True)
            expd = jnp.exp(scores - top)
            total = jnp.sum(expd, axis=-1, keepdims=True)
            probs = short(expd * (1.0 / total))
            mixed[head, here, :] = short(dot(probs, qkv[2 * group + head]))
            lane = lax.broadcasted_iota(jnp.int32, (2 * CHUNK, 128), 1)
            logsum[here, :] = jnp.where(lane == head, top + jnp.log(total), logsum[here, :])
            return carry

        lax.fori_loop(0, group, one_head, 0)
        return carry

    logsum[...] = jnp.zeros_like(logsum)
    lax.fori_loop(0, 2, step, 0)
    y = quarter >> 1
    for index, out in enumerate(outs):
        for side in range(2):
            chunk = 2 * (y ^ side) + (core ^ index)
            for head in range(group):
                out[
                    side * CHUNK : (side + 1) * CHUNK, head * HEAD_DIM : (head + 1) * HEAD_DIM
                ] = mixed[head, some_chunks(chunk, 1), :]


def attend_near_kernel(
    mine, other, far, heads_own, g1, g2, g3, h1, h2, h3, bias, seg_col, seg_row,
    qkv, m0, m1, logsum, weight, mixed,
):
    _, quarter, _, own = where_am_i()
    ctx = lax.axis_index("ctx")
    shard = heads_own.shape[0]
    part = shard // 2
    y = quarter >> 1
    weight[some_rows(own * shard, shard), :] = heads_own[...]
    for step, near_half, far_half in ((1, g1, h1), (2, g2, h2), (3, g3, h3)):
        at = ((own + step) & 3) * shard
        weight[some_rows(at + part * y, part), :] = near_half[0:part, :]
        weight[some_rows(at + part * (1 - y), part), :] = far_half[0:part, :]
    index = 0
    for source in (mine, other, far):
        for first in range(0, source.shape[0], 2 * CHUNK):
            low = short(dot(source[first : first + 2 * CHUNK, :], weight[...]) + bias[...])
            for half in range(2):
                at = pl.multiple_of(chunk_of(ctx, index) * CHUNK, CHUNK)
                for slot in range(qkv.shape[0]):
                    qkv[slot, pl.ds(at, CHUNK), :] = low[
                        half * CHUNK : (half + 1) * CHUNK,
                        slot * HEAD_DIM : (slot + 1) * HEAD_DIM,
                    ]
                index += 1
    attend_rows(qkv, seg_col, seg_row, 0, (m0, m1), logsum, mixed)


def attend_far_kernel(qkv, seg_col, seg_row, m2, m3, logsum, mixed):
    attend_rows(qkv, seg_col, seg_row, 1, (m2, m3), logsum, mixed)


def project_kernel(m0, m1, m2, m3, mine, vec, wo, *refs):
    pieces, (first_sum, first_low, out_full, sems) = refs[:12], refs[12:]
    _, quarter, group, own = where_am_i()
    shard = wo.shape[0]
    part = shard // 4
    copies = [(wo, out_full.at[some_rows(own * shard, shard), :])]
    for index, piece in enumerate(pieces):
        at = ((own + 1 + index // 4) & 3) * shard + part * (quarter ^ (index % 4))
        rows = piece.shape[0]
        copies.append((piece.at[rows - part : rows, :], out_full.at[some_rows(at, part), :]))
    copies = [
        pltpu.make_async_copy(source, target, sems.at[index])
        for index, (source, target) in enumerate(copies)
    ]
    for copy in copies:
        copy.start()
    total = wide(mine[...]) + vec[2:3, :]
    for copy in copies:
        copy.wait()
    for code, ref in enumerate((m0, m1, m2, m3)):
        total += dot(ref[...], out_full[some_rows((group ^ code) * shard, shard), :])
    first_sum[...] = total
    first_low[...] = short(norm_parts(total)[0] * vec[3:4, :] + vec[4:5, :])


def forward_kernel(near, far, bias, inner_half, outer_half, *refs):
    pieces, (keep, send, slope, active, wi_full, wo2_full, wi, wo2, sems) = refs[:12], refs[12:]
    _, quarter, _, own = where_am_i()
    shard, half = inner_half.shape[0], outer_half.shape[0]
    dim = keep.shape[1]
    part, step = shard // 4, half // 4
    first = [(inner_half, wi.at[some_rows(own * shard, shard), :])]
    second = [(outer_half, wo2.at[some_rows(own * half, half), :])]
    for index, piece in enumerate(pieces):
        row, spot = (own + 1 + index // 4) & 3, quarter ^ (index % 4)
        rows = some_rows(row * shard + part * spot, part)
        for side in range(2):
            first.append(
                (
                    piece.at[side * part : (side + 1) * part, :],
                    wi.at[rows, side * dim : (side + 1) * dim],
                )
            )
        rows = some_rows(row * half + step * spot, step)
        second.append((piece.at[2 * part : 2 * part + step, :], wo2.at[rows, :]))
    copies = [
        pltpu.make_async_copy(source, target, sems.at[index])
        for index, (source, target) in enumerate(first + second)
    ]
    for copy in copies:
        copy.start()
    for copy in copies[: len(first)]:
        copy.wait()
    back = [
        pltpu.make_async_copy(wi, wi_full, sems.at[len(copies)]),
        pltpu.make_async_copy(wo2, wo2_full, sems.at[len(copies) + 1]),
    ]
    back[0].start()
    count = near.shape[0]
    chunk = 512
    waiting = True
    for index, (source, out) in enumerate(((far, send), (near, keep))):
        at = (1 - index) * count
        total = None
        for lane in range(0, slope.shape[1], chunk):
            lanes = slice(lane, lane + chunk)
            value, rate = gelu_parts(dot(source[...], wi[:, lanes]) + bias[:, lanes])
            low = short(value)
            slope[at : at + count, lanes] = short(rate)
            active[at : at + count, lanes] = low
            if waiting:
                for copy in copies[len(first) :]:
                    copy.wait()
                back[1].start()
                waiting = False
            added = dot(low, wo2[lanes, :])
            total = added if total is None else total + added
        out[...] = total
    for copy in back:
        copy.wait()


def turnaround_kernel(first_sum, keep, got, vec, cot0, cot1, out0, out1, dsecond, douter, sums):
    rows = cot0.shape[0]
    first = norm_parts(first_sum[...])[0] * vec[3:4, :] + vec[4:5, :]
    normed, root = norm_parts(first + vec[5:6, :] + keep[...] + got[...])
    output = short(normed * vec[6:7, :] + vec[7:8, :])
    out0[...] = output[:rows]
    out1[...] = output[rows:]
    upstream = jnp.concatenate([wide(cot0[...]), wide(cot1[...])])
    back = norm_back(upstream, normed, root, vec[6:7, :])
    low = short(back)
    dsecond[...] = back
    douter[...] = low
    sums[0:1, :] = jnp.sum(wide(low), axis=0, keepdims=True)
    sums[1:2, :] = jnp.sum(upstream * normed, axis=0, keepdims=True)
    sums[2:3, :] = jnp.sum(upstream, axis=0, keepdims=True)
    sums[3:, :] = jnp.zeros_like(sums[3:, :])


def backward_kernel(near, far, slope, wo2, wi_full, keep, send, dinner, sums, wi, sem):
    copy = pltpu.make_async_copy(wi_full, wi, sem)
    copy.start()
    count, dim = near.shape
    chunk = 512
    waiting = True
    for index, (source, out) in enumerate(((far, send), (near, keep))):
        at = (1 - index) * count
        total = None
        for lane in range(0, slope.shape[1], chunk):
            lanes = slice(lane, lane + chunk)
            rate = wide(slope[at : at + count, lanes])
            low = short(dot_back(source[...], wo2[lanes, :]) * rate)
            dinner[at : at + count, lanes] = low
            if waiting:
                copy.wait()
                waiting = False
            added = dot_back(low, wi[:, lanes])
            total = added if total is None else total + added
        out[...] = total
    total = jnp.sum(wide(dinner[...]), axis=0, keepdims=True)
    sums[0:1, :] = total[:, :dim]
    sums[1:2, :] = total[:, dim:]
    sums[2:, :] = jnp.zeros_like(sums[2:, :])


def weights_kernel(first0, first1, douter0, douter1, dinner, active, ak, az, bk, bz, left, right):
    _, quarter, _, _ = where_am_i()
    x, y = quarter & 1, quarter >> 1
    count = first0.shape[0]
    part, step = first0.shape[1] // 16, active.shape[1] // 16
    left[...] = short(dot_sum(first0[...], dinner[:count]) + dot_sum(first1[...], dinner[count:]))
    for block in range(8):
        rows = slice(block * part, (block + 1) * part)
        ak[rows, :] = left[some_rows((2 * block + x) * part, part), :]
        az[rows, :] = left[some_rows((2 * block + 1 - x) * part, part), :]
    right[...] = short(
        dot_sum(active[:count], douter0[...]) + dot_sum(active[count:], douter1[...])
    )
    for block in range(8):
        row, side = block // 2, block % 2
        rows = slice(block * step, (block + 1) * step)
        bk[rows, :] = right[some_rows((4 * row + 2 * y + side) * step, step), :]
        bz[rows, :] = right[some_rows((4 * row + 2 * (1 - y) + side) * step, step), :]


def branch_kernel(first_sum, dsecond, keep, got, vec, out_full, dfirst_sum, dbranch, d0, d1, d2, d3, sums):
    _, _, group, _ = where_am_i()
    shard = d0.shape[1]
    normed, root = norm_parts(first_sum[...])
    dfirst = dsecond[...] + keep[...] + got[...]
    back = norm_back(dfirst, normed, root, vec[3:4, :])
    low = short(back)
    dfirst_sum[...] = back
    dbranch[...] = low
    for code, ref in enumerate((d0, d1, d2, d3)):
        ref[...] = short(dot_back(low, out_full[some_rows((group ^ code) * shard, shard), :]))
    sums[0:1, :] = jnp.sum(wide(low), axis=0, keepdims=True)
    sums[1:2, :] = jnp.sum(dfirst * normed, axis=0, keepdims=True)
    sums[2:3, :] = jnp.sum(dfirst, axis=0, keepdims=True)
    sums[3:, :] = jnp.zeros_like(sums[3:, :])


def out_weight_kernel(m0, m1, m2, m3, dbranch, sums1, sums2, sums3, ck, cz, whole):
    core, _, group, _ = where_am_i()
    shard, dim = m0.shape[1], dbranch.shape[1]
    half = dim // 2
    for code, ref in enumerate((m0, m1, m2, m3)):
        whole[some_rows((group ^ code) * shard, shard), :] = short(
            dot_sum(ref[...], dbranch[...])
        )
    for side in range(2):

        @pl.when(core == side)
        def _():
            for ref, which in ((ck, side), (cz, 1 - side)):
                ref[0:dim, :] = whole[:, which * half : (which + 1) * half]

    rows = short(
        jnp.concatenate([sums1[0:3, :], sums2[0:3, :], sums3[0:2, :], jnp.zeros_like(sums1[...])])
    )
    for ref in (ck, cz):
        ref[dim : dim + 16, :] = rows[:, :half]
        ref[dim + 16 :, :] = rows[:, half:]


def out_split_kernel(packed, got, ck, cz):
    core, quarter, _, _ = where_am_i()
    x = quarter & 1
    dim = packed.shape[0] - 32
    part = dim // 16
    for block in range(8):
        rows = slice(block * part, (block + 1) * part)
        for ref, side in ((ck, x), (cz, 1 - x)):
            take = some_rows((2 * block + side) * part, part)
            ref[rows, :] = short(wide(packed[take, :]) + wide(got[take, :]))
    for lanes in range(2):
        at = dim + 16 * lanes
        mine, other = wide(packed[at : at + 16, :]), wide(got[at : at + 16, :])
        low = jnp.where(core == 0, mine, other)[6:8]
        high = jnp.where(core == 0, other, mine)[6:8]
        rows = jnp.concatenate([(mine + other)[0:6], low, high, jnp.zeros_like(mine[0:6])])
        at = 8 * part + 16 * lanes
        for ref in (ck, cz):
            ref[at : at + 16, :] = short(rows)


def reduce_rows(keep, got, outs, bit):
    size = keep.shape[0] // 8
    size -= size % 16
    width = keep.shape[1] // len(outs)
    for lane, pair_of in enumerate(outs):
        lanes = slice(lane * width, (lane + 1) * width)
        for block in range(4):
            for out, side in zip(pair_of, (bit, 1 - bit)):
                take = some_rows((2 * block + side) * size, size)
                out[block * size : (block + 1) * size, :] = short(
                    wide(keep[take, lanes]) + wide(got[take, lanes])
                )
        if keep.shape[0] > 8 * size:
            for out in pair_of:
                out[4 * size :, :] = short(
                    wide(keep[8 * size :, lanes]) + wide(got[8 * size :, lanes])
                )


def reduce_kernel(ak, ar, bk, br, *outs):
    _, quarter, _, _ = where_am_i()
    reduce_rows(ak, ar, (outs[0:2], outs[4:6]), quarter >> 1)
    reduce_rows(bk, br, (outs[2:4], outs[6:8]), quarter & 1)


def reduce_out_kernel(ck, cr, c2k, c2z):
    _, quarter, _, _ = where_am_i()
    reduce_rows(ck, cr, ((c2k, c2z),), quarter >> 1)


def owners_kernel(*refs):
    inputs, outs = refs[:-4], refs[-4:]
    _, _, _, own = where_am_i()
    ak, ar, bk, br = inputs[:4]
    half = bk.shape[1]
    part = ak.shape[0] // 4
    for index, out in enumerate(outs):
        row = (own - index) & 3
        rows = some_rows(row * part, part)
        out[0:part, :] = (wide(ak[rows, :]) + wide(ar[rows, :])).astype(out.dtype)
        for side in range(2):
            rows = some_rows((2 * row + side) * part, part)
            out[part : 2 * part, side * half : (side + 1) * half] = (
                wide(bk[rows, :]) + wide(br[rows, :])
            ).astype(out.dtype)
        if len(inputs) > 4:
            ck, cr = inputs[4:]
            at = 2 * part
            rows = some_rows(row * part, part)
            out[at:, 0:half] = (wide(ck[rows, :]) + wide(cr[rows, :])).astype(out.dtype)
            tail = wide(ck[4 * part :, :]) + wide(cr[4 * part :, :])
            out[at : at + 32, half:] = tail.astype(out.dtype)
            out[at + 32 :, half:] = jnp.zeros((part - 32, half), out.dtype)


def total_kernel(mine, *refs):
    total = wide(mine[...])
    for ref in refs[:-1]:
        total += wide(ref[...])
    refs[-1][...] = short(total)


def finish_kernel(*refs):
    pieces, (dwi, dwo2, dwo, small) = refs[:16], refs[16:]
    core, quarter, _, _ = where_am_i()
    part, half = dwi.shape[0] // 4, dwi.shape[1] // 8
    for side in range(2):

        @pl.when(core == side)
        def _():
            for index, piece in enumerate(pieces):
                lane, index = index // 8, index % 8
                spot = quarter ^ (index % 4)
                which = side if index < 4 else 1 - side
                rows = some_rows(spot * part, part)
                for block in range(2):
                    at = (2 * lane + block) * 2 * half + which * half
                    dwi[rows, at : at + half] = wide(piece[0:part, block * half : (block + 1) * half])
                    at = which * half + spot * 2 * part + block * part
                    dwo2[some_rows(at, part), lane * half : (lane + 1) * half] = wide(
                        piece[part : 2 * part, block * half : (block + 1) * half]
                    )
                if lane == 1:
                    dwo[rows, which * half : (which + 1) * half] = wide(piece[2 * part :, 0:half])

    last = pieces[8]
    small[:, 0:half] = wide(last[2 * part : 2 * part + 16, half:])
    small[:, half:] = wide(last[2 * part + 16 : 2 * part + 32, half:])


def attend_back_kernel(
    bounds, qkv, logsum0, logsum1, seg_col, seg_row, p0, p1, p2, p3, mine, other, far,
    h0, h1, h2, h3, grads, dqueries, dkeys, dvalues, dweight, dmixed, logsum, whole,
):
    _, quarter, _, own = where_am_i()
    ctx = lax.axis_index("ctx")
    x = quarter & 1
    scale = HEAD_DIM ** (-0.5)
    group = qkv.shape[0] // 3
    width = group * HEAD_DIM
    block = p0.shape[0]
    dkeys[...] = jnp.zeros_like(dkeys)
    dvalues[...] = jnp.zeros_like(dvalues)
    for index, part in enumerate((p0, p2, p1, p3)):
        for side in range(2):
            chunk = chunk_of(ctx, 2 * index + side)
            for head in range(group):
                dmixed[head, some_chunks(chunk, 1), :] = part[
                    side * CHUNK : (side + 1) * CHUNK, head * HEAD_DIM : (head + 1) * HEAD_DIM
                ]
    for side in range(2):
        rows = slice(2 * side * CHUNK, 2 * (side + 1) * CHUNK)
        logsum[some_chunks(2 * (2 * side + x), 2), :] = logsum0[rows, :]
        logsum[some_chunks(2 * (2 * side + 1 - x), 2), :] = logsum1[rows, :]

    def step(index, carry):
        rows = some_chunks(2 * index, 2)

        def visit(window):
            def one_head(head, carry):
                mask = seg_col[rows, :] == seg_row[:, window]
                query = qkv[head, rows, :]
                grad = dmixed[head, rows, :]
                keys = qkv[group + head, window, :]
                lane = lax.broadcasted_iota(jnp.int32, (2 * CHUNK, 128), 1)
                sums = jnp.sum(
                    jnp.where(lane == head, logsum[rows, :], 0.0), axis=-1, keepdims=True
                )
                scores = jnp.where(mask, dot_back(query, keys) * scale, NEG)
                probs = jnp.exp(scores - sums)
                dprobs = dot_back(grad, qkv[2 * group + head, window, :])
                delta = jnp.sum(probs * dprobs, axis=-1, keepdims=True)
                dscores = short(probs * (dprobs - delta))
                dqueries[head, rows, :] = short(dot(dscores, keys) * scale)
                dkeys[head, window, :] += dot_sum(dscores, query)
                dvalues[head, window, :] += dot_sum(short(probs), grad)
                return carry

            lax.fori_loop(0, group, one_head, 0)

        over_window(bounds, index, WINDOWS, visit)
        return carry

    lax.fori_loop(0, 4, step, 0)
    for head in range(group):
        whole[:, head * HEAD_DIM : (head + 1) * HEAD_DIM] = dqueries[head]
        at = width + head * HEAD_DIM
        whole[:, at : at + HEAD_DIM] = short(dkeys[head] * scale)
        whole[:, at + width : at + width + HEAD_DIM] = short(dvalues[head])
    for index in range(8):
        grads[index * CHUNK : (index + 1) * CHUNK, :] = whole[
            some_chunks(chunk_of(ctx, index), 1), :
        ]
    rows = 2 * block
    dweight[...] = (
        dot_sum(mine[...], grads[:block])
        + dot_sum(other[...], grads[block:rows])
        + dot_sum(far[...], grads[rows:])
    )
    sums = jnp.sum(wide(grads[...]), axis=0, keepdims=True)
    tail = jnp.concatenate([sums, jnp.zeros((15, sums.shape[1]), F32)])
    for index, out in enumerate((h0, h1, h2, h3)):
        take = pl.ds(pl.multiple_of(((own - index) & 3) * width, 16), width)
        out[0:width, :] = dweight[take, :].astype(out.dtype)
        out[width:, :] = tail.astype(out.dtype)


def tokens_kernel(grads, weight, keep, send):
    rows = keep.shape[0]
    keep[...] = dot_back(grads[:rows], weight[...])
    send[...] = short(dot_back(grads[rows:], weight[...]))


def merge_kernel(keep, got, base, near, far):
    total = keep[...] + wide(got[...])
    count = near.shape[0]
    near[...] = total[:count] + base[...]
    far[...] = short(total[count:])


def heads_kernel(s0, s1, s2, s3, dq, dk, dv, bias):
    _, _, group, own = where_am_i()
    shard = dq.shape[0]
    for index in range(4):

        @pl.when(group == index)
        def _():
            for code, ref in enumerate((s0, s1, s2, s3)):
                at = (index ^ code) * shard
                for slot, out in enumerate((dq, dk, dv)):
                    out[:, at : at + shard] = wide(
                        ref[0:shard, slot * shard : (slot + 1) * shard]
                    )

                @pl.when(own == index ^ code)
                def _():
                    bias[...] = wide(ref[shard:, :])


def plane_steps(
    tokens,
    doc_lengths,
    query_weight,
    query_bias,
    key_weight,
    value_weight,
    value_bias,
    out_weight,
    out_bias,
    first_gain,
    first_shift,
    inner_weight,
    inner_bias,
    outer_weight,
    outer_bias,
    second_gain,
    second_shift,
    cotangent,
):
    ctx, own = lax.axis_index("ctx"), lax.axis_index("wt")
    core, y, group = ctx & 1, ctx >> 2, ctx & 3
    rows, dim = tokens.shape[2], tokens.shape[3]
    shard = query_weight.shape[0]
    hidden = outer_weight.shape[0]
    half = hidden // 2
    count = 2 * rows

    mine = jnp.concatenate([pick(tokens[:, 0], y), flip(pick(tokens[:, 0], 1 - y), 4)])
    other = flip(mine, 2)
    far = flip(jnp.concatenate([mine, other]), 1)

    vector_list = (
        query_bias,
        value_bias,
        out_bias,
        first_gain,
        first_shift,
        outer_bias,
        second_gain,
        second_shift,
        *[inner_bias[at : at + shard] for at in range(0, 4 * shard, shard)],
    )
    line = lax.broadcasted_iota(jnp.int32, (16, shard), 0)
    vec = jnp.zeros((16, shard), BF)
    for index, value in enumerate(vector_list):
        vec = jnp.where(line == index, value[None, :], vec)
    heads_own, heads_send = run(
        prepare_heads_kernel,
        [((shard, 3 * shard), BF), ((shard // 2 + 16, 3 * shard), BF)],
        (query_weight, key_weight, value_weight, vec),
    )
    w2_send, inner_half, outer_half = run(
        prepare_kernel,
        [((shard // 4 * 3 + half // 4, dim), BF), ((shard, 4 * half), BF), ((half, dim), BF)],
        (out_weight, inner_weight, outer_weight),
    )
    got = [turn(heads_send, step) for step in (1, 2, 3)]
    gone = [flip(value, 4) for value in got]
    pieces = []
    for step in (1, 2, 3):
        piece = turn(w2_send, step)
        pieces += [piece] + [flip(piece, bits) for bits in (2, 4, 6)]

    at = shard // 2
    rel = jnp.stack([vec] + [value[at:, :shard] for value in got])
    vectors = wide(lax.dynamic_slice_in_dim(jnp.concatenate([rel, rel]), (4 - own) % 4, 4))
    mine_b = pick(vectors, group)
    heads_bias = jnp.concatenate([mine_b[0], jnp.zeros_like(mine_b[0]), mine_b[1]])[None]
    inner_b = pick(vectors[:, 8:12].reshape(4, 2, half), core, 1).reshape(1, 4 * half)
    vectors = jnp.swapaxes(vectors[:, :8], 0, 1).reshape(8, dim)

    lengths = pick(doc_lengths[:, 0], y)
    starts = jnp.cumsum(lengths) - lengths
    total = 8 * rows
    positions = jnp.arange(total, dtype=jnp.int32)
    seg = jnp.sum((starts[None, :] <= positions[:, None]).astype(jnp.int32), axis=-1) - 1
    segs = (seg[:, None], seg[None, :])
    first = jnp.arange(4, dtype=jnp.int32)[:, None] * (2 * CHUNK)
    low = jnp.max(jnp.where(starts[None, :] <= first, starts[None, :], 0), axis=-1) // CHUNK
    ends = jnp.where(starts[None, :] >= first + 2 * CHUNK, starts[None, :], total)
    bounds = jnp.stack([low, (jnp.min(ends, axis=-1) - 1) // CHUNK - low + 1])

    qkv, m0, m1, logsum0, heads_weight = run(
        attend_near_kernel,
        [
            ((9, total, HEAD_DIM), BF),
            ((count, shard), BF),
            ((count, shard), BF),
            ((2 * count, 128), F32),
            ((dim, 3 * shard), BF),
        ],
        (mine, other, far, heads_own, *got, *gone, heads_bias, *segs),
        [pltpu.VMEM((3, 2 * count, HEAD_DIM), BF)],
    )
    m2, m3, logsum1 = run(
        attend_far_kernel,
        [((count, shard), BF), ((count, shard), BF), ((2 * count, 128), F32)],
        (qkv, *segs),
        [pltpu.VMEM((3, 2 * count, HEAD_DIM), BF)],
    )
    mixed = [m0, flip(m1, 1), flip(m2, 2), flip(m3, 3)]

    first_sum, first_low, out_full = run(
        project_kernel,
        [((count, dim), F32), ((count, dim), BF), ((dim, dim), BF)],
        (*mixed, mine, vectors, out_weight, *pieces),
        [pltpu.SemaphoreType.DMA((13,))],
        specs=[WHOLE] * 6 + [LEFT] * 13,
    )
    first_far = flip(first_low, 1)
    keep, send, slope, active, wi_full, wo2_full = run(
        forward_kernel,
        [
            ((count, dim), F32),
            ((count, dim), F32),
            ((2 * count, 4 * half), BF),
            ((2 * count, 4 * half), BF),
            ((dim, 4 * half), BF),
            ((4 * half, dim), BF),
        ],
        (first_low, first_far, inner_b, inner_half, outer_half, *pieces),
        [
            pltpu.VMEM((dim, 4 * half), BF),
            pltpu.VMEM((4 * half, dim), BF),
            pltpu.SemaphoreType.DMA((40,)),
        ],
        specs=[WHOLE] * 3 + [LEFT] * 14,
        out_specs=[WHOLE] * 4 + [LEFT] * 2,
    )
    cot = pick(cotangent[:, 0], y), flip(pick(cotangent[:, 0], 1 - y), 4)
    out0, out1, dsecond, douter, sums2 = run(
        turnaround_kernel,
        [
            ((rows, dim), BF),
            ((rows, dim), BF),
            ((count, dim), F32),
            ((count, dim), BF),
            ((8, dim), F32),
        ],
        (first_sum, keep, flip(send, 1), vectors, *cot),
    )
    output = pair(out0, flip(out1, 4), y)

    douter_far = flip(douter, 1)
    keep, send, dinner, sums3 = run(
        backward_kernel,
        [
            ((count, dim), F32),
            ((count, dim), F32),
            ((2 * count, 4 * half), BF),
            ((8, dim), F32),
        ],
        (douter, douter_far, slope, wo2_full, wi_full),
        [pltpu.VMEM((dim, 4 * half), BF), pltpu.SemaphoreType.DMA],
        specs=[WHOLE] * 4 + [LEFT],
    )
    dfirst_sum, dbranch, d0, d1, d2, d3, sums1 = run(
        branch_kernel,
        [((count, dim), F32), ((count, dim), BF)] + [((count, shard), BF)] * 4 + [((8, dim), F32)],
        (first_sum, dsecond, keep, flip(send, 1), vectors, out_full),
    )
    dmixed = [d0, flip(d1, 1), flip(d2, 2), flip(d3, 3)]

    ak, az, bk, bz = run(
        weights_kernel,
        [((dim // 2, 4 * half), BF)] * 2 + [((2 * half, dim), BF)] * 2,
        (first_low, first_far, douter, douter_far, dinner, active),
        [pltpu.VMEM((dim, 4 * half), BF), pltpu.VMEM((4 * half, dim), BF)],
    )
    ar, br = flip(az, 2), flip(bz, 4)
    ck, cz = run(
        out_weight_kernel,
        [((dim + 32, dim // 2), BF)] * 2,
        (*mixed, dbranch, sums1, sums2, sums3),
        [pltpu.VMEM((dim, dim), BF)],
    )
    ck, cz = run(out_split_kernel, [((dim // 2 + 32, dim // 2), BF)] * 2, (ck, flip(cz, 1)))
    cr = flip(cz, 2)

    h0, h1, h2, h3, grads = run(
        attend_back_kernel,
        [((shard + 16, 3 * shard), F32)]
        + [((shard + 16, 3 * shard), BF)] * 3
        + [((4 * count, 3 * shard), BF)],
        (qkv, logsum0, logsum1, *segs, *dmixed, mine, other, far),
        [
            pltpu.VMEM((3, 4 * count, HEAD_DIM), BF),
            pltpu.VMEM((3, 4 * count, HEAD_DIM), F32),
            pltpu.VMEM((3, 4 * count, HEAD_DIM), F32),
            pltpu.VMEM((dim, 3 * shard), F32),
            pltpu.VMEM((3, total, HEAD_DIM), BF),
            pltpu.VMEM((total, 128), F32),
            pltpu.VMEM((total, 3 * shard), BF),
        ],
        scalars=(bounds,),
    )
    keep, send = run(
        tokens_kernel, [((2 * count, dim), F32), ((2 * count, dim), BF)], (grads, heads_weight)
    )

    c2k, c2z = run(reduce_out_kernel, [((dim // 4 + 32, dim // 2), BF)] * 2, (ck, cr))
    reduced = run(
        reduce_kernel,
        ([((dim // 4, 2 * half), BF)] * 2 + [((half, dim // 2), BF)] * 2) * 2,
        (ak, ar, bk, br),
    )
    plane = []
    for lane in range(2):
        a2k, a2z, b2k, b2z = reduced[4 * lane : 4 * lane + 4]
        last = [a2k, flip(a2z, 4), b2k, flip(b2z, 2)]
        size = shard // 4 * 2
        if lane == 1:
            last += [c2k, flip(c2z, 4)]
            size = shard // 4 * 3
        p0, p1, p2, p3 = run(owners_kernel, [((size, dim), F32)] + [((size, dim), BF)] * 3, last)
        turned = [turn(p, step) for step, p in ((1, p1), (2, p2), (3, p3))]
        (piece,) = run(total_kernel, [((size, dim), BF)], (p0, *turned))
        near = [piece] + [flip(piece, bits) for bits in (2, 4, 6)]
        plane += near + [flip(p, 1) for p in near]
    dinner_w, douter_w, dout_w, small = run(
        finish_kernel,
        [((shard, 8 * half), F32), ((hidden, dim), F32), ((shard, dim), F32), ((16, dim), F32)],
        plane,
    )
    dinner_b = pick(small[6:10].reshape(2, 4, half), own, 1).reshape(hidden)
    small = lax.dynamic_slice_in_dim(small[:6], own * shard, shard, 1)

    (heads,) = run(
        total_kernel, [((shard + 16, 3 * shard), BF)], (h0, turn(h1, 1), turn(h2, 2), turn(h3, 3))
    )
    (heads,) = run(total_kernel, [((shard + 16, 3 * shard), BF)], (heads, flip(heads, 4)))
    dquery_w, dkey_w, dvalue_w, heads_b = run(
        heads_kernel,
        [((shard, dim), F32)] * 3 + [((16, 3 * shard), F32)],
        (heads, flip(heads, 1), flip(heads, 2), flip(heads, 3)),
    )

    near_t, far_t = run(
        merge_kernel, [((count, dim), F32), ((count, dim), BF)], (keep, flip(send, 1), dfirst_sum)
    )
    dtokens = near_t + wide(flip(far_t, 2))
    tokens_grad = pair(dtokens[:rows], wide(flip(short(dtokens[rows:]), 4)), y)

    return (
        output[:, None],
        tokens_grad[:, None],
        dquery_w,
        heads_b[0, :shard],
        dkey_w,
        dvalue_w,
        heads_b[0, 2 * shard :],
        dout_w,
        small[0],
        small[1],
        small[2],
        dinner_w,
        dinner_b,
        douter_w,
        small[3],
        small[4],
        small[5],
    )


def plane_device(*args):
    return plane_steps(*args)


def solution(mesh):
    placed = (
        P(None, "wt", "ctx", None),
        P(None, "wt", None),
        P("wt", None),
        P("wt"),
        P("wt", None),
        P("wt", None),
        P("wt"),
        P("wt", None),
        P("wt"),
        P("wt"),
        P("wt"),
        P("wt", None),
        P("wt"),
        P("wt", None),
        P("wt"),
        P("wt"),
        P("wt"),
        P(None, "wt", "ctx", None),
    )
    fits = mesh.shape["ctx"] == 8 and mesh.shape["wt"] == 4
    return jax.shard_map(
        plane_device if fits else general_device,
        mesh=mesh,
        in_specs=placed,
        out_specs=(
            P(None, "wt", "ctx", None),
            P(None, "wt", "ctx", None),
            P("wt", None),
            P("wt"),
            P("wt", None),
            P("wt", None),
            P("wt"),
            P("wt", None),
            P("wt"),
            P("wt"),
            P("wt"),
            P("wt", None),
            P("wt"),
            P("wt", None),
            P("wt"),
            P("wt"),
            P("wt"),
        ),
        check_vma=False,
    )
```

```python
import math

import jax
import jax.numpy as jnp
from jax import lax
from jax.experimental import pallas as pl
from jax.experimental.pallas import tpu as pltpu
from jax.sharding import PartitionSpec as P


HEADS = 12
HEAD_DIM = 64


EPS = 1e-12
NEG = -1e30
ROOT_HALF = 0.7071067811865476


def for_sending(shard):

    def short(part):
        return part.astype(jnp.bfloat16) if part.dtype == jnp.float32 else part

    return jax.tree.map(short, shard)


def normalize(rows, gain, shift):
    mean = jnp.mean(rows, axis=-1, keepdims=True)
    centered = rows - mean
    spread = jnp.mean(centered * centered, axis=-1, keepdims=True)
    return centered * lax.rsqrt(spread + EPS) * gain + shift


def gelu(inner):
    return 0.5 * inner * (1.0 + lax.erf(inner * ROOT_HALF))


def segment_of(starts, positions):
    found = (starts[:, None, :] <= positions[:, :, None]).astype(jnp.int32)
    return jnp.sum(found, axis=-1) - 1


def project(inputs, weight):
    return jnp.einsum("btd,de->bte", inputs, weight, preferred_element_type=jnp.float32)


def project_back(grads, weight):
    return jnp.einsum("bte,de->btd", grads, weight, preferred_element_type=jnp.float32)


def outer_sum(inputs, grads):
    return jnp.einsum("btd,bte->de", inputs, grads, preferred_element_type=jnp.float32)


def row_sum(grads):
    return jnp.sum(grads.astype(jnp.float32), axis=(0, 1))


def heads_of(array):
    return array.reshape(array.shape[0], array.shape[1], HEADS, HEAD_DIM)


def block_loop(width, carry, visit):
    block = math.gcd(width, 512)

    def step(state, index):
        return (visit(state, index * block, block), None)

    carry, _ = lax.scan(step, carry, jnp.arange(width // block, dtype=jnp.int32))
    return carry


def reaches(starts, own_seg, first, count):
    positions = first + jnp.arange(count, dtype=jnp.int32)
    other = segment_of(starts, jnp.broadcast_to(positions, (starts.shape[0], count)))
    touch = jnp.any((other[:, 0] <= own_seg[:, -1]) & (other[:, -1] >= own_seg[:, 0]))
    return (other, touch)


def keep_state(state):
    return state


def forward_attention(queries, query_seg, starts, keys, values):
    scale = HEAD_DIM ** (-0.5)
    batch, rows = (queries.shape[0], queries.shape[1])
    query_heads = heads_of(queries)

    def forward_fold(carry, piece, start):
        key_piece, value_piece = piece

        def visit(state, offset, count):
            other, touch = reaches(starts, query_seg, offset, count)

            def compute(state):
                top, total, accum = state
                key_block = heads_of(lax.dynamic_slice_in_dim(key_piece, offset, count, 1))
                value_block = heads_of(lax.dynamic_slice_in_dim(value_piece, offset, count, 1))
                scores = (
                    jnp.einsum(
                        "bqhd,bkhd->bhqk",
                        query_heads,
                        key_block,
                        preferred_element_type=jnp.float32,
                    )
                    * scale
                )
                mask = (query_seg[:, :, None] == other[:, None, :])[:, None]
                scores = jnp.where(mask, scores, NEG)
                new_top = jnp.maximum(top, jnp.max(scores, axis=-1))
                expd = jnp.where(mask, jnp.exp(scores - new_top[..., None]), 0.0)
                factor = jnp.exp(top - new_top)
                total = total * factor + jnp.sum(expd, axis=-1)
                added = jnp.einsum(
                    "bhqk,bkhd->bqhd",
                    expd.astype(jnp.bfloat16),
                    value_block,
                    preferred_element_type=jnp.float32,
                )
                accum = accum * jnp.transpose(factor, (0, 2, 1))[..., None] + added
                return (new_top, total, accum)

            return lax.cond(touch, compute, keep_state, state)

        return block_loop(key_piece.shape[1], carry, visit)

    init = (
        jnp.full((batch, HEADS, rows), NEG, jnp.float32),
        jnp.zeros((batch, HEADS, rows), jnp.float32),
        jnp.zeros((batch, rows, HEADS, HEAD_DIM), jnp.float32),
    )
    whole = (keys, values)
    top, total, accum = forward_fold(
        init,
        (
            lax.all_gather(keys, "ctx", axis=1, tiled=True),
            lax.all_gather(values, "ctx", axis=1, tiled=True),
        ),
        jnp.int32(0),
    )
    mixed = accum / jnp.transpose(total, (0, 2, 1))[..., None]
    return (mixed, top + jnp.log(total), whole)


def query_gradient(queries, query_seg, starts, keys, values, dmixed, logsum, delta):
    scale = HEAD_DIM ** (-0.5)
    query_heads = heads_of(queries)
    grad_heads = heads_of(dmixed)

    def query_fold(carry, piece, start):
        key_piece, value_piece = piece

        def visit(state, offset, count):
            other, touch = reaches(starts, query_seg, offset, count)

            def compute(state):
                key_block = heads_of(lax.dynamic_slice_in_dim(key_piece, offset, count, 1))
                value_block = heads_of(lax.dynamic_slice_in_dim(value_piece, offset, count, 1))
                scores = (
                    jnp.einsum(
                        "bqhd,bkhd->bhqk",
                        query_heads,
                        key_block,
                        preferred_element_type=jnp.float32,
                    )
                    * scale
                )
                mask = (query_seg[:, :, None] == other[:, None, :])[:, None]
                probs = jnp.where(
                    mask, jnp.exp(jnp.where(mask, scores, NEG) - logsum[..., None]), 0.0
                )
                dprobs = jnp.einsum(
                    "bqhd,bkhd->bhqk", grad_heads, value_block, preferred_element_type=jnp.float32
                )
                dscores = (probs * (dprobs - delta[..., None])).astype(jnp.bfloat16)
                return (
                    state
                    + jnp.einsum(
                        "bhqk,bkhd->bqhd", dscores, key_block, preferred_element_type=jnp.float32
                    )
                    * scale
                )

            return lax.cond(touch, compute, keep_state, state)

        return block_loop(key_piece.shape[1], carry, visit)

    init = jnp.zeros(query_heads.shape, jnp.float32)
    return query_fold(
        init,
        (
            lax.all_gather(keys, "ctx", axis=1, tiled=True),
            lax.all_gather(values, "ctx", axis=1, tiled=True),
        ),
        jnp.int32(0),
    )


def key_gradient(keys, values, key_seg, starts, queries, dmixed, logsum, delta):
    scale = HEAD_DIM ** (-0.5)
    key_heads = heads_of(keys)
    value_heads = heads_of(values)
    every_top, every_delta = (
        lax.all_gather(logsum, "ctx", axis=2, tiled=True),
        lax.all_gather(delta, "ctx", axis=2, tiled=True),
    )

    def key_fold(carry, piece, start):
        query_piece, grad_piece = piece

        def visit(state, offset, count):
            other, touch = reaches(starts, key_seg, offset, count)

            def compute(state):
                dkeys, dvalues = state
                query_block = heads_of(lax.dynamic_slice_in_dim(query_piece, offset, count, 1))
                grad_block = heads_of(lax.dynamic_slice_in_dim(grad_piece, offset, count, 1))
                top_block = lax.dynamic_slice_in_dim(every_top, offset, count, 2)
                delta_block = lax.dynamic_slice_in_dim(every_delta, offset, count, 2)
                scores = (
                    jnp.einsum(
                        "bqhd,bkhd->bhqk",
                        query_block,
                        key_heads,
                        preferred_element_type=jnp.float32,
                    )
                    * scale
                )
                mask = (other[:, :, None] == key_seg[:, None, :])[:, None]
                probs = jnp.where(
                    mask, jnp.exp(jnp.where(mask, scores, NEG) - top_block[..., None]), 0.0
                )
                dvalues = dvalues + jnp.einsum(
                    "bhqk,bqhd->bkhd",
                    probs.astype(jnp.bfloat16),
                    grad_block,
                    preferred_element_type=jnp.float32,
                )
                dprobs = jnp.einsum(
                    "bqhd,bkhd->bhqk", grad_block, value_heads, preferred_element_type=jnp.float32
                )
                dscores = (probs * (dprobs - delta_block[..., None])).astype(jnp.bfloat16)
                dkeys = (
                    dkeys
                    + jnp.einsum(
                        "bhqk,bqhd->bkhd", dscores, query_block, preferred_element_type=jnp.float32
                    )
                    * scale
                )
                return (dkeys, dvalues)

            return lax.cond(touch, compute, keep_state, state)

        return block_loop(query_piece.shape[1], carry, visit)

    empty = jnp.zeros(key_heads.shape, jnp.float32)
    return key_fold(
        (empty, empty),
        (
            lax.all_gather(queries, "ctx", axis=1, tiled=True),
            lax.all_gather(dmixed, "ctx", axis=1, tiled=True),
        ),
        jnp.int32(0),
    )


def forward_pass(tokens, starts, weights, base):
    (
        query_weight,
        query_bias,
        key_weight,
        value_weight,
        value_bias,
        out_weight,
        out_bias,
        first_gain,
        first_shift,
        inner_weight,
        inner_bias,
        outer_weight,
        outer_bias,
        second_gain,
        second_shift,
    ) = weights
    rows = tokens.shape[1]
    positions = base + jnp.arange(rows, dtype=jnp.int32)
    query_seg = segment_of(starts, jnp.broadcast_to(positions, (tokens.shape[0], rows)))
    queries = (project(tokens, query_weight) + query_bias.astype(jnp.float32)).astype(jnp.bfloat16)
    keys = project(tokens, key_weight).astype(jnp.bfloat16)
    values = (project(tokens, value_weight) + value_bias.astype(jnp.float32)).astype(jnp.bfloat16)
    mixed, logsum, whole = forward_attention(queries, query_seg, starts, keys, values)
    mixed_low = mixed.reshape(tokens.shape).astype(jnp.bfloat16)
    first_sum = (
        tokens.astype(jnp.float32) + project(mixed_low, out_weight) + out_bias.astype(jnp.float32)
    )
    first = normalize(first_sum, first_gain.astype(jnp.float32), first_shift.astype(jnp.float32))
    first_low = first.astype(jnp.bfloat16)
    inner = project(first_low, inner_weight) + inner_bias.astype(jnp.float32)
    active = gelu(inner).astype(jnp.bfloat16)
    second_sum = first + project(active, outer_weight) + outer_bias.astype(jnp.float32)
    output = normalize(
        second_sum, second_gain.astype(jnp.float32), second_shift.astype(jnp.float32)
    ).astype(jnp.bfloat16)
    saved = (
        tokens,
        query_seg,
        queries,
        keys,
        values,
        mixed,
        logsum,
        mixed_low,
        first_sum,
        first_low,
        inner,
        active,
        second_sum,
        whole,
    )
    return (output, saved)


def backward_pass(saved, starts, weights, cotangent):
    (
        query_weight,
        _,
        key_weight,
        value_weight,
        _,
        out_weight,
        _,
        first_gain,
        first_shift,
        inner_weight,
        _,
        outer_weight,
        _,
        second_gain,
        second_shift,
    ) = weights
    (
        tokens,
        query_seg,
        queries,
        keys,
        values,
        mixed,
        logsum,
        mixed_low,
        first_sum,
        first_low,
        inner,
        active,
        second_sum,
        _,
    ) = saved
    unused, second_back = jax.vjp(
        normalize, second_sum, second_gain.astype(jnp.float32), second_shift.astype(jnp.float32)
    )
    dsecond, dgain_second, dshift_second = second_back(cotangent.astype(jnp.float32))
    douter = dsecond.astype(jnp.bfloat16)
    dactive = project_back(douter, outer_weight)
    unused, gelu_back = jax.vjp(gelu, inner)
    dinner = gelu_back(dactive)[0].astype(jnp.bfloat16)
    dfirst = dsecond + project_back(dinner, inner_weight)
    unused, first_back = jax.vjp(
        normalize, first_sum, first_gain.astype(jnp.float32), first_shift.astype(jnp.float32)
    )
    dfirst_sum, dgain_first, dshift_first = first_back(dfirst)
    dbranch = dfirst_sum.astype(jnp.bfloat16)
    dmixed = project_back(dbranch, out_weight).astype(jnp.bfloat16)
    delta = jnp.einsum("bqhd,bqhd->bhq", heads_of(dmixed).astype(jnp.float32), mixed)
    dqueries = query_gradient(queries, query_seg, starts, keys, values, dmixed, logsum, delta)
    dkeys, dvalues = key_gradient(keys, values, query_seg, starts, queries, dmixed, logsum, delta)
    dqueries = dqueries.reshape(tokens.shape).astype(jnp.bfloat16)
    dkeys = dkeys.reshape(tokens.shape).astype(jnp.bfloat16)
    dvalues = dvalues.reshape(tokens.shape).astype(jnp.bfloat16)
    tokens_grad = (
        dfirst_sum
        + project_back(dqueries, query_weight)
        + project_back(dkeys, key_weight)
        + project_back(dvalues, value_weight)
    )
    sums = (
        outer_sum(tokens, dqueries),
        row_sum(dqueries),
        outer_sum(tokens, dkeys),
        outer_sum(tokens, dvalues),
        row_sum(dvalues),
        outer_sum(mixed_low, dbranch),
        row_sum(dbranch),
        dgain_first,
        dshift_first,
        outer_sum(first_low, dinner),
        row_sum(dinner),
        outer_sum(active, douter),
        row_sum(douter),
        dgain_second,
        dshift_second,
    )
    return (tokens_grad, sums)


def general_device(
    tokens,
    doc_lengths,
    query_weight,
    query_bias,
    key_weight,
    value_weight,
    value_bias,
    out_weight,
    out_bias,
    first_gain,
    first_shift,
    inner_weight,
    inner_bias,
    outer_weight,
    outer_bias,
    second_gain,
    second_shift,
    cotangent,
):
    params = (
        query_weight,
        query_bias,
        key_weight,
        value_weight,
        value_bias,
        out_weight,
        out_bias,
        first_gain,
        first_shift,
        inner_weight,
        inner_bias,
        outer_weight,
        outer_bias,
        second_gain,
        second_shift,
    )
    rows = tokens.shape[2]
    base = lax.axis_index("ctx") * rows
    lengths = doc_lengths[:, 0]
    starts = jnp.cumsum(lengths, axis=-1) - lengths
    outputs = []
    token_parts = []
    sums = None
    for index in range(tokens.shape[0]):
        weights = (
            lax.all_gather(params[0], "wt", axis=0, tiled=True),
            lax.all_gather(params[1], "wt", axis=0, tiled=True),
            lax.all_gather(params[2], "wt", axis=0, tiled=True),
            lax.all_gather(params[3], "wt", axis=0, tiled=True),
            lax.all_gather(params[4], "wt", axis=0, tiled=True),
            lax.all_gather(params[5], "wt", axis=0, tiled=True),
            lax.all_gather(params[6], "wt", axis=0, tiled=True),
            lax.all_gather(params[7], "wt", axis=0, tiled=True),
            lax.all_gather(params[8], "wt", axis=0, tiled=True),
            lax.all_gather(params[9], "wt", axis=0, tiled=True),
            lax.all_gather(params[10], "wt", axis=0, tiled=True),
            lax.all_gather(params[11], "wt", axis=0, tiled=True),
            lax.all_gather(params[12], "wt", axis=0, tiled=True),
            lax.all_gather(params[13], "wt", axis=0, tiled=True),
            lax.all_gather(params[14], "wt", axis=0, tiled=True),
        )
        part_out, saved = forward_pass(
            tokens[index : index + 1, 0], starts[index : index + 1], weights, base
        )
        again = (
            lax.all_gather(params[0], "wt", axis=0, tiled=True),
            lax.all_gather(params[1], "wt", axis=0, tiled=True),
            lax.all_gather(params[2], "wt", axis=0, tiled=True),
            lax.all_gather(params[3], "wt", axis=0, tiled=True),
            lax.all_gather(params[4], "wt", axis=0, tiled=True),
            lax.all_gather(params[5], "wt", axis=0, tiled=True),
            lax.all_gather(params[6], "wt", axis=0, tiled=True),
            lax.all_gather(params[7], "wt", axis=0, tiled=True),
            lax.all_gather(params[8], "wt", axis=0, tiled=True),
            lax.all_gather(params[9], "wt", axis=0, tiled=True),
            lax.all_gather(params[10], "wt", axis=0, tiled=True),
            lax.all_gather(params[11], "wt", axis=0, tiled=True),
            lax.all_gather(params[12], "wt", axis=0, tiled=True),
            lax.all_gather(params[13], "wt", axis=0, tiled=True),
            lax.all_gather(params[14], "wt", axis=0, tiled=True),
        )
        part_grad, part_sums = backward_pass(
            saved, starts[index : index + 1], again, cotangent[index : index + 1, 0]
        )
        outputs.append(part_out)
        token_parts.append(part_grad)
        sums = part_sums if sums is None else jax.tree.map(jnp.add, sums, part_sums)
    output = jnp.concatenate(outputs, axis=0)
    tokens_grad = jnp.concatenate(token_parts, axis=0)
    shards = jax.tree.map(
        lambda part: part.astype(jnp.float32),
        lax.psum_scatter(for_sending(sums), "wt", scatter_dimension=0, tiled=True),
    )
    totals = lax.psum(shards, "ctx")
    return (output[:, None], tokens_grad[:, None]) + tuple(totals)


def flip(value, bits):
    return lax.ppermute(value, "ctx", [(i, i ^ bits) for i in range(8)])


def turn(value, step):
    return lax.ppermute(value, "wt", [(i, (i - step) % 4) for i in range(4)])


def pick(value, index, axis=0):
    return lax.dynamic_index_in_dim(value, index, axis, keepdims=False)


def pair(own, other, bit, axis=0):
    return jnp.where(bit == 0, jnp.stack([own, other], axis), jnp.stack([other, own], axis))


def short(value):
    return value.astype(jnp.bfloat16)


def wide(value):
    return value.astype(jnp.float32)


def dot(left, right):
    return jnp.dot(left, right, preferred_element_type=jnp.float32)


def dot_back(left, right):
    return lax.dot_general(
        left, right, (((1,), (1,)), ((), ())), preferred_element_type=jnp.float32
    )


def dot_sum(left, right):
    return lax.dot_general(
        left, right, (((0,), (0,)), ((), ())), preferred_element_type=jnp.float32
    )


def norm_parts(rows):
    mean = jnp.mean(rows, axis=-1, keepdims=True)
    centered = rows - mean
    spread = jnp.mean(centered * centered, axis=-1, keepdims=True)
    root = lax.rsqrt(spread + EPS)
    return centered * root, root


def norm_back(upstream, normed, root, gain):
    grad = upstream * gain
    mean = jnp.mean(grad, axis=-1, keepdims=True)
    along = jnp.mean(grad * normed, axis=-1, keepdims=True)
    return root * (grad - mean - normed * along)


def gelu_parts(inner):
    rise = 0.5 * (1.0 + lax.erf(inner * ROOT_HALF))
    bell = jnp.exp(-0.5 * inner * inner) * (1.0 / math.sqrt(2.0 * math.pi))
    return inner * rise, rise + inner * bell


def run(kernel, outs, args, scratch=(), scalars=(), specs=None, out_specs=None):
    shapes = tuple(jax.ShapeDtypeStruct(shape, dtype) for shape, dtype in outs)
    whole = pl.BlockSpec(memory_space=pltpu.VMEM)
    in_specs = [pl.BlockSpec(memory_space=pltpu.SMEM)] * len(scalars)
    in_specs += [whole] * len(args) if specs is None else specs
    return pl.pallas_call(
        kernel,
        out_shape=shapes,
        in_specs=in_specs,
        out_specs=tuple([whole] * len(outs) if out_specs is None else out_specs),
        scratch_shapes=list(scratch),
    )(*scalars, *args)


WHOLE = pl.BlockSpec(memory_space=pltpu.VMEM)
LEFT = pl.BlockSpec(memory_space=pl.ANY)
BF = jnp.bfloat16
F32 = jnp.float32


def where_am_i():
    ctx, own = lax.axis_index("ctx"), lax.axis_index("wt")
    return ctx & 1, (ctx >> 1) & 3, ctx & 3, own


def some_rows(start, count):
    return pl.ds(pl.multiple_of(start, 16), count)


def prepare_heads_kernel(wq, wk, wv, vec, heads_own, heads_send):
    _, quarter, group, _ = where_am_i()
    shard, dim = wq.shape
    width = dim // 4
    for index in range(4):

        @pl.when(group == index)
        def _():
            for slot, ref in enumerate((wq, wk, wv)):
                heads_own[:, slot * width : (slot + 1) * width] = ref[
                    :, index * width : (index + 1) * width
                ]

    part = shard // 2
    heads_send[0:part, :] = heads_own[some_rows((quarter >> 1) * part, part), :]
    heads_send[part:, 0:width] = vec[...]
    heads_send[part:, width:] = jnp.zeros((16, 2 * width), BF)


def prepare_kernel(wo, wi, wo2, w2_send, inner_half, outer_half):
    core, quarter, _, _ = where_am_i()
    shard, dim = wo.shape
    half = wo2.shape[0] // 2
    for index in range(2):

        @pl.when(core == index)
        def _():
            for block in range(4):
                at = block * 2 * half + index * half
                inner_half[:, block * half : (block + 1) * half] = wi[:, at : at + half]
            outer_half[...] = wo2[index * half : (index + 1) * half, :]

    part = shard // 4
    rows = some_rows(quarter * part, part)
    w2_send[0:part, :] = inner_half[rows, 0:dim]
    w2_send[part : 2 * part, :] = inner_half[rows, dim:]
    step = half // 4
    w2_send[2 * part : 2 * part + step, :] = outer_half[some_rows(quarter * step, step), :]
    w2_send[2 * part + step :, :] = wo[rows, :]


CHUNK = 128
WINDOWS = (3, 5, 6, 8)


def chunk_of(ctx, index):
    return ctx ^ ((index >> 2) | (index & 2) | ((index & 1) << 2))


def some_chunks(start, count):
    return pl.ds(pl.multiple_of(start * CHUNK, CHUNK), count * CHUNK)


def over_window(bounds, block, windows, visit):
    if len(windows) == 1:
        visit(pl.ds(0, windows[0] * CHUNK))
        return
    low, count = bounds[0, block], bounds[1, block]
    least = 0
    for size in windows:

        @pl.when((count > least) & (count <= size))
        def _(size=size):
            visit(some_chunks(jnp.minimum(low, windows[-1] - size), size))

        least = size


def attend_rows(qkv, seg_col, seg_row, far, outs, logsum, mixed):
    core, quarter, _, _ = where_am_i()
    group = qkv.shape[0] // 3

    def step(side, carry):
        rows = some_chunks(2 * (2 * side + ((quarter & 1) ^ far)), 2)
        here = some_chunks(2 * side, 2)

        def one_head(head, carry):
            mask = seg_col[rows, :] == seg_row[...]
            scores = dot_back(qkv[head, rows, :], qkv[group + head])
            scores = jnp.where(mask, scores, NEG)
            top = jnp.max(scores, axis=-1, keepdims=True)
            expd = jnp.exp(scores - top)
            total = jnp.sum(expd, axis=-1, keepdims=True)
            probs = short(expd * (1.0 / total))
            mixed[head, here, :] = short(dot(probs, qkv[2 * group + head]))
            lane = lax.broadcasted_iota(jnp.int32, (2 * CHUNK, 128), 1)
            logsum[here, :] = jnp.where(lane == head, top + jnp.log(total), logsum[here, :])
            return carry

        lax.fori_loop(0, group, one_head, 0)
        return carry

    logsum[...] = jnp.zeros_like(logsum)
    lax.fori_loop(0, 2, step, 0)
    y = quarter >> 1
    for index, out in enumerate(outs):
        for side in range(2):
            chunk = 2 * (y ^ side) + (core ^ index)
            for head in range(group):
                out[
                    side * CHUNK : (side + 1) * CHUNK, head * HEAD_DIM : (head + 1) * HEAD_DIM
                ] = mixed[head, some_chunks(chunk, 1), :]


def attend_near_kernel(
    mine, other, far, heads_own, g1, g2, g3, h1, h2, h3, vec, seg_col, seg_row,
    qkv, m0, m1, logsum, weight, vectors, inner_b, mixed, bias,
):
    core, quarter, group, own = where_am_i()
    ctx = lax.axis_index("ctx")
    shard = heads_own.shape[0]
    part = shard // 2
    y = quarter >> 1
    bias[:, shard : 2 * shard] = jnp.zeros_like(bias[:, :shard])
    for index in range(4):

        @pl.when(own == index)
        def _():
            for step, ref, at in ((0, vec, 0), (1, g1, part), (2, g2, part), (3, g3, part)):
                row = (index + step) % 4
                block = wide(ref[at : at + 16, 0:shard])
                lane = row * shard
                vectors[:, lane : lane + shard] = block[0:8]
                lines = jnp.where(core == 0, block[8:10], block[10:12])
                for side in range(2):
                    lane = (2 * row + side) * shard
                    inner_b[:, lane : lane + shard] = lines[side : side + 1]

                @pl.when(group == row)
                def _():
                    bias[:, 0:shard] = block[0:1]
                    bias[:, 2 * shard :] = block[1:2]

    weight[some_rows(own * shard, shard), :] = heads_own[...]
    for step, near_half, far_half in ((1, g1, h1), (2, g2, h2), (3, g3, h3)):
        at = ((own + step) & 3) * shard
        weight[some_rows(at + part * y, part), :] = near_half[0:part, :]
        weight[some_rows(at + part * (1 - y), part), :] = far_half[0:part, :]
    index = 0
    for source in (mine, other, far):
        for first in range(0, source.shape[0], 2 * CHUNK):
            low = short(dot(source[first : first + 2 * CHUNK, :], weight[...]) + bias[...])
            for half in range(2):
                at = pl.multiple_of(chunk_of(ctx, index) * CHUNK, CHUNK)
                for slot in range(qkv.shape[0]):
                    value = low[
                        half * CHUNK : (half + 1) * CHUNK,
                        slot * HEAD_DIM : (slot + 1) * HEAD_DIM,
                    ]
                    if slot < qkv.shape[0] // 3:
                        value = value * jnp.asarray(HEAD_DIM ** (-0.5), BF)
                    qkv[slot, pl.ds(at, CHUNK), :] = value
                index += 1
    attend_rows(qkv, seg_col, seg_row, 0, (m0, m1), logsum, mixed)


def attend_far_kernel(qkv, seg_col, seg_row, m2, m3, logsum, mixed):
    attend_rows(qkv, seg_col, seg_row, 1, (m2, m3), logsum, mixed)


def project_kernel(m0, m1, m2, m3, mine, vec, wo, *refs):
    pieces, (first_sum, first_low, out_full, sems) = refs[:12], refs[12:]
    _, quarter, group, own = where_am_i()
    shard = wo.shape[0]
    part = shard // 4
    copies = [(wo, out_full.at[some_rows(own * shard, shard), :])]
    for index, piece in enumerate(pieces):
        at = ((own + 1 + index // 4) & 3) * shard + part * (quarter ^ (index % 4))
        rows = piece.shape[0]
        copies.append((piece.at[rows - part : rows, :], out_full.at[some_rows(at, part), :]))
    copies = [
        pltpu.make_async_copy(source, target, sems.at[index])
        for index, (source, target) in enumerate(copies)
    ]
    for copy in copies:
        copy.start()
    total = wide(mine[...]) + vec[2:3, :]
    for copy in copies:
        copy.wait()
    for code, ref in enumerate((m0, m1, m2, m3)):
        total += dot(ref[...], out_full[some_rows((group ^ code) * shard, shard), :])
    first_sum[...] = total
    first_low[...] = short(norm_parts(total)[0] * vec[3:4, :] + vec[4:5, :])


def forward_kernel(near, far, bias, inner_half, outer_half, *refs):
    pieces, (keep, send, slope, active, wi_full, wo2_full, wi, wo2, sems) = refs[:12], refs[12:]
    _, quarter, _, own = where_am_i()
    shard, half = inner_half.shape[0], outer_half.shape[0]
    dim = keep.shape[1]
    part, step = shard // 4, half // 4
    first = [(inner_half, wi.at[some_rows(own * shard, shard), :])]
    second = [(outer_half, wo2.at[some_rows(own * half, half), :])]
    for index, piece in enumerate(pieces):
        row, spot = (own + 1 + index // 4) & 3, quarter ^ (index % 4)
        rows = some_rows(row * shard + part * spot, part)
        for side in range(2):
            first.append(
                (
                    piece.at[side * part : (side + 1) * part, :],
                    wi.at[rows, side * dim : (side + 1) * dim],
                )
            )
        rows = some_rows(row * half + step * spot, step)
        second.append((piece.at[2 * part : 2 * part + step, :], wo2.at[rows, :]))
    copies = [
        pltpu.make_async_copy(source, target, sems.at[index])
        for index, (source, target) in enumerate(first + second)
    ]
    for copy in copies:
        copy.start()
    for copy in copies[: len(first)]:
        copy.wait()
    back = [
        pltpu.make_async_copy(wi, wi_full, sems.at[len(copies)]),
        pltpu.make_async_copy(wo2, wo2_full, sems.at[len(copies) + 1]),
    ]
    back[0].start()
    count = near.shape[0]
    chunk = 512
    waiting = True
    for index, (source, out) in enumerate(((far, send), (near, keep))):
        at = (1 - index) * count
        total = None
        for lane in range(0, slope.shape[1], chunk):
            lanes = slice(lane, lane + chunk)
            value, rate = gelu_parts(dot(source[...], wi[:, lanes]) + bias[:, lanes])
            low = short(value)
            slope[at : at + count, lanes] = short(rate)
            active[at : at + count, lanes] = low
            if waiting:
                for copy in copies[len(first) :]:
                    copy.wait()
                back[1].start()
                waiting = False
            added = dot(low, wo2[lanes, :])
            total = added if total is None else total + added
        out[...] = total
    for copy in back:
        copy.wait()


def turnaround_kernel(first_sum, keep, got, vec, cot0, cot1, out0, out1, dsecond, douter, sums):
    rows = cot0.shape[0]
    first = norm_parts(first_sum[...])[0] * vec[3:4, :] + vec[4:5, :]
    normed, root = norm_parts(first + vec[5:6, :] + keep[...] + got[...])
    output = short(normed * vec[6:7, :] + vec[7:8, :])
    out0[...] = output[:rows]
    out1[...] = output[rows:]
    upstream = jnp.concatenate([wide(cot0[...]), wide(cot1[...])])
    back = norm_back(upstream, normed, root, vec[6:7, :])
    low = short(back)
    dsecond[...] = back
    douter[...] = low
    sums[0:1, :] = jnp.sum(wide(low), axis=0, keepdims=True)
    sums[1:2, :] = jnp.sum(upstream * normed, axis=0, keepdims=True)
    sums[2:3, :] = jnp.sum(upstream, axis=0, keepdims=True)
    sums[3:, :] = jnp.zeros_like(sums[3:, :])


def backward_kernel(near, far, slope, wo2, wi_full, keep, send, dinner, sums, wi, sem):
    copy = pltpu.make_async_copy(wi_full, wi, sem)
    copy.start()
    count, dim = near.shape
    chunk = 512
    waiting = True
    for index, (source, out) in enumerate(((far, send), (near, keep))):
        at = (1 - index) * count
        total = None
        for lane in range(0, slope.shape[1], chunk):
            lanes = slice(lane, lane + chunk)
            rate = wide(slope[at : at + count, lanes])
            low = short(dot_back(source[...], wo2[lanes, :]) * rate)
            dinner[at : at + count, lanes] = low
            if waiting:
                copy.wait()
                waiting = False
            added = dot_back(low, wi[:, lanes])
            total = added if total is None else total + added
        out[...] = total
    total = jnp.sum(wide(dinner[...]), axis=0, keepdims=True)
    sums[0:1, :] = total[:, :dim]
    sums[1:2, :] = total[:, dim:]
    sums[2:, :] = jnp.zeros_like(sums[2:, :])


def weights_kernel(first0, first1, douter0, douter1, dinner, active, ak, az, bk, bz, left, right):
    _, quarter, _, _ = where_am_i()
    x, y = quarter & 1, quarter >> 1
    count = first0.shape[0]
    part, step = first0.shape[1] // 16, active.shape[1] // 16
    left[...] = short(dot_sum(first0[...], dinner[:count]) + dot_sum(first1[...], dinner[count:]))
    for block in range(8):
        rows = slice(block * part, (block + 1) * part)
        ak[rows, :] = left[some_rows((2 * block + x) * part, part), :]
        az[rows, :] = left[some_rows((2 * block + 1 - x) * part, part), :]
    right[...] = short(
        dot_sum(active[:count], douter0[...]) + dot_sum(active[count:], douter1[...])
    )
    for block in range(8):
        row, side = block // 2, block % 2
        rows = slice(block * step, (block + 1) * step)
        bk[rows, :] = right[some_rows((4 * row + 2 * y + side) * step, step), :]
        bz[rows, :] = right[some_rows((4 * row + 2 * (1 - y) + side) * step, step), :]


def branch_kernel(first_sum, dsecond, keep, got, vec, out_full, dfirst_sum, dbranch, d0, d1, d2, d3, sums):
    _, _, group, _ = where_am_i()
    shard = d0.shape[1]
    normed, root = norm_parts(first_sum[...])
    dfirst = dsecond[...] + keep[...] + got[...]
    back = norm_back(dfirst, normed, root, vec[3:4, :])
    low = short(back)
    dfirst_sum[...] = back
    dbranch[...] = low
    for code, ref in enumerate((d0, d1, d2, d3)):
        ref[...] = short(dot_back(low, out_full[some_rows((group ^ code) * shard, shard), :]))
    sums[0:1, :] = jnp.sum(wide(low), axis=0, keepdims=True)
    sums[1:2, :] = jnp.sum(dfirst * normed, axis=0, keepdims=True)
    sums[2:3, :] = jnp.sum(dfirst, axis=0, keepdims=True)
    sums[3:, :] = jnp.zeros_like(sums[3:, :])


def out_weight_kernel(m0, m1, m2, m3, dbranch, sums1, sums2, sums3, ck, cz, whole):
    core, _, group, _ = where_am_i()
    shard, dim = m0.shape[1], dbranch.shape[1]
    half = dim // 2
    for code, ref in enumerate((m0, m1, m2, m3)):
        whole[some_rows((group ^ code) * shard, shard), :] = short(
            dot_sum(ref[...], dbranch[...])
        )
    for side in range(2):

        @pl.when(core == side)
        def _():
            for ref, which in ((ck, side), (cz, 1 - side)):
                ref[0:dim, :] = whole[:, which * half : (which + 1) * half]

    rows = short(
        jnp.concatenate([sums1[0:3, :], sums2[0:3, :], sums3[0:2, :], jnp.zeros_like(sums1[...])])
    )
    for ref in (ck, cz):
        ref[dim : dim + 16, :] = rows[:, :half]
        ref[dim + 16 :, :] = rows[:, half:]


def out_split_kernel(packed, got, ck, cz):
    core, quarter, _, _ = where_am_i()
    x = quarter & 1
    dim = packed.shape[0] - 32
    part = dim // 16
    for block in range(8):
        rows = slice(block * part, (block + 1) * part)
        for ref, side in ((ck, x), (cz, 1 - x)):
            take = some_rows((2 * block + side) * part, part)
            ref[rows, :] = short(wide(packed[take, :]) + wide(got[take, :]))
    for lanes in range(2):
        at = dim + 16 * lanes
        mine, other = wide(packed[at : at + 16, :]), wide(got[at : at + 16, :])
        low = jnp.where(core == 0, mine, other)[6:8]
        high = jnp.where(core == 0, other, mine)[6:8]
        rows = jnp.concatenate([(mine + other)[0:6], low, high, jnp.zeros_like(mine[0:6])])
        at = 8 * part + 16 * lanes
        for ref in (ck, cz):
            ref[at : at + 16, :] = short(rows)


def reduce_rows(keep, got, outs, bit):
    size = keep.shape[0] // 8
    size -= size % 16
    width = keep.shape[1] // len(outs)
    for lane, pair_of in enumerate(outs):
        lanes = slice(lane * width, (lane + 1) * width)
        for block in range(4):
            for out, side in zip(pair_of, (bit, 1 - bit)):
                take = some_rows((2 * block + side) * size, size)
                out[block * size : (block + 1) * size, :] = short(
                    wide(keep[take, lanes]) + wide(got[take, lanes])
                )
        if keep.shape[0] > 8 * size:
            for out in pair_of:
                out[4 * size :, :] = short(
                    wide(keep[8 * size :, lanes]) + wide(got[8 * size :, lanes])
                )


def reduce_kernel(ak, ar, bk, br, *outs):
    _, quarter, _, _ = where_am_i()
    reduce_rows(ak, ar, (outs[0:2], outs[4:6]), quarter >> 1)
    reduce_rows(bk, br, (outs[2:4], outs[6:8]), quarter & 1)


def reduce_out_kernel(ck, cr, c2k, c2z):
    _, quarter, _, _ = where_am_i()
    reduce_rows(ck, cr, ((c2k, c2z),), quarter >> 1)


def owners_kernel(*refs):
    inputs, outs = refs[:-4], refs[-4:]
    _, _, _, own = where_am_i()
    ak, ar, bk, br = inputs[:4]
    half = bk.shape[1]
    part = ak.shape[0] // 4
    for index, out in enumerate(outs):
        row = (own - index) & 3
        rows = some_rows(row * part, part)
        out[0:part, :] = (wide(ak[rows, :]) + wide(ar[rows, :])).astype(out.dtype)
        for side in range(2):
            rows = some_rows((2 * row + side) * part, part)
            out[part : 2 * part, side * half : (side + 1) * half] = (
                wide(bk[rows, :]) + wide(br[rows, :])
            ).astype(out.dtype)
        if len(inputs) > 4:
            ck, cr = inputs[4:]
            at = 2 * part
            rows = some_rows(row * part, part)
            out[at:, 0:half] = (wide(ck[rows, :]) + wide(cr[rows, :])).astype(out.dtype)
            tail = wide(ck[4 * part :, :]) + wide(cr[4 * part :, :])
            out[at : at + 32, half:] = tail.astype(out.dtype)
            out[at + 32 :, half:] = jnp.zeros((part - 32, half), out.dtype)


def total_kernel(mine, *refs):
    total = wide(mine[...])
    for ref in refs[:-1]:
        total += wide(ref[...])
    refs[-1][...] = short(total)


def finish_kernel(*refs):
    pieces, (dwi, dwo2, dwo, small) = refs[:16], refs[16:]
    core, quarter, _, _ = where_am_i()
    part, half = dwi.shape[0] // 4, dwi.shape[1] // 8
    for side in range(2):

        @pl.when(core == side)
        def _():
            for index, piece in enumerate(pieces):
                lane, index = index // 8, index % 8
                spot = quarter ^ (index % 4)
                which = side if index < 4 else 1 - side
                rows = some_rows(spot * part, part)
                for block in range(2):
                    at = (2 * lane + block) * 2 * half + which * half
                    dwi[rows, at : at + half] = wide(piece[0:part, block * half : (block + 1) * half])
                    at = which * half + spot * 2 * part + block * part
                    dwo2[some_rows(at, part), lane * half : (lane + 1) * half] = wide(
                        piece[part : 2 * part, block * half : (block + 1) * half]
                    )
                if lane == 1:
                    dwo[rows, which * half : (which + 1) * half] = wide(piece[2 * part :, 0:half])

    last = pieces[8]
    small[:, 0:half] = wide(last[2 * part : 2 * part + 16, half:])
    small[:, half:] = wide(last[2 * part + 16 : 2 * part + 32, half:])


def attend_back_kernel(
    bounds, qkv, logsum0, logsum1, seg_col, seg_row, p0, p1, p2, p3, mine, other, far,
    h0, h1, h2, h3, grads, dqueries, dkeys, dvalues, dweight, dmixed, logsum, whole,
):
    _, quarter, _, own = where_am_i()
    ctx = lax.axis_index("ctx")
    x = quarter & 1
    scale = HEAD_DIM ** (-0.5)
    group = qkv.shape[0] // 3
    width = group * HEAD_DIM
    block = p0.shape[0]
    dkeys[...] = jnp.zeros_like(dkeys)
    dvalues[...] = jnp.zeros_like(dvalues)
    for index, part in enumerate((p0, p2, p1, p3)):
        for side in range(2):
            chunk = chunk_of(ctx, 2 * index + side)
            for head in range(group):
                dmixed[head, some_chunks(chunk, 1), :] = part[
                    side * CHUNK : (side + 1) * CHUNK, head * HEAD_DIM : (head + 1) * HEAD_DIM
                ]
    for side in range(2):
        rows = slice(2 * side * CHUNK, 2 * (side + 1) * CHUNK)
        logsum[some_chunks(2 * (2 * side + x), 2), :] = logsum0[rows, :]
        logsum[some_chunks(2 * (2 * side + 1 - x), 2), :] = logsum1[rows, :]

    def step(index, carry):
        rows = some_chunks(2 * index, 2)

        def visit(window):
            def one_head(head, carry):
                mask = seg_col[rows, :] == seg_row[:, window]
                query = qkv[head, rows, :]
                grad = dmixed[head, rows, :]
                keys = qkv[group + head, window, :]
                lane = lax.broadcasted_iota(jnp.int32, (2 * CHUNK, 128), 1)
                sums = jnp.sum(
                    jnp.where(lane == head, logsum[rows, :], 0.0), axis=-1, keepdims=True
                )
                scores = jnp.where(mask, dot_back(query, keys), NEG)
                probs = jnp.exp(scores - sums)
                dprobs = dot_back(grad, qkv[2 * group + head, window, :])
                delta = jnp.sum(probs * dprobs, axis=-1, keepdims=True)
                dscores = short(probs * (dprobs - delta))
                dqueries[head, rows, :] = short(dot(dscores, keys) * scale)
                dkeys[head, window, :] += dot_sum(dscores, query)
                dvalues[head, window, :] += dot_sum(short(probs), grad)
                return carry

            lax.fori_loop(0, group, one_head, 0)

        over_window(bounds, index, WINDOWS, visit)
        return carry

    lax.fori_loop(0, 4, step, 0)
    for head in range(group):
        whole[:, head * HEAD_DIM : (head + 1) * HEAD_DIM] = dqueries[head]
        at = width + head * HEAD_DIM
        whole[:, at : at + HEAD_DIM] = short(dkeys[head])
        whole[:, at + width : at + width + HEAD_DIM] = short(dvalues[head])
    for index in range(8):
        grads[index * CHUNK : (index + 1) * CHUNK, :] = whole[
            some_chunks(chunk_of(ctx, index), 1), :
        ]
    rows = 2 * block
    dweight[...] = (
        dot_sum(mine[...], grads[:block])
        + dot_sum(other[...], grads[block:rows])
        + dot_sum(far[...], grads[rows:])
    )
    sums = jnp.sum(wide(grads[...]), axis=0, keepdims=True)
    tail = jnp.concatenate([sums, jnp.zeros((15, sums.shape[1]), F32)])
    for index, out in enumerate((h0, h1, h2, h3)):
        take = pl.ds(pl.multiple_of(((own - index) & 3) * width, 16), width)
        out[0:width, :] = dweight[take, :].astype(out.dtype)
        out[width:, :] = tail.astype(out.dtype)


def tokens_kernel(grads, weight, keep, send):
    rows = keep.shape[0]
    keep[...] = dot_back(grads[:rows], weight[...])
    send[...] = short(dot_back(grads[rows:], weight[...]))


def merge_kernel(keep, got, base, near, far):
    total = keep[...] + wide(got[...])
    count = near.shape[0]
    near[...] = total[:count] + base[...]
    far[...] = short(total[count:])


def heads_kernel(s0, s1, s2, s3, dq, dk, dv, bias):
    _, _, group, own = where_am_i()
    shard = dq.shape[0]
    for index in range(4):

        @pl.when(group == index)
        def _():
            for code, ref in enumerate((s0, s1, s2, s3)):
                at = (index ^ code) * shard
                for slot, out in enumerate((dq, dk, dv)):
                    out[:, at : at + shard] = wide(
                        ref[0:shard, slot * shard : (slot + 1) * shard]
                    )

                @pl.when(own == index ^ code)
                def _():
                    bias[...] = wide(ref[shard:, :])


def plane_steps(
    tokens,
    doc_lengths,
    query_weight,
    query_bias,
    key_weight,
    value_weight,
    value_bias,
    out_weight,
    out_bias,
    first_gain,
    first_shift,
    inner_weight,
    inner_bias,
    outer_weight,
    outer_bias,
    second_gain,
    second_shift,
    cotangent,
):
    ctx, own = lax.axis_index("ctx"), lax.axis_index("wt")
    y = ctx >> 2
    rows, dim = tokens.shape[2], tokens.shape[3]
    shard = query_weight.shape[0]
    hidden = outer_weight.shape[0]
    half = hidden // 2
    count = 2 * rows

    mine = jnp.concatenate([pick(tokens[:, 0], y), flip(pick(tokens[:, 0], 1 - y), 4)])
    other = flip(mine, 2)
    far = flip(jnp.concatenate([mine, other]), 1)

    vector_list = (
        query_bias,
        value_bias,
        out_bias,
        first_gain,
        first_shift,
        outer_bias,
        second_gain,
        second_shift,
        *[inner_bias[at : at + shard] for at in range(0, 4 * shard, shard)],
    )
    line = lax.broadcasted_iota(jnp.int32, (16, shard), 0)
    vec = jnp.zeros((16, shard), BF)
    for index, value in enumerate(vector_list):
        vec = jnp.where(line == index, value[None, :], vec)
    heads_own, heads_send = run(
        prepare_heads_kernel,
        [((shard, 3 * shard), BF), ((shard // 2 + 16, 3 * shard), BF)],
        (query_weight, key_weight, value_weight, vec),
    )
    w2_send, inner_half, outer_half = run(
        prepare_kernel,
        [((shard // 4 * 3 + half // 4, dim), BF), ((shard, 4 * half), BF), ((half, dim), BF)],
        (out_weight, inner_weight, outer_weight),
    )
    got = [turn(heads_send, step) for step in (1, 2, 3)]
    gone = [flip(value, 4) for value in got]
    pieces = []
    for step in (1, 2, 3):
        piece = turn(w2_send, step)
        pieces += [piece] + [flip(piece, bits) for bits in (2, 4, 6)]

    lengths = pick(doc_lengths[:, 0], y)
    starts = jnp.cumsum(lengths) - lengths
    total = 8 * rows
    positions = jnp.arange(total, dtype=jnp.int32)
    seg = jnp.sum((starts[None, :] <= positions[:, None]).astype(jnp.int32), axis=-1) - 1
    segs = (seg[:, None], seg[None, :])
    first = jnp.arange(4, dtype=jnp.int32)[:, None] * (2 * CHUNK)
    low = jnp.max(jnp.where(starts[None, :] <= first, starts[None, :], 0), axis=-1) // CHUNK
    ends = jnp.where(starts[None, :] >= first + 2 * CHUNK, starts[None, :], total)
    bounds = jnp.stack([low, (jnp.min(ends, axis=-1) - 1) // CHUNK - low + 1])

    qkv, m0, m1, logsum0, heads_weight, vectors, inner_b = run(
        attend_near_kernel,
        [
            ((9, total, HEAD_DIM), BF),
            ((count, shard), BF),
            ((count, shard), BF),
            ((2 * count, 128), F32),
            ((dim, 3 * shard), BF),
            ((8, dim), F32),
            ((1, 4 * half), F32),
        ],
        (mine, other, far, heads_own, *got, *gone, vec, *segs),
        [pltpu.VMEM((3, 2 * count, HEAD_DIM), BF), pltpu.VMEM((1, 3 * shard), F32)],
    )
    m2, m3, logsum1 = run(
        attend_far_kernel,
        [((count, shard), BF), ((count, shard), BF), ((2 * count, 128), F32)],
        (qkv, *segs),
        [pltpu.VMEM((3, 2 * count, HEAD_DIM), BF)],
    )
    mixed = [m0, flip(m1, 1), flip(m2, 2), flip(m3, 3)]

    first_sum, first_low, out_full = run(
        project_kernel,
        [((count, dim), F32), ((count, dim), BF), ((dim, dim), BF)],
        (*mixed, mine, vectors, out_weight, *pieces),
        [pltpu.SemaphoreType.DMA((13,))],
        specs=[WHOLE] * 6 + [LEFT] * 13,
    )
    first_far = flip(first_low, 1)
    keep, send, slope, active, wi_full, wo2_full = run(
        forward_kernel,
        [
            ((count, dim), F32),
            ((count, dim), F32),
            ((2 * count, 4 * half), BF),
            ((2 * count, 4 * half), BF),
            ((dim, 4 * half), BF),
            ((4 * half, dim), BF),
        ],
        (first_low, first_far, inner_b, inner_half, outer_half, *pieces),
        [
            pltpu.VMEM((dim, 4 * half), BF),
            pltpu.VMEM((4 * half, dim), BF),
            pltpu.SemaphoreType.DMA((40,)),
        ],
        specs=[WHOLE] * 3 + [LEFT] * 14,
        out_specs=[WHOLE] * 4 + [LEFT] * 2,
    )
    cot = pick(cotangent[:, 0], y), flip(pick(cotangent[:, 0], 1 - y), 4)
    out0, out1, dsecond, douter, sums2 = run(
        turnaround_kernel,
        [
            ((rows, dim), BF),
            ((rows, dim), BF),
            ((count, dim), F32),
            ((count, dim), BF),
            ((8, dim), F32),
        ],
        (first_sum, keep, flip(send, 1), vectors, *cot),
    )
    output = pair(out0, flip(out1, 4), y)

    douter_far = flip(douter, 1)
    keep, send, dinner, sums3 = run(
        backward_kernel,
        [
            ((count, dim), F32),
            ((count, dim), F32),
            ((2 * count, 4 * half), BF),
            ((8, dim), F32),
        ],
        (douter, douter_far, slope, wo2_full, wi_full),
        [pltpu.VMEM((dim, 4 * half), BF), pltpu.SemaphoreType.DMA],
        specs=[WHOLE] * 4 + [LEFT],
    )
    dfirst_sum, dbranch, d0, d1, d2, d3, sums1 = run(
        branch_kernel,
        [((count, dim), F32), ((count, dim), BF)] + [((count, shard), BF)] * 4 + [((8, dim), F32)],
        (first_sum, dsecond, keep, flip(send, 1), vectors, out_full),
    )
    dmixed = [d0, flip(d1, 1), flip(d2, 2), flip(d3, 3)]

    ak, az, bk, bz = run(
        weights_kernel,
        [((dim // 2, 4 * half), BF)] * 2 + [((2 * half, dim), BF)] * 2,
        (first_low, first_far, douter, douter_far, dinner, active),
        [pltpu.VMEM((dim, 4 * half), BF), pltpu.VMEM((4 * half, dim), BF)],
    )
    ar, br = flip(az, 2), flip(bz, 4)
    ck, cz = run(
        out_weight_kernel,
        [((dim + 32, dim // 2), BF)] * 2,
        (*mixed, dbranch, sums1, sums2, sums3),
        [pltpu.VMEM((dim, dim), BF)],
    )
    ck, cz = run(out_split_kernel, [((dim // 2 + 32, dim // 2), BF)] * 2, (ck, flip(cz, 1)))
    cr = flip(cz, 2)

    h0, h1, h2, h3, grads = run(
        attend_back_kernel,
        [((shard + 16, 3 * shard), F32)]
        + [((shard + 16, 3 * shard), BF)] * 3
        + [((4 * count, 3 * shard), BF)],
        (qkv, logsum0, logsum1, *segs, *dmixed, mine, other, far),
        [
            pltpu.VMEM((3, 4 * count, HEAD_DIM), BF),
            pltpu.VMEM((3, 4 * count, HEAD_DIM), F32),
            pltpu.VMEM((3, 4 * count, HEAD_DIM), F32),
            pltpu.VMEM((dim, 3 * shard), F32),
            pltpu.VMEM((3, total, HEAD_DIM), BF),
            pltpu.VMEM((total, 128), F32),
            pltpu.VMEM((total, 3 * shard), BF),
        ],
        scalars=(bounds,),
    )
    keep, send = run(
        tokens_kernel, [((2 * count, dim), F32), ((2 * count, dim), BF)], (grads, heads_weight)
    )

    c2k, c2z = run(reduce_out_kernel, [((dim // 4 + 32, dim // 2), BF)] * 2, (ck, cr))
    reduced = run(
        reduce_kernel,
        ([((dim // 4, 2 * half), BF)] * 2 + [((half, dim // 2), BF)] * 2) * 2,
        (ak, ar, bk, br),
    )
    plane = []
    for lane in range(2):
        a2k, a2z, b2k, b2z = reduced[4 * lane : 4 * lane + 4]
        last = [a2k, flip(a2z, 4), b2k, flip(b2z, 2)]
        size = shard // 4 * 2
        if lane == 1:
            last += [c2k, flip(c2z, 4)]
            size = shard // 4 * 3
        p0, p1, p2, p3 = run(owners_kernel, [((size, dim), F32)] + [((size, dim), BF)] * 3, last)
        turned = [turn(p, step) for step, p in ((1, p1), (2, p2), (3, p3))]
        (piece,) = run(total_kernel, [((size, dim), BF)], (p0, *turned))
        near = [piece] + [flip(piece, bits) for bits in (2, 4, 6)]
        plane += near + [flip(p, 1) for p in near]
    dinner_w, douter_w, dout_w, small = run(
        finish_kernel,
        [((shard, 8 * half), F32), ((hidden, dim), F32), ((shard, dim), F32), ((16, dim), F32)],
        plane,
    )
    dinner_b = pick(small[6:10].reshape(2, 4, half), own, 1).reshape(hidden)
    small = lax.dynamic_slice_in_dim(small[:6], own * shard, shard, 1)

    (heads,) = run(
        total_kernel, [((shard + 16, 3 * shard), BF)], (h0, turn(h1, 1), turn(h2, 2), turn(h3, 3))
    )
    (heads,) = run(total_kernel, [((shard + 16, 3 * shard), BF)], (heads, flip(heads, 4)))
    dquery_w, dkey_w, dvalue_w, heads_b = run(
        heads_kernel,
        [((shard, dim), F32)] * 3 + [((16, 3 * shard), F32)],
        (heads, flip(heads, 1), flip(heads, 2), flip(heads, 3)),
    )

    near_t, far_t = run(
        merge_kernel, [((count, dim), F32), ((count, dim), BF)], (keep, flip(send, 1), dfirst_sum)
    )
    dtokens = near_t + wide(flip(far_t, 2))
    tokens_grad = pair(dtokens[:rows], wide(flip(short(dtokens[rows:]), 4)), y)

    return (
        output[:, None],
        tokens_grad[:, None],
        dquery_w,
        heads_b[0, :shard],
        dkey_w,
        dvalue_w,
        heads_b[0, 2 * shard :],
        dout_w,
        small[0],
        small[1],
        small[2],
        dinner_w,
        dinner_b,
        douter_w,
        small[3],
        small[4],
        small[5],
    )


def plane_device(*args):
    return plane_steps(*args)


def solution(mesh):
    placed = (
        P(None, "wt", "ctx", None),
        P(None, "wt", None),
        P("wt", None),
        P("wt"),
        P("wt", None),
        P("wt", None),
        P("wt"),
        P("wt", None),
        P("wt"),
        P("wt"),
        P("wt"),
        P("wt", None),
        P("wt"),
        P("wt", None),
        P("wt"),
        P("wt"),
        P("wt"),
        P(None, "wt", "ctx", None),
    )
    fits = mesh.shape["ctx"] == 8 and mesh.shape["wt"] == 4
    return jax.shard_map(
        plane_device if fits else general_device,
        mesh=mesh,
        in_specs=placed,
        out_specs=(
            P(None, "wt", "ctx", None),
            P(None, "wt", "ctx", None),
            P("wt", None),
            P("wt"),
            P("wt", None),
            P("wt", None),
            P("wt"),
            P("wt", None),
            P("wt"),
            P("wt"),
            P("wt"),
            P("wt", None),
            P("wt"),
            P("wt", None),
            P("wt"),
            P("wt"),
            P("wt"),
        ),
        check_vma=False,
    )
```

```python
import math

import jax
import jax.numpy as jnp
from jax import lax
from jax.experimental import pallas as pl
from jax.experimental.pallas import tpu as pltpu
from jax.sharding import PartitionSpec as P


HEADS = 12
HEAD_DIM = 64


EPS = 1e-12
NEG = -1e30
ROOT_HALF = 0.7071067811865476


def for_sending(shard):

    def short(part):
        return part.astype(jnp.bfloat16) if part.dtype == jnp.float32 else part

    return jax.tree.map(short, shard)


def normalize(rows, gain, shift):
    mean = jnp.mean(rows, axis=-1, keepdims=True)
    centered = rows - mean
    spread = jnp.mean(centered * centered, axis=-1, keepdims=True)
    return centered * lax.rsqrt(spread + EPS) * gain + shift


def gelu(inner):
    return 0.5 * inner * (1.0 + lax.erf(inner * ROOT_HALF))


def segment_of(starts, positions):
    found = (starts[:, None, :] <= positions[:, :, None]).astype(jnp.int32)
    return jnp.sum(found, axis=-1) - 1


def project(inputs, weight):
    return jnp.einsum("btd,de->bte", inputs, weight, preferred_element_type=jnp.float32)


def project_back(grads, weight):
    return jnp.einsum("bte,de->btd", grads, weight, preferred_element_type=jnp.float32)


def outer_sum(inputs, grads):
    return jnp.einsum("btd,bte->de", inputs, grads, preferred_element_type=jnp.float32)


def row_sum(grads):
    return jnp.sum(grads.astype(jnp.float32), axis=(0, 1))


def heads_of(array):
    return array.reshape(array.shape[0], array.shape[1], HEADS, HEAD_DIM)


def block_loop(width, carry, visit):
    block = math.gcd(width, 512)

    def step(state, index):
        return (visit(state, index * block, block), None)

    carry, _ = lax.scan(step, carry, jnp.arange(width // block, dtype=jnp.int32))
    return carry


def reaches(starts, own_seg, first, count):
    positions = first + jnp.arange(count, dtype=jnp.int32)
    other = segment_of(starts, jnp.broadcast_to(positions, (starts.shape[0], count)))
    touch = jnp.any((other[:, 0] <= own_seg[:, -1]) & (other[:, -1] >= own_seg[:, 0]))
    return (other, touch)


def keep_state(state):
    return state


def forward_attention(queries, query_seg, starts, keys, values):
    scale = HEAD_DIM ** (-0.5)
    batch, rows = (queries.shape[0], queries.shape[1])
    query_heads = heads_of(queries)

    def forward_fold(carry, piece, start):
        key_piece, value_piece = piece

        def visit(state, offset, count):
            other, touch = reaches(starts, query_seg, offset, count)

            def compute(state):
                top, total, accum = state
                key_block = heads_of(lax.dynamic_slice_in_dim(key_piece, offset, count, 1))
                value_block = heads_of(lax.dynamic_slice_in_dim(value_piece, offset, count, 1))
                scores = (
                    jnp.einsum(
                        "bqhd,bkhd->bhqk",
                        query_heads,
                        key_block,
                        preferred_element_type=jnp.float32,
                    )
                    * scale
                )
                mask = (query_seg[:, :, None] == other[:, None, :])[:, None]
                scores = jnp.where(mask, scores, NEG)
                new_top = jnp.maximum(top, jnp.max(scores, axis=-1))
                expd = jnp.where(mask, jnp.exp(scores - new_top[..., None]), 0.0)
                factor = jnp.exp(top - new_top)
                total = total * factor + jnp.sum(expd, axis=-1)
                added = jnp.einsum(
                    "bhqk,bkhd->bqhd",
                    expd.astype(jnp.bfloat16),
                    value_block,
                    preferred_element_type=jnp.float32,
                )
                accum = accum * jnp.transpose(factor, (0, 2, 1))[..., None] + added
                return (new_top, total, accum)

            return lax.cond(touch, compute, keep_state, state)

        return block_loop(key_piece.shape[1], carry, visit)

    init = (
        jnp.full((batch, HEADS, rows), NEG, jnp.float32),
        jnp.zeros((batch, HEADS, rows), jnp.float32),
        jnp.zeros((batch, rows, HEADS, HEAD_DIM), jnp.float32),
    )
    whole = (keys, values)
    top, total, accum = forward_fold(
        init,
        (
            lax.all_gather(keys, "ctx", axis=1, tiled=True),
            lax.all_gather(values, "ctx", axis=1, tiled=True),
        ),
        jnp.int32(0),
    )
    mixed = accum / jnp.transpose(total, (0, 2, 1))[..., None]
    return (mixed, top + jnp.log(total), whole)


def query_gradient(queries, query_seg, starts, keys, values, dmixed, logsum, delta):
    scale = HEAD_DIM ** (-0.5)
    query_heads = heads_of(queries)
    grad_heads = heads_of(dmixed)

    def query_fold(carry, piece, start):
        key_piece, value_piece = piece

        def visit(state, offset, count):
            other, touch = reaches(starts, query_seg, offset, count)

            def compute(state):
                key_block = heads_of(lax.dynamic_slice_in_dim(key_piece, offset, count, 1))
                value_block = heads_of(lax.dynamic_slice_in_dim(value_piece, offset, count, 1))
                scores = (
                    jnp.einsum(
                        "bqhd,bkhd->bhqk",
                        query_heads,
                        key_block,
                        preferred_element_type=jnp.float32,
                    )
                    * scale
                )
                mask = (query_seg[:, :, None] == other[:, None, :])[:, None]
                probs = jnp.where(
                    mask, jnp.exp(jnp.where(mask, scores, NEG) - logsum[..., None]), 0.0
                )
                dprobs = jnp.einsum(
                    "bqhd,bkhd->bhqk", grad_heads, value_block, preferred_element_type=jnp.float32
                )
                dscores = (probs * (dprobs - delta[..., None])).astype(jnp.bfloat16)
                return (
                    state
                    + jnp.einsum(
                        "bhqk,bkhd->bqhd", dscores, key_block, preferred_element_type=jnp.float32
                    )
                    * scale
                )

            return lax.cond(touch, compute, keep_state, state)

        return block_loop(key_piece.shape[1], carry, visit)

    init = jnp.zeros(query_heads.shape, jnp.float32)
    return query_fold(
        init,
        (
            lax.all_gather(keys, "ctx", axis=1, tiled=True),
            lax.all_gather(values, "ctx", axis=1, tiled=True),
        ),
        jnp.int32(0),
    )


def key_gradient(keys, values, key_seg, starts, queries, dmixed, logsum, delta):
    scale = HEAD_DIM ** (-0.5)
    key_heads = heads_of(keys)
    value_heads = heads_of(values)
    every_top, every_delta = (
        lax.all_gather(logsum, "ctx", axis=2, tiled=True),
        lax.all_gather(delta, "ctx", axis=2, tiled=True),
    )

    def key_fold(carry, piece, start):
        query_piece, grad_piece = piece

        def visit(state, offset, count):
            other, touch = reaches(starts, key_seg, offset, count)

            def compute(state):
                dkeys, dvalues = state
                query_block = heads_of(lax.dynamic_slice_in_dim(query_piece, offset, count, 1))
                grad_block = heads_of(lax.dynamic_slice_in_dim(grad_piece, offset, count, 1))
                top_block = lax.dynamic_slice_in_dim(every_top, offset, count, 2)
                delta_block = lax.dynamic_slice_in_dim(every_delta, offset, count, 2)
                scores = (
                    jnp.einsum(
                        "bqhd,bkhd->bhqk",
                        query_block,
                        key_heads,
                        preferred_element_type=jnp.float32,
                    )
                    * scale
                )
                mask = (other[:, :, None] == key_seg[:, None, :])[:, None]
                probs = jnp.where(
                    mask, jnp.exp(jnp.where(mask, scores, NEG) - top_block[..., None]), 0.0
                )
                dvalues = dvalues + jnp.einsum(
                    "bhqk,bqhd->bkhd",
                    probs.astype(jnp.bfloat16),
                    grad_block,
                    preferred_element_type=jnp.float32,
                )
                dprobs = jnp.einsum(
                    "bqhd,bkhd->bhqk", grad_block, value_heads, preferred_element_type=jnp.float32
                )
                dscores = (probs * (dprobs - delta_block[..., None])).astype(jnp.bfloat16)
                dkeys = (
                    dkeys
                    + jnp.einsum(
                        "bhqk,bqhd->bkhd", dscores, query_block, preferred_element_type=jnp.float32
                    )
                    * scale
                )
                return (dkeys, dvalues)

            return lax.cond(touch, compute, keep_state, state)

        return block_loop(query_piece.shape[1], carry, visit)

    empty = jnp.zeros(key_heads.shape, jnp.float32)
    return key_fold(
        (empty, empty),
        (
            lax.all_gather(queries, "ctx", axis=1, tiled=True),
            lax.all_gather(dmixed, "ctx", axis=1, tiled=True),
        ),
        jnp.int32(0),
    )


def forward_pass(tokens, starts, weights, base):
    (
        query_weight,
        query_bias,
        key_weight,
        value_weight,
        value_bias,
        out_weight,
        out_bias,
        first_gain,
        first_shift,
        inner_weight,
        inner_bias,
        outer_weight,
        outer_bias,
        second_gain,
        second_shift,
    ) = weights
    rows = tokens.shape[1]
    positions = base + jnp.arange(rows, dtype=jnp.int32)
    query_seg = segment_of(starts, jnp.broadcast_to(positions, (tokens.shape[0], rows)))
    queries = (project(tokens, query_weight) + query_bias.astype(jnp.float32)).astype(jnp.bfloat16)
    keys = project(tokens, key_weight).astype(jnp.bfloat16)
    values = (project(tokens, value_weight) + value_bias.astype(jnp.float32)).astype(jnp.bfloat16)
    mixed, logsum, whole = forward_attention(queries, query_seg, starts, keys, values)
    mixed_low = mixed.reshape(tokens.shape).astype(jnp.bfloat16)
    first_sum = (
        tokens.astype(jnp.float32) + project(mixed_low, out_weight) + out_bias.astype(jnp.float32)
    )
    first = normalize(first_sum, first_gain.astype(jnp.float32), first_shift.astype(jnp.float32))
    first_low = first.astype(jnp.bfloat16)
    inner = project(first_low, inner_weight) + inner_bias.astype(jnp.float32)
    active = gelu(inner).astype(jnp.bfloat16)
    second_sum = first + project(active, outer_weight) + outer_bias.astype(jnp.float32)
    output = normalize(
        second_sum, second_gain.astype(jnp.float32), second_shift.astype(jnp.float32)
    ).astype(jnp.bfloat16)
    saved = (
        tokens,
        query_seg,
        queries,
        keys,
        values,
        mixed,
        logsum,
        mixed_low,
        first_sum,
        first_low,
        inner,
        active,
        second_sum,
        whole,
    )
    return (output, saved)


def backward_pass(saved, starts, weights, cotangent):
    (
        query_weight,
        _,
        key_weight,
        value_weight,
        _,
        out_weight,
        _,
        first_gain,
        first_shift,
        inner_weight,
        _,
        outer_weight,
        _,
        second_gain,
        second_shift,
    ) = weights
    (
        tokens,
        query_seg,
        queries,
        keys,
        values,
        mixed,
        logsum,
        mixed_low,
        first_sum,
        first_low,
        inner,
        active,
        second_sum,
        _,
    ) = saved
    unused, second_back = jax.vjp(
        normalize, second_sum, second_gain.astype(jnp.float32), second_shift.astype(jnp.float32)
    )
    dsecond, dgain_second, dshift_second = second_back(cotangent.astype(jnp.float32))
    douter = dsecond.astype(jnp.bfloat16)
    dactive = project_back(douter, outer_weight)
    unused, gelu_back = jax.vjp(gelu, inner)
    dinner = gelu_back(dactive)[0].astype(jnp.bfloat16)
    dfirst = dsecond + project_back(dinner, inner_weight)
    unused, first_back = jax.vjp(
        normalize, first_sum, first_gain.astype(jnp.float32), first_shift.astype(jnp.float32)
    )
    dfirst_sum, dgain_first, dshift_first = first_back(dfirst)
    dbranch = dfirst_sum.astype(jnp.bfloat16)
    dmixed = project_back(dbranch, out_weight).astype(jnp.bfloat16)
    delta = jnp.einsum("bqhd,bqhd->bhq", heads_of(dmixed).astype(jnp.float32), mixed)
    dqueries = query_gradient(queries, query_seg, starts, keys, values, dmixed, logsum, delta)
    dkeys, dvalues = key_gradient(keys, values, query_seg, starts, queries, dmixed, logsum, delta)
    dqueries = dqueries.reshape(tokens.shape).astype(jnp.bfloat16)
    dkeys = dkeys.reshape(tokens.shape).astype(jnp.bfloat16)
    dvalues = dvalues.reshape(tokens.shape).astype(jnp.bfloat16)
    tokens_grad = (
        dfirst_sum
        + project_back(dqueries, query_weight)
        + project_back(dkeys, key_weight)
        + project_back(dvalues, value_weight)
    )
    sums = (
        outer_sum(tokens, dqueries),
        row_sum(dqueries),
        outer_sum(tokens, dkeys),
        outer_sum(tokens, dvalues),
        row_sum(dvalues),
        outer_sum(mixed_low, dbranch),
        row_sum(dbranch),
        dgain_first,
        dshift_first,
        outer_sum(first_low, dinner),
        row_sum(dinner),
        outer_sum(active, douter),
        row_sum(douter),
        dgain_second,
        dshift_second,
    )
    return (tokens_grad, sums)


def general_device(
    tokens,
    doc_lengths,
    query_weight,
    query_bias,
    key_weight,
    value_weight,
    value_bias,
    out_weight,
    out_bias,
    first_gain,
    first_shift,
    inner_weight,
    inner_bias,
    outer_weight,
    outer_bias,
    second_gain,
    second_shift,
    cotangent,
):
    params = (
        query_weight,
        query_bias,
        key_weight,
        value_weight,
        value_bias,
        out_weight,
        out_bias,
        first_gain,
        first_shift,
        inner_weight,
        inner_bias,
        outer_weight,
        outer_bias,
        second_gain,
        second_shift,
    )
    rows = tokens.shape[2]
    base = lax.axis_index("ctx") * rows
    lengths = doc_lengths[:, 0]
    starts = jnp.cumsum(lengths, axis=-1) - lengths
    outputs = []
    token_parts = []
    sums = None
    for index in range(tokens.shape[0]):
        weights = (
            lax.all_gather(params[0], "wt", axis=0, tiled=True),
            lax.all_gather(params[1], "wt", axis=0, tiled=True),
            lax.all_gather(params[2], "wt", axis=0, tiled=True),
            lax.all_gather(params[3], "wt", axis=0, tiled=True),
            lax.all_gather(params[4], "wt", axis=0, tiled=True),
            lax.all_gather(params[5], "wt", axis=0, tiled=True),
            lax.all_gather(params[6], "wt", axis=0, tiled=True),
            lax.all_gather(params[7], "wt", axis=0, tiled=True),
            lax.all_gather(params[8], "wt", axis=0, tiled=True),
            lax.all_gather(params[9], "wt", axis=0, tiled=True),
            lax.all_gather(params[10], "wt", axis=0, tiled=True),
            lax.all_gather(params[11], "wt", axis=0, tiled=True),
            lax.all_gather(params[12], "wt", axis=0, tiled=True),
            lax.all_gather(params[13], "wt", axis=0, tiled=True),
            lax.all_gather(params[14], "wt", axis=0, tiled=True),
        )
        part_out, saved = forward_pass(
            tokens[index : index + 1, 0], starts[index : index + 1], weights, base
        )
        again = (
            lax.all_gather(params[0], "wt", axis=0, tiled=True),
            lax.all_gather(params[1], "wt", axis=0, tiled=True),
            lax.all_gather(params[2], "wt", axis=0, tiled=True),
            lax.all_gather(params[3], "wt", axis=0, tiled=True),
            lax.all_gather(params[4], "wt", axis=0, tiled=True),
            lax.all_gather(params[5], "wt", axis=0, tiled=True),
            lax.all_gather(params[6], "wt", axis=0, tiled=True),
            lax.all_gather(params[7], "wt", axis=0, tiled=True),
            lax.all_gather(params[8], "wt", axis=0, tiled=True),
            lax.all_gather(params[9], "wt", axis=0, tiled=True),
            lax.all_gather(params[10], "wt", axis=0, tiled=True),
            lax.all_gather(params[11], "wt", axis=0, tiled=True),
            lax.all_gather(params[12], "wt", axis=0, tiled=True),
            lax.all_gather(params[13], "wt", axis=0, tiled=True),
            lax.all_gather(params[14], "wt", axis=0, tiled=True),
        )
        part_grad, part_sums = backward_pass(
            saved, starts[index : index + 1], again, cotangent[index : index + 1, 0]
        )
        outputs.append(part_out)
        token_parts.append(part_grad)
        sums = part_sums if sums is None else jax.tree.map(jnp.add, sums, part_sums)
    output = jnp.concatenate(outputs, axis=0)
    tokens_grad = jnp.concatenate(token_parts, axis=0)
    shards = jax.tree.map(
        lambda part: part.astype(jnp.float32),
        lax.psum_scatter(for_sending(sums), "wt", scatter_dimension=0, tiled=True),
    )
    totals = lax.psum(shards, "ctx")
    return (output[:, None], tokens_grad[:, None]) + tuple(totals)


def flip(value, bits):
    return lax.ppermute(value, "ctx", [(i, i ^ bits) for i in range(8)])


def turn(value, step):
    return lax.ppermute(value, "wt", [(i, (i - step) % 4) for i in range(4)])


def pick(value, index, axis=0):
    return lax.dynamic_index_in_dim(value, index, axis, keepdims=False)


def pair(own, other, bit, axis=0):
    return jnp.where(bit == 0, jnp.stack([own, other], axis), jnp.stack([other, own], axis))


def short(value):
    return value.astype(jnp.bfloat16)


def wide(value):
    return value.astype(jnp.float32)


def dot(left, right):
    return jnp.dot(left, right, preferred_element_type=jnp.float32)


def dot_back(left, right):
    return lax.dot_general(
        left, right, (((1,), (1,)), ((), ())), preferred_element_type=jnp.float32
    )


def dot_sum(left, right):
    return lax.dot_general(
        left, right, (((0,), (0,)), ((), ())), preferred_element_type=jnp.float32
    )


def norm_parts(rows):
    mean = jnp.mean(rows, axis=-1, keepdims=True)
    centered = rows - mean
    spread = jnp.mean(centered * centered, axis=-1, keepdims=True)
    root = lax.rsqrt(spread + EPS)
    return centered * root, root


def norm_back(upstream, normed, root, gain):
    grad = upstream * gain
    mean = jnp.mean(grad, axis=-1, keepdims=True)
    along = jnp.mean(grad * normed, axis=-1, keepdims=True)
    return root * (grad - mean - normed * along)


def gelu_parts(inner):
    rise = 0.5 * (1.0 + lax.erf(inner * ROOT_HALF))
    bell = jnp.exp(-0.5 * inner * inner) * (1.0 / math.sqrt(2.0 * math.pi))
    return inner * rise, rise + inner * bell


def run(kernel, outs, args, scratch=(), scalars=(), specs=None, out_specs=None, aliases=None):
    shapes = tuple(jax.ShapeDtypeStruct(shape, dtype) for shape, dtype in outs)
    whole = pl.BlockSpec(memory_space=pltpu.VMEM)
    in_specs = [pl.BlockSpec(memory_space=pltpu.SMEM)] * len(scalars)
    in_specs += [whole] * len(args) if specs is None else specs
    return pl.pallas_call(
        kernel,
        out_shape=shapes,
        in_specs=in_specs,
        out_specs=tuple([whole] * len(outs) if out_specs is None else out_specs),
        scratch_shapes=list(scratch),
        input_output_aliases=aliases or {},
    )(*scalars, *args)


WHOLE = pl.BlockSpec(memory_space=pltpu.VMEM)
LEFT = pl.BlockSpec(memory_space=pl.ANY)
BF = jnp.bfloat16
F32 = jnp.float32


def where_am_i():
    ctx, own = lax.axis_index("ctx"), lax.axis_index("wt")
    return ctx & 1, (ctx >> 1) & 3, ctx & 3, own


def some_rows(start, count):
    return pl.ds(pl.multiple_of(start, 16), count)


def prepare_heads_kernel(wq, wk, wv, vec, heads_own, heads_send):
    _, quarter, group, _ = where_am_i()
    shard, dim = wq.shape
    width = dim // 4
    for index in range(4):

        @pl.when(group == index)
        def _():
            for slot, ref in enumerate((wq, wk, wv)):
                heads_own[:, slot * width : (slot + 1) * width] = ref[
                    :, index * width : (index + 1) * width
                ]

    part = shard // 2
    heads_send[0:part, :] = heads_own[some_rows((quarter >> 1) * part, part), :]
    heads_send[part:, 0:width] = vec[...]
    heads_send[part:, width:] = jnp.zeros((16, 2 * width), BF)


def prepare_kernel(wo, wi, wo2, w2_send, inner_half, outer_half):
    core, quarter, _, _ = where_am_i()
    shard, dim = wo.shape
    half = wo2.shape[0] // 2
    for index in range(2):

        @pl.when(core == index)
        def _():
            for block in range(4):
                at = block * 2 * half + index * half
                inner_half[:, block * half : (block + 1) * half] = wi[:, at : at + half]
            outer_half[...] = wo2[index * half : (index + 1) * half, :]

    part = shard // 4
    rows = some_rows(quarter * part, part)
    w2_send[0:part, :] = inner_half[rows, 0:dim]
    w2_send[part : 2 * part, :] = inner_half[rows, dim:]
    step = half // 4
    w2_send[2 * part : 2 * part + step, :] = outer_half[some_rows(quarter * step, step), :]
    w2_send[2 * part + step :, :] = wo[rows, :]


CHUNK = 128
WINDOWS = (3, 5, 6, 8)


def chunk_of(ctx, index):
    return ctx ^ ((index >> 2) | (index & 2) | ((index & 1) << 2))


def some_chunks(start, count):
    return pl.ds(pl.multiple_of(start * CHUNK, CHUNK), count * CHUNK)


def over_window(bounds, block, windows, visit):
    if len(windows) == 1:
        visit(pl.ds(0, windows[0] * CHUNK))
        return
    low, count = bounds[0, block], bounds[1, block]
    least = 0
    for size in windows:

        @pl.when((count > least) & (count <= size))
        def _(size=size):
            visit(some_chunks(jnp.minimum(low, windows[-1] - size), size))

        least = size


def attend_rows(qkv, seg_col, seg_row, far, outs, logsum, mixed):
    core, quarter, _, _ = where_am_i()
    group = qkv.shape[0] // 3

    def step(side, carry):
        rows = some_chunks(2 * (2 * side + ((quarter & 1) ^ far)), 2)
        here = some_chunks(2 * side, 2)

        def one_head(head, carry):
            mask = seg_col[rows, :] == seg_row[...]
            scores = dot_back(qkv[head, rows, :], qkv[group + head])
            scores = jnp.where(mask, scores, NEG)
            top = jnp.max(scores, axis=-1, keepdims=True)
            expd = jnp.exp(scores - top)
            total = jnp.sum(expd, axis=-1, keepdims=True)
            probs = short(expd * (1.0 / total))
            mixed[head, here, :] = short(dot(probs, qkv[2 * group + head]))
            lane = lax.broadcasted_iota(jnp.int32, (2 * CHUNK, 128), 1)
            logsum[here, :] = jnp.where(lane == head, top + jnp.log(total), logsum[here, :])
            return carry

        lax.fori_loop(0, group, one_head, 0)
        return carry

    logsum[...] = jnp.zeros_like(logsum)
    lax.fori_loop(0, 2, step, 0)
    y = quarter >> 1
    for index, out in enumerate(outs):
        for side in range(2):
            chunk = 2 * (y ^ side) + (core ^ index)
            for head in range(group):
                out[
                    side * CHUNK : (side + 1) * CHUNK, head * HEAD_DIM : (head + 1) * HEAD_DIM
                ] = mixed[head, some_chunks(chunk, 1), :]


def attend_near_kernel(
    mine, other, far, heads_own, g1, g2, g3, h1, h2, h3, vec, seg_col, seg_row,
    qkv, m0, m1, logsum, weight, vectors, inner_b, mixed, bias,
):
    core, quarter, group, own = where_am_i()
    ctx = lax.axis_index("ctx")
    shard = heads_own.shape[0]
    part = shard // 2
    y = quarter >> 1
    bias[:, shard : 2 * shard] = jnp.zeros_like(bias[:, :shard])
    for index in range(4):

        @pl.when(own == index)
        def _():
            for step, ref, at in ((0, vec, 0), (1, g1, part), (2, g2, part), (3, g3, part)):
                row = (index + step) % 4
                block = wide(ref[at : at + 16, 0:shard])
                lane = row * shard
                vectors[:, lane : lane + shard] = block[0:8]
                lines = jnp.where(core == 0, block[8:10], block[10:12])
                for side in range(2):
                    lane = (2 * row + side) * shard
                    inner_b[:, lane : lane + shard] = lines[side : side + 1]

                @pl.when(group == row)
                def _():
                    bias[:, 0:shard] = block[0:1]
                    bias[:, 2 * shard :] = block[1:2]

    weight[some_rows(own * shard, shard), :] = heads_own[...]
    for step, near_half, far_half in ((1, g1, h1), (2, g2, h2), (3, g3, h3)):
        at = ((own + step) & 3) * shard
        weight[some_rows(at + part * y, part), :] = near_half[0:part, :]
        weight[some_rows(at + part * (1 - y), part), :] = far_half[0:part, :]
    index = 0
    for source in (mine, other, far):
        for first in range(0, source.shape[0], 2 * CHUNK):
            low = short(dot(source[first : first + 2 * CHUNK, :], weight[...]) + bias[...])
            for half in range(2):
                at = pl.multiple_of(chunk_of(ctx, index) * CHUNK, CHUNK)
                for slot in range(qkv.shape[0]):
                    value = low[
                        half * CHUNK : (half + 1) * CHUNK,
                        slot * HEAD_DIM : (slot + 1) * HEAD_DIM,
                    ]
                    if slot < qkv.shape[0] // 3:
                        value = value * jnp.asarray(HEAD_DIM ** (-0.5), BF)
                    qkv[slot, pl.ds(at, CHUNK), :] = value
                index += 1
    attend_rows(qkv, seg_col, seg_row, 0, (m0, m1), logsum, mixed)


def attend_far_kernel(qkv, seg_col, seg_row, m2, m3, logsum, mixed):
    attend_rows(qkv, seg_col, seg_row, 1, (m2, m3), logsum, mixed)


def project_kernel(m0, m1, m2, m3, mine, vec, wo, *refs):
    pieces, (first_sum, first_low, out_full, sems) = refs[:12], refs[12:]
    _, quarter, group, own = where_am_i()
    shard = wo.shape[0]
    part = shard // 4
    copies = [(wo, out_full.at[some_rows(own * shard, shard), :])]
    for index, piece in enumerate(pieces):
        at = ((own + 1 + index // 4) & 3) * shard + part * (quarter ^ (index % 4))
        rows = piece.shape[0]
        copies.append((piece.at[rows - part : rows, :], out_full.at[some_rows(at, part), :]))
    copies = [
        pltpu.make_async_copy(source, target, sems.at[index])
        for index, (source, target) in enumerate(copies)
    ]
    for copy in copies:
        copy.start()
    total = wide(mine[...]) + vec[2:3, :]
    for copy in copies:
        copy.wait()
    for code, ref in enumerate((m0, m1, m2, m3)):
        total += dot(ref[...], out_full[some_rows((group ^ code) * shard, shard), :])
    first_sum[...] = total
    first_low[...] = short(norm_parts(total)[0] * vec[3:4, :] + vec[4:5, :])


def forward_kernel(near, far, bias, inner_half, outer_half, *refs):
    pieces, (keep, send, slope, active, wi_full, wo2_full, wi, wo2, sems) = refs[:12], refs[12:]
    _, quarter, _, own = where_am_i()
    shard, half = inner_half.shape[0], outer_half.shape[0]
    dim = keep.shape[1]
    part, step = shard // 4, half // 4
    first = [(inner_half, wi.at[some_rows(own * shard, shard), :])]
    second = [(outer_half, wo2.at[some_rows(own * half, half), :])]
    for index, piece in enumerate(pieces):
        row, spot = (own + 1 + index // 4) & 3, quarter ^ (index % 4)
        rows = some_rows(row * shard + part * spot, part)
        for side in range(2):
            first.append(
                (
                    piece.at[side * part : (side + 1) * part, :],
                    wi.at[rows, side * dim : (side + 1) * dim],
                )
            )
        rows = some_rows(row * half + step * spot, step)
        second.append((piece.at[2 * part : 2 * part + step, :], wo2.at[rows, :]))
    copies = [
        pltpu.make_async_copy(source, target, sems.at[index])
        for index, (source, target) in enumerate(first + second)
    ]
    for copy in copies:
        copy.start()
    for copy in copies[: len(first)]:
        copy.wait()
    back = [
        pltpu.make_async_copy(wi, wi_full, sems.at[len(copies)]),
        pltpu.make_async_copy(wo2, wo2_full, sems.at[len(copies) + 1]),
    ]
    back[0].start()
    count = near.shape[0]
    chunk = 512
    waiting = True
    for index, (source, out) in enumerate(((far, send), (near, keep))):
        at = (1 - index) * count
        total = None
        for lane in range(0, slope.shape[1], chunk):
            lanes = slice(lane, lane + chunk)
            value, rate = gelu_parts(dot(source[...], wi[:, lanes]) + bias[:, lanes])
            low = short(value)
            slope[at : at + count, lanes] = short(rate)
            active[at : at + count, lanes] = low
            if waiting:
                for copy in copies[len(first) :]:
                    copy.wait()
                back[1].start()
                waiting = False
            added = dot(low, wo2[lanes, :])
            total = added if total is None else total + added
        out[...] = total
    for copy in back:
        copy.wait()


def turnaround_kernel(first_sum, keep, got, vec, cot0, cot1, out0, out1, dsecond, douter, sums):
    rows = cot0.shape[0]
    first = norm_parts(first_sum[...])[0] * vec[3:4, :] + vec[4:5, :]
    normed, root = norm_parts(first + vec[5:6, :] + keep[...] + got[...])
    output = short(normed * vec[6:7, :] + vec[7:8, :])
    out0[...] = output[:rows]
    out1[...] = output[rows:]
    upstream = jnp.concatenate([wide(cot0[...]), wide(cot1[...])])
    back = norm_back(upstream, normed, root, vec[6:7, :])
    low = short(back)
    dsecond[...] = back
    douter[...] = low
    sums[0:1, :] = jnp.sum(wide(low), axis=0, keepdims=True)
    sums[1:2, :] = jnp.sum(upstream * normed, axis=0, keepdims=True)
    sums[2:3, :] = jnp.sum(upstream, axis=0, keepdims=True)
    sums[3:, :] = jnp.zeros_like(sums[3:, :])


def backward_kernel(near, far, slope, wo2, wi_full, keep, send, dinner, sums, wi, sem):
    copy = pltpu.make_async_copy(wi_full, wi, sem)
    copy.start()
    count, dim = near.shape
    chunk = 512
    waiting = True
    for index, (source, out) in enumerate(((far, send), (near, keep))):
        at = (1 - index) * count
        total = None
        for lane in range(0, slope.shape[1], chunk):
            lanes = slice(lane, lane + chunk)
            rate = wide(slope[at : at + count, lanes])
            low = short(dot_back(source[...], wo2[lanes, :]) * rate)
            dinner[at : at + count, lanes] = low
            if waiting:
                copy.wait()
                waiting = False
            added = dot_back(low, wi[:, lanes])
            total = added if total is None else total + added
        out[...] = total
    total = jnp.sum(wide(dinner[...]), axis=0, keepdims=True)
    sums[0:1, :] = total[:, :dim]
    sums[1:2, :] = total[:, dim:]
    sums[2:, :] = jnp.zeros_like(sums[2:, :])


def weights_kernel(first0, first1, douter0, douter1, dinner, active, ak, az, bk, bz, left, right):
    _, quarter, _, _ = where_am_i()
    x, y = quarter & 1, quarter >> 1
    count = first0.shape[0]
    part, step = first0.shape[1] // 16, active.shape[1] // 16
    left[...] = short(dot_sum(first0[...], dinner[:count]) + dot_sum(first1[...], dinner[count:]))
    for block in range(8):
        rows = slice(block * part, (block + 1) * part)
        ak[rows, :] = left[some_rows((2 * block + x) * part, part), :]
        az[rows, :] = left[some_rows((2 * block + 1 - x) * part, part), :]
    right[...] = short(
        dot_sum(active[:count], douter0[...]) + dot_sum(active[count:], douter1[...])
    )
    for block in range(8):
        row, side = block // 2, block % 2
        rows = slice(block * step, (block + 1) * step)
        bk[rows, :] = right[some_rows((4 * row + 2 * y + side) * step, step), :]
        bz[rows, :] = right[some_rows((4 * row + 2 * (1 - y) + side) * step, step), :]


def branch_kernel(first_sum, dsecond, keep, got, vec, out_full, dfirst_sum, dbranch, d0, d1, d2, d3, sums):
    _, _, group, _ = where_am_i()
    shard = d0.shape[1]
    normed, root = norm_parts(first_sum[...])
    dfirst = dsecond[...] + keep[...] + got[...]
    back = norm_back(dfirst, normed, root, vec[3:4, :])
    low = short(back)
    dfirst_sum[...] = back
    dbranch[...] = low
    for code, ref in enumerate((d0, d1, d2, d3)):
        ref[...] = short(dot_back(low, out_full[some_rows((group ^ code) * shard, shard), :]))
    sums[0:1, :] = jnp.sum(wide(low), axis=0, keepdims=True)
    sums[1:2, :] = jnp.sum(dfirst * normed, axis=0, keepdims=True)
    sums[2:3, :] = jnp.sum(dfirst, axis=0, keepdims=True)
    sums[3:, :] = jnp.zeros_like(sums[3:, :])


def out_weight_kernel(m0, m1, m2, m3, dbranch, sums1, sums2, sums3, ck, cz, whole):
    core, _, group, _ = where_am_i()
    shard, dim = m0.shape[1], dbranch.shape[1]
    half = dim // 2
    for code, ref in enumerate((m0, m1, m2, m3)):
        whole[some_rows((group ^ code) * shard, shard), :] = short(
            dot_sum(ref[...], dbranch[...])
        )
    for side in range(2):

        @pl.when(core == side)
        def _():
            for ref, which in ((ck, side), (cz, 1 - side)):
                ref[0:dim, :] = whole[:, which * half : (which + 1) * half]

    rows = short(
        jnp.concatenate([sums1[0:3, :], sums2[0:3, :], sums3[0:2, :], jnp.zeros_like(sums1[...])])
    )
    for ref in (ck, cz):
        ref[dim : dim + 16, :] = rows[:, :half]
        ref[dim + 16 :, :] = rows[:, half:]


def out_split_kernel(packed, got, ck, cz):
    core, quarter, _, _ = where_am_i()
    x = quarter & 1
    dim = packed.shape[0] - 32
    part = dim // 16
    for block in range(8):
        rows = slice(block * part, (block + 1) * part)
        for ref, side in ((ck, x), (cz, 1 - x)):
            take = some_rows((2 * block + side) * part, part)
            ref[rows, :] = short(wide(packed[take, :]) + wide(got[take, :]))
    for lanes in range(2):
        at = dim + 16 * lanes
        mine, other = wide(packed[at : at + 16, :]), wide(got[at : at + 16, :])
        low = jnp.where(core == 0, mine, other)[6:8]
        high = jnp.where(core == 0, other, mine)[6:8]
        rows = jnp.concatenate([(mine + other)[0:6], low, high, jnp.zeros_like(mine[0:6])])
        at = 8 * part + 16 * lanes
        for ref in (ck, cz):
            ref[at : at + 16, :] = short(rows)


def reduce_rows(keep, got, outs, bit):
    size = keep.shape[0] // 8
    size -= size % 16
    width = keep.shape[1] // len(outs)
    for lane, pair_of in enumerate(outs):
        lanes = slice(lane * width, (lane + 1) * width)
        for block in range(4):
            for out, side in zip(pair_of, (bit, 1 - bit)):
                take = some_rows((2 * block + side) * size, size)
                out[block * size : (block + 1) * size, :] = short(
                    wide(keep[take, lanes]) + wide(got[take, lanes])
                )
        if keep.shape[0] > 8 * size:
            for out in pair_of:
                out[4 * size :, :] = short(
                    wide(keep[8 * size :, lanes]) + wide(got[8 * size :, lanes])
                )


def reduce_kernel(ak, ar, bk, br, *outs):
    _, quarter, _, _ = where_am_i()
    reduce_rows(ak, ar, (outs[0:2], outs[4:6]), quarter >> 1)
    reduce_rows(bk, br, (outs[2:4], outs[6:8]), quarter & 1)


def reduce_out_kernel(ck, cr, c2k, c2z):
    _, quarter, _, _ = where_am_i()
    reduce_rows(ck, cr, ((c2k, c2z),), quarter >> 1)


def owners_kernel(*refs):
    inputs, outs = refs[:-4], refs[-4:]
    _, _, _, own = where_am_i()
    ak, ar, bk, br = inputs[:4]
    half = bk.shape[1]
    part = ak.shape[0] // 4
    for index, out in enumerate(outs):
        row = (own - index) & 3
        rows = some_rows(row * part, part)
        out[0:part, :] = (wide(ak[rows, :]) + wide(ar[rows, :])).astype(out.dtype)
        for side in range(2):
            rows = some_rows((2 * row + side) * part, part)
            out[part : 2 * part, side * half : (side + 1) * half] = (
                wide(bk[rows, :]) + wide(br[rows, :])
            ).astype(out.dtype)
        if len(inputs) > 4:
            ck, cr = inputs[4:]
            at = 2 * part
            rows = some_rows(row * part, part)
            out[at:, 0:half] = (wide(ck[rows, :]) + wide(cr[rows, :])).astype(out.dtype)
            tail = wide(ck[4 * part :, :]) + wide(cr[4 * part :, :])
            out[at : at + 32, half:] = tail.astype(out.dtype)
            out[at + 32 :, half:] = jnp.zeros((part - 32, half), out.dtype)


def total_kernel(mine, *refs):
    total = wide(mine[...])
    for ref in refs[:-1]:
        total += wide(ref[...])
    refs[-1][...] = short(total)


def finish_rows(pieces, part, half, spread):
    core, quarter, _, _ = where_am_i()
    dwi, dwo2, dwo = spread
    for side in range(2):

        @pl.when(core == side)
        def _():
            for index, piece in enumerate(pieces):
                spot = quarter ^ (index % 4)
                which = side if index < 4 else 1 - side
                rows = some_rows(spot * part, part)
                for block in range(2):
                    at = block * 2 * half + which * half
                    dwi[rows, at : at + half] = wide(piece[0:part, block * half : (block + 1) * half])
                    at = which * half + spot * 2 * part + block * part
                    dwo2[some_rows(at, part), :] = wide(
                        piece[part : 2 * part, block * half : (block + 1) * half]
                    )
                if dwo is not None:
                    dwo[rows, which * half : (which + 1) * half] = wide(piece[2 * part :, 0:half])


def send_lane(lane, dwi, dwo2, wi_out, wo2_out, sems):
    width, half = dwi.shape[1], dwo2.shape[1]
    copies = [
        pltpu.make_async_copy(dwi, wi_out.at[:, lane * width : (lane + 1) * width], sems.at[0]),
        pltpu.make_async_copy(dwo2, wo2_out.at[:, lane * half : (lane + 1) * half], sems.at[1]),
    ]
    for copy in copies:
        copy.start()
    for copy in copies:
        copy.wait()


def finish_first_kernel(*refs):
    pieces, (wi_out, wo2_out, dwi, dwo2, sems) = refs[:8], refs[8:]
    part, half = dwi.shape[0] // 4, dwo2.shape[1]
    finish_rows(pieces, part, half, (dwi, dwo2, None))
    send_lane(0, dwi, dwo2, wi_out, wo2_out, sems)


def finish_kernel(*refs):
    pieces, (unused0, unused1, wi_out, wo2_out, dwo, small, dwi, dwo2, sems) = refs[:8], refs[8:]
    part, half = dwi.shape[0] // 4, dwo2.shape[1]
    finish_rows(pieces, part, half, (dwi, dwo2, dwo))
    last = pieces[0]
    small[:, 0:half] = wide(last[2 * part : 2 * part + 16, half:])
    small[:, half:] = wide(last[2 * part + 16 : 2 * part + 32, half:])
    send_lane(1, dwi, dwo2, wi_out, wo2_out, sems)


def attend_back_kernel(
    bounds, qkv, logsum0, logsum1, seg_col, seg_row, p0, p1, p2, p3, mine, other, far,
    h0, h1, h2, h3, grads, dqueries, dkeys, dvalues, dweight, dmixed, logsum, whole,
):
    _, quarter, _, own = where_am_i()
    ctx = lax.axis_index("ctx")
    x = quarter & 1
    scale = HEAD_DIM ** (-0.5)
    group = qkv.shape[0] // 3
    width = group * HEAD_DIM
    block = p0.shape[0]
    dkeys[...] = jnp.zeros_like(dkeys)
    dvalues[...] = jnp.zeros_like(dvalues)
    for index, part in enumerate((p0, p2, p1, p3)):
        for side in range(2):
            chunk = chunk_of(ctx, 2 * index + side)
            for head in range(group):
                dmixed[head, some_chunks(chunk, 1), :] = part[
                    side * CHUNK : (side + 1) * CHUNK, head * HEAD_DIM : (head + 1) * HEAD_DIM
                ]
    for side in range(2):
        rows = slice(2 * side * CHUNK, 2 * (side + 1) * CHUNK)
        logsum[some_chunks(2 * (2 * side + x), 2), :] = logsum0[rows, :]
        logsum[some_chunks(2 * (2 * side + 1 - x), 2), :] = logsum1[rows, :]

    def step(index, carry):
        rows = some_chunks(2 * index, 2)

        def visit(window):
            def one_head(head, carry):
                mask = seg_col[rows, :] == seg_row[:, window]
                query = qkv[head, rows, :]
                grad = dmixed[head, rows, :]
                keys = qkv[group + head, window, :]
                lane = lax.broadcasted_iota(jnp.int32, (2 * CHUNK, 128), 1)
                sums = jnp.sum(
                    jnp.where(lane == head, logsum[rows, :], 0.0), axis=-1, keepdims=True
                )
                scores = jnp.where(mask, dot_back(query, keys), NEG)
                probs = jnp.exp(scores - sums)
                dprobs = dot_back(grad, qkv[2 * group + head, window, :])
                delta = jnp.sum(probs * dprobs, axis=-1, keepdims=True)
                dscores = short(probs * (dprobs - delta))
                dqueries[head, rows, :] = short(dot(dscores, keys) * scale)
                dkeys[head, window, :] += dot_sum(dscores, query)
                dvalues[head, window, :] += dot_sum(short(probs), grad)
                return carry

            lax.fori_loop(0, group, one_head, 0)

        over_window(bounds, index, WINDOWS, visit)
        return carry

    lax.fori_loop(0, 4, step, 0)
    for head in range(group):
        whole[:, head * HEAD_DIM : (head + 1) * HEAD_DIM] = dqueries[head]
        at = width + head * HEAD_DIM
        whole[:, at : at + HEAD_DIM] = short(dkeys[head])
        whole[:, at + width : at + width + HEAD_DIM] = short(dvalues[head])
    for index in range(8):
        grads[index * CHUNK : (index + 1) * CHUNK, :] = whole[
            some_chunks(chunk_of(ctx, index), 1), :
        ]
    rows = 2 * block
    dweight[...] = (
        dot_sum(mine[...], grads[:block])
        + dot_sum(other[...], grads[block:rows])
        + dot_sum(far[...], grads[rows:])
    )
    sums = jnp.sum(wide(grads[...]), axis=0, keepdims=True)
    lines = sums.shape[1] // HEAD_DIM
    for index, out in enumerate((h0, h1, h2, h3)):
        take = pl.ds(pl.multiple_of(((own - index) & 3) * width, 16), width)
        out[:, 0 : 3 * width] = dweight[take, :].astype(out.dtype)
        out[:, 3 * width :] = jnp.zeros((width, HEAD_DIM), out.dtype)
        for line in range(lines):
            out[line : line + 1, 3 * width :] = sums[
                :, line * HEAD_DIM : (line + 1) * HEAD_DIM
            ].astype(out.dtype)


def tokens_kernel(grads, weight, keep, send):
    rows = keep.shape[0]
    keep[...] = dot_back(grads[:rows], weight[...])
    send[...] = short(dot_back(grads[rows:], weight[...]))


def merge_kernel(keep, got, base, near, far):
    total = keep[...] + wide(got[...])
    count = near.shape[0]
    near[...] = total[:count] + base[...]
    far[...] = short(total[count:])


def heads_kernel(s0, s1, s2, s3, dq, dk, dv, bias):
    _, _, group, own = where_am_i()
    shard = dq.shape[0]
    for index in range(4):

        @pl.when(group == index)
        def _():
            for code, ref in enumerate((s0, s1, s2, s3)):
                at = (index ^ code) * shard
                for slot, out in enumerate((dq, dk, dv)):
                    out[:, at : at + shard] = wide(
                        ref[0:shard, slot * shard : (slot + 1) * shard]
                    )

                @pl.when(own == index ^ code)
                def _():
                    for line in range(bias.shape[1] // HEAD_DIM):
                        bias[0:1, line * HEAD_DIM : (line + 1) * HEAD_DIM] = wide(
                            ref[line : line + 1, 3 * shard :]
                        )


def plane_steps(
    tokens,
    doc_lengths,
    query_weight,
    query_bias,
    key_weight,
    value_weight,
    value_bias,
    out_weight,
    out_bias,
    first_gain,
    first_shift,
    inner_weight,
    inner_bias,
    outer_weight,
    outer_bias,
    second_gain,
    second_shift,
    cotangent,
):
    ctx, own = lax.axis_index("ctx"), lax.axis_index("wt")
    y = ctx >> 2
    rows, dim = tokens.shape[2], tokens.shape[3]
    shard = query_weight.shape[0]
    hidden = outer_weight.shape[0]
    half = hidden // 2
    count = 2 * rows

    mine = jnp.concatenate([pick(tokens[:, 0], y), flip(pick(tokens[:, 0], 1 - y), 4)])
    other = flip(mine, 2)
    far = flip(jnp.concatenate([mine, other]), 1)

    vector_list = (
        query_bias,
        value_bias,
        out_bias,
        first_gain,
        first_shift,
        outer_bias,
        second_gain,
        second_shift,
        *[inner_bias[at : at + shard] for at in range(0, 4 * shard, shard)],
    )
    line = lax.broadcasted_iota(jnp.int32, (16, shard), 0)
    vec = jnp.zeros((16, shard), BF)
    for index, value in enumerate(vector_list):
        vec = jnp.where(line == index, value[None, :], vec)
    heads_own, heads_send = run(
        prepare_heads_kernel,
        [((shard, 3 * shard), BF), ((shard // 2 + 16, 3 * shard), BF)],
        (query_weight, key_weight, value_weight, vec),
    )
    w2_send, inner_half, outer_half = run(
        prepare_kernel,
        [((shard // 4 * 3 + half // 4, dim), BF), ((shard, 4 * half), BF), ((half, dim), BF)],
        (out_weight, inner_weight, outer_weight),
    )
    got = [turn(heads_send, step) for step in (1, 2, 3)]
    gone = [flip(value, 4) for value in got]
    pieces = []
    for step in (1, 2, 3):
        piece = turn(w2_send, step)
        pieces += [piece] + [flip(piece, bits) for bits in (2, 4, 6)]

    lengths = pick(doc_lengths[:, 0], y)
    starts = jnp.cumsum(lengths) - lengths
    total = 8 * rows
    positions = jnp.arange(total, dtype=jnp.int32)
    seg = jnp.sum((starts[None, :] <= positions[:, None]).astype(jnp.int32), axis=-1) - 1
    segs = (seg[:, None], seg[None, :])
    first = jnp.arange(4, dtype=jnp.int32)[:, None] * (2 * CHUNK)
    low = jnp.max(jnp.where(starts[None, :] <= first, starts[None, :], 0), axis=-1) // CHUNK
    ends = jnp.where(starts[None, :] >= first + 2 * CHUNK, starts[None, :], total)
    bounds = jnp.stack([low, (jnp.min(ends, axis=-1) - 1) // CHUNK - low + 1])

    qkv, m0, m1, logsum0, heads_weight, vectors, inner_b = run(
        attend_near_kernel,
        [
            ((9, total, HEAD_DIM), BF),
            ((count, shard), BF),
            ((count, shard), BF),
            ((2 * count, 128), F32),
            ((dim, 3 * shard), BF),
            ((8, dim), F32),
            ((1, 4 * half), F32),
        ],
        (mine, other, far, heads_own, *got, *gone, vec, *segs),
        [pltpu.VMEM((3, 2 * count, HEAD_DIM), BF), pltpu.VMEM((1, 3 * shard), F32)],
    )
    m2, m3, logsum1 = run(
        attend_far_kernel,
        [((count, shard), BF), ((count, shard), BF), ((2 * count, 128), F32)],
        (qkv, *segs),
        [pltpu.VMEM((3, 2 * count, HEAD_DIM), BF)],
    )
    mixed = [m0, flip(m1, 1), flip(m2, 2), flip(m3, 3)]

    first_sum, first_low, out_full = run(
        project_kernel,
        [((count, dim), F32), ((count, dim), BF), ((dim, dim), BF)],
        (*mixed, mine, vectors, out_weight, *pieces),
        [pltpu.SemaphoreType.DMA((13,))],
        specs=[WHOLE] * 6 + [LEFT] * 13,
    )
    first_far = flip(first_low, 1)
    keep, send, slope, active, wi_full, wo2_full = run(
        forward_kernel,
        [
            ((count, dim), F32),
            ((count, dim), F32),
            ((2 * count, 4 * half), BF),
            ((2 * count, 4 * half), BF),
            ((dim, 4 * half), BF),
            ((4 * half, dim), BF),
        ],
        (first_low, first_far, inner_b, inner_half, outer_half, *pieces),
        [
            pltpu.VMEM((dim, 4 * half), BF),
            pltpu.VMEM((4 * half, dim), BF),
            pltpu.SemaphoreType.DMA((40,)),
        ],
        specs=[WHOLE] * 3 + [LEFT] * 14,
        out_specs=[WHOLE] * 4 + [LEFT] * 2,
    )
    cot = pick(cotangent[:, 0], y), flip(pick(cotangent[:, 0], 1 - y), 4)
    out0, out1, dsecond, douter, sums2 = run(
        turnaround_kernel,
        [
            ((rows, dim), BF),
            ((rows, dim), BF),
            ((count, dim), F32),
            ((count, dim), BF),
            ((8, dim), F32),
        ],
        (first_sum, keep, flip(send, 1), vectors, *cot),
    )
    output = pair(out0, flip(out1, 4), y)

    douter_far = flip(douter, 1)
    keep, send, dinner, sums3 = run(
        backward_kernel,
        [
            ((count, dim), F32),
            ((count, dim), F32),
            ((2 * count, 4 * half), BF),
            ((8, dim), F32),
        ],
        (douter, douter_far, slope, wo2_full, wi_full),
        [pltpu.VMEM((dim, 4 * half), BF), pltpu.SemaphoreType.DMA],
        specs=[WHOLE] * 4 + [LEFT],
    )
    dfirst_sum, dbranch, d0, d1, d2, d3, sums1 = run(
        branch_kernel,
        [((count, dim), F32), ((count, dim), BF)] + [((count, shard), BF)] * 4 + [((8, dim), F32)],
        (first_sum, dsecond, keep, flip(send, 1), vectors, out_full),
    )
    dmixed = [d0, flip(d1, 1), flip(d2, 2), flip(d3, 3)]

    ak, az, bk, bz = run(
        weights_kernel,
        [((dim // 2, 4 * half), BF)] * 2 + [((2 * half, dim), BF)] * 2,
        (first_low, first_far, douter, douter_far, dinner, active),
        [pltpu.VMEM((dim, 4 * half), BF), pltpu.VMEM((4 * half, dim), BF)],
    )
    ar, br = flip(az, 2), flip(bz, 4)
    ck, cz = run(
        out_weight_kernel,
        [((dim + 32, dim // 2), BF)] * 2,
        (*mixed, dbranch, sums1, sums2, sums3),
        [pltpu.VMEM((dim, dim), BF)],
    )
    ck, cz = run(out_split_kernel, [((dim // 2 + 32, dim // 2), BF)] * 2, (ck, flip(cz, 1)))
    cr = flip(cz, 2)

    h0, h1, h2, h3, grads = run(
        attend_back_kernel,
        [((shard, 3 * shard + HEAD_DIM), F32)]
        + [((shard, 3 * shard + HEAD_DIM), BF)] * 3
        + [((4 * count, 3 * shard), BF)],
        (qkv, logsum0, logsum1, *segs, *dmixed, mine, other, far),
        [
            pltpu.VMEM((3, 4 * count, HEAD_DIM), BF),
            pltpu.VMEM((3, 4 * count, HEAD_DIM), F32),
            pltpu.VMEM((3, 4 * count, HEAD_DIM), F32),
            pltpu.VMEM((dim, 3 * shard), F32),
            pltpu.VMEM((3, total, HEAD_DIM), BF),
            pltpu.VMEM((total, 128), F32),
            pltpu.VMEM((total, 3 * shard), BF),
        ],
        scalars=(bounds,),
    )
    keep, send = run(
        tokens_kernel, [((2 * count, dim), F32), ((2 * count, dim), BF)], (grads, heads_weight)
    )

    c2k, c2z = run(reduce_out_kernel, [((dim // 4 + 32, dim // 2), BF)] * 2, (ck, cr))
    reduced = run(
        reduce_kernel,
        ([((dim // 4, 2 * half), BF)] * 2 + [((half, dim // 2), BF)] * 2) * 2,
        (ak, ar, bk, br),
    )
    plane = []
    for lane in range(2):
        a2k, a2z, b2k, b2z = reduced[4 * lane : 4 * lane + 4]
        last = [a2k, flip(a2z, 4), b2k, flip(b2z, 2)]
        size = shard // 4 * 2
        if lane == 1:
            last += [c2k, flip(c2z, 4)]
            size = shard // 4 * 3
        p0, p1, p2, p3 = run(owners_kernel, [((size, dim), F32)] + [((size, dim), BF)] * 3, last)
        turned = [turn(p, step) for step, p in ((1, p1), (2, p2), (3, p3))]
        (piece,) = run(total_kernel, [((size, dim), BF)], (p0, *turned))
        near = [piece] + [flip(piece, bits) for bits in (2, 4, 6)]
        plane.append(near + [flip(p, 1) for p in near])
    staged = [
        pltpu.VMEM((shard, 4 * half), F32),
        pltpu.VMEM((hidden, half), F32),
        pltpu.SemaphoreType.DMA((2,)),
    ]
    grown = [((shard, 8 * half), F32), ((hidden, dim), F32)]
    first_lane = run(finish_first_kernel, grown, plane[0], staged, out_specs=[LEFT] * 2)
    dinner_w, douter_w, dout_w, small = run(
        finish_kernel,
        grown + [((shard, dim), F32), ((16, dim), F32)],
        (*plane[1], *first_lane),
        staged,
        specs=[WHOLE] * 8 + [LEFT] * 2,
        out_specs=[LEFT] * 2 + [WHOLE] * 2,
        aliases={8: 0, 9: 1},
    )
    dinner_b = pick(small[6:10].reshape(2, 4, half), own, 1).reshape(hidden)
    small = lax.dynamic_slice_in_dim(small[:6], own * shard, shard, 1)

    (heads,) = run(
        total_kernel,
        [((shard, 3 * shard + HEAD_DIM), BF)],
        (h0, turn(h1, 1), turn(h2, 2), turn(h3, 3)),
    )
    (heads,) = run(total_kernel, [((shard, 3 * shard + HEAD_DIM), BF)], (heads, flip(heads, 4)))
    dquery_w, dkey_w, dvalue_w, heads_b = run(
        heads_kernel,
        [((shard, dim), F32)] * 3 + [((8, 3 * shard), F32)],
        (heads, flip(heads, 1), flip(heads, 2), flip(heads, 3)),
    )

    near_t, far_t = run(
        merge_kernel, [((count, dim), F32), ((count, dim), BF)], (keep, flip(send, 1), dfirst_sum)
    )
    dtokens = near_t + wide(flip(far_t, 2))
    swapped = flip(short(dtokens[rows:]), 4)
    tokens_grad = pair(dtokens[:rows], wide(swapped), y)

    return (
        output[:, None],
        tokens_grad[:, None],
        dquery_w,
        heads_b[0, :shard],
        dkey_w,
        dvalue_w,
        heads_b[0, 2 * shard :],
        dout_w,
        small[0],
        small[1],
        small[2],
        dinner_w,
        dinner_b,
        douter_w,
        small[3],
        small[4],
        small[5],
    )


def plane_device(*args):
    return plane_steps(*args)


def solution(mesh):
    placed = (
        P(None, "wt", "ctx", None),
        P(None, "wt", None),
        P("wt", None),
        P("wt"),
        P("wt", None),
        P("wt", None),
        P("wt"),
        P("wt", None),
        P("wt"),
        P("wt"),
        P("wt"),
        P("wt", None),
        P("wt"),
        P("wt", None),
        P("wt"),
        P("wt"),
        P("wt"),
        P(None, "wt", "ctx", None),
    )
    fits = mesh.shape["ctx"] == 8 and mesh.shape["wt"] == 4
    return jax.shard_map(
        plane_device if fits else general_device,
        mesh=mesh,
        in_specs=placed,
        out_specs=(
            P(None, "wt", "ctx", None),
            P(None, "wt", "ctx", None),
            P("wt", None),
            P("wt"),
            P("wt", None),
            P("wt", None),
            P("wt"),
            P("wt", None),
            P("wt"),
            P("wt"),
            P("wt"),
            P("wt", None),
            P("wt"),
            P("wt", None),
            P("wt"),
            P("wt"),
            P("wt"),
        ),
        check_vma=False,
    )
```

```python
import math

import jax
import jax.numpy as jnp
from jax import lax
from jax.experimental import pallas as pl
from jax.experimental.pallas import tpu as pltpu
from jax.sharding import PartitionSpec as P


HEADS = 12
HEAD_DIM = 64


EPS = 1e-12
NEG = -1e30
ROOT_HALF = 0.7071067811865476


def for_sending(shard):

    def short(part):
        return part.astype(jnp.bfloat16) if part.dtype == jnp.float32 else part

    return jax.tree.map(short, shard)


def normalize(rows, gain, shift):
    mean = jnp.mean(rows, axis=-1, keepdims=True)
    centered = rows - mean
    spread = jnp.mean(centered * centered, axis=-1, keepdims=True)
    return centered * lax.rsqrt(spread + EPS) * gain + shift


def gelu(inner):
    return 0.5 * inner * (1.0 + lax.erf(inner * ROOT_HALF))


def segment_of(starts, positions):
    found = (starts[:, None, :] <= positions[:, :, None]).astype(jnp.int32)
    return jnp.sum(found, axis=-1) - 1


def project(inputs, weight):
    return jnp.einsum("btd,de->bte", inputs, weight, preferred_element_type=jnp.float32)


def project_back(grads, weight):
    return jnp.einsum("bte,de->btd", grads, weight, preferred_element_type=jnp.float32)


def outer_sum(inputs, grads):
    return jnp.einsum("btd,bte->de", inputs, grads, preferred_element_type=jnp.float32)


def row_sum(grads):
    return jnp.sum(grads.astype(jnp.float32), axis=(0, 1))


def heads_of(array):
    return array.reshape(array.shape[0], array.shape[1], HEADS, HEAD_DIM)


def block_loop(width, carry, visit):
    block = math.gcd(width, 512)

    def step(state, index):
        return (visit(state, index * block, block), None)

    carry, _ = lax.scan(step, carry, jnp.arange(width // block, dtype=jnp.int32))
    return carry


def reaches(starts, own_seg, first, count):
    positions = first + jnp.arange(count, dtype=jnp.int32)
    other = segment_of(starts, jnp.broadcast_to(positions, (starts.shape[0], count)))
    touch = jnp.any((other[:, 0] <= own_seg[:, -1]) & (other[:, -1] >= own_seg[:, 0]))
    return (other, touch)


def keep_state(state):
    return state


def forward_attention(queries, query_seg, starts, keys, values):
    scale = HEAD_DIM ** (-0.5)
    batch, rows = (queries.shape[0], queries.shape[1])
    query_heads = heads_of(queries)

    def forward_fold(carry, piece, start):
        key_piece, value_piece = piece

        def visit(state, offset, count):
            other, touch = reaches(starts, query_seg, offset, count)

            def compute(state):
                top, total, accum = state
                key_block = heads_of(lax.dynamic_slice_in_dim(key_piece, offset, count, 1))
                value_block = heads_of(lax.dynamic_slice_in_dim(value_piece, offset, count, 1))
                scores = (
                    jnp.einsum(
                        "bqhd,bkhd->bhqk",
                        query_heads,
                        key_block,
                        preferred_element_type=jnp.float32,
                    )
                    * scale
                )
                mask = (query_seg[:, :, None] == other[:, None, :])[:, None]
                scores = jnp.where(mask, scores, NEG)
                new_top = jnp.maximum(top, jnp.max(scores, axis=-1))
                expd = jnp.where(mask, jnp.exp(scores - new_top[..., None]), 0.0)
                factor = jnp.exp(top - new_top)
                total = total * factor + jnp.sum(expd, axis=-1)
                added = jnp.einsum(
                    "bhqk,bkhd->bqhd",
                    expd.astype(jnp.bfloat16),
                    value_block,
                    preferred_element_type=jnp.float32,
                )
                accum = accum * jnp.transpose(factor, (0, 2, 1))[..., None] + added
                return (new_top, total, accum)

            return lax.cond(touch, compute, keep_state, state)

        return block_loop(key_piece.shape[1], carry, visit)

    init = (
        jnp.full((batch, HEADS, rows), NEG, jnp.float32),
        jnp.zeros((batch, HEADS, rows), jnp.float32),
        jnp.zeros((batch, rows, HEADS, HEAD_DIM), jnp.float32),
    )
    whole = (keys, values)
    top, total, accum = forward_fold(
        init,
        (
            lax.all_gather(keys, "ctx", axis=1, tiled=True),
            lax.all_gather(values, "ctx", axis=1, tiled=True),
        ),
        jnp.int32(0),
    )
    mixed = accum / jnp.transpose(total, (0, 2, 1))[..., None]
    return (mixed, top + jnp.log(total), whole)


def query_gradient(queries, query_seg, starts, keys, values, dmixed, logsum, delta):
    scale = HEAD_DIM ** (-0.5)
    query_heads = heads_of(queries)
    grad_heads = heads_of(dmixed)

    def query_fold(carry, piece, start):
        key_piece, value_piece = piece

        def visit(state, offset, count):
            other, touch = reaches(starts, query_seg, offset, count)

            def compute(state):
                key_block = heads_of(lax.dynamic_slice_in_dim(key_piece, offset, count, 1))
                value_block = heads_of(lax.dynamic_slice_in_dim(value_piece, offset, count, 1))
                scores = (
                    jnp.einsum(
                        "bqhd,bkhd->bhqk",
                        query_heads,
                        key_block,
                        preferred_element_type=jnp.float32,
                    )
                    * scale
                )
                mask = (query_seg[:, :, None] == other[:, None, :])[:, None]
                probs = jnp.where(
                    mask, jnp.exp(jnp.where(mask, scores, NEG) - logsum[..., None]), 0.0
                )
                dprobs = jnp.einsum(
                    "bqhd,bkhd->bhqk", grad_heads, value_block, preferred_element_type=jnp.float32
                )
                dscores = (probs * (dprobs - delta[..., None])).astype(jnp.bfloat16)
                return (
                    state
                    + jnp.einsum(
                        "bhqk,bkhd->bqhd", dscores, key_block, preferred_element_type=jnp.float32
                    )
                    * scale
                )

            return lax.cond(touch, compute, keep_state, state)

        return block_loop(key_piece.shape[1], carry, visit)

    init = jnp.zeros(query_heads.shape, jnp.float32)
    return query_fold(
        init,
        (
            lax.all_gather(keys, "ctx", axis=1, tiled=True),
            lax.all_gather(values, "ctx", axis=1, tiled=True),
        ),
        jnp.int32(0),
    )


def key_gradient(keys, values, key_seg, starts, queries, dmixed, logsum, delta):
    scale = HEAD_DIM ** (-0.5)
    key_heads = heads_of(keys)
    value_heads = heads_of(values)
    every_top, every_delta = (
        lax.all_gather(logsum, "ctx", axis=2, tiled=True),
        lax.all_gather(delta, "ctx", axis=2, tiled=True),
    )

    def key_fold(carry, piece, start):
        query_piece, grad_piece = piece

        def visit(state, offset, count):
            other, touch = reaches(starts, key_seg, offset, count)

            def compute(state):
                dkeys, dvalues = state
                query_block = heads_of(lax.dynamic_slice_in_dim(query_piece, offset, count, 1))
                grad_block = heads_of(lax.dynamic_slice_in_dim(grad_piece, offset, count, 1))
                top_block = lax.dynamic_slice_in_dim(every_top, offset, count, 2)
                delta_block = lax.dynamic_slice_in_dim(every_delta, offset, count, 2)
                scores = (
                    jnp.einsum(
                        "bqhd,bkhd->bhqk",
                        query_block,
                        key_heads,
                        preferred_element_type=jnp.float32,
                    )
                    * scale
                )
                mask = (other[:, :, None] == key_seg[:, None, :])[:, None]
                probs = jnp.where(
                    mask, jnp.exp(jnp.where(mask, scores, NEG) - top_block[..., None]), 0.0
                )
                dvalues = dvalues + jnp.einsum(
                    "bhqk,bqhd->bkhd",
                    probs.astype(jnp.bfloat16),
                    grad_block,
                    preferred_element_type=jnp.float32,
                )
                dprobs = jnp.einsum(
                    "bqhd,bkhd->bhqk", grad_block, value_heads, preferred_element_type=jnp.float32
                )
                dscores = (probs * (dprobs - delta_block[..., None])).astype(jnp.bfloat16)
                dkeys = (
                    dkeys
                    + jnp.einsum(
                        "bhqk,bqhd->bkhd", dscores, query_block, preferred_element_type=jnp.float32
                    )
                    * scale
                )
                return (dkeys, dvalues)

            return lax.cond(touch, compute, keep_state, state)

        return block_loop(query_piece.shape[1], carry, visit)

    empty = jnp.zeros(key_heads.shape, jnp.float32)
    return key_fold(
        (empty, empty),
        (
            lax.all_gather(queries, "ctx", axis=1, tiled=True),
            lax.all_gather(dmixed, "ctx", axis=1, tiled=True),
        ),
        jnp.int32(0),
    )


def forward_pass(tokens, starts, weights, base):
    (
        query_weight,
        query_bias,
        key_weight,
        value_weight,
        value_bias,
        out_weight,
        out_bias,
        first_gain,
        first_shift,
        inner_weight,
        inner_bias,
        outer_weight,
        outer_bias,
        second_gain,
        second_shift,
    ) = weights
    rows = tokens.shape[1]
    positions = base + jnp.arange(rows, dtype=jnp.int32)
    query_seg = segment_of(starts, jnp.broadcast_to(positions, (tokens.shape[0], rows)))
    queries = (project(tokens, query_weight) + query_bias.astype(jnp.float32)).astype(jnp.bfloat16)
    keys = project(tokens, key_weight).astype(jnp.bfloat16)
    values = (project(tokens, value_weight) + value_bias.astype(jnp.float32)).astype(jnp.bfloat16)
    mixed, logsum, whole = forward_attention(queries, query_seg, starts, keys, values)
    mixed_low = mixed.reshape(tokens.shape).astype(jnp.bfloat16)
    first_sum = (
        tokens.astype(jnp.float32) + project(mixed_low, out_weight) + out_bias.astype(jnp.float32)
    )
    first = normalize(first_sum, first_gain.astype(jnp.float32), first_shift.astype(jnp.float32))
    first_low = first.astype(jnp.bfloat16)
    inner = project(first_low, inner_weight) + inner_bias.astype(jnp.float32)
    active = gelu(inner).astype(jnp.bfloat16)
    second_sum = first + project(active, outer_weight) + outer_bias.astype(jnp.float32)
    output = normalize(
        second_sum, second_gain.astype(jnp.float32), second_shift.astype(jnp.float32)
    ).astype(jnp.bfloat16)
    saved = (
        tokens,
        query_seg,
        queries,
        keys,
        values,
        mixed,
        logsum,
        mixed_low,
        first_sum,
        first_low,
        inner,
        active,
        second_sum,
        whole,
    )
    return (output, saved)


def backward_pass(saved, starts, weights, cotangent):
    (
        query_weight,
        _,
        key_weight,
        value_weight,
        _,
        out_weight,
        _,
        first_gain,
        first_shift,
        inner_weight,
        _,
        outer_weight,
        _,
        second_gain,
        second_shift,
    ) = weights
    (
        tokens,
        query_seg,
        queries,
        keys,
        values,
        mixed,
        logsum,
        mixed_low,
        first_sum,
        first_low,
        inner,
        active,
        second_sum,
        _,
    ) = saved
    unused, second_back = jax.vjp(
        normalize, second_sum, second_gain.astype(jnp.float32), second_shift.astype(jnp.float32)
    )
    dsecond, dgain_second, dshift_second = second_back(cotangent.astype(jnp.float32))
    douter = dsecond.astype(jnp.bfloat16)
    dactive = project_back(douter, outer_weight)
    unused, gelu_back = jax.vjp(gelu, inner)
    dinner = gelu_back(dactive)[0].astype(jnp.bfloat16)
    dfirst = dsecond + project_back(dinner, inner_weight)
    unused, first_back = jax.vjp(
        normalize, first_sum, first_gain.astype(jnp.float32), first_shift.astype(jnp.float32)
    )
    dfirst_sum, dgain_first, dshift_first = first_back(dfirst)
    dbranch = dfirst_sum.astype(jnp.bfloat16)
    dmixed = project_back(dbranch, out_weight).astype(jnp.bfloat16)
    delta = jnp.einsum("bqhd,bqhd->bhq", heads_of(dmixed).astype(jnp.float32), mixed)
    dqueries = query_gradient(queries, query_seg, starts, keys, values, dmixed, logsum, delta)
    dkeys, dvalues = key_gradient(keys, values, query_seg, starts, queries, dmixed, logsum, delta)
    dqueries = dqueries.reshape(tokens.shape).astype(jnp.bfloat16)
    dkeys = dkeys.reshape(tokens.shape).astype(jnp.bfloat16)
    dvalues = dvalues.reshape(tokens.shape).astype(jnp.bfloat16)
    tokens_grad = (
        dfirst_sum
        + project_back(dqueries, query_weight)
        + project_back(dkeys, key_weight)
        + project_back(dvalues, value_weight)
    )
    sums = (
        outer_sum(tokens, dqueries),
        row_sum(dqueries),
        outer_sum(tokens, dkeys),
        outer_sum(tokens, dvalues),
        row_sum(dvalues),
        outer_sum(mixed_low, dbranch),
        row_sum(dbranch),
        dgain_first,
        dshift_first,
        outer_sum(first_low, dinner),
        row_sum(dinner),
        outer_sum(active, douter),
        row_sum(douter),
        dgain_second,
        dshift_second,
    )
    return (tokens_grad, sums)


def general_device(
    tokens,
    doc_lengths,
    query_weight,
    query_bias,
    key_weight,
    value_weight,
    value_bias,
    out_weight,
    out_bias,
    first_gain,
    first_shift,
    inner_weight,
    inner_bias,
    outer_weight,
    outer_bias,
    second_gain,
    second_shift,
    cotangent,
):
    params = (
        query_weight,
        query_bias,
        key_weight,
        value_weight,
        value_bias,
        out_weight,
        out_bias,
        first_gain,
        first_shift,
        inner_weight,
        inner_bias,
        outer_weight,
        outer_bias,
        second_gain,
        second_shift,
    )
    rows = tokens.shape[2]
    base = lax.axis_index("ctx") * rows
    lengths = doc_lengths[:, 0]
    starts = jnp.cumsum(lengths, axis=-1) - lengths
    outputs = []
    token_parts = []
    sums = None
    for index in range(tokens.shape[0]):
        weights = (
            lax.all_gather(params[0], "wt", axis=0, tiled=True),
            lax.all_gather(params[1], "wt", axis=0, tiled=True),
            lax.all_gather(params[2], "wt", axis=0, tiled=True),
            lax.all_gather(params[3], "wt", axis=0, tiled=True),
            lax.all_gather(params[4], "wt", axis=0, tiled=True),
            lax.all_gather(params[5], "wt", axis=0, tiled=True),
            lax.all_gather(params[6], "wt", axis=0, tiled=True),
            lax.all_gather(params[7], "wt", axis=0, tiled=True),
            lax.all_gather(params[8], "wt", axis=0, tiled=True),
            lax.all_gather(params[9], "wt", axis=0, tiled=True),
            lax.all_gather(params[10], "wt", axis=0, tiled=True),
            lax.all_gather(params[11], "wt", axis=0, tiled=True),
            lax.all_gather(params[12], "wt", axis=0, tiled=True),
            lax.all_gather(params[13], "wt", axis=0, tiled=True),
            lax.all_gather(params[14], "wt", axis=0, tiled=True),
        )
        part_out, saved = forward_pass(
            tokens[index : index + 1, 0], starts[index : index + 1], weights, base
        )
        again = (
            lax.all_gather(params[0], "wt", axis=0, tiled=True),
            lax.all_gather(params[1], "wt", axis=0, tiled=True),
            lax.all_gather(params[2], "wt", axis=0, tiled=True),
            lax.all_gather(params[3], "wt", axis=0, tiled=True),
            lax.all_gather(params[4], "wt", axis=0, tiled=True),
            lax.all_gather(params[5], "wt", axis=0, tiled=True),
            lax.all_gather(params[6], "wt", axis=0, tiled=True),
            lax.all_gather(params[7], "wt", axis=0, tiled=True),
            lax.all_gather(params[8], "wt", axis=0, tiled=True),
            lax.all_gather(params[9], "wt", axis=0, tiled=True),
            lax.all_gather(params[10], "wt", axis=0, tiled=True),
            lax.all_gather(params[11], "wt", axis=0, tiled=True),
            lax.all_gather(params[12], "wt", axis=0, tiled=True),
            lax.all_gather(params[13], "wt", axis=0, tiled=True),
            lax.all_gather(params[14], "wt", axis=0, tiled=True),
        )
        part_grad, part_sums = backward_pass(
            saved, starts[index : index + 1], again, cotangent[index : index + 1, 0]
        )
        outputs.append(part_out)
        token_parts.append(part_grad)
        sums = part_sums if sums is None else jax.tree.map(jnp.add, sums, part_sums)
    output = jnp.concatenate(outputs, axis=0)
    tokens_grad = jnp.concatenate(token_parts, axis=0)
    shards = jax.tree.map(
        lambda part: part.astype(jnp.float32),
        lax.psum_scatter(for_sending(sums), "wt", scatter_dimension=0, tiled=True),
    )
    totals = lax.psum(shards, "ctx")
    return (output[:, None], tokens_grad[:, None]) + tuple(totals)


def flip(value, bits):
    return lax.ppermute(value, "ctx", [(i, i ^ bits) for i in range(8)])


def turn(value, step):
    return lax.ppermute(value, "wt", [(i, (i - step) % 4) for i in range(4)])


def pick(value, index, axis=0):
    return lax.dynamic_index_in_dim(value, index, axis, keepdims=False)


def pair(own, other, bit, axis=0):
    return jnp.where(bit == 0, jnp.stack([own, other], axis), jnp.stack([other, own], axis))


def short(value):
    return value.astype(jnp.bfloat16)


def wide(value):
    return value.astype(jnp.float32)


def dot(left, right):
    return jnp.dot(left, right, preferred_element_type=jnp.float32)


def dot_back(left, right):
    return lax.dot_general(
        left, right, (((1,), (1,)), ((), ())), preferred_element_type=jnp.float32
    )


def dot_sum(left, right):
    return lax.dot_general(
        left, right, (((0,), (0,)), ((), ())), preferred_element_type=jnp.float32
    )


def norm_parts(rows):
    mean = jnp.mean(rows, axis=-1, keepdims=True)
    centered = rows - mean
    spread = jnp.mean(centered * centered, axis=-1, keepdims=True)
    root = lax.rsqrt(spread + EPS)
    return centered * root, root


def norm_back(upstream, normed, root, gain):
    grad = upstream * gain
    mean = jnp.mean(grad, axis=-1, keepdims=True)
    along = jnp.mean(grad * normed, axis=-1, keepdims=True)
    return root * (grad - mean - normed * along)


def gelu_parts(inner):
    rise = 0.5 * (1.0 + lax.erf(inner * ROOT_HALF))
    bell = jnp.exp(-0.5 * inner * inner) * (1.0 / math.sqrt(2.0 * math.pi))
    return inner * rise, rise + inner * bell


def run(kernel, outs, args, scratch=(), scalars=(), specs=None, out_specs=None, aliases=None):
    shapes = tuple(jax.ShapeDtypeStruct(shape, dtype) for shape, dtype in outs)
    whole = pl.BlockSpec(memory_space=pltpu.VMEM)
    in_specs = [pl.BlockSpec(memory_space=pltpu.SMEM)] * len(scalars)
    in_specs += [whole] * len(args) if specs is None else specs
    return pl.pallas_call(
        kernel,
        out_shape=shapes,
        in_specs=in_specs,
        out_specs=tuple([whole] * len(outs) if out_specs is None else out_specs),
        scratch_shapes=list(scratch),
        input_output_aliases=aliases or {},
    )(*scalars, *args)


WHOLE = pl.BlockSpec(memory_space=pltpu.VMEM)
LEFT = pl.BlockSpec(memory_space=pl.ANY)
BF = jnp.bfloat16
F32 = jnp.float32


def where_am_i():
    ctx, own = lax.axis_index("ctx"), lax.axis_index("wt")
    return ctx & 1, (ctx >> 1) & 3, ctx & 3, own


def some_rows(start, count):
    return pl.ds(pl.multiple_of(start, 16), count)


def prepare_heads_kernel(wq, wk, wv, vec, heads_own, heads_send):
    _, quarter, group, _ = where_am_i()
    shard, dim = wq.shape
    width = dim // 4
    for index in range(4):

        @pl.when(group == index)
        def _():
            for slot, ref in enumerate((wq, wk, wv)):
                heads_own[:, slot * width : (slot + 1) * width] = ref[
                    :, index * width : (index + 1) * width
                ]

    part = shard // 2
    heads_send[0:part, :] = heads_own[some_rows((quarter >> 1) * part, part), :]
    heads_send[part:, 0:width] = vec[...]
    heads_send[part:, width:] = jnp.zeros((16, 2 * width), BF)


def prepare_kernel(wo, wi, wo2, w2_send, inner_half, outer_half):
    core, quarter, _, _ = where_am_i()
    shard, dim = wo.shape
    half = wo2.shape[0] // 2
    for index in range(2):

        @pl.when(core == index)
        def _():
            for block in range(4):
                at = block * 2 * half + index * half
                inner_half[:, block * half : (block + 1) * half] = wi[:, at : at + half]
            outer_half[...] = wo2[index * half : (index + 1) * half, :]

    part = shard // 4
    rows = some_rows(quarter * part, part)
    w2_send[0:part, :] = inner_half[rows, 0:dim]
    w2_send[part : 2 * part, :] = inner_half[rows, dim:]
    step = half // 4
    w2_send[2 * part : 2 * part + step, :] = outer_half[some_rows(quarter * step, step), :]
    w2_send[2 * part + step :, :] = wo[rows, :]


CHUNK = 128
WINDOWS = (3, 5, 6, 8)


def chunk_of(ctx, index):
    return ctx ^ ((index >> 2) | (index & 2) | ((index & 1) << 2))


def some_chunks(start, count):
    return pl.ds(pl.multiple_of(start * CHUNK, CHUNK), count * CHUNK)


def over_window(bounds, block, windows, visit):
    if len(windows) == 1:
        visit(pl.ds(0, windows[0] * CHUNK))
        return
    low, count = bounds[0, block], bounds[1, block]
    least = 0
    for size in windows:

        @pl.when((count > least) & (count <= size))
        def _(size=size):
            visit(some_chunks(jnp.minimum(low, windows[-1] - size), size))

        least = size


def attend_rows(qkv, seg_col, seg_row, far, outs, logsum, mixed):
    core, quarter, _, _ = where_am_i()
    group = qkv.shape[0] // 3

    def step(side, carry):
        rows = some_chunks(2 * (2 * side + ((quarter & 1) ^ far)), 2)
        here = some_chunks(2 * side, 2)

        def one_head(head, carry):
            mask = seg_col[rows, :] == seg_row[...]
            scores = dot_back(qkv[head, rows, :], qkv[group + head])
            scores = jnp.where(mask, scores, NEG)
            top = jnp.max(scores, axis=-1, keepdims=True)
            expd = jnp.exp(scores - top)
            total = jnp.sum(expd, axis=-1, keepdims=True)
            probs = short(expd * (1.0 / total))
            mixed[head, here, :] = short(dot(probs, qkv[2 * group + head]))
            lane = lax.broadcasted_iota(jnp.int32, (2 * CHUNK, 128), 1)
            logsum[here, :] = jnp.where(lane == head, top + jnp.log(total), logsum[here, :])
            return carry

        lax.fori_loop(0, group, one_head, 0)
        return carry

    logsum[...] = jnp.zeros_like(logsum)
    lax.fori_loop(0, 2, step, 0)
    y = quarter >> 1
    for index, out in enumerate(outs):
        for side in range(2):
            chunk = 2 * (y ^ side) + (core ^ index)
            for head in range(group):
                out[
                    side * CHUNK : (side + 1) * CHUNK, head * HEAD_DIM : (head + 1) * HEAD_DIM
                ] = mixed[head, some_chunks(chunk, 1), :]


def attend_near_kernel(
    mine, other, far, heads_own, g1, g2, g3, h1, h2, h3, vec, seg_col, seg_row,
    qkv, m0, m1, logsum, weight, vectors, inner_b, mixed, bias,
):
    core, quarter, group, own = where_am_i()
    ctx = lax.axis_index("ctx")
    shard = heads_own.shape[0]
    part = shard // 2
    y = quarter >> 1
    bias[:, shard : 2 * shard] = jnp.zeros_like(bias[:, :shard])
    for index in range(4):

        @pl.when(own == index)
        def _():
            for step, ref, at in ((0, vec, 0), (1, g1, part), (2, g2, part), (3, g3, part)):
                row = (index + step) % 4
                block = wide(ref[at : at + 16, 0:shard])
                lane = row * shard
                vectors[:, lane : lane + shard] = block[0:8]
                lines = jnp.where(core == 0, block[8:10], block[10:12])
                for side in range(2):
                    lane = (2 * row + side) * shard
                    inner_b[:, lane : lane + shard] = lines[side : side + 1]

                @pl.when(group == row)
                def _():
                    bias[:, 0:shard] = block[0:1]
                    bias[:, 2 * shard :] = block[1:2]

    weight[some_rows(own * shard, shard), :] = heads_own[...]
    for step, near_half, far_half in ((1, g1, h1), (2, g2, h2), (3, g3, h3)):
        at = ((own + step) & 3) * shard
        weight[some_rows(at + part * y, part), :] = near_half[0:part, :]
        weight[some_rows(at + part * (1 - y), part), :] = far_half[0:part, :]
    index = 0
    for source in (mine, other, far):
        for first in range(0, source.shape[0], 2 * CHUNK):
            low = short(dot(source[first : first + 2 * CHUNK, :], weight[...]) + bias[...])
            for half in range(2):
                at = pl.multiple_of(chunk_of(ctx, index) * CHUNK, CHUNK)
                for slot in range(qkv.shape[0]):
                    value = low[
                        half * CHUNK : (half + 1) * CHUNK,
                        slot * HEAD_DIM : (slot + 1) * HEAD_DIM,
                    ]
                    if slot < qkv.shape[0] // 3:
                        value = value * jnp.asarray(HEAD_DIM ** (-0.5), BF)
                    qkv[slot, pl.ds(at, CHUNK), :] = value
                index += 1
    attend_rows(qkv, seg_col, seg_row, 0, (m0, m1), logsum, mixed)


def attend_far_kernel(qkv, seg_col, seg_row, m2, m3, logsum, mixed):
    attend_rows(qkv, seg_col, seg_row, 1, (m2, m3), logsum, mixed)


def project_kernel(m0, m1, m2, m3, mine, vec, wo, *refs):
    pieces, (first_sum, first_low, out_full, sems) = refs[:12], refs[12:]
    _, quarter, group, own = where_am_i()
    shard = wo.shape[0]
    part = shard // 4
    copies = [(wo, out_full.at[some_rows(own * shard, shard), :])]
    for index, piece in enumerate(pieces):
        at = ((own + 1 + index // 4) & 3) * shard + part * (quarter ^ (index % 4))
        rows = piece.shape[0]
        copies.append((piece.at[rows - part : rows, :], out_full.at[some_rows(at, part), :]))
    copies = [
        pltpu.make_async_copy(source, target, sems.at[index])
        for index, (source, target) in enumerate(copies)
    ]
    for copy in copies:
        copy.start()
    total = wide(mine[...]) + vec[2:3, :]
    for copy in copies:
        copy.wait()
    for code, ref in enumerate((m0, m1, m2, m3)):
        total += dot(ref[...], out_full[some_rows((group ^ code) * shard, shard), :])
    first_sum[...] = total
    first_low[...] = short(norm_parts(total)[0] * vec[3:4, :] + vec[4:5, :])


def forward_kernel(near, far, bias, inner_half, outer_half, *refs):
    pieces, (keep, send, slope, active, wi_full, wo2_full, wi, wo2, sems) = refs[:12], refs[12:]
    _, quarter, _, own = where_am_i()
    shard, half = inner_half.shape[0], outer_half.shape[0]
    dim = keep.shape[1]
    part, step = shard // 4, half // 4
    first = [(inner_half, wi.at[some_rows(own * shard, shard), :])]
    second = [(outer_half, wo2.at[some_rows(own * half, half), :])]
    for index, piece in enumerate(pieces):
        row, spot = (own + 1 + index // 4) & 3, quarter ^ (index % 4)
        rows = some_rows(row * shard + part * spot, part)
        for side in range(2):
            first.append(
                (
                    piece.at[side * part : (side + 1) * part, :],
                    wi.at[rows, side * dim : (side + 1) * dim],
                )
            )
        rows = some_rows(row * half + step * spot, step)
        second.append((piece.at[2 * part : 2 * part + step, :], wo2.at[rows, :]))
    copies = [
        pltpu.make_async_copy(source, target, sems.at[index])
        for index, (source, target) in enumerate(first + second)
    ]
    for copy in copies:
        copy.start()
    for copy in copies[: len(first)]:
        copy.wait()
    back = [
        pltpu.make_async_copy(wi, wi_full, sems.at[len(copies)]),
        pltpu.make_async_copy(wo2, wo2_full, sems.at[len(copies) + 1]),
    ]
    back[0].start()
    count = near.shape[0]
    chunk = 512
    waiting = True
    for index, (source, out) in enumerate(((far, send), (near, keep))):
        at = (1 - index) * count
        total = None
        for lane in range(0, slope.shape[1], chunk):
            lanes = slice(lane, lane + chunk)
            value, rate = gelu_parts(dot(source[...], wi[:, lanes]) + bias[:, lanes])
            low = short(value)
            slope[at : at + count, lanes] = short(rate)
            active[at : at + count, lanes] = low
            if waiting:
                for copy in copies[len(first) :]:
                    copy.wait()
                back[1].start()
                waiting = False
            added = dot(low, wo2[lanes, :])
            total = added if total is None else total + added
        out[...] = total
    for copy in back:
        copy.wait()


def turnaround_kernel(first_sum, keep, got, vec, cot0, cot1, out0, out1, dsecond, douter, sums):
    rows = cot0.shape[0]
    first = norm_parts(first_sum[...])[0] * vec[3:4, :] + vec[4:5, :]
    normed, root = norm_parts(first + vec[5:6, :] + keep[...] + got[...])
    output = short(normed * vec[6:7, :] + vec[7:8, :])
    out0[...] = output[:rows]
    out1[...] = output[rows:]
    upstream = jnp.concatenate([wide(cot0[...]), wide(cot1[...])])
    back = norm_back(upstream, normed, root, vec[6:7, :])
    low = short(back)
    dsecond[...] = back
    douter[...] = low
    sums[0:1, :] = jnp.sum(wide(low), axis=0, keepdims=True)
    sums[1:2, :] = jnp.sum(upstream * normed, axis=0, keepdims=True)
    sums[2:3, :] = jnp.sum(upstream, axis=0, keepdims=True)
    sums[3:, :] = jnp.zeros_like(sums[3:, :])


def backward_kernel(near, far, slope, wo2, wi_full, keep, send, dinner, sums, wi, sem):
    copy = pltpu.make_async_copy(wi_full, wi, sem)
    copy.start()
    count, dim = near.shape
    chunk = 512
    waiting = True
    for index, (source, out) in enumerate(((far, send), (near, keep))):
        at = (1 - index) * count
        total = None
        for lane in range(0, slope.shape[1], chunk):
            lanes = slice(lane, lane + chunk)
            rate = wide(slope[at : at + count, lanes])
            low = short(dot_back(source[...], wo2[lanes, :]) * rate)
            dinner[at : at + count, lanes] = low
            if waiting:
                copy.wait()
                waiting = False
            added = dot_back(low, wi[:, lanes])
            total = added if total is None else total + added
        out[...] = total
    total = jnp.sum(wide(dinner[...]), axis=0, keepdims=True)
    sums[0:1, :] = total[:, :dim]
    sums[1:2, :] = total[:, dim:]
    sums[2:, :] = jnp.zeros_like(sums[2:, :])


def weights_kernel(
    first0, first1, dinner, douter0, douter1, active, ak, az, bk, bz, left, right, held, grads, sems
):
    _, quarter, _, _ = where_am_i()
    x, y = quarter & 1, quarter >> 1
    count = first0.shape[0]
    part, step = first0.shape[1] // 16, active.shape[1] // 16
    loads = [
        pltpu.make_async_copy(source, target, sems.at[index])
        for index, (source, target) in enumerate(
            ((active, held), (douter0, grads.at[:count, :]), (douter1, grads.at[count:, :]))
        )
    ]
    for copy in loads:
        copy.start()
    left[...] = short(dot_sum(first0[...], dinner[:count]) + dot_sum(first1[...], dinner[count:]))
    stores = []
    for block in range(8):
        rows = slice(block * part, (block + 1) * part)
        for ref, side in ((ak, x), (az, 1 - x)):
            take = some_rows((2 * block + side) * part, part)
            at = 3 + len(stores)
            stores.append(pltpu.make_async_copy(left.at[take, :], ref.at[rows, :], sems.at[at]))
            stores[-1].start()
    for copy in loads:
        copy.wait()
    right[...] = short(dot_sum(held[...], grads[...]))
    for block in range(8):
        row, side = block // 2, block % 2
        rows = slice(block * step, (block + 1) * step)
        for ref, place in ((bk, y), (bz, 1 - y)):
            take = some_rows((4 * row + 2 * place + side) * step, step)
            at = 3 + len(stores)
            stores.append(pltpu.make_async_copy(right.at[take, :], ref.at[rows, :], sems.at[at]))
            stores[-1].start()
    for copy in stores:
        copy.wait()


def branch_kernel(first_sum, dsecond, keep, got, vec, out_full, dfirst_sum, dbranch, d0, d1, d2, d3, sums):
    _, _, group, _ = where_am_i()
    shard = d0.shape[1]
    normed, root = norm_parts(first_sum[...])
    dfirst = dsecond[...] + keep[...] + got[...]
    back = norm_back(dfirst, normed, root, vec[3:4, :])
    low = short(back)
    dfirst_sum[...] = back
    dbranch[...] = low
    for code, ref in enumerate((d0, d1, d2, d3)):
        ref[...] = short(dot_back(low, out_full[some_rows((group ^ code) * shard, shard), :]))
    sums[0:1, :] = jnp.sum(wide(low), axis=0, keepdims=True)
    sums[1:2, :] = jnp.sum(dfirst * normed, axis=0, keepdims=True)
    sums[2:3, :] = jnp.sum(dfirst, axis=0, keepdims=True)
    sums[3:, :] = jnp.zeros_like(sums[3:, :])


def out_weight_kernel(m0, m1, m2, m3, dbranch, sums1, sums2, sums3, ck, cz, whole):
    core, _, group, _ = where_am_i()
    shard, dim = m0.shape[1], dbranch.shape[1]
    half = dim // 2
    for code, ref in enumerate((m0, m1, m2, m3)):
        whole[some_rows((group ^ code) * shard, shard), :] = short(
            dot_sum(ref[...], dbranch[...])
        )
    for side in range(2):

        @pl.when(core == side)
        def _():
            for ref, which in ((ck, side), (cz, 1 - side)):
                ref[0:dim, :] = whole[:, which * half : (which + 1) * half]

    rows = short(
        jnp.concatenate([sums1[0:3, :], sums2[0:3, :], sums3[0:2, :], jnp.zeros_like(sums1[...])])
    )
    for ref in (ck, cz):
        ref[dim : dim + 16, :] = rows[:, :half]
        ref[dim + 16 :, :] = rows[:, half:]


def out_split_kernel(packed, got, ck, cz):
    core, quarter, _, _ = where_am_i()
    x = quarter & 1
    dim = packed.shape[0] - 32
    part = dim // 16
    for block in range(8):
        rows = slice(block * part, (block + 1) * part)
        for ref, side in ((ck, x), (cz, 1 - x)):
            take = some_rows((2 * block + side) * part, part)
            ref[rows, :] = short(wide(packed[take, :]) + wide(got[take, :]))
    for lanes in range(2):
        at = dim + 16 * lanes
        mine, other = wide(packed[at : at + 16, :]), wide(got[at : at + 16, :])
        low = jnp.where(core == 0, mine, other)[6:8]
        high = jnp.where(core == 0, other, mine)[6:8]
        rows = jnp.concatenate([(mine + other)[0:6], low, high, jnp.zeros_like(mine[0:6])])
        at = 8 * part + 16 * lanes
        for ref in (ck, cz):
            ref[at : at + 16, :] = short(rows)


def reduce_rows(keep, got, outs, bit):
    size = keep.shape[0] // 8
    size -= size % 16
    width = keep.shape[1] // len(outs)
    for lane, pair_of in enumerate(outs):
        lanes = slice(lane * width, (lane + 1) * width)
        for block in range(4):
            for out, side in zip(pair_of, (bit, 1 - bit)):
                take = some_rows((2 * block + side) * size, size)
                out[block * size : (block + 1) * size, :] = short(
                    wide(keep[take, lanes]) + wide(got[take, lanes])
                )
        if keep.shape[0] > 8 * size:
            for out in pair_of:
                out[4 * size :, :] = short(
                    wide(keep[8 * size :, lanes]) + wide(got[8 * size :, lanes])
                )


def reduce_kernel(ak, ar, bk, br, *outs):
    _, quarter, _, _ = where_am_i()
    reduce_rows(ak, ar, (outs[0:2], outs[4:6]), quarter >> 1)
    reduce_rows(bk, br, (outs[2:4], outs[6:8]), quarter & 1)


def reduce_out_kernel(ck, cr, c2k, c2z):
    _, quarter, _, _ = where_am_i()
    reduce_rows(ck, cr, ((c2k, c2z),), quarter >> 1)


def owners_kernel(*refs):
    inputs, outs = refs[:-4], refs[-4:]
    _, _, _, own = where_am_i()
    ak, ar, bk, br = inputs[:4]
    half = bk.shape[1]
    part = ak.shape[0] // 4
    for index, out in enumerate(outs):
        row = (own - index) & 3
        rows = some_rows(row * part, part)
        out[0:part, :] = (wide(ak[rows, :]) + wide(ar[rows, :])).astype(out.dtype)
        for side in range(2):
            rows = some_rows((2 * row + side) * part, part)
            out[part : 2 * part, side * half : (side + 1) * half] = (
                wide(bk[rows, :]) + wide(br[rows, :])
            ).astype(out.dtype)
        if len(inputs) > 4:
            ck, cr = inputs[4:]
            at = 2 * part
            rows = some_rows(row * part, part)
            out[at:, 0:half] = (wide(ck[rows, :]) + wide(cr[rows, :])).astype(out.dtype)
            tail = wide(ck[4 * part :, :]) + wide(cr[4 * part :, :])
            out[at : at + 32, half:] = tail.astype(out.dtype)
            out[at + 32 :, half:] = jnp.zeros((part - 32, half), out.dtype)


def total_kernel(mine, *refs):
    total = wide(mine[...])
    for ref in refs[:-1]:
        total += wide(ref[...])
    refs[-1][...] = short(total)


def finish_rows(pieces, part, half, spread):
    core, quarter, _, _ = where_am_i()
    dwi, dwo2, dwo = spread
    for side in range(2):

        @pl.when(core == side)
        def _():
            for index, piece in enumerate(pieces):
                spot = quarter ^ (index % 4)
                which = side if index < 4 else 1 - side
                rows = some_rows(spot * part, part)
                for block in range(2):
                    at = block * 2 * half + which * half
                    dwi[rows, at : at + half] = wide(piece[0:part, block * half : (block + 1) * half])
                    at = which * half + spot * 2 * part + block * part
                    dwo2[some_rows(at, part), :] = wide(
                        piece[part : 2 * part, block * half : (block + 1) * half]
                    )
                if dwo is not None:
                    dwo[rows, which * half : (which + 1) * half] = wide(piece[2 * part :, 0:half])


def send_lane(lane, dwi, dwo2, wi_out, wo2_out, sems):
    width, half = dwi.shape[1], dwo2.shape[1]
    copies = [
        pltpu.make_async_copy(dwi, wi_out.at[:, lane * width : (lane + 1) * width], sems.at[0]),
        pltpu.make_async_copy(dwo2, wo2_out.at[:, lane * half : (lane + 1) * half], sems.at[1]),
    ]
    for copy in copies:
        copy.start()
    for copy in copies:
        copy.wait()


def finish_first_kernel(*refs):
    pieces, (wi_out, wo2_out, dwi, dwo2, sems) = refs[:8], refs[8:]
    part, half = dwi.shape[0] // 4, dwo2.shape[1]
    finish_rows(pieces, part, half, (dwi, dwo2, None))
    send_lane(0, dwi, dwo2, wi_out, wo2_out, sems)


def finish_kernel(*refs):
    pieces, (unused0, unused1, wi_out, wo2_out, dwo, small, dwi, dwo2, sems) = refs[:8], refs[8:]
    part, half = dwi.shape[0] // 4, dwo2.shape[1]
    finish_rows(pieces, part, half, (dwi, dwo2, dwo))
    last = pieces[0]
    small[:, 0:half] = wide(last[2 * part : 2 * part + 16, half:])
    small[:, half:] = wide(last[2 * part + 16 : 2 * part + 32, half:])
    send_lane(1, dwi, dwo2, wi_out, wo2_out, sems)


def attend_back_kernel(
    bounds, qkv, logsum0, logsum1, seg_col, seg_row, p0, p1, p2, p3, mine_in, other_in, far_in,
    h0, h1, h2, h3, grads, dqueries, dkeys, dvalues, dweight, dmixed, logsum, whole, tokens, sems,
):
    _, quarter, _, own = where_am_i()
    ctx = lax.axis_index("ctx")
    x = quarter & 1
    scale = HEAD_DIM ** (-0.5)
    group = qkv.shape[0] // 3
    width = group * HEAD_DIM
    block = p0.shape[0]
    loads = [
        pltpu.make_async_copy(source, tokens.at[at : at + source.shape[0], :], sems.at[index])
        for index, (source, at) in enumerate(((mine_in, 0), (other_in, block), (far_in, 2 * block)))
    ]
    for copy in loads:
        copy.start()
    dkeys[...] = jnp.zeros_like(dkeys)
    dvalues[...] = jnp.zeros_like(dvalues)
    for index, part in enumerate((p0, p2, p1, p3)):
        for side in range(2):
            chunk = chunk_of(ctx, 2 * index + side)
            for head in range(group):
                dmixed[head, some_chunks(chunk, 1), :] = part[
                    side * CHUNK : (side + 1) * CHUNK, head * HEAD_DIM : (head + 1) * HEAD_DIM
                ]
    for side in range(2):
        rows = slice(2 * side * CHUNK, 2 * (side + 1) * CHUNK)
        logsum[some_chunks(2 * (2 * side + x), 2), :] = logsum0[rows, :]
        logsum[some_chunks(2 * (2 * side + 1 - x), 2), :] = logsum1[rows, :]

    def step(index, carry):
        rows = some_chunks(2 * index, 2)

        def visit(window):
            def one_head(head, carry):
                mask = seg_col[rows, :] == seg_row[:, window]
                query = qkv[head, rows, :]
                grad = dmixed[head, rows, :]
                keys = qkv[group + head, window, :]
                lane = lax.broadcasted_iota(jnp.int32, (2 * CHUNK, 128), 1)
                sums = jnp.sum(
                    jnp.where(lane == head, logsum[rows, :], 0.0), axis=-1, keepdims=True
                )
                scores = jnp.where(mask, dot_back(query, keys), NEG)
                probs = jnp.exp(scores - sums)
                dprobs = dot_back(grad, qkv[2 * group + head, window, :])
                delta = jnp.sum(probs * dprobs, axis=-1, keepdims=True)
                dscores = short(probs * (dprobs - delta))
                dqueries[head, rows, :] = short(dot(dscores, keys) * scale)
                dkeys[head, window, :] += dot_sum(dscores, query)
                dvalues[head, window, :] += dot_sum(short(probs), grad)
                return carry

            lax.fori_loop(0, group, one_head, 0)

        over_window(bounds, index, WINDOWS, visit)
        return carry

    lax.fori_loop(0, 4, step, 0)
    for head in range(group):
        whole[:, head * HEAD_DIM : (head + 1) * HEAD_DIM] = dqueries[head]
        at = width + head * HEAD_DIM
        whole[:, at : at + HEAD_DIM] = short(dkeys[head])
        whole[:, at + width : at + width + HEAD_DIM] = short(dvalues[head])
    for index in range(8):
        grads[index * CHUNK : (index + 1) * CHUNK, :] = whole[
            some_chunks(chunk_of(ctx, index), 1), :
        ]
    for copy in loads:
        copy.wait()
    dweight[...] = dot_sum(tokens[...], grads[...])
    sums = jnp.sum(wide(grads[...]), axis=0, keepdims=True)
    lines = sums.shape[1] // HEAD_DIM
    for index, out in enumerate((h0, h1, h2, h3)):
        take = pl.ds(pl.multiple_of(((own - index) & 3) * width, 16), width)
        out[:, 0 : 3 * width] = dweight[take, :].astype(out.dtype)
        out[:, 3 * width :] = jnp.zeros((width, HEAD_DIM), out.dtype)
        for line in range(lines):
            out[line : line + 1, 3 * width :] = sums[
                :, line * HEAD_DIM : (line + 1) * HEAD_DIM
            ].astype(out.dtype)


def tokens_kernel(grads, weight, keep, send):
    rows = keep.shape[0]
    keep[...] = dot_back(grads[:rows], weight[...])
    send[...] = short(dot_back(grads[rows:], weight[...]))


def merge_kernel(keep, got, base, near, far):
    total = keep[...] + wide(got[...])
    count = near.shape[0]
    near[...] = total[:count] + base[...]
    far[...] = short(total[count:])


def heads_kernel(s0, s1, s2, s3, dq, dk, dv, bias):
    _, _, group, own = where_am_i()
    shard = dq.shape[0]
    for index in range(4):

        @pl.when(group == index)
        def _():
            for code, ref in enumerate((s0, s1, s2, s3)):
                at = (index ^ code) * shard
                for slot, out in enumerate((dq, dk, dv)):
                    out[:, at : at + shard] = wide(
                        ref[0:shard, slot * shard : (slot + 1) * shard]
                    )

                @pl.when(own == index ^ code)
                def _():
                    for line in range(bias.shape[1] // HEAD_DIM):
                        bias[0:1, line * HEAD_DIM : (line + 1) * HEAD_DIM] = wide(
                            ref[line : line + 1, 3 * shard :]
                        )


def plane_steps(
    tokens,
    doc_lengths,
    query_weight,
    query_bias,
    key_weight,
    value_weight,
    value_bias,
    out_weight,
    out_bias,
    first_gain,
    first_shift,
    inner_weight,
    inner_bias,
    outer_weight,
    outer_bias,
    second_gain,
    second_shift,
    cotangent,
):
    ctx, own = lax.axis_index("ctx"), lax.axis_index("wt")
    y = ctx >> 2
    rows, dim = tokens.shape[2], tokens.shape[3]
    shard = query_weight.shape[0]
    hidden = outer_weight.shape[0]
    half = hidden // 2
    count = 2 * rows

    mine = jnp.concatenate([pick(tokens[:, 0], y), flip(pick(tokens[:, 0], 1 - y), 4)])
    other = flip(mine, 2)
    far = flip(jnp.concatenate([mine, other]), 1)

    vector_list = (
        query_bias,
        value_bias,
        out_bias,
        first_gain,
        first_shift,
        outer_bias,
        second_gain,
        second_shift,
        *[inner_bias[at : at + shard] for at in range(0, 4 * shard, shard)],
    )
    line = lax.broadcasted_iota(jnp.int32, (16, shard), 0)
    vec = jnp.zeros((16, shard), BF)
    for index, value in enumerate(vector_list):
        vec = jnp.where(line == index, value[None, :], vec)
    heads_own, heads_send = run(
        prepare_heads_kernel,
        [((shard, 3 * shard), BF), ((shard // 2 + 16, 3 * shard), BF)],
        (query_weight, key_weight, value_weight, vec),
    )
    w2_send, inner_half, outer_half = run(
        prepare_kernel,
        [((shard // 4 * 3 + half // 4, dim), BF), ((shard, 4 * half), BF), ((half, dim), BF)],
        (out_weight, inner_weight, outer_weight),
    )
    got = [turn(heads_send, step) for step in (1, 2, 3)]
    gone = [flip(value, 4) for value in got]
    pieces = []
    for step in (1, 2, 3):
        piece = turn(w2_send, step)
        pieces += [piece] + [flip(piece, bits) for bits in (2, 4, 6)]

    lengths = pick(doc_lengths[:, 0], y)
    starts = jnp.cumsum(lengths) - lengths
    total = 8 * rows
    positions = jnp.arange(total, dtype=jnp.int32)
    seg = jnp.sum((starts[None, :] <= positions[:, None]).astype(jnp.int32), axis=-1) - 1
    segs = (seg[:, None], seg[None, :])
    first = jnp.arange(4, dtype=jnp.int32)[:, None] * (2 * CHUNK)
    low = jnp.max(jnp.where(starts[None, :] <= first, starts[None, :], 0), axis=-1) // CHUNK
    ends = jnp.where(starts[None, :] >= first + 2 * CHUNK, starts[None, :], total)
    bounds = jnp.stack([low, (jnp.min(ends, axis=-1) - 1) // CHUNK - low + 1])

    qkv, m0, m1, logsum0, heads_weight, vectors, inner_b = run(
        attend_near_kernel,
        [
            ((9, total, HEAD_DIM), BF),
            ((count, shard), BF),
            ((count, shard), BF),
            ((2 * count, 128), F32),
            ((dim, 3 * shard), BF),
            ((8, dim), F32),
            ((1, 4 * half), F32),
        ],
        (mine, other, far, heads_own, *got, *gone, vec, *segs),
        [pltpu.VMEM((3, 2 * count, HEAD_DIM), BF), pltpu.VMEM((1, 3 * shard), F32)],
    )
    m2, m3, logsum1 = run(
        attend_far_kernel,
        [((count, shard), BF), ((count, shard), BF), ((2 * count, 128), F32)],
        (qkv, *segs),
        [pltpu.VMEM((3, 2 * count, HEAD_DIM), BF)],
    )
    mixed = [m0, flip(m1, 1), flip(m2, 2), flip(m3, 3)]

    first_sum, first_low, out_full = run(
        project_kernel,
        [((count, dim), F32), ((count, dim), BF), ((dim, dim), BF)],
        (*mixed, mine, vectors, out_weight, *pieces),
        [pltpu.SemaphoreType.DMA((13,))],
        specs=[WHOLE] * 6 + [LEFT] * 13,
    )
    first_far = flip(first_low, 1)
    keep, send, slope, active, wi_full, wo2_full = run(
        forward_kernel,
        [
            ((count, dim), F32),
            ((count, dim), F32),
            ((2 * count, 4 * half), BF),
            ((2 * count, 4 * half), BF),
            ((dim, 4 * half), BF),
            ((4 * half, dim), BF),
        ],
        (first_low, first_far, inner_b, inner_half, outer_half, *pieces),
        [
            pltpu.VMEM((dim, 4 * half), BF),
            pltpu.VMEM((4 * half, dim), BF),
            pltpu.SemaphoreType.DMA((40,)),
        ],
        specs=[WHOLE] * 3 + [LEFT] * 14,
        out_specs=[WHOLE] * 4 + [LEFT] * 2,
    )
    cot = pick(cotangent[:, 0], y), flip(pick(cotangent[:, 0], 1 - y), 4)
    out0, out1, dsecond, douter, sums2 = run(
        turnaround_kernel,
        [
            ((rows, dim), BF),
            ((rows, dim), BF),
            ((count, dim), F32),
            ((count, dim), BF),
            ((8, dim), F32),
        ],
        (first_sum, keep, flip(send, 1), vectors, *cot),
    )
    output = pair(out0, flip(out1, 4), y)

    douter_far = flip(douter, 1)
    keep, send, dinner, sums3 = run(
        backward_kernel,
        [
            ((count, dim), F32),
            ((count, dim), F32),
            ((2 * count, 4 * half), BF),
            ((8, dim), F32),
        ],
        (douter, douter_far, slope, wo2_full, wi_full),
        [pltpu.VMEM((dim, 4 * half), BF), pltpu.SemaphoreType.DMA],
        specs=[WHOLE] * 4 + [LEFT],
    )
    dfirst_sum, dbranch, d0, d1, d2, d3, sums1 = run(
        branch_kernel,
        [((count, dim), F32), ((count, dim), BF)] + [((count, shard), BF)] * 4 + [((8, dim), F32)],
        (first_sum, dsecond, keep, flip(send, 1), vectors, out_full),
    )
    dmixed = [d0, flip(d1, 1), flip(d2, 2), flip(d3, 3)]

    ak, az, bk, bz = run(
        weights_kernel,
        [((dim // 2, 4 * half), BF)] * 2 + [((2 * half, dim), BF)] * 2,
        (first_low, first_far, dinner, douter, douter_far, active),
        [
            pltpu.VMEM((dim, 4 * half), BF),
            pltpu.VMEM((4 * half, dim), BF),
            pltpu.VMEM((2 * count, 4 * half), BF),
            pltpu.VMEM((2 * count, dim), BF),
            pltpu.SemaphoreType.DMA((35,)),
        ],
        specs=[WHOLE] * 3 + [LEFT] * 3,
        out_specs=[LEFT] * 4,
    )
    ar, br = flip(az, 2), flip(bz, 4)
    ck, cz = run(
        out_weight_kernel,
        [((dim + 32, dim // 2), BF)] * 2,
        (*mixed, dbranch, sums1, sums2, sums3),
        [pltpu.VMEM((dim, dim), BF)],
    )
    ck, cz = run(out_split_kernel, [((dim // 2 + 32, dim // 2), BF)] * 2, (ck, flip(cz, 1)))
    cr = flip(cz, 2)

    h0, h1, h2, h3, grads = run(
        attend_back_kernel,
        [((shard, 3 * shard + HEAD_DIM), F32)]
        + [((shard, 3 * shard + HEAD_DIM), BF)] * 3
        + [((4 * count, 3 * shard), BF)],
        (qkv, logsum0, logsum1, *segs, *dmixed, mine, other, far),
        [
            pltpu.VMEM((3, 4 * count, HEAD_DIM), BF),
            pltpu.VMEM((3, 4 * count, HEAD_DIM), F32),
            pltpu.VMEM((3, 4 * count, HEAD_DIM), F32),
            pltpu.VMEM((dim, 3 * shard), F32),
            pltpu.VMEM((3, total, HEAD_DIM), BF),
            pltpu.VMEM((total, 128), F32),
            pltpu.VMEM((total, 3 * shard), BF),
            pltpu.VMEM((total, dim), BF),
            pltpu.SemaphoreType.DMA((3,)),
        ],
        scalars=(bounds,),
        specs=[WHOLE] * 9 + [LEFT] * 3,
    )
    keep, send = run(
        tokens_kernel, [((2 * count, dim), F32), ((2 * count, dim), BF)], (grads, heads_weight)
    )

    c2k, c2z = run(reduce_out_kernel, [((dim // 4 + 32, dim // 2), BF)] * 2, (ck, cr))
    reduced = run(
        reduce_kernel,
        ([((dim // 4, 2 * half), BF)] * 2 + [((half, dim // 2), BF)] * 2) * 2,
        (ak, ar, bk, br),
    )
    plane = []
    for lane in range(2):
        a2k, a2z, b2k, b2z = reduced[4 * lane : 4 * lane + 4]
        last = [a2k, flip(a2z, 4), b2k, flip(b2z, 2)]
        size = shard // 4 * 2
        if lane == 1:
            last += [c2k, flip(c2z, 4)]
            size = shard // 4 * 3
        p0, p1, p2, p3 = run(owners_kernel, [((size, dim), F32)] + [((size, dim), BF)] * 3, last)
        turned = [turn(p, step) for step, p in ((1, p1), (2, p2), (3, p3))]
        (piece,) = run(total_kernel, [((size, dim), BF)], (p0, *turned))
        near = [piece] + [flip(piece, bits) for bits in (2, 4, 6)]
        plane.append(near + [flip(p, 1) for p in near])
    staged = [
        pltpu.VMEM((shard, 4 * half), F32),
        pltpu.VMEM((hidden, half), F32),
        pltpu.SemaphoreType.DMA((2,)),
    ]
    grown = [((shard, 8 * half), F32), ((hidden, dim), F32)]
    first_lane = run(finish_first_kernel, grown, plane[0], staged, out_specs=[LEFT] * 2)
    dinner_w, douter_w, dout_w, small = run(
        finish_kernel,
        grown + [((shard, dim), F32), ((16, dim), F32)],
        (*plane[1], *first_lane),
        staged,
        specs=[WHOLE] * 8 + [LEFT] * 2,
        out_specs=[LEFT] * 2 + [WHOLE] * 2,
        aliases={8: 0, 9: 1},
    )
    dinner_b = pick(small[6:10].reshape(2, 4, half), own, 1).reshape(hidden)
    small = lax.dynamic_slice_in_dim(small[:6], own * shard, shard, 1)

    (heads,) = run(
        total_kernel,
        [((shard, 3 * shard + HEAD_DIM), BF)],
        (h0, turn(h1, 1), turn(h2, 2), turn(h3, 3)),
    )
    (heads,) = run(total_kernel, [((shard, 3 * shard + HEAD_DIM), BF)], (heads, flip(heads, 4)))
    dquery_w, dkey_w, dvalue_w, heads_b = run(
        heads_kernel,
        [((shard, dim), F32)] * 3 + [((8, 3 * shard), F32)],
        (heads, flip(heads, 1), flip(heads, 2), flip(heads, 3)),
    )

    near_t, far_t = run(
        merge_kernel, [((count, dim), F32), ((count, dim), BF)], (keep, flip(send, 1), dfirst_sum)
    )
    dtokens = near_t + wide(flip(far_t, 2))
    swapped = flip(short(dtokens[rows:]), 4)
    tokens_grad = pair(dtokens[:rows], wide(swapped), y)

    return (
        output[:, None],
        tokens_grad[:, None],
        dquery_w,
        heads_b[0, :shard],
        dkey_w,
        dvalue_w,
        heads_b[0, 2 * shard :],
        dout_w,
        small[0],
        small[1],
        small[2],
        dinner_w,
        dinner_b,
        douter_w,
        small[3],
        small[4],
        small[5],
    )


def plane_device(*args):
    return plane_steps(*args)


def solution(mesh):
    placed = (
        P(None, "wt", "ctx", None),
        P(None, "wt", None),
        P("wt", None),
        P("wt"),
        P("wt", None),
        P("wt", None),
        P("wt"),
        P("wt", None),
        P("wt"),
        P("wt"),
        P("wt"),
        P("wt", None),
        P("wt"),
        P("wt", None),
        P("wt"),
        P("wt"),
        P("wt"),
        P(None, "wt", "ctx", None),
    )
    fits = mesh.shape["ctx"] == 8 and mesh.shape["wt"] == 4
    return jax.shard_map(
        plane_device if fits else general_device,
        mesh=mesh,
        in_specs=placed,
        out_specs=(
            P(None, "wt", "ctx", None),
            P(None, "wt", "ctx", None),
            P("wt", None),
            P("wt"),
            P("wt", None),
            P("wt", None),
            P("wt"),
            P("wt", None),
            P("wt"),
            P("wt"),
            P("wt"),
            P("wt", None),
            P("wt"),
            P("wt", None),
            P("wt"),
            P("wt"),
            P("wt"),
        ),
        check_vma=False,
    )
```
